32 devices in a mesh: seq: 8 (over y, x, core), head: 4 (over z).
Axes of the slice: x: 2, y: 2, z: 4, core: 2. Of those that a mesh axis runs over, the one named last changes fastest.
Arguments:
- image_rows: bfloat16 [8192, 1536], P('seq'), may hold values from -6 to 6
- condition: bfloat16 [4, 1024], replicated, may hold values from -6 to 6
- text_feats: bfloat16 [2048, 4096], P('seq'), may hold values from -6 to 6
- grid_shape: int32 [4, 2], replicated, may hold values from 11 to 128, as said below
- text_slot: int32 [4], replicated, may hold values from 0 to 7, as said below
- attn_gain: float32 [1536], replicated, may hold values from 0.1 to 1.9
- ffn_gain: float32 [1536], replicated, may hold values from 0.1 to 1.9
- mod_weight: bfloat16 [1024, 6144], P(None, 'head'), may hold values from -0.1875 to 0.1875
- mod_bias: float32 [4, 1536], P('head'), may hold values from -3 to 3
- qkv_weight: bfloat16 [1536, 3, 1536], P(None, None, 'head'), may hold values from -0.15625 to 0.15625
- qk_gains: float32 [3, 24, 64], P(None, 'head'), may hold values from 0.1 to 1.9
- text_kv_weight: bfloat16 [4096, 2, 1536], P(None, None, 'head'), may hold values from -0.09375 to 0.09375
- cross_gate: float32 [24], P('head'), may hold values from 0.3 to 0.7
- out_weight: bfloat16 [1536, 1536], P('head'), may hold values from -2.5 to 2.5
- gate_up_weight: bfloat16 [1536, 2, 4096], P(None, None, 'head'), may hold values from -0.15625 to 0.15625
- down_weight: bfloat16 [4096, 1536], P('head'), may hold values from -0.09375 to 0.09375
- cotangent: bfloat16 [8192, 1536], P('seq'), may hold values from -6 to 6
Outputs:
- output: bfloat16 [8192, 1536], P('seq')
- rows_grad: bfloat16 [8192, 1536], P('seq')
- text_grad: float32 [2048, 4096], P('seq', 'head')
- attn_gain_grad: float32 [1536], P('seq')
- ffn_gain_grad: float32 [1536], P('seq')
- mod_weight_grad: float32 [1024, 6144], P('seq', 'head')
- mod_bias_grad: float32 [4, 1536], P('head', 'seq')
- qkv_weight_grad: float32 [1536, 3, 1536], P('seq', None, 'head')
- qk_gains_grad: float32 [3, 24, 64], P(None, 'head', 'seq')
- text_kv_weight_grad: float32 [4096, 2, 1536], P('seq', None, 'head')
- cross_gate_grad: float32 [24], P('head')
- out_weight_grad: float32 [1536, 1536], P('head', 'seq')
- gate_up_weight_grad: float32 [1536, 2, 4096], P('seq', None, 'head')
- down_weight_grad: float32 [4096, 1536], P('head', 'seq')
The draws below stay inside these ranges and needn't reach their ends.
Inputs may be any that keep to these rules, and one draw needn't show every extreme that they name: Image i's patch grid has grid_shape[i, 0] rows of grid_shape[i, 1] patches, each row followed by one nextline token; its token count grid_shape[i, 0] * (grid_shape[i, 1] + 1) is more than 1024 and at most 2048. `text_slot`: no two images use the same caption block.
All inputs are finite; a program needn't handle non-finite values.
Results may differ from the reference program's by a relative error of at most 0.024.
Values may be sent and summed in bfloat16 or wider, within the bound.
A program may use at most 256 MiB of HBM per device.

```python
import jax
import jax.numpy as jnp
from jax import lax

D = 1536
H = 24
HD = 64
FF = 4096
CAP = 4096
DC = 1024
TXT = 256
TOK_DEV = 1024
IMAGES = 4
TOKENS = 8192
TEXT_ROWS = 2048
N_HEAD = 4


def draw_grid_shape(key, part):
    capacity = 2 * TOK_DEV
    fewest_rows = max(2, capacity // 64)
    most_rows = max(3, capacity // 16)
    key_rows, key_trim, key_first, key_second = jax.random.split(key, 4)
    grid_rows = jax.random.randint(key_rows, (IMAGES,), fewest_rows, most_rows + 1)
    first_pick = jax.random.randint(key_first, (), 0, IMAGES)
    second_pick = (first_pick + 1 + jax.random.randint(key_second, (), 0, IMAGES - 1)) % IMAGES
    positions = jnp.arange(IMAGES)
    grid_rows = jnp.where(positions == first_pick, fewest_rows, grid_rows)
    grid_rows = jnp.where(positions == second_pick, most_rows, grid_rows)
    base_cols = capacity // grid_rows
    most_trim = base_cols // 4
    trim_cols = jax.random.randint(key_trim, (IMAGES,), 0, most_trim + 1)
    trim_cols = jnp.where(positions == first_pick, 0, trim_cols)
    trim_cols = jnp.where(positions == second_pick, most_trim, trim_cols)
    grid_cols = base_cols - trim_cols - 1
    return jnp.stack([grid_rows, grid_cols], axis=1).astype(jnp.int32)


def draw_text_slot(key, part):
    block_total = TEXT_ROWS // TXT
    key_perm, key_top, key_bottom = jax.random.split(jax.random.fold_in(key, 7), 3)
    chosen = jax.random.permutation(key_perm, block_total)[:IMAGES].astype(jnp.int32)
    positions = jnp.arange(IMAGES)
    top_place = jax.random.randint(key_top, (), 0, IMAGES)
    bottom_place = (top_place + 1 + jax.random.randint(key_bottom, (), 0, IMAGES - 1)) % IMAGES
    has_top = jnp.any(chosen == block_total - 1)
    chosen = jnp.where(jnp.logical_and(positions == top_place, jnp.logical_not(has_top)), block_total - 1, chosen)
    has_bottom = jnp.any(chosen == 0)
    chosen = jnp.where(jnp.logical_and(positions == bottom_place, jnp.logical_not(has_bottom)), 0, chosen)
    return chosen.astype(jnp.int32)


def level_of(rng, shape, cuts, smallest, largest):
    gain, own = 1.0, jax.random.fold_in(rng, 6)
    for position, blocks in cuts:
        heights = jnp.exp(jax.random.uniform(jax.random.fold_in(own, position), (blocks,), jnp.float32, smallest / len(cuts), largest / len(cuts)))
        gain = gain * jnp.repeat(heights, shape[position] // blocks).reshape([-1 if axis == position else 1 for axis in range(len(shape))])
    return gain


def normal_values(key, dims, deviation, reach, cuts=(), kind=jnp.bfloat16):
    array = deviation * jax.random.normal(key, dims, jnp.float32)
    if cuts:
        array = array * level_of(key, dims, cuts, -0.22, 0.18)
    return jnp.clip(array, -reach, reach).astype(kind)


def setup_inputs(seed: int = 0) -> dict:
    arg_keys = jax.random.split(jax.random.key(seed), 18)
    image_rows = normal_values(arg_keys[0], (TOKENS, D), 1.0, 6.0, ((0, 8),))
    condition = normal_values(arg_keys[1], (IMAGES, DC), 1.0, 6.0)
    text_feats = normal_values(arg_keys[2], (TEXT_ROWS, CAP), 1.0, 6.0, ((0, 8),))
    grid_shape = draw_grid_shape(jax.random.fold_in(arg_keys[17], 71), 0)
    text_slot = draw_text_slot(jax.random.fold_in(arg_keys[17], 71), 0)
    attn_gain = jnp.clip(1.0 + 0.18 * jax.random.normal(arg_keys[5], (D,), jnp.float32), 0.1, 1.9)
    ffn_gain = jnp.clip(1.0 + 0.18 * jax.random.normal(arg_keys[6], (D,), jnp.float32), 0.1, 1.9)
    mod_weight = normal_values(arg_keys[7], (DC, 4 * D), DC ** -0.5, 0.1875, ((1, 4),))
    mod_bias = normal_values(arg_keys[8], (4, D), 0.5, 3.0, ((0, 4),), jnp.float32)
    qkv_weight = normal_values(arg_keys[9], (D, 3, D), D ** -0.5, 0.15625, ((2, 4),))
    qk_gains = jnp.clip(1.0 + 0.18 * jax.random.normal(arg_keys[10], (3, H, HD), jnp.float32), 0.1, 1.9)
    text_kv_weight = normal_values(arg_keys[11], (CAP, 2, D), CAP ** -0.5, 0.09375, ((2, 4),))
    cross_gate = jnp.clip(0.3 + 0.39999998 * jax.random.uniform(arg_keys[12], (H,), jnp.float32) ** level_of(arg_keys[12], (H,), ((0, 4),), -0.2, 0.2), 0.3, 0.7)
    out_weight = normal_values(arg_keys[13], (D, D), (max(2, D // 256)) ** -0.5, 2.5, ((0, 4),))
    gate_up_weight = normal_values(arg_keys[14], (D, 2, FF), D ** -0.5, 0.15625, ((2, 4),))
    down_weight = normal_values(arg_keys[15], (FF, D), FF ** -0.5, 0.09375, ((0, 4),))
    cotangent = normal_values(arg_keys[16], (TOKENS, D), 1.0, 6.0, ((0, 8),))
    return {"image_rows": image_rows, "condition": condition, "text_feats": text_feats, "grid_shape": grid_shape, "text_slot": text_slot, "attn_gain": attn_gain, "ffn_gain": ffn_gain, "mod_weight": mod_weight, "mod_bias": mod_bias, "qkv_weight": qkv_weight, "qk_gains": qk_gains, "text_kv_weight": text_kv_weight, "cross_gate": cross_gate, "out_weight": out_weight, "gate_up_weight": gate_up_weight, "down_weight": down_weight, "cotangent": cotangent}


EPSILON = 1e-06
ROPE_BASE = 10000.0
MASKED_SCORE = -1e+30
PRECISE = lax.Precision.HIGHEST

@jax.custom_vjp
def low(v):
    return lax.optimization_barrier(v.astype(jnp.bfloat16)).astype(jnp.float32)

@jax.custom_vjp
def low_back(v):
    return v

def low_keep(v):
    return (low(v), None)

def low_pass(kept, grad):
    return (grad,)

def back_keep(v):
    return (v, None)

def back_low(kept, grad):
    return (low(grad),)
low.defvjp(low_keep, low_pass)
low_back.defvjp(back_keep, back_low)

def matmul_high(left_op, right_op):
    return jnp.dot(left_op, right_op, precision=PRECISE, preferred_element_type=jnp.float32)

def norm_rows(values, gain_vec):
    return values * lax.rsqrt(lax.optimization_barrier(jnp.mean(values * values, axis=-1, keepdims=True)) + EPSILON) * gain_vec

def rotate(values, cosine, sine_tab):
    half_dim = values.shape[-1] // 2
    front_half = values[..., :half_dim]
    back_half = values[..., half_dim:]
    cosine = cosine[:, None, :]
    sine_tab = sine_tab[:, None, :]
    return jnp.concatenate([front_half * cosine - back_half * sine_tab, front_half * sine_tab + back_half * cosine], axis=-1)

def rope_tables(grid_rows, grid_cols, first_token, row_count, head_size):
    stride = grid_cols + 1
    tokens = first_token + jnp.arange(row_count, dtype=jnp.int32)
    valid_rows = tokens < grid_rows * stride
    row_pos = (tokens // stride).astype(jnp.float32)
    col_pos = (tokens % stride).astype(jnp.float32)
    quarter = head_size // 4
    pair_ids = jnp.arange(head_size // 2, dtype=jnp.int32)
    frequency = ROPE_BASE ** (-(pair_ids % quarter).astype(jnp.float32) / quarter)
    angles = jnp.where(pair_ids[None, :] < quarter, row_pos[:, None], col_pos[:, None]) * frequency[None, :]
    return (jnp.cos(angles), jnp.sin(angles), valid_rows)

def image_layer(weight_set, rows_img, text_block, cond_row, grid_pair):
    attn_gain, ffn_gain, mod_weight, mod_bias, qkv_weight, qk_gains, text_kv_weight, cross_gate, out_weight, gate_up_weight, down_weight = weight_set
    row_count = rows_img.shape[0]
    heads_local = H // N_HEAD
    inner_width = heads_local * HD
    ff_local = FF // N_HEAD
    score_scale = HD ** (-0.5)
    cosine, sine_tab, valid_rows = rope_tables(grid_pair[0], grid_pair[1], 0, row_count, HD)
    keep_mask = valid_rows.astype(jnp.float32)[:, None]
    cond_low = low(jax.nn.silu(cond_row))
    modulation = matmul_high(cond_low[None, :], mod_weight).reshape(4, D) + mod_bias
    normed = low(norm_rows(rows_img, attn_gain) * (1.0 + modulation[0]))
    pieces = []
    for group_id in range(N_HEAD):
        weight_part = qkv_weight[:, :, group_id * inner_width:(group_id + 1) * inner_width].reshape(D, 3 * inner_width)
        pieces.append(matmul_high(low_back(normed), weight_part).reshape(row_count, 3, heads_local, HD))
    projected = low_back(jnp.concatenate(pieces, axis=2))
    query_rows = low(rotate(norm_rows(projected[:, 0], qk_gains[0]), cosine, sine_tab))
    key_rows = low(rotate(norm_rows(projected[:, 1], qk_gains[1]), cosine, sine_tab))
    value_rows = low(projected[:, 2])
    text_proj = low_back(matmul_high(text_block, text_kv_weight.reshape(CAP, 2 * D)).reshape(TXT, 2, H, HD))
    caption_key = low(norm_rows(text_proj[:, 0], qk_gains[2]))
    caption_value = low(text_proj[:, 1])
    gate_head = jnp.tanh(cross_gate)

    def attend(query_block):
        self_scores = low_back(jnp.einsum('qhd,khd->hqk', query_block, key_rows, precision=PRECISE) * score_scale)
        self_scores = jnp.where(valid_rows[None, None, :], self_scores, MASKED_SCORE)
        self_weights = low(jax.nn.softmax(self_scores, axis=-1))
        self_out = jnp.einsum('hqk,khd->qhd', self_weights, value_rows, precision=PRECISE)
        cap_scores = low_back(jnp.einsum('qhd,khd->hqk', query_block, caption_key, precision=PRECISE) * score_scale)
        cap_weights = low(jax.nn.softmax(cap_scores, axis=-1))
        cross_out = low_back(jnp.einsum('hqk,khd->qhd', cap_weights, caption_value, precision=PRECISE))
        return self_out + gate_head[None, :, None] * cross_out
    block_rows = min(512, row_count)
    mixed_all = lax.map(jax.checkpoint(attend), query_rows.reshape(row_count // block_rows, block_rows, H, HD))
    mixed_all = low(low_back(mixed_all.reshape(row_count, D)))
    attn_parts = []
    for group_id in range(N_HEAD):
        lower = group_id * inner_width
        attn_parts.append(low(matmul_high(mixed_all[:, lower:lower + inner_width], out_weight[lower:lower + inner_width])))
    attn_out = low_back(sum(attn_parts))
    mod_gates = jnp.tanh(modulation)
    middle = rows_img + keep_mask * mod_gates[1] * attn_out
    ffn_in = low(norm_rows(middle, ffn_gain) * (1.0 + modulation[2]))
    ffn_parts = []
    for group_id in range(N_HEAD):
        lower = group_id * ff_local
        gate_up = low_back(matmul_high(low_back(ffn_in), gate_up_weight[:, :, lower:lower + ff_local].reshape(D, 2 * ff_local)))
        hidden = low(jax.nn.silu(gate_up[:, :ff_local]) * gate_up[:, ff_local:])
        ffn_parts.append(low(matmul_high(hidden, down_weight[lower:lower + ff_local])))
    ffn_out = low_back(sum(ffn_parts))
    return middle + keep_mask * mod_gates[3] * ffn_out

def reference(image_rows, condition, text_feats, grid_shape, text_slot, attn_gain, ffn_gain, mod_weight, mod_bias, qkv_weight, qk_gains, text_kv_weight, cross_gate, out_weight, gate_up_weight, down_weight, cotangent):
    weight_set = tuple((entry.astype(jnp.float32) for entry in (attn_gain, ffn_gain, mod_weight, mod_bias, qkv_weight, qk_gains, text_kv_weight, cross_gate, out_weight, gate_up_weight, down_weight)))
    rows_all = image_rows.astype(jnp.float32).reshape(IMAGES, 2 * TOK_DEV, D)
    text_all = text_feats.astype(jnp.float32).reshape(TEXT_ROWS // TXT, TXT, CAP)
    cond_all = condition.astype(jnp.float32)

    def forward(weights_in, rows_in, text_in):

        def image_step(scan_carry, scan_item):
            rows_img, cond_row, grid_pair, caption_slot = scan_item
            text_block = lax.dynamic_index_in_dim(text_in, caption_slot, 0, keepdims=False)
            return (scan_carry, image_layer(weights_in, rows_img, text_block, cond_row, grid_pair))
        _, layer_out = lax.scan(jax.checkpoint(image_step), jnp.zeros((), jnp.float32), (rows_in, cond_all, grid_shape, text_slot))
        return layer_out
    layer_out, pullback = jax.vjp(forward, weight_set, rows_all, text_all)
    weight_grads, rows_grad, text_grad = pullback(cotangent.astype(jnp.float32).reshape(IMAGES, 2 * TOK_DEV, D))
    return (layer_out.reshape(TOKENS, D).astype(jnp.bfloat16), rows_grad.reshape(TOKENS, D).astype(jnp.bfloat16), text_grad.reshape(TEXT_ROWS, CAP), weight_grads[0], weight_grads[1], weight_grads[2], weight_grads[3], weight_grads[4], weight_grads[5], weight_grads[6], weight_grads[7], weight_grads[8], weight_grads[9], weight_grads[10])
```

```python
import functools

import jax
import jax.numpy as jnp
from jax import lax
from jax.experimental import pallas as pl
from jax.experimental.pallas import tpu as pltpu
from jax.sharding import PartitionSpec as P

TXT = 256
EPSILON = 1e-06
ROPE_BASE = 10000.0
LOG2E = 1.4426950408889634
F32 = jnp.float32
BF = jnp.bfloat16
VMEM_BYTES = 67043328
HIGHEST = lax.Precision.HIGHEST
VM = pl.BlockSpec(memory_space=pltpu.VMEM)
S = jax.ShapeDtypeStruct


def nt(a, b):
    return lax.dot_general(a, b, (((1,), (1,)), ((), ())), preferred_element_type=F32)


def nn(a, b):
    return lax.dot_general(a, b, (((1,), (0,)), ((), ())), preferred_element_type=F32)


def tn(a, b):
    return lax.dot_general(a, b, (((0,), (0,)), ((), ())), preferred_element_type=F32)


def head_mean(x):
    rows = lax.broadcasted_iota(jnp.int32, (128, 128), 0) // 64
    cols = lax.broadcasted_iota(jnp.int32, (128, 128), 1) // 64
    same = jnp.where(rows == cols, 1.0 / 64, 0.0).astype(BF)
    high = x.astype(BF)
    rest = (x - high.astype(F32)).astype(BF)
    return nn(high, same) + nn(rest, same)


def swap_halves(x):
    lane = lax.broadcasted_iota(jnp.int32, x.shape, 1) % 64
    return jnp.where(lane < 32, pltpu.roll(x, 96, 1), pltpu.roll(x, 32, 1))


def qkv_kernel(x_ref, gain_ref, w_ref, hg_ref, cos_ref, sin_ref, live_ref, h_ref, pre_ref, q_ref, kv_ref):
    x = x_ref[...].astype(F32)
    n = lax.rsqrt(jnp.mean(x * x, axis=-1, keepdims=True) + EPSILON)
    h = (x * n * gain_ref[...]).astype(BF)
    h_ref[...] = h
    width = w_ref.shape[2]
    cos, sin, live = cos_ref[...], sin_ref[...], live_ref[...]
    for part in range(2):
        pre = nn(h, w_ref[part])
        pre_ref[:, part * width : (part + 1) * width] = pre
        for p in range(width // 128):
            v = pre[:, p * 128 : (p + 1) * 128]
            r = lax.rsqrt(head_mean(v * v) + EPSILON)
            t = v * r * hg_ref[part : part + 1, p * 128 : (p + 1) * 128]
            y = t * cos + swap_halves(t) * sin
            if part == 0:
                q_ref[:, p * 128 : (p + 1) * 128] = y.astype(BF)
            else:
                kv_ref[:, p * 128 : (p + 1) * 128] = (y * live).astype(BF)
    val = nn(h, w_ref[2])
    for p in range(width // 128):
        kv_ref[:, width + p * 128 : width + (p + 1) * 128] = (val[:, p * 128 : (p + 1) * 128] * live).astype(BF)


def make_qkv(x, gain, w, head_gains, cos, sin, live):
    rows, width = x.shape
    inner = w.shape[2]
    rb = min(256, rows)
    return pl.pallas_call(
        qkv_kernel,
        grid=(rows // rb,),
        in_specs=[
            pl.BlockSpec((rb, width), lambda i: (i, 0)),
            pl.BlockSpec((1, width), lambda i: (0, 0)),
            pl.BlockSpec(w.shape, lambda i: (0, 0, 0)),
            pl.BlockSpec((8, inner), lambda i: (0, 0)),
            pl.BlockSpec((rb, 128), lambda i: (i, 0)),
            pl.BlockSpec((rb, 128), lambda i: (i, 0)),
            pl.BlockSpec((rb, 128), lambda i: (i, 0)),
        ],
        out_specs=(
            pl.BlockSpec((rb, width), lambda i: (i, 0)),
            pl.BlockSpec((rb, 2 * inner), lambda i: (i, 0)),
            pl.BlockSpec((rb, inner), lambda i: (i, 0)),
            pl.BlockSpec((rb, 2 * inner), lambda i: (i, 0)),
        ),
        out_shape=(S((rows, width), BF), S((rows, 2 * inner), F32), S((rows, inner), BF), S((rows, 2 * inner), BF)),
        compiler_params=pltpu.CompilerParams(vmem_limit_bytes=VMEM_BYTES // 2),
        cost_estimate=pl.CostEstimate(flops=6 * rows * width * inner, bytes_accessed=12 * rows * width, transcendentals=0),
        name="make_qkv",
    )(x, gain, w, head_gains, cos, sin, live)


def qkv_back_kernel(dq_ref, dkv_ref, peer_ref, pre_ref, hg_ref, cos_ref, sin_ref, w_ref, dpre_ref, gg_ref, dh_ref):
    width = dq_ref.shape[1]
    rows = dq_ref.shape[0]

    @pl.when(pl.program_id(0) == 0)
    def _():
        gg_ref[...] = jnp.zeros_like(gg_ref)

    cos, sin = cos_ref[...], sin_ref[...]
    total = None
    for part in range(2):
        for p in range(width // 128):
            ls = slice(p * 128, (p + 1) * 128)
            pls = slice(part * width + p * 128, part * width + (p + 1) * 128)
            if part == 0:
                dy = dq_ref[:, ls]
            else:
                dy = dkv_ref[:, ls] + peer_ref[:, ls].astype(F32)
            dt = dy * cos - swap_halves(dy) * sin
            v = pre_ref[:, pls]
            r = lax.rsqrt(head_mean(v * v) + EPSILON)
            u = v * r
            w = dt * hg_ref[part : part + 1, ls]
            dv = r * (w - u * head_mean(w * u))
            dpre_ref[:, pls] = dv.astype(BF)
            gg_ref[part * 8 : part * 8 + 8, ls] += jnp.sum((dt * u).reshape(rows // 8, 8, 128), axis=0)
        g = nt(dpre_ref[:, part * width : (part + 1) * width], w_ref[part])
        total = g if total is None else total + g
    dpre_ref[:, 2 * width :] = (dkv_ref[:, width:] + peer_ref[:, width:].astype(F32)).astype(BF)
    total = total + nt(dpre_ref[:, 2 * width :], w_ref[2])
    dh_ref[...] = total.astype(BF)


def qkv_back(dq, dkv, peer, pre, head_gains, cos, sin, w):
    rows, inner = dq.shape
    width = w.shape[1]
    rb = min(256, rows)
    blk = lambda c: pl.BlockSpec((rb, c), lambda i: (i, 0))
    return pl.pallas_call(
        qkv_back_kernel,
        grid=(rows // rb,),
        in_specs=[
            blk(inner),
            blk(2 * inner),
            blk(2 * inner),
            blk(2 * inner),
            pl.BlockSpec((8, inner), lambda i: (0, 0)),
            blk(128),
            blk(128),
            pl.BlockSpec(w.shape, lambda i: (0, 0, 0)),
        ],
        out_specs=(blk(3 * inner), pl.BlockSpec((16, inner), lambda i: (0, 0)), blk(width)),
        out_shape=(S((rows, 3 * inner), BF), S((16, inner), F32), S((rows, width), BF)),
        compiler_params=pltpu.CompilerParams(vmem_limit_bytes=VMEM_BYTES // 2),
        cost_estimate=pl.CostEstimate(flops=6 * rows * width * inner, bytes_accessed=12 * rows * width, transcendentals=0),
        name="qkv_back",
    )(dq, dkv, peer, pre, head_gains, cos, sin, w)


def attend_kernel(
    scale, qb, kc, q_ref, kv_ref, peer_ref, live_ref, ck_ref, cv_ref, gate_ref, mixed_ref, self_ref, cross_ref, lse_ref, va_ref, cva_ref
):
    rows, width = q_ref.shape
    txt = ck_ref.shape[0]
    c = scale * LOG2E
    va_ref[:, 128:] = live_ref[...]
    cva_ref[:, 128:] = jnp.ones((txt, 128), BF)
    first = lax.broadcasted_iota(jnp.int32, (qb, 128), 1) < 64

    def pair(p, _):
        lanes = pl.ds(pl.multiple_of(p * 128, 128), 128)
        vlanes = pl.ds(pl.multiple_of(width + p * 128, 128), 128)
        va_ref[:rows, :128] = kv_ref[:, vlanes]
        va_ref[rows:, :128] = peer_ref[:, vlanes]
        cva_ref[:, :128] = cv_ref[:, lanes]
        gate = gate_ref[:, lanes]

        def block(b, _):
            rs = pl.ds(pl.multiple_of(b * qb, qb), qb)
            qp = q_ref[rs, lanes]
            outs, couts = [], []
            for a in range(2):
                qm = jnp.where(first if a == 0 else jnp.logical_not(first), qp, jnp.zeros_like(qp))
                acc = None
                for side in range(2):
                    keys = kv_ref if side == 0 else peer_ref
                    for j in range(0, rows, kc):
                        s = nt(qm, keys[j : j + kc, lanes])
                        pr = jnp.exp2(s * c).astype(BF)
                        o = nn(pr, va_ref[side * rows + j : side * rows + j + kc, :])
                        acc = o if acc is None else acc + o
                outs.append(acc)
                s = nt(qm, ck_ref[:, lanes])
                couts.append(nn(jnp.exp2(s * c).astype(BF), cva_ref[...]))
            so = jnp.where(first, outs[0][:, :128], outs[1][:, :128])
            sl = jnp.where(first, outs[0][:, 128:], outs[1][:, 128:])
            co = jnp.where(first, couts[0][:, :128], couts[1][:, :128])
            cl = jnp.where(first, couts[0][:, 128:], couts[1][:, 128:])
            so = so / sl
            co = co / cl
            mixed_ref[rs, lanes] = (so + gate * co).astype(BF)
            self_ref[rs, lanes] = so
            cross_ref[rs, lanes] = co
            lt = jnp.log2(sl).T
            ct = jnp.log2(cl).T
            lse_ref[p, :, rs] = jnp.concatenate([lt[0:1], lt[64:65], ct[0:1], ct[64:65], lt[0:4]], axis=0)
            return 0

        lax.fori_loop(0, rows // qb, block, 0)
        return 0

    lax.fori_loop(0, width // 128, pair, 0)


def attend(q, kv, peer, live, ck, cv, gate, scale, qb=256, kc=1024):
    rows, width = q.shape
    txt = ck.shape[0]
    qb, kc = min(qb, rows), min(kc, rows)
    return pl.pallas_call(
        functools.partial(attend_kernel, scale, qb, kc),
        out_shape=(S((rows, width), BF), S((rows, width), F32), S((rows, width), F32), S((width // 128, 8, rows), F32)),
        in_specs=[VM] * 7,
        out_specs=(VM,) * 4,
        scratch_shapes=[pltpu.VMEM((2 * rows, 256), BF), pltpu.VMEM((txt, 256), BF)],
        compiler_params=pltpu.CompilerParams(vmem_limit_bytes=VMEM_BYTES // 2),
        cost_estimate=pl.CostEstimate(flops=32 * rows * rows * width, bytes_accessed=12 * rows * width, transcendentals=0),
        name="attend",
    )(q, kv, peer, live, ck, cv, gate)


def attend_back_kernel(
    scale,
    qb,
    kc,
    q_ref,
    kv_ref,
    peer_ref,
    live_ref,
    ck_ref,
    cv_ref,
    gate_ref,
    self_ref,
    cross_ref,
    lse_ref,
    dm_ref,
    dq_ref,
    dkv_ref,
    dpeer_ref,
    dck_ref,
    dcv_ref,
    gg_ref,
    kt_ref,
    ckt_ref,
    p_ref,
    d_ref,
    ak_ref,
    av_ref,
):
    rows, width = q_ref.shape
    txt = ck_ref.shape[0]
    c = scale * LOG2E
    first = lax.broadcasted_iota(jnp.int32, (qb, 128), 1) < 64
    head_row = lax.broadcasted_iota(jnp.int32, (8, 128), 0)
    head_lane = lax.broadcasted_iota(jnp.int32, (8, 128), 1) // 64
    ind = (head_row == head_lane).astype(F32)

    def head_sum(x):
        return lax.dot_general(ind, x, (((1,), (1,)), ((), ())), preferred_element_type=F32, precision=HIGHEST)

    def pair(p, _):
        lanes = pl.ds(pl.multiple_of(p * 128, 128), 128)
        vlanes = pl.ds(pl.multiple_of(width + p * 128, 128), 128)
        kt_ref[:, :rows] = kv_ref[:, lanes].T
        kt_ref[:, rows:] = peer_ref[:, lanes].T
        ckt_ref[...] = ck_ref[:, lanes].T
        gate = gate_ref[:, lanes]
        ak_ref[...] = jnp.zeros_like(ak_ref)
        av_ref[...] = jnp.zeros_like(av_ref)
        dck_ref[:, lanes] = jnp.zeros((txt, 128), F32)
        dcv_ref[:, lanes] = jnp.zeros((txt, 128), F32)
        gg_ref[:, lanes] = jnp.zeros((8, 128), F32)

        def block(b, _):
            rs = pl.ds(pl.multiple_of(b * qb, qb), qb)
            qp = q_ref[rs, lanes]
            dm = dm_ref[rs, lanes]
            dmf = dm.astype(F32)
            dcf = (gate * dmf).astype(BF)
            delta = head_sum(dmf * self_ref[rs, lanes])
            ce = dmf * cross_ref[rs, lanes]
            gg_ref[:, lanes] += jnp.sum(ce.reshape(qb // 8, 8, 128), axis=0)
            cdelta = head_sum(dcf.astype(F32) * cross_ref[rs, lanes])
            z = jnp.zeros_like(qp)
            masks = (first, jnp.logical_not(first))
            qs = [jnp.where(m, qp, z) for m in masks]
            dms = [jnp.where(m, dm, z) for m in masks]
            dcs = [jnp.where(m, dcf, z) for m in masks]
            qstack = jnp.concatenate(qs, axis=0)
            dstack = jnp.concatenate(dms, axis=0)
            dcstack = jnp.concatenate(dcs, axis=0)
            lse = lse_ref[p, :, rs]
            dqt = [None, None]
            for side in range(2):
                src = kv_ref if side == 0 else peer_ref
                for j in range(0, rows, kc):
                    at = side * rows + j
                    for a in range(2):
                        s = nt(src[j : j + kc, lanes], qs[a])
                        pr = jnp.exp2(s * c - lse[a : a + 1])
                        dp = nt(src[j : j + kc, vlanes], dms[a])
                        p_ref[:, a * qb : (a + 1) * qb] = pr.astype(BF)
                        dd = (pr * (dp - delta[a : a + 1])).astype(BF)
                        d_ref[:, a * qb : (a + 1) * qb] = dd
                        t = nn(kt_ref[a * 64 : (a + 1) * 64, at : at + kc], dd)
                        dqt[a] = t if dqt[a] is None else dqt[a] + t
                    av_ref[at : at + kc] += nn(p_ref[...], dstack)
                    ak_ref[at : at + kc] += nn(d_ref[...], qstack)
            for a in range(2):
                s = nt(ck_ref[:, lanes], qs[a])
                pr = jnp.exp2(s * c - lse[2 + a : 3 + a])
                dp = nt(cv_ref[:, lanes], dcs[a])
                p_ref[:txt, a * qb : (a + 1) * qb] = pr.astype(BF)
                dd = (pr * (dp - cdelta[a : a + 1])).astype(BF)
                d_ref[:txt, a * qb : (a + 1) * qb] = dd
                dqt[a] = dqt[a] + nn(ckt_ref[a * 64 : (a + 1) * 64, :], dd)
            dcv_ref[:, lanes] += nn(p_ref[:txt, :], dcstack)
            dck_ref[:, lanes] += nn(d_ref[:txt, :], qstack)
            dq_ref[rs, lanes] = (jnp.concatenate(dqt, axis=0) * scale).T
            return 0

        lax.fori_loop(0, rows // qb, block, 0)
        live = live_ref[...].astype(F32)
        dkv_ref[:, lanes] = ak_ref[:rows] * (live[:rows] * scale)
        dkv_ref[:, vlanes] = av_ref[:rows] * live[:rows]
        dpeer_ref[:, lanes] = (ak_ref[rows:] * (live[rows:] * scale)).astype(BF)
        dpeer_ref[:, vlanes] = (av_ref[rows:] * live[rows:]).astype(BF)
        dck_ref[:, lanes] = dck_ref[:, lanes] * scale
        return 0

    lax.fori_loop(0, width // 128, pair, 0)


def attend_back(q, kv, peer, live, ck, cv, gate, so, co, lse, dm, scale, qb=256, kc=512):
    rows, width = q.shape
    txt = ck.shape[0]
    qb, kc = min(qb, rows), min(kc, rows)
    return pl.pallas_call(
        functools.partial(attend_back_kernel, scale, qb, kc),
        out_shape=(
            S((rows, width), F32),
            S((rows, 2 * width), F32),
            S((rows, 2 * width), BF),
            S((txt, width), F32),
            S((txt, width), F32),
            S((8, width), F32),
        ),
        in_specs=[VM] * 11,
        out_specs=(VM,) * 6,
        scratch_shapes=[
            pltpu.VMEM((128, 2 * rows), BF),
            pltpu.VMEM((128, txt), BF),
            pltpu.VMEM((kc, 2 * qb), BF),
            pltpu.VMEM((kc, 2 * qb), BF),
            pltpu.VMEM((2 * rows, 128), F32),
            pltpu.VMEM((2 * rows, 128), F32),
        ],
        compiler_params=pltpu.CompilerParams(vmem_limit_bytes=VMEM_BYTES // 2),
        cost_estimate=pl.CostEstimate(flops=80 * rows * rows * width, bytes_accessed=20 * rows * width, transcendentals=0),
        name="attend_back",
    )(q, kv, peer, live, ck, cv, gate, so, co, lse, dm)


def pair_swap(value):
    pairs = [(source, source ^ 1) for source in range(lax.axis_size("seq"))]
    return lax.ppermute(value, "seq", pairs)


def rope_tables(grid_rows, grid_cols, first_token, row_count, head_size):
    stride = grid_cols + 1
    tokens = first_token + jnp.arange(row_count, dtype=jnp.int32)
    valid = tokens < grid_rows * stride
    row_pos = (tokens // stride).astype(F32)
    col_pos = (tokens % stride).astype(F32)
    quarter = head_size // 4
    half = head_size // 2
    lane = jnp.arange(128, dtype=jnp.int32) % half
    frequency = ROPE_BASE ** (-(lane % quarter).astype(F32) / quarter)
    angles = jnp.where(lane[None, :] < quarter, row_pos[:, None], col_pos[:, None]) * frequency[None, :]
    sign = jnp.where(jnp.arange(128) % head_size < half, -1.0, 1.0)
    return jnp.cos(angles), jnp.sin(angles) * sign[None, :], valid


def norm_back(dh, values, gain, one_plus):
    r = lax.rsqrt(jnp.mean(values * values, axis=-1, keepdims=True) + EPSILON)
    u = values * r
    w = dh * (gain * one_plus)
    back = r * (w - u * jnp.mean(w * u, axis=-1, keepdims=True))
    return back, jnp.sum(dh * u, axis=0)


def local(
    image_rows,
    condition,
    text_feats,
    grid_shape,
    text_slot,
    attn_gain,
    ffn_gain,
    mod_weight,
    mod_bias,
    qkv_weight,
    qk_gains,
    text_kv_weight,
    cross_gate,
    out_weight,
    gate_up_weight,
    down_weight,
    cotangent,
):
    row_count, model_width = image_rows.shape
    head_local, head_size = qk_gains.shape[1], qk_gains.shape[2]
    inner = head_local * head_size
    ff_local = down_weight.shape[0]
    text_local, cap_width = text_feats.shape
    head_count = lax.axis_size("head")
    seq_count = lax.axis_size("seq")
    seq_index = lax.axis_index("seq")
    head_index = lax.axis_index("head")
    image_index = seq_index // 2
    pair_half = seq_index % 2
    score_scale = head_size ** (-0.5)
    image_count = condition.shape[0]

    grid_pair = lax.dynamic_index_in_dim(grid_shape, image_index, 0, keepdims=False)
    cos, sin, valid = rope_tables(grid_pair[0], grid_pair[1], pair_half * row_count, row_count, head_size)
    keep = valid.astype(F32)[:, None]
    live_own = jnp.broadcast_to(keep, (row_count, 128))
    peer_tokens = (1 - pair_half) * row_count + jnp.arange(row_count, dtype=jnp.int32)
    keep_peer = (peer_tokens < grid_pair[0] * (grid_pair[1] + 1)).astype(F32)[:, None]
    live_all = jnp.concatenate([live_own, jnp.broadcast_to(keep_peer, (row_count, 128))], axis=0).astype(BF)

    cond_all = jax.nn.silu(condition.astype(F32)).astype(BF)
    cond_low = lax.dynamic_index_in_dim(cond_all, image_index, 0, keepdims=True)
    mod_piece = jnp.dot(cond_low, mod_weight, preferred_element_type=F32) + mod_bias
    modulation = lax.all_gather(mod_piece, "head", axis=0, tiled=True)
    one_attn = 1.0 + modulation[0]
    one_ffn = 1.0 + modulation[2]
    tanh_attn = jnp.tanh(modulation[1])
    tanh_ffn = jnp.tanh(modulation[3])

    head_gains = jnp.concatenate([qk_gains.reshape(3, inner), jnp.zeros((5, inner), F32)], axis=0)
    gate_head = jnp.tanh(cross_gate)
    gate_lanes = jnp.repeat(gate_head, head_size)[None, :]
    qkv_mats = jnp.transpose(qkv_weight, (1, 0, 2))
    same_head = (jnp.arange(inner)[:, None] // head_size == jnp.arange(inner)[None, :] // head_size).astype(F32) / head_size

    text_kv_flat = text_kv_weight.reshape(cap_width, 2 * inner)
    text_proj = jnp.dot(text_feats, text_kv_flat, preferred_element_type=F32)
    cap_pre = text_proj[:, :inner]
    cap_r = lax.rsqrt(jnp.dot(cap_pre * cap_pre, same_head, precision=HIGHEST) + EPSILON)
    cap_u = cap_pre * cap_r
    cap_kv = jnp.concatenate([cap_u * head_gains[2:3], text_proj[:, inner:]], axis=1).astype(BF)
    caps = lax.all_gather(cap_kv, "seq", axis=0, tiled=False)
    slot = lax.dynamic_index_in_dim(text_slot, image_index, 0, keepdims=False)
    cap_own = lax.dynamic_index_in_dim(caps, slot, 0, keepdims=False)
    cap_key, cap_value = cap_own[:, :inner], cap_own[:, inner:]

    normed, pre, query, kv = make_qkv(image_rows, (attn_gain * one_attn)[None, :], qkv_mats, head_gains, cos, sin, live_own)
    kv_peer = pair_swap(kv)
    mixed, self_out, cross_out, lse = attend(query, kv, kv_peer, live_all, cap_key, cap_value, gate_lanes, score_scale)

    rows_float = image_rows.astype(F32)
    attn_part = jnp.dot(mixed, out_weight, preferred_element_type=F32).astype(BF)
    attn_out = lax.psum(attn_part, "head").astype(F32)
    middle = rows_float + keep * tanh_attn * attn_out
    mid_r = lax.rsqrt(jnp.mean(middle * middle, axis=-1, keepdims=True) + EPSILON)
    ffn_low = (middle * mid_r * (ffn_gain * one_ffn)).astype(BF)
    gate_up_flat = gate_up_weight.reshape(model_width, 2 * ff_local)
    gate_up = jnp.dot(ffn_low, gate_up_flat, preferred_element_type=F32)
    gate_pre, up_pre = gate_up[:, :ff_local], gate_up[:, ff_local:]
    sig = jax.nn.sigmoid(gate_pre)
    hidden_low = (gate_pre * sig * up_pre).astype(BF)
    grad_out = cotangent.astype(F32)
    ffn_grad_low = (grad_out * keep * tanh_ffn).astype(BF)
    hidden_grad = nt(ffn_grad_low, down_weight)
    gate_grad = hidden_grad * up_pre * sig * (1.0 + gate_pre * (1.0 - sig))
    up_grad = hidden_grad * (gate_pre * sig)
    gate_up_grad_low = jnp.concatenate([gate_grad.astype(BF), up_grad.astype(BF)], axis=1)
    ffn_in_part = nt(gate_up_grad_low, gate_up_flat).astype(BF)
    ffn_in_grad = lax.psum(ffn_in_part, "head").astype(F32)
    ffn_part = jnp.dot(hidden_low, down_weight, preferred_element_type=F32).astype(BF)
    ffn_out = lax.psum(ffn_part, "head").astype(F32)
    output = (middle + keep * tanh_ffn * ffn_out).astype(BF)
    gate_ffn_grad = jnp.sum(grad_out * keep * ffn_out, axis=0) * (1.0 - tanh_ffn * tanh_ffn)
    gate_up_grad = tn(ffn_low, gate_up_grad_low).astype(BF)
    down_grad = tn(ffn_grad_low, hidden_low).astype(BF)

    mid_back, ffn_sum = norm_back(ffn_in_grad, middle, ffn_gain, one_ffn)
    middle_grad = grad_out + mid_back
    attn_grad_low = (middle_grad * keep * tanh_attn).astype(BF)
    gate_attn_grad = jnp.sum(middle_grad * keep * attn_out, axis=0) * (1.0 - tanh_attn * tanh_attn)
    mixed_grad = nt(attn_grad_low, out_weight).astype(BF)
    out_grad = tn(attn_grad_low, mixed).astype(BF)

    dq, dkv, dpeer, dck, dcv, gate_rows = attend_back(
        query, kv, kv_peer, live_all, cap_key, cap_value, gate_lanes, self_out, cross_out, lse, mixed_grad, score_scale
    )
    from_peer = pair_swap(dpeer)
    grad_pre, gain_rows, attn_in_part = qkv_back(dq, dkv, from_peer, pre, head_gains, cos, sin, qkv_mats)
    attn_in_grad = lax.psum(attn_in_part, "head").astype(F32)
    qkv_grad = tn(normed, grad_pre).astype(BF)
    rows_back, attn_sum = norm_back(attn_in_grad, rows_float, attn_gain, one_attn)
    rows_grad = (middle_grad + rows_back).astype(BF)

    cap_half = jnp.concatenate([dck, dcv], axis=1)
    cap_grads = lax.all_gather(cap_half.astype(BF), "seq", axis=0, tiled=False)
    own_image = jnp.sum(jnp.where(text_slot == seq_index, jnp.arange(image_count), 0))
    used = jnp.any(text_slot == seq_index).astype(F32)
    two = lax.dynamic_slice_in_dim(cap_grads, 2 * own_image, 2, 0).astype(F32)
    cap_grad = (two[0] + two[1]) * used
    cap_dy, cap_dv = cap_grad[:, :inner], cap_grad[:, inner:]
    cap_w = cap_dy * head_gains[2:3]
    cap_pre_grad = cap_r * (cap_w - cap_u * jnp.dot(cap_w * cap_u, same_head, precision=HIGHEST))
    cap_gain = jnp.sum(cap_dy * cap_u, axis=0)
    text_low = jnp.concatenate([cap_pre_grad, cap_dv], axis=1).astype(BF)
    text_weight_grad = tn(text_feats, text_low).astype(BF)
    text_part = nt(text_low, text_kv_flat).astype(BF)
    text_grad = lax.psum_scatter(text_part, "head", scatter_dimension=1, tiled=True).astype(F32)

    mod_grad = jnp.stack([attn_sum * attn_gain, gate_attn_grad, ffn_sum * ffn_gain, gate_ffn_grad])
    own_mod = lax.dynamic_index_in_dim(mod_grad, head_index, 0, keepdims=False)
    gain_grad = jnp.concatenate([gain_rows[0:8].sum(0), gain_rows[8:16].sum(0), cap_gain])
    gate_grad_head = gate_rows.sum(0)
    small = jnp.concatenate([attn_sum * one_attn, ffn_sum * one_ffn, own_mod, gain_grad, gate_grad_head])
    smalls = lax.all_gather(small, "seq", axis=0, tiled=False)
    total = jnp.sum(smalls, axis=0)
    d = model_width
    dl = d // seq_count
    attn_gain_sum = lax.dynamic_slice_in_dim(total[:d], seq_index * dl, dl)
    ffn_gain_sum = lax.dynamic_slice_in_dim(total[d : 2 * d], seq_index * dl, dl)
    mod_bias_sum = lax.dynamic_slice_in_dim(total[2 * d : 3 * d], seq_index * dl, dl)[None, :]
    qk_all = total[3 * d : 3 * d + 3 * inner].reshape(3, head_local, seq_count, head_size // seq_count)
    qk_gain_sum = lax.dynamic_index_in_dim(qk_all, seq_index, 2, keepdims=False)
    gate_sum = total[3 * d + 3 * inner :].reshape(head_local, head_size).sum(-1) * (1.0 - gate_head * gate_head)
    cond_cols = condition.shape[1] // seq_count
    cond_part = lax.dynamic_slice_in_dim(cond_all, seq_index * cond_cols, cond_cols, 1).astype(F32)
    image_mods = smalls[:, 2 * d : 3 * d].reshape(image_count, 2, d).sum(1)
    mod_weight_sum = lax.dot_general(cond_part, image_mods, (((0,), (0,)), ((), ())), precision=HIGHEST)

    def scatter(v):
        return lax.psum_scatter(v, "seq", scatter_dimension=0, tiled=True).astype(F32)

    qkv_sum = scatter(qkv_grad).reshape(-1, 3, inner)
    out_sum = scatter(out_grad).T
    text_weight_sum = scatter(text_weight_grad).reshape(-1, 2, inner)
    gate_up_sum = scatter(gate_up_grad).reshape(-1, 2, ff_local)
    down_sum = scatter(down_grad).T
    return (
        output,
        rows_grad,
        text_grad,
        attn_gain_sum,
        ffn_gain_sum,
        mod_weight_sum,
        mod_bias_sum,
        qkv_sum,
        qk_gain_sum,
        text_weight_sum,
        gate_sum,
        out_sum,
        gate_up_sum,
        down_sum,
    )


def solution(mesh):
    return jax.shard_map(
        local,
        mesh=mesh,
        in_specs=(
            P("seq", None),
            P(),
            P("seq", None),
            P(),
            P(),
            P(),
            P(),
            P(None, "head"),
            P("head", None),
            P(None, None, "head"),
            P(None, "head", None),
            P(None, None, "head"),
            P("head"),
            P("head", None),
            P(None, None, "head"),
            P("head", None),
            P("seq", None),
        ),
        out_specs=(
            P("seq", None),
            P("seq", None),
            P("seq", "head"),
            P("seq"),
            P("seq"),
            P("seq", "head"),
            P("head", "seq"),
            P("seq", None, "head"),
            P(None, "head", "seq"),
            P("seq", None, "head"),
            P("head"),
            P("head", "seq"),
            P("seq", None, "head"),
            P("head", "seq"),
        ),
        check_vma=False,
    )
```

```python
import functools

import jax
import jax.numpy as jnp
from jax import lax
from jax.experimental import pallas as pl
from jax.experimental.pallas import tpu as pltpu
from jax.sharding import PartitionSpec as P

TXT = 256
EPSILON = 1e-06
ROPE_BASE = 10000.0
LOG2E = 1.4426950408889634
F32 = jnp.float32
BF = jnp.bfloat16
VMEM_BYTES = 67043328
HIGHEST = lax.Precision.HIGHEST
VM = pl.BlockSpec(memory_space=pltpu.VMEM)
S = jax.ShapeDtypeStruct


def nt(a, b):
    return lax.dot_general(a, b, (((1,), (1,)), ((), ())), preferred_element_type=F32)


def nn(a, b):
    return lax.dot_general(a, b, (((1,), (0,)), ((), ())), preferred_element_type=F32)


def tn(a, b):
    return lax.dot_general(a, b, (((0,), (0,)), ((), ())), preferred_element_type=F32)


def head_mean(x):
    rows = lax.broadcasted_iota(jnp.int32, (128, 128), 0) // 64
    cols = lax.broadcasted_iota(jnp.int32, (128, 128), 1) // 64
    same = jnp.where(rows == cols, 1.0 / 64, 0.0).astype(BF)
    high = x.astype(BF)
    rest = (x - high.astype(F32)).astype(BF)
    return nn(high, same) + nn(rest, same)


def swap_halves(x):
    lane = lax.broadcasted_iota(jnp.int32, x.shape, 1) % 64
    return jnp.where(lane < 32, pltpu.roll(x, 96, 1), pltpu.roll(x, 32, 1))


def to_head(z):
    return {"head": z}


def both(a, b):
    return jnp.logical_and(a, b)


def line_barrier(z, n):
    bar = pltpu.get_barrier_semaphore()
    for ok, other in ((z > 0, z - 1), (z < n - 1, z + 1)):

        @pl.when(ok)
        def _(other=other):
            pl.semaphore_signal(bar, inc=1, device_id=to_head(other), device_id_type=pl.DeviceIdType.MESH)

    end = jnp.logical_or(z == 0, z == n - 1)

    @pl.when(end)
    def _():
        pl.semaphore_wait(bar, 1)

    @pl.when(jnp.logical_not(end))
    def _():
        pl.semaphore_wait(bar, 2)


class Chain:
    def __init__(self, n, subs, lag, part_ref, out_ref, rbuf, lbuf, ssem, rsem, finalize=None):
        self.z, self.n, self.subs, self.lag = lax.axis_index("head"), n, subs, lag
        self.part, self.out, self.rbuf, self.lbuf, self.ssem, self.rsem = part_ref, out_ref, rbuf, lbuf, ssem, rsem
        self.half = part_ref.shape[0] // 2
        self.unit = self.half // subs
        self.finalize = finalize
        self.steps = subs + 2 * lag * (n - 1)

    def near(self, s):
        return pl.ds(pl.multiple_of(s * self.unit, self.unit), self.unit)

    def far(self, s):
        return pl.ds(pl.multiple_of(self.half + s * self.unit, self.unit), self.unit)

    def copy(self, kind, s, first=False):
        src, at, to = (
            (self.rbuf, self.near(s), self.near(s)),
            (self.lbuf, self.near(s), self.near(s)),
            (self.out, self.near(s), self.near(s)),
            (self.out, self.far(s), self.far(s)),
        )[kind]
        dst = src
        if first:
            src, at = self.part, (self.far(s) if kind == 0 else self.near(s))
        return pltpu.make_async_remote_copy(
            src_ref=src.at[at],
            dst_ref=dst.at[to],
            send_sem=self.ssem.at[kind, s],
            recv_sem=self.rsem.at[kind, s],
            device_id=to_head(self.z + (1 if kind % 2 == 0 else -1)),
            device_id_type=pl.DeviceIdType.MESH,
        )

    def step(self, k):
        z, lag, last = self.z, self.lag, self.n - 1

        def inside(s):
            return both(s >= 0, s < self.subs)

        for kind, buf in ((0, self.rbuf), (1, self.lbuf)):
            hops = z if kind == 0 else last - z
            s = k - lag * hops

            @pl.when(both(inside(s), hops == 0))
            def _(kind=kind, s=s):
                self.copy(kind, s, True).start()

            @pl.when(both(inside(s), both(hops > 0, hops < last)))
            def _(kind=kind, s=s, buf=buf):
                self.copy(kind, s).wait_recv()
                at = self.near(s)
                own = self.part[self.far(s) if kind == 0 else at]
                buf[at] = (buf[at].astype(F32) + own.astype(F32)).astype(BF)
                self.copy(kind, s).start()

            @pl.when(both(inside(s), hops == last))
            def _(kind=kind, s=s, buf=buf):
                self.copy(kind, s).wait_recv()
                to = self.far(s) if kind == 0 else self.near(s)
                total = buf[self.near(s)].astype(F32) + self.part[to].astype(F32)
                if self.finalize is not None:
                    total = self.finalize(self.near(s), total)
                self.out[to] = total.astype(BF)
                self.copy(3 - kind, s).start()

        for kind in (2, 3):
            hops = z if kind == 2 else last - z
            s = k - lag * (last + hops)

            @pl.when(both(inside(s), hops > 0))
            def _(kind=kind, s=s, hops=hops):
                self.copy(kind, s).wait_recv()

                @pl.when(hops < last)
                def _():
                    self.copy(kind, s).start()

    def run(self, first, last):
        def one(k, c):
            self.step(k)
            return c

        lax.fori_loop(first, last, one, 0)

    def drain(self):
        def one(s, c):
            for kind in range(4):

                @pl.when(self.z < self.n - 1 if kind % 2 == 0 else self.z > 0)
                def _(kind=kind):
                    self.copy(kind, s).wait_send()

            return c

        lax.fori_loop(0, self.subs, one, 0)


def chain_scratch(rows, width, subs):
    return [
        pltpu.VMEM((rows // 2, width), BF),
        pltpu.VMEM((rows // 2, width), BF),
        pltpu.SemaphoreType.DMA((4, subs)),
        pltpu.SemaphoreType.DMA((4, subs)),
    ]


SUBS, LAG = 16, 2
ANY = pl.BlockSpec(memory_space=pl.ANY)
BIG = VMEM_BYTES - (1 << 20)


def norm_parts(values):
    r = lax.rsqrt(jnp.mean(values * values, axis=-1, keepdims=True) + EPSILON)
    return r, values * r


def fold8(x):
    return jnp.sum(x.reshape(x.shape[0] // 8, 8, x.shape[1]), axis=0)


def half_loads(z, n, half, whole, halves, sem):
    at = pl.ds(pl.multiple_of(jnp.where(z == 0, 0, half), half), half)
    pairs = [(ref.at[at], to) for ref, to in whole] + halves
    return [pltpu.make_async_copy(ref, to, sem.at[i]) for i, (ref, to) in enumerate(pairs)]


def run_with_loads(ch, end, loads):
    @pl.when(end)
    def _():
        for c in loads:
            c.start()

    need = ch.lag * (ch.n - 1)
    ch.run(0, need)

    @pl.when(end)
    def _():
        for c in loads:
            c.wait()

    ch.run(need, ch.steps)


def chain_ffn_kernel(
    n, part_ref, g_ref, live_ref, x_ref, attn_ref, vec_ref, out_ref, dmid_ref, sum_ref, rbuf, lbuf, ssem, rsem, gv, lv, xv, av, csem
):
    z = lax.axis_index("head")
    line_barrier(z, n)
    sum_ref[...] = jnp.zeros_like(sum_ref)
    tanh_attn, gain = vec_ref[0:1], vec_ref[1:2]

    def finalize(at, dh):
        attn, live = av[at], lv[at, 0:1]
        mid = xv[at].astype(F32) + live * tanh_attn * attn
        r, u = norm_parts(mid)
        w = dh * gain
        dmid = gv[at].astype(F32) + r * (w - u * jnp.mean(w * u, axis=-1, keepdims=True))
        dmid_ref[at] = dmid
        masked = dmid * live
        sum_ref[0:8] += fold8(dh * u)
        sum_ref[8:16] += fold8(masked * attn)
        return masked * tanh_attn

    ch = Chain(n, SUBS, LAG, part_ref, out_ref, rbuf, lbuf, ssem, rsem, finalize)
    loads = half_loads(z, n, ch.half, [(g_ref, gv), (live_ref, lv), (x_ref, xv), (attn_ref, av)], [], csem)
    run_with_loads(ch, jnp.logical_or(z == 0, z == n - 1), loads)
    ch.drain()


def chain_ffn(part, g, live, x, attn, vec, cid):
    n = lax.axis_size("head")
    rows, width = part.shape
    half = rows // 2
    return pl.pallas_call(
        functools.partial(chain_ffn_kernel, n),
        out_shape=(S((rows, width), BF), S((half, width), F32), S((16, width), F32)),
        in_specs=[VM, ANY, ANY, ANY, ANY, VM],
        out_specs=(VM,) * 3,
        scratch_shapes=chain_scratch(rows, width, SUBS)
        + [
            pltpu.VMEM((half, width), BF),
            pltpu.VMEM((half, 128), F32),
            pltpu.VMEM((half, width), BF),
            pltpu.VMEM((half, width), F32),
            pltpu.SemaphoreType.DMA((4,)),
        ],
        compiler_params=pltpu.CompilerParams(collective_id=cid, has_side_effects=True, vmem_limit_bytes=VMEM_BYTES // 2),
        cost_estimate=pl.CostEstimate(flops=80_000_000_000, bytes_accessed=20 * rows * width, transcendentals=0),
        name="chain_ffn",
    )(part, g, live, x, attn, vec)


def chain_rows_kernel(
    n, part_ref, x_ref, dmid_ref, gain_ref, sum_ref, out_ref, tot_ref, rbuf, lbuf, ssem, rsem, xv, dv, csem, acc, ends, esem, fsem
):
    z = lax.axis_index("head")
    line_barrier(z, n)
    acc[...] = jnp.zeros_like(acc)
    gain = gain_ref[0:1]

    def finalize(at, dh):
        r, u = norm_parts(xv[at].astype(F32))
        w = dh * gain
        acc[...] += fold8(dh * u)
        return dv[at] + r * (w - u * jnp.mean(w * u, axis=-1, keepdims=True))

    ch = Chain(n, SUBS, LAG, part_ref, out_ref, rbuf, lbuf, ssem, rsem, finalize)
    loads = half_loads(z, n, ch.half, [(x_ref, xv)], [(dmid_ref, dv)], csem)
    run_with_loads(ch, jnp.logical_or(z == 0, z == n - 1), loads)

    width = acc.shape[1]
    rows = [sum_ref[0:8], sum_ref[8:16], acc[...]]
    mine = jnp.concatenate([jnp.sum(r, axis=0, keepdims=True) for r in rows] + [jnp.zeros((5, width), F32)], axis=0)
    for e, where in ((0, 0), (1, n - 1)):

        @pl.when(z == where)
        def _(e=e):
            ends[e] = mine

    def copy(e):
        return pltpu.make_async_remote_copy(
            src_ref=ends.at[e],
            dst_ref=ends.at[e],
            send_sem=esem.at[e],
            recv_sem=fsem.at[e],
            device_id=to_head(z + (1 if e == 0 else -1)),
            device_id_type=pl.DeviceIdType.MESH,
        )

    for e, source, sink in ((0, 0, n - 1), (1, n - 1, 0)):

        @pl.when(z == source)
        def _(e=e):
            copy(e).start()

    for e, source, sink in ((0, 0, n - 1), (1, n - 1, 0)):

        @pl.when(z != source)
        def _(e=e, sink=sink):
            copy(e).wait_recv()

            @pl.when(z != sink)
            def _():
                copy(e).start()

    tot_ref[...] = ends[0] + ends[1]
    for e, sink in ((0, n - 1), (1, 0)):

        @pl.when(z != sink)
        def _(e=e):
            copy(e).wait_send()

    ch.drain()


def chain_rows(part, x, dmid, gain, sums, cid):
    n = lax.axis_size("head")
    rows, width = part.shape
    half = rows // 2
    return pl.pallas_call(
        functools.partial(chain_rows_kernel, n),
        out_shape=(S((rows, width), BF), S((8, width), F32)),
        in_specs=[VM, ANY, ANY, VM, VM],
        out_specs=(VM,) * 2,
        scratch_shapes=chain_scratch(rows, width, SUBS)
        + [
            pltpu.VMEM((half, width), BF),
            pltpu.VMEM((half, width), F32),
            pltpu.SemaphoreType.DMA((2,)),
            pltpu.VMEM((8, width), F32),
            pltpu.VMEM((2, 8, width), F32),
            pltpu.SemaphoreType.DMA((2,)),
            pltpu.SemaphoreType.DMA((2,)),
        ],
        compiler_params=pltpu.CompilerParams(collective_id=cid, has_side_effects=True, vmem_limit_bytes=VMEM_BYTES // 2),
        cost_estimate=pl.CostEstimate(flops=80_000_000_000, bytes_accessed=20 * rows * width, transcendentals=0),
        name="chain_rows",
    )(part, x, dmid, gain, sums)


def wgrad_kernel(a_ref, b_ref, c_ref, d_ref, o_ref):
    nb = b_ref.shape[1]
    o_ref[:, :nb] = tn(a_ref[...], b_ref[...]).astype(BF)
    o_ref[:, nb:] = tn(c_ref[...], d_ref[...]).astype(BF)


def wgrad_pair(a, b, c, d):
    rows, width = a.shape
    cols = b.shape[1] + d.shape[1]
    wb = min(256, width)
    return pl.pallas_call(
        wgrad_kernel,
        grid=(width // wb,),
        in_specs=[
            pl.BlockSpec((rows, wb), lambda i: (0, i)),
            pl.BlockSpec(b.shape, lambda i: (0, 0)),
            pl.BlockSpec((rows, wb), lambda i: (0, i)),
            pl.BlockSpec(d.shape, lambda i: (0, 0)),
        ],
        out_specs=pl.BlockSpec((wb, cols), lambda i: (i, 0)),
        out_shape=S((width, cols), BF),
        compiler_params=pltpu.CompilerParams(vmem_limit_bytes=VMEM_BYTES // 2),
        cost_estimate=pl.CostEstimate(flops=2 * rows * width * cols, bytes_accessed=2 * width * cols, transcendentals=0),
        name="wgrad_pair",
    )(a, b, c, d)


def qkv_kernel(x_ref, gain_ref, w_ref, hg_ref, cos_ref, sin_ref, live_ref, h_ref, pre_ref, q_ref, kv_ref):
    x = x_ref[...].astype(F32)
    n = lax.rsqrt(jnp.mean(x * x, axis=-1, keepdims=True) + EPSILON)
    h = (x * n * gain_ref[...]).astype(BF)
    h_ref[...] = h
    width = w_ref.shape[2]
    cos, sin, live = cos_ref[...], sin_ref[...], live_ref[...]
    for part in range(2):
        pre = nn(h, w_ref[part])
        pre_ref[:, part * width : (part + 1) * width] = pre
        for p in range(width // 128):
            v = pre[:, p * 128 : (p + 1) * 128]
            r = lax.rsqrt(head_mean(v * v) + EPSILON)
            t = v * r * hg_ref[part : part + 1, p * 128 : (p + 1) * 128]
            y = t * cos + swap_halves(t) * sin
            if part == 0:
                q_ref[:, p * 128 : (p + 1) * 128] = y.astype(BF)
            else:
                kv_ref[:, p * 128 : (p + 1) * 128] = (y * live).astype(BF)
    val = nn(h, w_ref[2])
    for p in range(width // 128):
        kv_ref[:, width + p * 128 : width + (p + 1) * 128] = (val[:, p * 128 : (p + 1) * 128] * live).astype(BF)


def make_qkv(x, gain, w, head_gains, cos, sin, live):
    rows, width = x.shape
    inner = w.shape[2]
    rb = min(256, rows)
    return pl.pallas_call(
        qkv_kernel,
        grid=(rows // rb,),
        in_specs=[
            pl.BlockSpec((rb, width), lambda i: (i, 0)),
            pl.BlockSpec((1, width), lambda i: (0, 0)),
            pl.BlockSpec(w.shape, lambda i: (0, 0, 0)),
            pl.BlockSpec((8, inner), lambda i: (0, 0)),
            pl.BlockSpec((rb, 128), lambda i: (i, 0)),
            pl.BlockSpec((rb, 128), lambda i: (i, 0)),
            pl.BlockSpec((rb, 128), lambda i: (i, 0)),
        ],
        out_specs=(
            pl.BlockSpec((rb, width), lambda i: (i, 0)),
            pl.BlockSpec((rb, 2 * inner), lambda i: (i, 0)),
            pl.BlockSpec((rb, inner), lambda i: (i, 0)),
            pl.BlockSpec((rb, 2 * inner), lambda i: (i, 0)),
        ),
        out_shape=(S((rows, width), BF), S((rows, 2 * inner), F32), S((rows, inner), BF), S((rows, 2 * inner), BF)),
        compiler_params=pltpu.CompilerParams(vmem_limit_bytes=VMEM_BYTES // 2),
        cost_estimate=pl.CostEstimate(flops=6 * rows * width * inner, bytes_accessed=12 * rows * width, transcendentals=0),
        name="make_qkv",
    )(x, gain, w, head_gains, cos, sin, live)


def qkv_back_kernel(dq_ref, dkv_ref, peer_ref, pre_ref, hg_ref, cos_ref, sin_ref, w_ref, dpre_ref, gg_ref, dh_ref):
    width = dq_ref.shape[1]
    rows = dq_ref.shape[0]

    @pl.when(pl.program_id(0) == 0)
    def _():
        gg_ref[...] = jnp.zeros_like(gg_ref)

    cos, sin = cos_ref[...], sin_ref[...]
    total = None
    for part in range(2):
        for p in range(width // 128):
            ls = slice(p * 128, (p + 1) * 128)
            pls = slice(part * width + p * 128, part * width + (p + 1) * 128)
            if part == 0:
                dy = dq_ref[:, ls]
            else:
                dy = dkv_ref[:, ls] + peer_ref[:, ls].astype(F32)
            dt = dy * cos - swap_halves(dy) * sin
            v = pre_ref[:, pls]
            r = lax.rsqrt(head_mean(v * v) + EPSILON)
            u = v * r
            w = dt * hg_ref[part : part + 1, ls]
            dv = r * (w - u * head_mean(w * u))
            dpre_ref[:, pls] = dv.astype(BF)
            gg_ref[part * 8 : part * 8 + 8, ls] += jnp.sum((dt * u).reshape(rows // 8, 8, 128), axis=0)
        g = nt(dpre_ref[:, part * width : (part + 1) * width], w_ref[part])
        total = g if total is None else total + g
    dpre_ref[:, 2 * width :] = (dkv_ref[:, width:] + peer_ref[:, width:].astype(F32)).astype(BF)
    total = total + nt(dpre_ref[:, 2 * width :], w_ref[2])
    dh_ref[...] = total.astype(BF)


def qkv_back(dq, dkv, peer, pre, head_gains, cos, sin, w):
    rows, inner = dq.shape
    width = w.shape[1]
    rb = min(256, rows)
    blk = lambda c: pl.BlockSpec((rb, c), lambda i: (i, 0))
    return pl.pallas_call(
        qkv_back_kernel,
        grid=(rows // rb,),
        in_specs=[
            blk(inner),
            blk(2 * inner),
            blk(2 * inner),
            blk(2 * inner),
            pl.BlockSpec((8, inner), lambda i: (0, 0)),
            blk(128),
            blk(128),
            pl.BlockSpec(w.shape, lambda i: (0, 0, 0)),
        ],
        out_specs=(blk(3 * inner), pl.BlockSpec((16, inner), lambda i: (0, 0)), blk(width)),
        out_shape=(S((rows, 3 * inner), BF), S((16, inner), F32), S((rows, width), BF)),
        compiler_params=pltpu.CompilerParams(vmem_limit_bytes=VMEM_BYTES // 2),
        cost_estimate=pl.CostEstimate(flops=6 * rows * width * inner, bytes_accessed=12 * rows * width, transcendentals=0),
        name="qkv_back",
    )(dq, dkv, peer, pre, head_gains, cos, sin, w)


def middle_kernel(mixed_ref, w_ref, x_ref, live_ref, vec_ref, attn_ref, h_ref):
    total = None
    for g in range(mixed_ref.shape[0]):
        t = nn(mixed_ref[g], w_ref[g]).astype(BF).astype(F32)
        total = t if total is None else total + t
    attn_ref[...] = total
    mid = x_ref[...].astype(F32) + live_ref[:, 0:1] * vec_ref[0:1] * total
    _, u = norm_parts(mid)
    h_ref[...] = (u * vec_ref[1:2]).astype(BF)


def make_middle(mixed_all, w_all, x, live, vec):
    n, rows, inner = mixed_all.shape
    width = x.shape[1]
    rb = min(256, rows)
    blk = lambda c: pl.BlockSpec((rb, c), lambda i: (i, 0))
    return pl.pallas_call(
        middle_kernel,
        grid=(rows // rb,),
        in_specs=[
            pl.BlockSpec((n, rb, inner), lambda i: (0, i, 0)),
            pl.BlockSpec(w_all.shape, lambda i: (0, 0, 0)),
            blk(width),
            blk(128),
            pl.BlockSpec((8, width), lambda i: (0, 0)),
        ],
        out_specs=(blk(width), blk(width)),
        out_shape=(S((rows, width), F32), S((rows, width), BF)),
        compiler_params=pltpu.CompilerParams(vmem_limit_bytes=VMEM_BYTES // 2),
        cost_estimate=pl.CostEstimate(flops=2 * n * rows * width * inner, bytes_accessed=14 * rows * width, transcendentals=0),
        name="make_middle",
    )(mixed_all, w_all, x, live, vec)


def attend_kernel(
    n, scale, qb, kc, q_ref, kv_ref, peer_ref, live_ref, ck_ref, cv_ref, gate_ref, mixed_ref, self_ref, cross_ref, lse_ref,
    va_ref, cva_ref, ssem, rsem,
):
    z = lax.axis_index("head")
    line_barrier(z, n)
    rows, width = q_ref.shape
    txt = ck_ref.shape[0]
    c = scale * LOG2E
    va_ref[:, 128:] = live_ref[...]
    cva_ref[:, 128:] = jnp.ones((txt, 128), BF)
    first = lax.broadcasted_iota(jnp.int32, (qb, 128), 1) < 64

    def copy(kind, o, p):
        view = mixed_ref.at[o, :, pl.ds(pl.multiple_of(p * 128, 128), 128)]
        return pltpu.make_async_remote_copy(
            src_ref=view,
            dst_ref=view,
            send_sem=ssem.at[kind, o, p],
            recv_sem=rsem.at[kind, o, p],
            device_id=to_head(z + (1 if kind == 0 else -1)),
            device_id_type=pl.DeviceIdType.MESH,
        )

    def send_own(p):
        @pl.when(z < n - 1)
        def _():
            copy(0, z, p).start()

        @pl.when(z > 0)
        def _():
            copy(1, z, p).start()

    def relay(d, p):
        @pl.when(z - d >= 0)
        def _():
            copy(0, z - d, p).wait_recv()

            @pl.when(z < n - 1)
            def _():
                copy(0, z - d, p).start()

        @pl.when(z + d < n)
        def _():
            copy(1, z + d, p).wait_recv()

            @pl.when(z > 0)
            def _():
                copy(1, z + d, p).start()

    def pair(p, _):
        lanes = pl.ds(pl.multiple_of(p * 128, 128), 128)
        vlanes = pl.ds(pl.multiple_of(width + p * 128, 128), 128)
        va_ref[:rows, :128] = kv_ref[:, vlanes]
        va_ref[rows:, :128] = peer_ref[:, vlanes]
        cva_ref[:, :128] = cv_ref[:, lanes]
        gate = gate_ref[:, lanes]

        def block(b, _):
            rs = pl.ds(pl.multiple_of(b * qb, qb), qb)
            qp = q_ref[rs, lanes]
            outs, couts = [], []
            for a in range(2):
                qm = jnp.where(first if a == 0 else jnp.logical_not(first), qp, jnp.zeros_like(qp))
                acc = None
                for side in range(2):
                    keys = kv_ref if side == 0 else peer_ref
                    for j in range(0, rows, kc):
                        s = nt(qm, keys[j : j + kc, lanes])
                        pr = jnp.exp2(s * c).astype(BF)
                        o = nn(pr, va_ref[side * rows + j : side * rows + j + kc, :])
                        acc = o if acc is None else acc + o
                outs.append(acc)
                s = nt(qm, ck_ref[:, lanes])
                couts.append(nn(jnp.exp2(s * c).astype(BF), cva_ref[...]))
            so = jnp.where(first, outs[0][:, :128], outs[1][:, :128])
            sl = jnp.where(first, outs[0][:, 128:], outs[1][:, 128:])
            co = jnp.where(first, couts[0][:, :128], couts[1][:, :128])
            cl = jnp.where(first, couts[0][:, 128:], couts[1][:, 128:])
            so = so / sl
            co = co / cl
            mixed_ref[z, rs, lanes] = (so + gate * co).astype(BF)
            self_ref[rs, lanes] = so
            cross_ref[rs, lanes] = co
            lt = jnp.log2(sl).T
            ct = jnp.log2(cl).T
            lse_ref[p, :, rs] = jnp.concatenate([lt[0:1], lt[64:65], ct[0:1], ct[64:65], lt[0:4]], axis=0)
            return 0

        lax.fori_loop(0, rows // qb, block, 0)

        @pl.when(p >= 1)
        def _():
            relay(1, p - 1)

        send_own(p)
        return 0

    pairs = width // 128
    lax.fori_loop(0, pairs, pair, 0)
    for t in range(pairs + n - 2):
        for d in range(1, n):
            if 0 <= t - (d - 1) < pairs and (d > 1 or t == pairs - 1):
                relay(d, t - (d - 1))
    for p in range(pairs):
        for o in range(n):

            @pl.when(both(z >= o, z < n - 1))
            def _(o=o, p=p):
                copy(0, o, p).wait_send()

            @pl.when(both(z <= o, z > 0))
            def _(o=o, p=p):
                copy(1, o, p).wait_send()


def attend(q, kv, peer, live, ck, cv, gate, scale, cid, qb=256, kc=1024):
    n = lax.axis_size("head")
    rows, width = q.shape
    txt = ck.shape[0]
    qb, kc = min(qb, rows), min(kc, rows)
    return pl.pallas_call(
        functools.partial(attend_kernel, n, scale, qb, kc),
        out_shape=(S((n, rows, width), BF), S((rows, width), F32), S((rows, width), F32), S((width // 128, 8, rows), F32)),
        in_specs=[VM] * 7,
        out_specs=(VM,) * 4,
        scratch_shapes=[
            pltpu.VMEM((2 * rows, 256), BF),
            pltpu.VMEM((txt, 256), BF),
            pltpu.SemaphoreType.DMA((2, n, width // 128)),
            pltpu.SemaphoreType.DMA((2, n, width // 128)),
        ],
        compiler_params=pltpu.CompilerParams(collective_id=cid, has_side_effects=True, vmem_limit_bytes=VMEM_BYTES // 2),
        cost_estimate=pl.CostEstimate(flops=32 * rows * rows * width, bytes_accessed=12 * rows * width, transcendentals=0),
        name="attend",
    )(q, kv, peer, live, ck, cv, gate)


def attend_back_kernel(
    n,
    per,
    scale,
    qb,
    kc,
    q_ref,
    kv_ref,
    peer_ref,
    live_ref,
    ck_ref,
    cv_ref,
    gate_ref,
    self_ref,
    cross_ref,
    lse_ref,
    dm_ref,
    part_ref,
    dq_ref,
    dkv_ref,
    dpeer_ref,
    dck_ref,
    dcv_ref,
    gg_ref,
    fsum_ref,
    kt_ref,
    ckt_ref,
    p_ref,
    d_ref,
    ak_ref,
    av_ref,
    rbuf,
    lbuf,
    ssem,
    rsem,
):
    line_barrier(lax.axis_index("head"), n)
    ch = Chain(n, SUBS, LAG, part_ref, fsum_ref, rbuf, lbuf, ssem, rsem)
    rows, width = q_ref.shape
    txt = ck_ref.shape[0]
    c = scale * LOG2E
    first = lax.broadcasted_iota(jnp.int32, (qb, 128), 1) < 64
    head_row = lax.broadcasted_iota(jnp.int32, (8, 128), 0)
    head_lane = lax.broadcasted_iota(jnp.int32, (8, 128), 1) // 64
    ind = (head_row == head_lane).astype(F32)

    def head_sum(x):
        return lax.dot_general(ind, x, (((1,), (1,)), ((), ())), preferred_element_type=F32, precision=HIGHEST)

    def pair(p, _):
        lanes = pl.ds(pl.multiple_of(p * 128, 128), 128)
        vlanes = pl.ds(pl.multiple_of(width + p * 128, 128), 128)
        kt_ref[:, :rows] = kv_ref[:, lanes].T
        kt_ref[:, rows:] = peer_ref[:, lanes].T
        ckt_ref[...] = ck_ref[:, lanes].T
        gate = gate_ref[:, lanes]
        ak_ref[...] = jnp.zeros_like(ak_ref)
        av_ref[...] = jnp.zeros_like(av_ref)
        dck_ref[:, lanes] = jnp.zeros((txt, 128), F32)
        dcv_ref[:, lanes] = jnp.zeros((txt, 128), F32)
        gg_ref[:, lanes] = jnp.zeros((8, 128), F32)

        def block(b, _):
            rs = pl.ds(pl.multiple_of(b * qb, qb), qb)
            qp = q_ref[rs, lanes]
            dm = dm_ref[rs, lanes]
            dmf = dm.astype(F32)
            dcf = (gate * dmf).astype(BF)
            delta = head_sum(dmf * self_ref[rs, lanes])
            ce = dmf * cross_ref[rs, lanes]
            gg_ref[:, lanes] += jnp.sum(ce.reshape(qb // 8, 8, 128), axis=0)
            cdelta = head_sum(dcf.astype(F32) * cross_ref[rs, lanes])
            z = jnp.zeros_like(qp)
            masks = (first, jnp.logical_not(first))
            qs = [jnp.where(m, qp, z) for m in masks]
            dms = [jnp.where(m, dm, z) for m in masks]
            dcs = [jnp.where(m, dcf, z) for m in masks]
            qstack = jnp.concatenate(qs, axis=0)
            dstack = jnp.concatenate(dms, axis=0)
            dcstack = jnp.concatenate(dcs, axis=0)
            lse = lse_ref[p, :, rs]
            dqt = [None, None]
            for side in range(2):
                src = kv_ref if side == 0 else peer_ref
                for j in range(0, rows, kc):
                    at = side * rows + j
                    for a in range(2):
                        s = nt(src[j : j + kc, lanes], qs[a])
                        pr = jnp.exp2(s * c - lse[a : a + 1])
                        dp = nt(src[j : j + kc, vlanes], dms[a])
                        p_ref[:, a * qb : (a + 1) * qb] = pr.astype(BF)
                        dd = (pr * (dp - delta[a : a + 1])).astype(BF)
                        d_ref[:, a * qb : (a + 1) * qb] = dd
                        t = nn(kt_ref[a * 64 : (a + 1) * 64, at : at + kc], dd)
                        dqt[a] = t if dqt[a] is None else dqt[a] + t
                    av_ref[at : at + kc] += nn(p_ref[...], dstack)
                    ak_ref[at : at + kc] += nn(d_ref[...], qstack)
            for a in range(2):
                s = nt(ck_ref[:, lanes], qs[a])
                pr = jnp.exp2(s * c - lse[2 + a : 3 + a])
                dp = nt(cv_ref[:, lanes], dcs[a])
                p_ref[:txt, a * qb : (a + 1) * qb] = pr.astype(BF)
                dd = (pr * (dp - cdelta[a : a + 1])).astype(BF)
                d_ref[:txt, a * qb : (a + 1) * qb] = dd
                dqt[a] = dqt[a] + nn(ckt_ref[a * 64 : (a + 1) * 64, :], dd)
            dcv_ref[:, lanes] += nn(p_ref[:txt, :], dcstack)
            dck_ref[:, lanes] += nn(d_ref[:txt, :], qstack)
            dq_ref[rs, lanes] = (jnp.concatenate(dqt, axis=0) * scale).T
            for i in range(per):
                k = (p * (rows // qb) + b) * per + i

                @pl.when(k < ch.steps)
                def _(k=k):
                    ch.step(k)

            return 0

        lax.fori_loop(0, rows // qb, block, 0)
        live = live_ref[...].astype(F32)
        dkv_ref[:, lanes] = ak_ref[:rows] * (live[:rows] * scale)
        dkv_ref[:, vlanes] = av_ref[:rows] * live[:rows]
        dpeer_ref[:, lanes] = (ak_ref[rows:] * (live[rows:] * scale)).astype(BF)
        dpeer_ref[:, vlanes] = (av_ref[rows:] * live[rows:]).astype(BF)
        dck_ref[:, lanes] = dck_ref[:, lanes] * scale
        return 0

    lax.fori_loop(0, width // 128, pair, 0)
    ch.run(min(ch.steps, (width // 128) * (rows // qb) * per), ch.steps)
    ch.drain()


def attend_back(q, kv, peer, live, ck, cv, gate, so, co, lse, dm, part, scale, cid, qb=256, kc=512, per=2):
    n = lax.axis_size("head")
    rows, width = q.shape
    txt = ck.shape[0]
    qb, kc = min(qb, rows), min(kc, rows)
    return pl.pallas_call(
        functools.partial(attend_back_kernel, n, per, scale, qb, kc),
        out_shape=(
            S((rows, width), F32),
            S((rows, 2 * width), F32),
            S((rows, 2 * width), BF),
            S((txt, width), F32),
            S((txt, width), F32),
            S((8, width), F32),
            S(part.shape, BF),
        ),
        in_specs=[VM] * 12,
        out_specs=(VM,) * 7,
        scratch_shapes=[
            pltpu.VMEM((128, 2 * rows), BF),
            pltpu.VMEM((128, txt), BF),
            pltpu.VMEM((kc, 2 * qb), BF),
            pltpu.VMEM((kc, 2 * qb), BF),
            pltpu.VMEM((2 * rows, 128), F32),
            pltpu.VMEM((2 * rows, 128), F32),
        ]
        + chain_scratch(*part.shape, SUBS),
        compiler_params=pltpu.CompilerParams(collective_id=cid, has_side_effects=True, vmem_limit_bytes=BIG),
        cost_estimate=pl.CostEstimate(flops=80 * rows * rows * width, bytes_accessed=20 * rows * width, transcendentals=0),
        name="attend_back",
    )(q, kv, peer, live, ck, cv, gate, so, co, lse, dm, part)


def pair_swap(value):
    pairs = [(source, source ^ 1) for source in range(lax.axis_size("seq"))]
    return lax.ppermute(value, "seq", pairs)


def rope_tables(grid_rows, grid_cols, first_token, row_count, head_size):
    stride = grid_cols + 1
    tokens = first_token + jnp.arange(row_count, dtype=jnp.int32)
    valid = tokens < grid_rows * stride
    row_pos = (tokens // stride).astype(F32)
    col_pos = (tokens % stride).astype(F32)
    quarter = head_size // 4
    half = head_size // 2
    lane = jnp.arange(128, dtype=jnp.int32) % half
    frequency = ROPE_BASE ** (-(lane % quarter).astype(F32) / quarter)
    angles = jnp.where(lane[None, :] < quarter, row_pos[:, None], col_pos[:, None]) * frequency[None, :]
    sign = jnp.where(jnp.arange(128) % head_size < half, -1.0, 1.0)
    return jnp.cos(angles), jnp.sin(angles) * sign[None, :], valid


def scatter(v):
    return lax.psum_scatter(v, "seq", scatter_dimension=0, tiled=True).astype(F32)


def local(
    image_rows,
    condition,
    text_feats,
    grid_shape,
    text_slot,
    attn_gain,
    ffn_gain,
    mod_weight,
    mod_bias,
    qkv_weight,
    qk_gains,
    text_kv_weight,
    cross_gate,
    out_weight,
    gate_up_weight,
    down_weight,
    cotangent,
):
    row_count, model_width = image_rows.shape
    head_local, head_size = qk_gains.shape[1], qk_gains.shape[2]
    inner = head_local * head_size
    ff_local = down_weight.shape[0]
    text_local, cap_width = text_feats.shape
    head_count = lax.axis_size("head")
    seq_count = lax.axis_size("seq")
    seq_index = lax.axis_index("seq")
    head_index = lax.axis_index("head")
    image_index = seq_index // 2
    pair_half = seq_index % 2
    score_scale = head_size ** (-0.5)
    image_count = condition.shape[0]

    grid_pair = lax.dynamic_index_in_dim(grid_shape, image_index, 0, keepdims=False)
    cos, sin, valid = rope_tables(grid_pair[0], grid_pair[1], pair_half * row_count, row_count, head_size)
    keep = valid.astype(F32)[:, None]
    live_own = jnp.broadcast_to(keep, (row_count, 128))
    peer_tokens = (1 - pair_half) * row_count + jnp.arange(row_count, dtype=jnp.int32)
    keep_peer = (peer_tokens < grid_pair[0] * (grid_pair[1] + 1)).astype(F32)[:, None]
    live_all = jnp.concatenate([live_own, jnp.broadcast_to(keep_peer, (row_count, 128))], axis=0).astype(BF)

    cond_all = jax.nn.silu(condition.astype(F32)).astype(BF)
    cond_low = lax.dynamic_index_in_dim(cond_all, image_index, 0, keepdims=True)
    mod_piece = jnp.dot(cond_low, mod_weight, preferred_element_type=F32) + mod_bias
    modulation = lax.all_gather(mod_piece, "head", axis=0, tiled=True)
    one_attn = 1.0 + modulation[0]
    one_ffn = 1.0 + modulation[2]
    tanh_attn = jnp.tanh(modulation[1])
    tanh_ffn = jnp.tanh(modulation[3])

    head_gains = jnp.concatenate([qk_gains.reshape(3, inner), jnp.zeros((5, inner), F32)], axis=0)
    gate_head = jnp.tanh(cross_gate)
    gate_lanes = jnp.repeat(gate_head, head_size)[None, :]
    qkv_mats = jnp.transpose(qkv_weight, (1, 0, 2))
    same_head = (jnp.arange(inner)[:, None] // head_size == jnp.arange(inner)[None, :] // head_size).astype(F32) / head_size

    text_kv_flat = text_kv_weight.reshape(cap_width, 2 * inner)
    text_proj = jnp.dot(text_feats, text_kv_flat, preferred_element_type=F32)
    cap_pre = text_proj[:, :inner]
    cap_r = lax.rsqrt(jnp.dot(cap_pre * cap_pre, same_head, precision=HIGHEST) + EPSILON)
    cap_u = cap_pre * cap_r
    cap_kv = jnp.concatenate([cap_u * head_gains[2:3], text_proj[:, inner:]], axis=1).astype(BF)
    caps = lax.all_gather(cap_kv, "seq", axis=0, tiled=False)
    slot = lax.dynamic_index_in_dim(text_slot, image_index, 0, keepdims=False)
    cap_own = lax.dynamic_index_in_dim(caps, slot, 0, keepdims=False)
    cap_key, cap_value = cap_own[:, :inner], cap_own[:, inner:]

    slice_rows = inner // seq_count
    out_slice = lax.dynamic_slice_in_dim(out_weight, seq_index * slice_rows, slice_rows, 0)
    out_all = lax.all_gather(out_slice, ("head", "seq"), axis=0, tiled=True).reshape(head_count, inner, model_width)

    normed, pre, query, kv = make_qkv(image_rows, (attn_gain * one_attn)[None, :], qkv_mats, head_gains, cos, sin, live_own)
    kv_peer = pair_swap(kv)
    mixed_all, self_out, cross_out, lse = attend(query, kv, kv_peer, live_all, cap_key, cap_value, gate_lanes, score_scale, 0)
    mixed = lax.dynamic_index_in_dim(mixed_all, head_index, 0, keepdims=False)
    vec = jnp.concatenate([jnp.stack([tanh_attn, ffn_gain * one_ffn, attn_gain * one_attn]), jnp.zeros((5, model_width), F32)])
    attn_out, ffn_low = make_middle(mixed_all, out_all, image_rows, live_own, vec)

    gate_up_flat = gate_up_weight.reshape(model_width, 2 * ff_local)
    gate_up = jnp.dot(ffn_low, gate_up_flat, preferred_element_type=F32)
    gate_pre, up_pre = gate_up[:, :ff_local], gate_up[:, ff_local:]
    sig = jax.nn.sigmoid(gate_pre)
    hidden_low = (gate_pre * sig * up_pre).astype(BF)
    grad_out = cotangent.astype(F32)
    ffn_grad_low = (grad_out * keep * tanh_ffn).astype(BF)
    hidden_grad = nt(ffn_grad_low, down_weight)
    gate_grad = hidden_grad * up_pre * sig * (1.0 + gate_pre * (1.0 - sig))
    up_grad = hidden_grad * (gate_pre * sig)
    gate_up_grad_low = jnp.concatenate([gate_grad.astype(BF), up_grad.astype(BF)], axis=1)
    ffn_in_part = nt(gate_up_grad_low, gate_up_flat).astype(BF)
    ffn_part = jnp.dot(hidden_low, down_weight, preferred_element_type=F32).astype(BF)
    ffn_wgrad = wgrad_pair(ffn_low, gate_up_grad_low, ffn_grad_low, hidden_low)
    ffn_in_part, ffn_wgrad, ffn_part = lax.optimization_barrier((ffn_in_part, ffn_wgrad, ffn_part))
    ffn_wsum = scatter(ffn_wgrad)

    attn_grad_low, middle_grad_half, ffn_rows = chain_ffn(ffn_in_part, cotangent, live_own, image_rows, attn_out, vec, 1)
    mixed_grad = nt(attn_grad_low, out_weight).astype(BF)
    dq, dkv, dpeer, dck, dcv, gate_rows, ffn_out = attend_back(
        query, kv, kv_peer, live_all, cap_key, cap_value, gate_lanes, self_out, cross_out, lse, mixed_grad, ffn_part, score_scale, 2
    )
    from_peer = pair_swap(dpeer)
    ffn_out = ffn_out.astype(F32)
    output = (image_rows.astype(F32) + keep * tanh_attn * attn_out + keep * tanh_ffn * ffn_out).astype(BF)
    gate_ffn_grad = jnp.sum(grad_out * keep * ffn_out, axis=0) * (1.0 - tanh_ffn * tanh_ffn)
    grad_pre, gain_rows, attn_in_part = qkv_back(dq, dkv, from_peer, pre, head_gains, cos, sin, qkv_mats)
    attn_wgrad = wgrad_pair(normed, grad_pre, attn_grad_low, mixed)
    attn_in_part, attn_wgrad = lax.optimization_barrier((attn_in_part, attn_wgrad))
    attn_wsum = scatter(attn_wgrad)
    rows_grad, row_sums = chain_rows(attn_in_part, image_rows, middle_grad_half, vec[2:], ffn_rows, 3)
    ffn_sum, attn_sum = row_sums[0], row_sums[2]
    gate_attn_grad = row_sums[1] * (1.0 - tanh_attn * tanh_attn)

    cap_half = jnp.concatenate([dck, dcv], axis=1)
    cap_grads = lax.all_gather(cap_half.astype(BF), "seq", axis=0, tiled=False)
    own_image = jnp.sum(jnp.where(text_slot == seq_index, jnp.arange(image_count), 0))
    used = jnp.any(text_slot == seq_index).astype(F32)
    two = lax.dynamic_slice_in_dim(cap_grads, 2 * own_image, 2, 0).astype(F32)
    cap_grad = (two[0] + two[1]) * used
    cap_dy, cap_dv = cap_grad[:, :inner], cap_grad[:, inner:]
    cap_w = cap_dy * head_gains[2:3]
    cap_pre_grad = cap_r * (cap_w - cap_u * jnp.dot(cap_w * cap_u, same_head, precision=HIGHEST))
    cap_gain = jnp.sum(cap_dy * cap_u, axis=0)
    text_low = jnp.concatenate([cap_pre_grad, cap_dv], axis=1).astype(BF)
    text_weight_grad = tn(text_feats, text_low).astype(BF)
    text_part = nt(text_low, text_kv_flat).astype(BF)
    text_grad = lax.psum_scatter(text_part, "head", scatter_dimension=1, tiled=True).astype(F32)

    mod_grad = jnp.stack([attn_sum * attn_gain, gate_attn_grad, ffn_sum * ffn_gain, gate_ffn_grad])
    own_mod = lax.dynamic_index_in_dim(mod_grad, head_index, 0, keepdims=False)
    gain_grad = jnp.concatenate([gain_rows[0:8].sum(0), gain_rows[8:16].sum(0), cap_gain])
    gate_grad_head = gate_rows.sum(0)
    small = jnp.concatenate([attn_sum * one_attn, ffn_sum * one_ffn, own_mod, gain_grad, gate_grad_head])
    smalls = lax.all_gather(small, "seq", axis=0, tiled=False)
    total = jnp.sum(smalls, axis=0)
    d = model_width
    dl = d // seq_count
    attn_gain_sum = lax.dynamic_slice_in_dim(total[:d], seq_index * dl, dl)
    ffn_gain_sum = lax.dynamic_slice_in_dim(total[d : 2 * d], seq_index * dl, dl)
    mod_bias_sum = lax.dynamic_slice_in_dim(total[2 * d : 3 * d], seq_index * dl, dl)[None, :]
    qk_all = total[3 * d : 3 * d + 3 * inner].reshape(3, head_local, seq_count, head_size // seq_count)
    qk_gain_sum = lax.dynamic_index_in_dim(qk_all, seq_index, 2, keepdims=False)
    gate_sum = total[3 * d + 3 * inner :].reshape(head_local, head_size).sum(-1) * (1.0 - gate_head * gate_head)
    cond_cols = condition.shape[1] // seq_count
    cond_part = lax.dynamic_slice_in_dim(cond_all, seq_index * cond_cols, cond_cols, 1).astype(F32)
    image_mods = smalls[:, 2 * d : 3 * d].reshape(image_count, 2, d).sum(1)
    mod_weight_sum = lax.dot_general(cond_part, image_mods, (((0,), (0,)), ((), ())), precision=HIGHEST)

    split = 2 * ff_local
    gate_up_sum = ffn_wsum[:, :split].reshape(-1, 2, ff_local)
    down_sum = ffn_wsum[:, split:].T
    qkv_sum = attn_wsum[:, : 3 * inner].reshape(-1, 3, inner)
    out_sum = attn_wsum[:, 3 * inner :].T
    text_weight_sum = scatter(text_weight_grad).reshape(-1, 2, inner)
    return (
        output,
        rows_grad,
        text_grad,
        attn_gain_sum,
        ffn_gain_sum,
        mod_weight_sum,
        mod_bias_sum,
        qkv_sum,
        qk_gain_sum,
        text_weight_sum,
        gate_sum,
        out_sum,
        gate_up_sum,
        down_sum,
    )


def solution(mesh):
    return jax.shard_map(
        local,
        mesh=mesh,
        in_specs=(
            P("seq", None),
            P(),
            P("seq", None),
            P(),
            P(),
            P(),
            P(),
            P(None, "head"),
            P("head", None),
            P(None, None, "head"),
            P(None, "head", None),
            P(None, None, "head"),
            P("head"),
            P("head", None),
            P(None, None, "head"),
            P("head", None),
            P("seq", None),
        ),
        out_specs=(
            P("seq", None),
            P("seq", None),
            P("seq", "head"),
            P("seq"),
            P("seq"),
            P("seq", "head"),
            P("head", "seq"),
            P("seq", None, "head"),
            P(None, "head", "seq"),
            P("seq", None, "head"),
            P("head"),
            P("head", "seq"),
            P("seq", None, "head"),
            P("head", "seq"),
        ),
        check_vma=False,
    )
```

```python
import functools

import jax
import jax.numpy as jnp
from jax import lax
from jax.experimental import pallas as pl
from jax.experimental.pallas import tpu as pltpu
from jax.sharding import PartitionSpec as P

TXT = 256
EPSILON = 1e-06
ROPE_BASE = 10000.0
LOG2E = 1.4426950408889634
F32 = jnp.float32
BF = jnp.bfloat16
VMEM_BYTES = 67043328
HIGHEST = lax.Precision.HIGHEST
VM = pl.BlockSpec(memory_space=pltpu.VMEM)
S = jax.ShapeDtypeStruct


def nt(a, b):
    return lax.dot_general(a, b, (((1,), (1,)), ((), ())), preferred_element_type=F32)


def nn(a, b):
    return lax.dot_general(a, b, (((1,), (0,)), ((), ())), preferred_element_type=F32)


def tn(a, b):
    return lax.dot_general(a, b, (((0,), (0,)), ((), ())), preferred_element_type=F32)


def head_mean(x):
    rows = lax.broadcasted_iota(jnp.int32, (128, 128), 0) // 64
    cols = lax.broadcasted_iota(jnp.int32, (128, 128), 1) // 64
    same = jnp.where(rows == cols, 1.0 / 64, 0.0).astype(BF)
    high = x.astype(BF)
    rest = (x - high.astype(F32)).astype(BF)
    return nn(high, same) + nn(rest, same)


def swap_halves(x):
    lane = lax.broadcasted_iota(jnp.int32, x.shape, 1) % 64
    return jnp.where(lane < 32, pltpu.roll(x, 96, 1), pltpu.roll(x, 32, 1))


def to_head(z):
    return {"head": z}


def both(a, b):
    return jnp.logical_and(a, b)


def line_barrier(z, n):
    bar = pltpu.get_barrier_semaphore()
    for ok, other in ((z > 0, z - 1), (z < n - 1, z + 1)):

        @pl.when(ok)
        def _(other=other):
            pl.semaphore_signal(bar, inc=1, device_id=to_head(other), device_id_type=pl.DeviceIdType.MESH)

    end = jnp.logical_or(z == 0, z == n - 1)

    @pl.when(end)
    def _():
        pl.semaphore_wait(bar, 1)

    @pl.when(jnp.logical_not(end))
    def _():
        pl.semaphore_wait(bar, 2)


def head_barrier(z, n):
    bar = pltpu.get_barrier_semaphore()
    for i in range(1, n):
        pl.semaphore_signal(bar, inc=1, device_id=to_head(lax.rem(z + i, n)), device_id_type=pl.DeviceIdType.MESH)
    pl.semaphore_wait(bar, n - 1)


class Chain:
    def __init__(self, n, subs, lag, part_ref, out_ref, rbuf, lbuf, ssem, rsem, finalize=None):
        self.z, self.n, self.subs, self.lag = lax.axis_index("head"), n, subs, lag
        self.part, self.out, self.rbuf, self.lbuf, self.ssem, self.rsem = part_ref, out_ref, rbuf, lbuf, ssem, rsem
        self.half = part_ref.shape[0] // 2
        self.unit = self.half // subs
        self.finalize = finalize
        self.steps = subs + 2 * lag * (n - 1)

    def near(self, s):
        return pl.ds(pl.multiple_of(s * self.unit, self.unit), self.unit)

    def far(self, s):
        return pl.ds(pl.multiple_of(self.half + s * self.unit, self.unit), self.unit)

    def copy(self, kind, s, first=False):
        src, at, to = (
            (self.rbuf, self.near(s), self.near(s)),
            (self.lbuf, self.near(s), self.near(s)),
            (self.out, self.near(s), self.near(s)),
            (self.out, self.far(s), self.far(s)),
        )[kind]
        dst = src
        if first:
            src, at = self.part, (self.far(s) if kind == 0 else self.near(s))
        return pltpu.make_async_remote_copy(
            src_ref=src.at[at],
            dst_ref=dst.at[to],
            send_sem=self.ssem.at[kind, s],
            recv_sem=self.rsem.at[kind, s],
            device_id=to_head(self.z + (1 if kind % 2 == 0 else -1)),
            device_id_type=pl.DeviceIdType.MESH,
        )

    def step(self, k):
        z, lag, last = self.z, self.lag, self.n - 1

        def inside(s):
            return both(s >= 0, s < self.subs)

        for kind, buf in ((0, self.rbuf), (1, self.lbuf)):
            hops = z if kind == 0 else last - z
            s = k - lag * hops

            @pl.when(both(inside(s), hops == 0))
            def _(kind=kind, s=s):
                self.copy(kind, s, True).start()

            @pl.when(both(inside(s), both(hops > 0, hops < last)))
            def _(kind=kind, s=s, buf=buf):
                self.copy(kind, s).wait_recv()
                at = self.near(s)
                own = self.part[self.far(s) if kind == 0 else at]
                buf[at] = (buf[at].astype(F32) + own.astype(F32)).astype(BF)
                self.copy(kind, s).start()

            @pl.when(both(inside(s), hops == last))
            def _(kind=kind, s=s, buf=buf):
                self.copy(kind, s).wait_recv()
                to = self.far(s) if kind == 0 else self.near(s)
                total = buf[self.near(s)].astype(F32) + self.part[to].astype(F32)
                if self.finalize is not None:
                    total = self.finalize(self.near(s), total)
                self.out[to] = total.astype(BF)
                self.copy(3 - kind, s).start()

        for kind in (2, 3):
            hops = z if kind == 2 else last - z
            s = k - lag * (last + hops)

            @pl.when(both(inside(s), hops > 0))
            def _(kind=kind, s=s, hops=hops):
                self.copy(kind, s).wait_recv()

                @pl.when(hops < last)
                def _():
                    self.copy(kind, s).start()

    def run(self, first, last):
        def one(k, c):
            self.step(k)
            return c

        lax.fori_loop(first, last, one, 0)

    def drain(self):
        def one(s, c):
            for kind in range(4):

                @pl.when(self.z < self.n - 1 if kind % 2 == 0 else self.z > 0)
                def _(kind=kind):
                    self.copy(kind, s).wait_send()

            return c

        lax.fori_loop(0, self.subs, one, 0)


def chain_scratch(rows, width, subs):
    return [
        pltpu.VMEM((rows // 2, width), BF),
        pltpu.VMEM((rows // 2, width), BF),
        pltpu.SemaphoreType.DMA((4, subs)),
        pltpu.SemaphoreType.DMA((4, subs)),
    ]


SUBS, LAG = 16, 2
ANY = pl.BlockSpec(memory_space=pl.ANY)
BIG = VMEM_BYTES - (1 << 20)


def norm_parts(values):
    r = lax.rsqrt(jnp.mean(values * values, axis=-1, keepdims=True) + EPSILON)
    return r, values * r


def fold8(x):
    return jnp.sum(x.reshape(x.shape[0] // 8, 8, x.shape[1]), axis=0)


def half_loads(z, n, half, whole, halves, sem):
    at = pl.ds(pl.multiple_of(jnp.where(z == 0, 0, half), half), half)
    pairs = [(ref.at[at], to) for ref, to in whole] + halves
    return [pltpu.make_async_copy(ref, to, sem.at[i]) for i, (ref, to) in enumerate(pairs)]


def run_with_loads(ch, end, loads):
    @pl.when(end)
    def _():
        for c in loads:
            c.start()

    need = ch.lag * (ch.n - 1)
    ch.run(0, need)

    @pl.when(end)
    def _():
        for c in loads:
            c.wait()

    ch.run(need, ch.steps)


def chain_ffn_kernel(
    n, part_ref, g_ref, live_ref, x_ref, attn_ref, vec_ref, out_ref, dmid_ref, sum_ref, rbuf, lbuf, ssem, rsem, gv, lv, xv, av, csem
):
    z = lax.axis_index("head")
    line_barrier(z, n)
    sum_ref[...] = jnp.zeros_like(sum_ref)
    tanh_attn, gain = vec_ref[0:1], vec_ref[1:2]

    def finalize(at, dh):
        attn, live = av[at], lv[at, 0:1]
        mid = xv[at].astype(F32) + live * tanh_attn * attn
        r, u = norm_parts(mid)
        w = dh * gain
        dmid = gv[at].astype(F32) + r * (w - u * jnp.mean(w * u, axis=-1, keepdims=True))
        dmid_ref[at] = dmid
        masked = dmid * live
        sum_ref[0:8] += fold8(dh * u)
        sum_ref[8:16] += fold8(masked * attn)
        return masked * tanh_attn

    ch = Chain(n, SUBS, LAG, part_ref, out_ref, rbuf, lbuf, ssem, rsem, finalize)
    loads = half_loads(z, n, ch.half, [(g_ref, gv), (live_ref, lv), (x_ref, xv), (attn_ref, av)], [], csem)
    run_with_loads(ch, jnp.logical_or(z == 0, z == n - 1), loads)
    ch.drain()


def chain_ffn(part, g, live, x, attn, vec, cid):
    n = lax.axis_size("head")
    rows, width = part.shape
    half = rows // 2
    return pl.pallas_call(
        functools.partial(chain_ffn_kernel, n),
        out_shape=(S((rows, width), BF), S((half, width), F32), S((16, width), F32)),
        in_specs=[VM, ANY, ANY, ANY, ANY, VM],
        out_specs=(VM,) * 3,
        scratch_shapes=chain_scratch(rows, width, SUBS)
        + [
            pltpu.VMEM((half, width), BF),
            pltpu.VMEM((half, 128), F32),
            pltpu.VMEM((half, width), BF),
            pltpu.VMEM((half, width), F32),
            pltpu.SemaphoreType.DMA((4,)),
        ],
        compiler_params=pltpu.CompilerParams(collective_id=cid, has_side_effects=True, vmem_limit_bytes=VMEM_BYTES // 2),
        cost_estimate=pl.CostEstimate(flops=80_000_000_000, bytes_accessed=20 * rows * width, transcendentals=0),
        name="chain_ffn",
    )(part, g, live, x, attn, vec)


def chain_rows_kernel(
    n, part_ref, x_ref, dmid_ref, gain_ref, sum_ref, out_ref, tot_ref, rbuf, lbuf, ssem, rsem, xv, dv, csem, acc, ends, esem, fsem
):
    z = lax.axis_index("head")
    line_barrier(z, n)
    acc[...] = jnp.zeros_like(acc)
    gain = gain_ref[0:1]

    def finalize(at, dh):
        r, u = norm_parts(xv[at].astype(F32))
        w = dh * gain
        acc[...] += fold8(dh * u)
        return dv[at] + r * (w - u * jnp.mean(w * u, axis=-1, keepdims=True))

    ch = Chain(n, SUBS, LAG, part_ref, out_ref, rbuf, lbuf, ssem, rsem, finalize)
    loads = half_loads(z, n, ch.half, [(x_ref, xv)], [(dmid_ref, dv)], csem)
    run_with_loads(ch, jnp.logical_or(z == 0, z == n - 1), loads)

    width = acc.shape[1]
    rows = [sum_ref[0:8], sum_ref[8:16], acc[...]]
    mine = jnp.concatenate([jnp.sum(r, axis=0, keepdims=True) for r in rows] + [jnp.zeros((5, width), F32)], axis=0)
    for e, where in ((0, 0), (1, n - 1)):

        @pl.when(z == where)
        def _(e=e):
            ends[e] = mine

    def copy(e):
        return pltpu.make_async_remote_copy(
            src_ref=ends.at[e],
            dst_ref=ends.at[e],
            send_sem=esem.at[e],
            recv_sem=fsem.at[e],
            device_id=to_head(z + (1 if e == 0 else -1)),
            device_id_type=pl.DeviceIdType.MESH,
        )

    for e, source, sink in ((0, 0, n - 1), (1, n - 1, 0)):

        @pl.when(z == source)
        def _(e=e):
            copy(e).start()

    for e, source, sink in ((0, 0, n - 1), (1, n - 1, 0)):

        @pl.when(z != source)
        def _(e=e, sink=sink):
            copy(e).wait_recv()

            @pl.when(z != sink)
            def _():
                copy(e).start()

    tot_ref[...] = ends[0] + ends[1]
    for e, sink in ((0, n - 1), (1, 0)):

        @pl.when(z != sink)
        def _(e=e):
            copy(e).wait_send()

    ch.drain()


def chain_rows(part, x, dmid, gain, sums, cid):
    n = lax.axis_size("head")
    rows, width = part.shape
    half = rows // 2
    return pl.pallas_call(
        functools.partial(chain_rows_kernel, n),
        out_shape=(S((rows, width), BF), S((8, width), F32)),
        in_specs=[VM, ANY, ANY, VM, VM],
        out_specs=(VM,) * 2,
        scratch_shapes=chain_scratch(rows, width, SUBS)
        + [
            pltpu.VMEM((half, width), BF),
            pltpu.VMEM((half, width), F32),
            pltpu.SemaphoreType.DMA((2,)),
            pltpu.VMEM((8, width), F32),
            pltpu.VMEM((2, 8, width), F32),
            pltpu.SemaphoreType.DMA((2,)),
            pltpu.SemaphoreType.DMA((2,)),
        ],
        compiler_params=pltpu.CompilerParams(collective_id=cid, has_side_effects=True, vmem_limit_bytes=VMEM_BYTES // 2),
        cost_estimate=pl.CostEstimate(flops=80_000_000_000, bytes_accessed=20 * rows * width, transcendentals=0),
        name="chain_rows",
    )(part, x, dmid, gain, sums)


def share_kernel(n, piece_ref, all_ref, ssem, rsem):
    z = lax.axis_index("head")
    head_barrier(z, n)

    def copy(i):
        return pltpu.make_async_remote_copy(
            src_ref=piece_ref,
            dst_ref=all_ref.at[z],
            send_sem=ssem.at[i],
            recv_sem=rsem.at[i],
            device_id=to_head(lax.rem(z + i, n)),
            device_id_type=pl.DeviceIdType.MESH,
        )

    for i in range(1, n):
        copy(i).start()
    all_ref[z] = piece_ref[...]
    for i in range(1, n):
        copy(i).wait()


def share(piece, cid):
    n = lax.axis_size("head")
    return pl.pallas_call(
        functools.partial(share_kernel, n),
        out_shape=S((n,) + piece.shape, piece.dtype),
        in_specs=[VM],
        out_specs=VM,
        scratch_shapes=[pltpu.SemaphoreType.DMA((n,)), pltpu.SemaphoreType.DMA((n,))],
        compiler_params=pltpu.CompilerParams(collective_id=cid, has_side_effects=True, vmem_limit_bytes=VMEM_BYTES // 2),
        name="share",
    )(piece)


def wgrad_kernel(a_ref, b_ref, c_ref, d_ref, o_ref):
    nb = b_ref.shape[1]
    o_ref[:, :nb] = tn(a_ref[...], b_ref[...]).astype(BF)
    o_ref[:, nb:] = tn(c_ref[...], d_ref[...]).astype(BF)


def wgrad_pair(a, b, c, d):
    rows, width = a.shape
    cols = b.shape[1] + d.shape[1]
    wb = min(256, width)
    return pl.pallas_call(
        wgrad_kernel,
        grid=(width // wb,),
        in_specs=[
            pl.BlockSpec((rows, wb), lambda i: (0, i)),
            pl.BlockSpec(b.shape, lambda i: (0, 0)),
            pl.BlockSpec((rows, wb), lambda i: (0, i)),
            pl.BlockSpec(d.shape, lambda i: (0, 0)),
        ],
        out_specs=pl.BlockSpec((wb, cols), lambda i: (i, 0)),
        out_shape=S((width, cols), BF),
        compiler_params=pltpu.CompilerParams(vmem_limit_bytes=VMEM_BYTES // 2),
        cost_estimate=pl.CostEstimate(flops=2 * rows * width * cols, bytes_accessed=2 * width * cols, transcendentals=0),
        name="wgrad_pair",
    )(a, b, c, d)


def qkv_kernel(
    n, x_ref, gain_ref, w_ref, hg_ref, cos_ref, sin_ref, live_ref, slice_ref, h_ref, pre_ref, q_ref, kv_ref, all_ref, ssem, rsem
):
    z = lax.axis_index("head")

    def copy(i):
        return pltpu.make_async_remote_copy(
            src_ref=slice_ref,
            dst_ref=all_ref.at[z],
            send_sem=ssem.at[i],
            recv_sem=rsem.at[i],
            device_id=to_head(lax.rem(z + i, n)),
            device_id_type=pl.DeviceIdType.MESH,
        )

    own = pltpu.make_async_copy(slice_ref, all_ref.at[z], ssem.at[0])

    @pl.when(pl.program_id(0) == 0)
    def _():
        head_barrier(z, n)
        own.start()
        for i in range(1, n):
            copy(i).start()

    x = x_ref[...].astype(F32)
    h = (x * lax.rsqrt(jnp.mean(x * x, axis=-1, keepdims=True) + EPSILON) * gain_ref[...]).astype(BF)
    h_ref[...] = h
    width = w_ref.shape[2]
    cos, sin, live = cos_ref[...], sin_ref[...], live_ref[...]
    for part in range(2):
        pre = nn(h, w_ref[part])
        pre_ref[:, part * width : (part + 1) * width] = pre
        for p in range(width // 128):
            v = pre[:, p * 128 : (p + 1) * 128]
            r = lax.rsqrt(head_mean(v * v) + EPSILON)
            t = v * r * hg_ref[part : part + 1, p * 128 : (p + 1) * 128]
            y = t * cos + swap_halves(t) * sin
            if part == 0:
                q_ref[:, p * 128 : (p + 1) * 128] = y.astype(BF)
            else:
                kv_ref[:, p * 128 : (p + 1) * 128] = (y * live).astype(BF)
    val = nn(h, w_ref[2])
    for p in range(width // 128):
        kv_ref[:, width + p * 128 : width + (p + 1) * 128] = (val[:, p * 128 : (p + 1) * 128] * live).astype(BF)

    @pl.when(pl.program_id(0) == pl.num_programs(0) - 1)
    def _():
        own.wait()
        for i in range(1, n):
            copy(i).wait()


def make_qkv(x, gain, w, head_gains, cos, sin, live, out_slice, cid):
    n = lax.axis_size("head")
    rows, width = x.shape
    inner = w.shape[2]
    rb = min(256, rows)
    return pl.pallas_call(
        functools.partial(qkv_kernel, n),
        grid=(rows // rb,),
        in_specs=[
            pl.BlockSpec((rb, width), lambda i: (i, 0)),
            pl.BlockSpec((1, width), lambda i: (0, 0)),
            pl.BlockSpec(w.shape, lambda i: (0, 0, 0)),
            pl.BlockSpec((8, inner), lambda i: (0, 0)),
            pl.BlockSpec((rb, 128), lambda i: (i, 0)),
            pl.BlockSpec((rb, 128), lambda i: (i, 0)),
            pl.BlockSpec((rb, 128), lambda i: (i, 0)),
            ANY,
        ],
        out_specs=(
            pl.BlockSpec((rb, width), lambda i: (i, 0)),
            pl.BlockSpec((rb, 2 * inner), lambda i: (i, 0)),
            pl.BlockSpec((rb, inner), lambda i: (i, 0)),
            pl.BlockSpec((rb, 2 * inner), lambda i: (i, 0)),
            ANY,
        ),
        out_shape=(
            S((rows, width), BF),
            S((rows, 2 * inner), F32),
            S((rows, inner), BF),
            S((rows, 2 * inner), BF),
            S((n,) + out_slice.shape, BF),
        ),
        scratch_shapes=[pltpu.SemaphoreType.DMA((n,)), pltpu.SemaphoreType.DMA((n,))],
        compiler_params=pltpu.CompilerParams(collective_id=cid, has_side_effects=True, vmem_limit_bytes=VMEM_BYTES // 2),
        cost_estimate=pl.CostEstimate(flops=6 * rows * width * inner, bytes_accessed=12 * rows * width, transcendentals=0),
        name="make_qkv",
    )(x, gain, w, head_gains, cos, sin, live, out_slice)


def qkv_back_kernel(dq_ref, dkv_ref, peer_ref, pre_ref, hg_ref, cos_ref, sin_ref, w_ref, dpre_ref, gg_ref, dh_ref):
    width = dq_ref.shape[1]
    rows = dq_ref.shape[0]

    @pl.when(pl.program_id(0) == 0)
    def _():
        gg_ref[...] = jnp.zeros_like(gg_ref)

    cos, sin = cos_ref[...], sin_ref[...]
    total = None
    for part in range(2):
        for p in range(width // 128):
            ls = slice(p * 128, (p + 1) * 128)
            pls = slice(part * width + p * 128, part * width + (p + 1) * 128)
            if part == 0:
                dy = dq_ref[:, ls]
            else:
                dy = dkv_ref[:, ls] + peer_ref[:, ls].astype(F32)
            dt = dy * cos - swap_halves(dy) * sin
            v = pre_ref[:, pls]
            r = lax.rsqrt(head_mean(v * v) + EPSILON)
            u = v * r
            w = dt * hg_ref[part : part + 1, ls]
            dv = r * (w - u * head_mean(w * u))
            dpre_ref[:, pls] = dv.astype(BF)
            gg_ref[part * 8 : part * 8 + 8, ls] += jnp.sum((dt * u).reshape(rows // 8, 8, 128), axis=0)
        g = nt(dpre_ref[:, part * width : (part + 1) * width], w_ref[part])
        total = g if total is None else total + g
    dpre_ref[:, 2 * width :] = (dkv_ref[:, width:] + peer_ref[:, width:].astype(F32)).astype(BF)
    total = total + nt(dpre_ref[:, 2 * width :], w_ref[2])
    dh_ref[...] = total.astype(BF)


def qkv_back(dq, dkv, peer, pre, head_gains, cos, sin, w):
    rows, inner = dq.shape
    width = w.shape[1]
    rb = min(256, rows)
    blk = lambda c: pl.BlockSpec((rb, c), lambda i: (i, 0))
    return pl.pallas_call(
        qkv_back_kernel,
        grid=(rows // rb,),
        in_specs=[
            blk(inner),
            blk(2 * inner),
            blk(2 * inner),
            blk(2 * inner),
            pl.BlockSpec((8, inner), lambda i: (0, 0)),
            blk(128),
            blk(128),
            pl.BlockSpec(w.shape, lambda i: (0, 0, 0)),
        ],
        out_specs=(blk(3 * inner), pl.BlockSpec((16, inner), lambda i: (0, 0)), blk(width)),
        out_shape=(S((rows, 3 * inner), BF), S((16, inner), F32), S((rows, width), BF)),
        compiler_params=pltpu.CompilerParams(vmem_limit_bytes=VMEM_BYTES // 2),
        cost_estimate=pl.CostEstimate(flops=6 * rows * width * inner, bytes_accessed=12 * rows * width, transcendentals=0),
        name="qkv_back",
    )(dq, dkv, peer, pre, head_gains, cos, sin, w)


def middle_kernel(mixed_ref, w_ref, x_ref, live_ref, vec_ref, attn_ref, h_ref):
    total = None
    for g in range(mixed_ref.shape[0]):
        t = nn(mixed_ref[g], w_ref[g]).astype(BF).astype(F32)
        total = t if total is None else total + t
    attn_ref[...] = total
    mid = x_ref[...].astype(F32) + live_ref[:, 0:1] * vec_ref[0:1] * total
    _, u = norm_parts(mid)
    h_ref[...] = (u * vec_ref[1:2]).astype(BF)


def make_middle(mixed_all, w_all, x, live, vec):
    n, rows, inner = mixed_all.shape
    width = x.shape[1]
    rb = min(256, rows)
    blk = lambda c: pl.BlockSpec((rb, c), lambda i: (i, 0))
    return pl.pallas_call(
        middle_kernel,
        grid=(rows // rb,),
        in_specs=[
            pl.BlockSpec((n, rb, inner), lambda i: (0, i, 0)),
            pl.BlockSpec(w_all.shape, lambda i: (0, 0, 0)),
            blk(width),
            blk(128),
            pl.BlockSpec((8, width), lambda i: (0, 0)),
        ],
        out_specs=(blk(width), blk(width)),
        out_shape=(S((rows, width), F32), S((rows, width), BF)),
        compiler_params=pltpu.CompilerParams(vmem_limit_bytes=VMEM_BYTES // 2),
        cost_estimate=pl.CostEstimate(flops=2 * n * rows * width * inner, bytes_accessed=14 * rows * width, transcendentals=0),
        name="make_middle",
    )(mixed_all, w_all, x, live, vec)


def attend_kernel(
    n, scale, qb, kc, q_ref, kv_ref, peer_ref, live_ref, ck_ref, cv_ref, gate_ref, mixed_ref, self_ref, cross_ref, lse_ref,
    va_ref, cva_ref, ssem, rsem,
):
    z = lax.axis_index("head")
    line_barrier(z, n)
    rows, width = q_ref.shape
    txt = ck_ref.shape[0]
    c = scale * LOG2E
    va_ref[:, 128:] = live_ref[...]
    cva_ref[:, 128:] = jnp.ones((txt, 128), BF)
    first = lax.broadcasted_iota(jnp.int32, (qb, 128), 1) < 64

    def copy(kind, o, p):
        view = mixed_ref.at[o, :, pl.ds(pl.multiple_of(p * 128, 128), 128)]
        return pltpu.make_async_remote_copy(
            src_ref=view,
            dst_ref=view,
            send_sem=ssem.at[kind, o, p],
            recv_sem=rsem.at[kind, o, p],
            device_id=to_head(z + (1 if kind == 0 else -1)),
            device_id_type=pl.DeviceIdType.MESH,
        )

    def send_own(p):
        @pl.when(z < n - 1)
        def _():
            copy(0, z, p).start()

        @pl.when(z > 0)
        def _():
            copy(1, z, p).start()

    def relay(d, p):
        @pl.when(z - d >= 0)
        def _():
            copy(0, z - d, p).wait_recv()

            @pl.when(z < n - 1)
            def _():
                copy(0, z - d, p).start()

        @pl.when(z + d < n)
        def _():
            copy(1, z + d, p).wait_recv()

            @pl.when(z > 0)
            def _():
                copy(1, z + d, p).start()

    def pair(p, _):
        lanes = pl.ds(pl.multiple_of(p * 128, 128), 128)
        vlanes = pl.ds(pl.multiple_of(width + p * 128, 128), 128)
        va_ref[:rows, :128] = kv_ref[:, vlanes]
        va_ref[rows:, :128] = peer_ref[:, vlanes]
        cva_ref[:, :128] = cv_ref[:, lanes]
        gate = gate_ref[:, lanes]

        def block(b, _):
            rs = pl.ds(pl.multiple_of(b * qb, qb), qb)
            qp = q_ref[rs, lanes]
            outs, couts = [], []
            for a in range(2):
                qm = jnp.where(first if a == 0 else jnp.logical_not(first), qp, jnp.zeros_like(qp))
                acc = None
                for side in range(2):
                    keys = kv_ref if side == 0 else peer_ref
                    for j in range(0, rows, kc):
                        s = nt(qm, keys[j : j + kc, lanes])
                        pr = jnp.exp2(s * c).astype(BF)
                        o = nn(pr, va_ref[side * rows + j : side * rows + j + kc, :])
                        acc = o if acc is None else acc + o
                outs.append(acc)
                s = nt(qm, ck_ref[:, lanes])
                couts.append(nn(jnp.exp2(s * c).astype(BF), cva_ref[...]))
            so = jnp.where(first, outs[0][:, :128], outs[1][:, :128])
            sl = jnp.where(first, outs[0][:, 128:], outs[1][:, 128:])
            co = jnp.where(first, couts[0][:, :128], couts[1][:, :128])
            cl = jnp.where(first, couts[0][:, 128:], couts[1][:, 128:])
            so = so / sl
            co = co / cl
            mixed_ref[z, rs, lanes] = (so + gate * co).astype(BF)
            self_ref[rs, lanes] = so
            cross_ref[rs, lanes] = co
            lt = jnp.log2(sl).T
            ct = jnp.log2(cl).T
            lse_ref[p, :, rs] = jnp.concatenate([lt[0:1], lt[64:65], ct[0:1], ct[64:65], lt[0:4]], axis=0)
            return 0

        lax.fori_loop(0, rows // qb, block, 0)

        @pl.when(p >= 1)
        def _():
            relay(1, p - 1)

        send_own(p)
        return 0

    pairs = width // 128
    lax.fori_loop(0, pairs, pair, 0)
    for t in range(pairs + n - 2):
        for d in range(1, n):
            if 0 <= t - (d - 1) < pairs and (d > 1 or t == pairs - 1):
                relay(d, t - (d - 1))
    for p in range(pairs):
        for o in range(n):

            @pl.when(both(z >= o, z < n - 1))
            def _(o=o, p=p):
                copy(0, o, p).wait_send()

            @pl.when(both(z <= o, z > 0))
            def _(o=o, p=p):
                copy(1, o, p).wait_send()


def attend(q, kv, peer, live, ck, cv, gate, scale, cid, qb=256, kc=1024):
    n = lax.axis_size("head")
    rows, width = q.shape
    txt = ck.shape[0]
    qb, kc = min(qb, rows), min(kc, rows)
    return pl.pallas_call(
        functools.partial(attend_kernel, n, scale, qb, kc),
        out_shape=(S((n, rows, width), BF), S((rows, width), F32), S((rows, width), F32), S((width // 128, 8, rows), F32)),
        in_specs=[VM] * 7,
        out_specs=(VM,) * 4,
        scratch_shapes=[
            pltpu.VMEM((2 * rows, 256), BF),
            pltpu.VMEM((txt, 256), BF),
            pltpu.SemaphoreType.DMA((2, n, width // 128)),
            pltpu.SemaphoreType.DMA((2, n, width // 128)),
        ],
        compiler_params=pltpu.CompilerParams(collective_id=cid, has_side_effects=True, vmem_limit_bytes=VMEM_BYTES // 2),
        cost_estimate=pl.CostEstimate(flops=32 * rows * rows * width, bytes_accessed=12 * rows * width, transcendentals=0),
        name="attend",
    )(q, kv, peer, live, ck, cv, gate)


def head_sum(x):
    ind = (lax.broadcasted_iota(jnp.int32, (8, 128), 0) == lax.broadcasted_iota(jnp.int32, (8, 128), 1) // 64).astype(F32)
    return lax.dot_general(ind, x, (((1,), (1,)), ((), ())), preferred_element_type=F32, precision=HIGHEST)


def cross_back_kernel(
    scale, qb, q_ref, ck_ref, cv_ref, gate_ref, cross_ref, lse_ref, dm_ref, dq_ref, dck_ref, dcv_ref, gg_ref, ckt_ref, p_ref, d_ref
):
    rows, width = q_ref.shape
    txt = ck_ref.shape[0]
    c = scale * LOG2E
    first = lax.broadcasted_iota(jnp.int32, (qb, 128), 1) < 64

    def pair(p, _):
        lanes = pl.ds(pl.multiple_of(p * 128, 128), 128)
        ckt_ref[...] = ck_ref[:, lanes].T
        gate = gate_ref[:, lanes]
        dck_ref[:, lanes] = jnp.zeros((txt, 128), F32)
        dcv_ref[:, lanes] = jnp.zeros((txt, 128), F32)
        gg_ref[:, lanes] = jnp.zeros((8, 128), F32)

        def block(b, _):
            rs = pl.ds(pl.multiple_of(b * qb, qb), qb)
            qp = q_ref[rs, lanes]
            dmf = dm_ref[rs, lanes].astype(F32)
            dcf = (gate * dmf).astype(BF)
            cross = cross_ref[rs, lanes]
            gg_ref[:, lanes] += fold8(dmf * cross)
            delta = head_sum(dcf.astype(F32) * cross)
            z = jnp.zeros_like(qp)
            masks = (first, jnp.logical_not(first))
            qs = [jnp.where(m, qp, z) for m in masks]
            dcs = [jnp.where(m, dcf, z) for m in masks]
            lse = lse_ref[p, :, rs]
            dqt = []
            for a in range(2):
                s = nt(ck_ref[:, lanes], qs[a])
                pr = jnp.exp2(s * c - lse[2 + a : 3 + a])
                dp = nt(cv_ref[:, lanes], dcs[a])
                p_ref[:, a * qb : (a + 1) * qb] = pr.astype(BF)
                dd = (pr * (dp - delta[a : a + 1])).astype(BF)
                d_ref[:, a * qb : (a + 1) * qb] = dd
                dqt.append(nn(ckt_ref[a * 64 : (a + 1) * 64, :], dd))
            dcv_ref[:, lanes] += nn(p_ref[...], jnp.concatenate(dcs, axis=0))
            dck_ref[:, lanes] += nn(d_ref[...], jnp.concatenate(qs, axis=0))
            dq_ref[rs, lanes] = (jnp.concatenate(dqt, axis=0) * scale).T
            return 0

        lax.fori_loop(0, rows // qb, block, 0)
        dck_ref[:, lanes] = dck_ref[:, lanes] * scale
        return 0

    lax.fori_loop(0, width // 128, pair, 0)


def cross_back(q, ck, cv, gate, co, lse, dm, scale, qb=512):
    rows, width = q.shape
    txt = ck.shape[0]
    qb = min(qb, rows)
    return pl.pallas_call(
        functools.partial(cross_back_kernel, scale, qb),
        out_shape=(S((rows, width), F32), S((txt, width), F32), S((txt, width), F32), S((8, width), F32)),
        in_specs=[VM] * 7,
        out_specs=(VM,) * 4,
        scratch_shapes=[pltpu.VMEM((128, txt), BF), pltpu.VMEM((txt, 2 * qb), BF), pltpu.VMEM((txt, 2 * qb), BF)],
        compiler_params=pltpu.CompilerParams(vmem_limit_bytes=VMEM_BYTES // 2),
        cost_estimate=pl.CostEstimate(flops=24 * rows * txt * width, bytes_accessed=12 * rows * width, transcendentals=0),
        name="cross_back",
    )(q, ck, cv, gate, co, lse, dm)


def attend_back_kernel(
    n,
    per,
    scale,
    qb,
    kc,
    q_ref,
    kv_ref,
    peer_ref,
    live_ref,
    self_ref,
    lse_ref,
    dm_ref,
    dqc_ref,
    part_ref,
    dq_ref,
    dkv_ref,
    dpeer_ref,
    fsum_ref,
    kt_ref,
    p_ref,
    d_ref,
    ak_ref,
    av_ref,
    rbuf,
    lbuf,
    ssem,
    rsem,
):
    line_barrier(lax.axis_index("head"), n)
    ch = Chain(n, SUBS, LAG, part_ref, fsum_ref, rbuf, lbuf, ssem, rsem)
    rows, width = q_ref.shape
    c = scale * LOG2E
    first = lax.broadcasted_iota(jnp.int32, (qb, 128), 1) < 64

    def pair(p, _):
        lanes = pl.ds(pl.multiple_of(p * 128, 128), 128)
        vlanes = pl.ds(pl.multiple_of(width + p * 128, 128), 128)
        kt_ref[:, :rows] = kv_ref[:, lanes].T
        kt_ref[:, rows:] = peer_ref[:, lanes].T
        ak_ref[...] = jnp.zeros_like(ak_ref)
        av_ref[...] = jnp.zeros_like(av_ref)

        def block(b, _):
            rs = pl.ds(pl.multiple_of(b * qb, qb), qb)
            qp = q_ref[rs, lanes]
            dm = dm_ref[rs, lanes]
            dmf = dm.astype(F32)
            delta = head_sum(dmf * self_ref[rs, lanes])
            z = jnp.zeros_like(qp)
            masks = (first, jnp.logical_not(first))
            qs = [jnp.where(m, qp, z) for m in masks]
            dms = [jnp.where(m, dm, z) for m in masks]
            qstack = jnp.concatenate(qs, axis=0)
            dstack = jnp.concatenate(dms, axis=0)
            lse = lse_ref[p, :, rs]
            dqt = [None, None]
            for side in range(2):
                src = kv_ref if side == 0 else peer_ref
                for j in range(0, rows, kc):
                    at = side * rows + j
                    for a in range(2):
                        s = nt(src[j : j + kc, lanes], qs[a])
                        pr = jnp.exp2(s * c - lse[a : a + 1])
                        dp = nt(src[j : j + kc, vlanes], dms[a])
                        p_ref[:, a * qb : (a + 1) * qb] = pr.astype(BF)
                        dd = (pr * (dp - delta[a : a + 1])).astype(BF)
                        d_ref[:, a * qb : (a + 1) * qb] = dd
                        t = nn(kt_ref[a * 64 : (a + 1) * 64, at : at + kc], dd)
                        dqt[a] = t if dqt[a] is None else dqt[a] + t
                    av_ref[at : at + kc] += nn(p_ref[...], dstack)
                    ak_ref[at : at + kc] += nn(d_ref[...], qstack)
            dq_ref[rs, lanes] = (jnp.concatenate(dqt, axis=0) * scale).T + dqc_ref[rs, lanes]
            for i in range(per):
                k = (p * (rows // qb) + b) * per + i

                @pl.when(k < ch.steps)
                def _(k=k):
                    ch.step(k)

            return 0

        lax.fori_loop(0, rows // qb, block, 0)
        live = live_ref[...].astype(F32)
        dkv_ref[:, lanes] = ak_ref[:rows] * (live[:rows] * scale)
        dkv_ref[:, vlanes] = av_ref[:rows] * live[:rows]
        dpeer_ref[:, lanes] = (ak_ref[rows:] * (live[rows:] * scale)).astype(BF)
        dpeer_ref[:, vlanes] = (av_ref[rows:] * live[rows:]).astype(BF)
        return 0

    lax.fori_loop(0, width // 128, pair, 0)
    ch.run(min(ch.steps, (width // 128) * (rows // qb) * per), ch.steps)
    ch.drain()


def attend_back(q, kv, peer, live, so, lse, dm, dqc, part, scale, cid, qb=256, kc=512, per=2):
    n = lax.axis_size("head")
    rows, width = q.shape
    qb, kc = min(qb, rows), min(kc, rows)
    return pl.pallas_call(
        functools.partial(attend_back_kernel, n, per, scale, qb, kc),
        out_shape=(
            S((rows, width), F32),
            S((rows, 2 * width), F32),
            S((rows, 2 * width), BF),
            S(part.shape, BF),
        ),
        in_specs=[VM] * 9,
        out_specs=(VM,) * 4,
        scratch_shapes=[
            pltpu.VMEM((128, 2 * rows), BF),
            pltpu.VMEM((kc, 2 * qb), BF),
            pltpu.VMEM((kc, 2 * qb), BF),
            pltpu.VMEM((2 * rows, 128), F32),
            pltpu.VMEM((2 * rows, 128), F32),
        ]
        + chain_scratch(*part.shape, SUBS),
        compiler_params=pltpu.CompilerParams(collective_id=cid, has_side_effects=True, vmem_limit_bytes=BIG),
        cost_estimate=pl.CostEstimate(flops=80 * rows * rows * width, bytes_accessed=20 * rows * width, transcendentals=0),
        name="attend_back",
    )(q, kv, peer, live, so, lse, dm, dqc, part)


def pair_swap(value):
    pairs = [(source, source ^ 1) for source in range(lax.axis_size("seq"))]
    return lax.ppermute(value, "seq", pairs)


def rope_tables(grid_rows, grid_cols, first_token, row_count, head_size):
    stride = grid_cols + 1
    tokens = first_token + jnp.arange(row_count, dtype=jnp.int32)
    valid = tokens < grid_rows * stride
    row_pos = (tokens // stride).astype(F32)
    col_pos = (tokens % stride).astype(F32)
    quarter = head_size // 4
    half = head_size // 2
    lane = jnp.arange(128, dtype=jnp.int32) % half
    frequency = ROPE_BASE ** (-(lane % quarter).astype(F32) / quarter)
    angles = jnp.where(lane[None, :] < quarter, row_pos[:, None], col_pos[:, None]) * frequency[None, :]
    sign = jnp.where(jnp.arange(128) % head_size < half, -1.0, 1.0)
    return jnp.cos(angles), jnp.sin(angles) * sign[None, :], valid


def scatter(v):
    return lax.psum_scatter(v, "seq", scatter_dimension=0, tiled=True)


def local(
    image_rows,
    condition,
    text_feats,
    grid_shape,
    text_slot,
    attn_gain,
    ffn_gain,
    mod_weight,
    mod_bias,
    qkv_weight,
    qk_gains,
    text_kv_weight,
    cross_gate,
    out_weight,
    gate_up_weight,
    down_weight,
    cotangent,
):
    row_count, model_width = image_rows.shape
    head_local, head_size = qk_gains.shape[1], qk_gains.shape[2]
    inner = head_local * head_size
    ff_local = down_weight.shape[0]
    text_local, cap_width = text_feats.shape
    head_count = lax.axis_size("head")
    seq_count = lax.axis_size("seq")
    seq_index = lax.axis_index("seq")
    head_index = lax.axis_index("head")
    image_index = seq_index // 2
    pair_half = seq_index % 2
    score_scale = head_size ** (-0.5)
    image_count = condition.shape[0]

    grid_pair = lax.dynamic_index_in_dim(grid_shape, image_index, 0, keepdims=False)
    cos, sin, valid = rope_tables(grid_pair[0], grid_pair[1], pair_half * row_count, row_count, head_size)
    keep = valid.astype(F32)[:, None]
    live_own = jnp.broadcast_to(keep, (row_count, 128))
    peer_tokens = (1 - pair_half) * row_count + jnp.arange(row_count, dtype=jnp.int32)
    keep_peer = (peer_tokens < grid_pair[0] * (grid_pair[1] + 1)).astype(F32)[:, None]
    live_all = jnp.concatenate([live_own, jnp.broadcast_to(keep_peer, (row_count, 128))], axis=0).astype(BF)

    cond_all = jax.nn.silu(condition.astype(F32)).astype(BF)
    cond_low = lax.dynamic_index_in_dim(cond_all, image_index, 0, keepdims=True)
    mod_piece = jnp.dot(cond_low, mod_weight, preferred_element_type=F32) + mod_bias
    modulation = share(jnp.broadcast_to(mod_piece, (8, model_width)), 4)[:, 0]
    one_attn = 1.0 + modulation[0]
    one_ffn = 1.0 + modulation[2]
    tanh_attn = jnp.tanh(modulation[1])
    tanh_ffn = jnp.tanh(modulation[3])

    head_gains = jnp.concatenate([qk_gains.reshape(3, inner), jnp.zeros((5, inner), F32)], axis=0)
    gate_head = jnp.tanh(cross_gate)
    gate_lanes = jnp.repeat(gate_head, head_size)[None, :]
    qkv_mats = jnp.transpose(qkv_weight, (1, 0, 2))
    same_head = (jnp.arange(inner)[:, None] // head_size == jnp.arange(inner)[None, :] // head_size).astype(F32) / head_size

    text_kv_flat = text_kv_weight.reshape(cap_width, 2 * inner)
    text_proj = jnp.dot(text_feats, text_kv_flat, preferred_element_type=F32)
    cap_pre = text_proj[:, :inner]
    cap_r = lax.rsqrt(jnp.dot(cap_pre * cap_pre, same_head, precision=HIGHEST) + EPSILON)
    cap_u = cap_pre * cap_r
    cap_kv = jnp.concatenate([cap_u * head_gains[2:3], text_proj[:, inner:]], axis=1).astype(BF)
    caps = lax.all_gather(cap_kv, "seq", axis=0, tiled=False)
    slot = lax.dynamic_index_in_dim(text_slot, image_index, 0, keepdims=False)
    cap_own = lax.dynamic_index_in_dim(caps, slot, 0, keepdims=False)
    cap_key, cap_value = cap_own[:, :inner], cap_own[:, inner:]

    slice_rows = inner // seq_count
    out_slice = lax.dynamic_slice_in_dim(out_weight, seq_index * slice_rows, slice_rows, 0)

    normed, pre, query, kv, out_slices = make_qkv(
        image_rows, (attn_gain * one_attn)[None, :], qkv_mats, head_gains, cos, sin, live_own, out_slice, 5
    )
    out_all = lax.all_gather(out_slices, "seq", axis=1, tiled=True)
    kv_peer = pair_swap(kv)
    mixed_all, self_out, cross_out, lse = attend(query, kv, kv_peer, live_all, cap_key, cap_value, gate_lanes, score_scale, 0)
    mixed = lax.dynamic_index_in_dim(mixed_all, head_index, 0, keepdims=False)
    vec = jnp.concatenate([jnp.stack([tanh_attn, ffn_gain * one_ffn, attn_gain * one_attn]), jnp.zeros((5, model_width), F32)])
    attn_out, ffn_low = make_middle(mixed_all, out_all, image_rows, live_own, vec)

    gate_up_flat = gate_up_weight.reshape(model_width, 2 * ff_local)
    gate_up = jnp.dot(ffn_low, gate_up_flat, preferred_element_type=F32)
    gate_pre, up_pre = gate_up[:, :ff_local], gate_up[:, ff_local:]
    sig = jax.nn.sigmoid(gate_pre)
    hidden_low = (gate_pre * sig * up_pre).astype(BF)
    grad_out = cotangent.astype(F32)
    ffn_grad_low = (grad_out * keep * tanh_ffn).astype(BF)
    hidden_grad = nt(ffn_grad_low, down_weight)
    gate_grad = hidden_grad * up_pre * sig * (1.0 + gate_pre * (1.0 - sig))
    up_grad = hidden_grad * (gate_pre * sig)
    gate_up_grad_low = jnp.concatenate([gate_grad.astype(BF), up_grad.astype(BF)], axis=1)
    ffn_in_part = nt(gate_up_grad_low, gate_up_flat).astype(BF)
    ffn_part = jnp.dot(hidden_low, down_weight, preferred_element_type=F32).astype(BF)
    ffn_wgrad = wgrad_pair(ffn_low, gate_up_grad_low, ffn_grad_low, hidden_low)
    ffn_in_part, ffn_wgrad, ffn_part = lax.optimization_barrier((ffn_in_part, ffn_wgrad, ffn_part))
    ffn_wsum = scatter(ffn_wgrad)

    attn_grad_low, middle_grad_half, ffn_rows = chain_ffn(ffn_in_part, cotangent, live_own, image_rows, attn_out, vec, 1)
    attn_grad_low, ffn_wsum = lax.optimization_barrier((attn_grad_low, ffn_wsum))
    mixed_grad = nt(attn_grad_low, out_weight).astype(BF)
    dq_cross, dck, dcv, gate_rows = cross_back(query, cap_key, cap_value, gate_lanes, cross_out, lse, mixed_grad, score_scale)
    cap_grads = lax.all_gather(jnp.concatenate([dck, dcv], axis=1).astype(BF), "seq", axis=0, tiled=False)
    dq, dkv, dpeer, ffn_out = attend_back(query, kv, kv_peer, live_all, self_out, lse, mixed_grad, dq_cross, ffn_part, score_scale, 2)
    from_peer = pair_swap(dpeer)
    dq, cap_grads = lax.optimization_barrier((dq, cap_grads))

    own_image = jnp.sum(jnp.where(text_slot == seq_index, jnp.arange(image_count), 0))
    used = jnp.any(text_slot == seq_index).astype(F32)
    two = lax.dynamic_slice_in_dim(cap_grads, 2 * own_image, 2, 0).astype(F32)
    cap_grad = (two[0] + two[1]) * used
    cap_dy, cap_dv = cap_grad[:, :inner], cap_grad[:, inner:]
    cap_w = cap_dy * head_gains[2:3]
    cap_pre_grad = cap_r * (cap_w - cap_u * jnp.dot(cap_w * cap_u, same_head, precision=HIGHEST))
    cap_gain = jnp.sum(cap_dy * cap_u, axis=0)
    text_low = jnp.concatenate([cap_pre_grad, cap_dv], axis=1).astype(BF)
    text_weight_grad = tn(text_feats, text_low).astype(BF)
    text_part = nt(text_low, text_kv_flat).astype(BF)
    dq, dkv, text_part, text_weight_grad = lax.optimization_barrier((dq, dkv, text_part, text_weight_grad))
    text_sum = lax.psum_scatter(text_part, "head", scatter_dimension=1, tiled=True)
    text_weight_sum = scatter(text_weight_grad)

    ffn_out = ffn_out.astype(F32)
    output = (image_rows.astype(F32) + keep * tanh_attn * attn_out + keep * tanh_ffn * ffn_out).astype(BF)
    gate_ffn_grad = jnp.sum(grad_out * keep * ffn_out, axis=0) * (1.0 - tanh_ffn * tanh_ffn)
    grad_pre, gain_rows, attn_in_part = qkv_back(dq, dkv, from_peer, pre, head_gains, cos, sin, qkv_mats)
    attn_wgrad = wgrad_pair(normed, grad_pre, attn_grad_low, mixed)
    attn_in_part, attn_wgrad, text_sum = lax.optimization_barrier((attn_in_part, attn_wgrad, text_sum))
    attn_wsum = scatter(attn_wgrad)
    text_grad = text_sum.astype(F32)
    rows_grad, row_sums = chain_rows(attn_in_part, image_rows, middle_grad_half, vec[2:], ffn_rows, 3)
    ffn_sum, attn_sum = row_sums[0], row_sums[2]
    gate_attn_grad = row_sums[1] * (1.0 - tanh_attn * tanh_attn)

    mod_grad = jnp.stack([attn_sum * attn_gain, gate_attn_grad, ffn_sum * ffn_gain, gate_ffn_grad])
    own_mod = lax.dynamic_index_in_dim(mod_grad, head_index, 0, keepdims=False)
    gain_grad = jnp.concatenate([gain_rows[0:8].sum(0), gain_rows[8:16].sum(0), cap_gain])
    gate_grad_head = gate_rows.sum(0)
    small = jnp.concatenate([attn_sum * one_attn, ffn_sum * one_ffn, own_mod, gain_grad, gate_grad_head])
    smalls = lax.all_gather(small, "seq", axis=0, tiled=False)
    total = jnp.sum(smalls, axis=0)
    d = model_width
    dl = d // seq_count
    attn_gain_sum = lax.dynamic_slice_in_dim(total[:d], seq_index * dl, dl)
    ffn_gain_sum = lax.dynamic_slice_in_dim(total[d : 2 * d], seq_index * dl, dl)
    mod_bias_sum = lax.dynamic_slice_in_dim(total[2 * d : 3 * d], seq_index * dl, dl)[None, :]
    qk_all = total[3 * d : 3 * d + 3 * inner].reshape(3, head_local, seq_count, head_size // seq_count)
    qk_gain_sum = lax.dynamic_index_in_dim(qk_all, seq_index, 2, keepdims=False)
    gate_sum = total[3 * d + 3 * inner :].reshape(head_local, head_size).sum(-1) * (1.0 - gate_head * gate_head)
    cond_cols = condition.shape[1] // seq_count
    cond_part = lax.dynamic_slice_in_dim(cond_all, seq_index * cond_cols, cond_cols, 1).astype(F32)
    image_mods = smalls[:, 2 * d : 3 * d].reshape(image_count, 2, d).sum(1)
    mod_weight_sum = lax.dot_general(cond_part, image_mods, (((0,), (0,)), ((), ())), precision=HIGHEST)

    split = 2 * ff_local
    ffn_wsum, attn_wsum = ffn_wsum.astype(F32), attn_wsum.astype(F32)
    gate_up_sum = ffn_wsum[:, :split].reshape(-1, 2, ff_local)
    down_sum = ffn_wsum[:, split:].T
    qkv_sum = attn_wsum[:, : 3 * inner].reshape(-1, 3, inner)
    out_sum = attn_wsum[:, 3 * inner :].T
    text_weight_sum = text_weight_sum.astype(F32).reshape(-1, 2, inner)
    return (
        output,
        rows_grad,
        text_grad,
        attn_gain_sum,
        ffn_gain_sum,
        mod_weight_sum,
        mod_bias_sum,
        qkv_sum,
        qk_gain_sum,
        text_weight_sum,
        gate_sum,
        out_sum,
        gate_up_sum,
        down_sum,
    )


def solution(mesh):
    return jax.shard_map(
        local,
        mesh=mesh,
        in_specs=(
            P("seq", None),
            P(),
            P("seq", None),
            P(),
            P(),
            P(),
            P(),
            P(None, "head"),
            P("head", None),
            P(None, None, "head"),
            P(None, "head", None),
            P(None, None, "head"),
            P("head"),
            P("head", None),
            P(None, None, "head"),
            P("head", None),
            P("seq", None),
        ),
        out_specs=(
            P("seq", None),
            P("seq", None),
            P("seq", "head"),
            P("seq"),
            P("seq"),
            P("seq", "head"),
            P("head", "seq"),
            P("seq", None, "head"),
            P(None, "head", "seq"),
            P("seq", None, "head"),
            P("head"),
            P("head", "seq"),
            P("seq", None, "head"),
            P("head", "seq"),
        ),
        check_vma=False,
    )
```

```python
import functools

import jax
import jax.numpy as jnp
from jax import lax
from jax.experimental import pallas as pl
from jax.experimental.pallas import tpu as pltpu
from jax.sharding import PartitionSpec as P

TXT = 256
EPSILON = 1e-06
ROPE_BASE = 10000.0
LOG2E = 1.4426950408889634
F32 = jnp.float32
BF = jnp.bfloat16
VMEM_BYTES = 67043328
HIGHEST = lax.Precision.HIGHEST
VM = pl.BlockSpec(memory_space=pltpu.VMEM)
S = jax.ShapeDtypeStruct


def nt(a, b):
    return lax.dot_general(a, b, (((1,), (1,)), ((), ())), preferred_element_type=F32)


def nn(a, b):
    return lax.dot_general(a, b, (((1,), (0,)), ((), ())), preferred_element_type=F32)


def tn(a, b):
    return lax.dot_general(a, b, (((0,), (0,)), ((), ())), preferred_element_type=F32)


def head_mean(x):
    rows = lax.broadcasted_iota(jnp.int32, (128, 128), 0) // 64
    cols = lax.broadcasted_iota(jnp.int32, (128, 128), 1) // 64
    same = jnp.where(rows == cols, 1.0 / 64, 0.0).astype(BF)
    high = x.astype(BF)
    rest = (x - high.astype(F32)).astype(BF)
    return nn(high, same) + nn(rest, same)


def swap_halves(x):
    lane = lax.broadcasted_iota(jnp.int32, x.shape, 1) % 64
    return jnp.where(lane < 32, pltpu.roll(x, 96, 1), pltpu.roll(x, 32, 1))


def to_head(z):
    return {"head": z}


def both(a, b):
    return jnp.logical_and(a, b)


def line_barrier(z, n):
    bar = pltpu.get_barrier_semaphore()
    for ok, other in ((z > 0, z - 1), (z < n - 1, z + 1)):

        @pl.when(ok)
        def _(other=other):
            pl.semaphore_signal(bar, inc=1, device_id=to_head(other), device_id_type=pl.DeviceIdType.MESH)

    end = jnp.logical_or(z == 0, z == n - 1)

    @pl.when(end)
    def _():
        pl.semaphore_wait(bar, 1)

    @pl.when(jnp.logical_not(end))
    def _():
        pl.semaphore_wait(bar, 2)


def head_barrier(z, n):
    bar = pltpu.get_barrier_semaphore()
    for i in range(1, n):
        pl.semaphore_signal(bar, inc=1, device_id=to_head(lax.rem(z + i, n)), device_id_type=pl.DeviceIdType.MESH)
    pl.semaphore_wait(bar, n - 1)


class Chain:
    def __init__(self, n, subs, lag, part_ref, out_ref, rbuf, lbuf, ssem, rsem, finalize=None):
        self.z, self.n, self.subs, self.lag = lax.axis_index("head"), n, subs, lag
        self.part, self.out, self.rbuf, self.lbuf, self.ssem, self.rsem = part_ref, out_ref, rbuf, lbuf, ssem, rsem
        self.half = part_ref.shape[0] // 2
        self.unit = self.half // subs
        self.finalize = finalize
        self.steps = subs + 2 * lag * (n - 1)

    def near(self, s):
        return pl.ds(pl.multiple_of(s * self.unit, self.unit), self.unit)

    def far(self, s):
        return pl.ds(pl.multiple_of(self.half + s * self.unit, self.unit), self.unit)

    def copy(self, kind, s, first=False):
        src, at, to = (
            (self.rbuf, self.near(s), self.near(s)),
            (self.lbuf, self.near(s), self.near(s)),
            (self.out, self.near(s), self.near(s)),
            (self.out, self.far(s), self.far(s)),
        )[kind]
        dst = src
        if first:
            src, at = self.part, (self.far(s) if kind == 0 else self.near(s))
        return pltpu.make_async_remote_copy(
            src_ref=src.at[at],
            dst_ref=dst.at[to],
            send_sem=self.ssem.at[kind, s],
            recv_sem=self.rsem.at[kind, s],
            device_id=to_head(self.z + (1 if kind % 2 == 0 else -1)),
            device_id_type=pl.DeviceIdType.MESH,
        )

    def step(self, k):
        z, lag, last = self.z, self.lag, self.n - 1

        def inside(s):
            return both(s >= 0, s < self.subs)

        for kind, buf in ((0, self.rbuf), (1, self.lbuf)):
            hops = z if kind == 0 else last - z
            s = k - lag * hops

            @pl.when(both(inside(s), hops == 0))
            def _(kind=kind, s=s):
                self.copy(kind, s, True).start()

            @pl.when(both(inside(s), both(hops > 0, hops < last)))
            def _(kind=kind, s=s, buf=buf):
                self.copy(kind, s).wait_recv()
                at = self.near(s)
                own = self.part[self.far(s) if kind == 0 else at]
                buf[at] = (buf[at].astype(F32) + own.astype(F32)).astype(BF)
                self.copy(kind, s).start()

            @pl.when(both(inside(s), hops == last))
            def _(kind=kind, s=s, buf=buf):
                self.copy(kind, s).wait_recv()
                to = self.far(s) if kind == 0 else self.near(s)
                total = buf[self.near(s)].astype(F32) + self.part[to].astype(F32)
                if self.finalize is not None:
                    total = self.finalize(self.near(s), to, total)
                self.out[to] = total.astype(BF)
                self.copy(3 - kind, s).start()

        for kind in (2, 3):
            hops = z if kind == 2 else last - z
            s = k - lag * (last + hops)

            @pl.when(both(inside(s), hops > 0))
            def _(kind=kind, s=s, hops=hops):
                self.copy(kind, s).wait_recv()

                @pl.when(hops < last)
                def _():
                    self.copy(kind, s).start()

    def run(self, first, last):
        def one(k, c):
            self.step(k)
            return c

        lax.fori_loop(first, last, one, 0)

    def drain(self):
        def one(s, c):
            for kind in range(4):

                @pl.when(self.z < self.n - 1 if kind % 2 == 0 else self.z > 0)
                def _(kind=kind):
                    self.copy(kind, s).wait_send()

            return c

        lax.fori_loop(0, self.subs, one, 0)


def chain_scratch(rows, width, subs):
    return [
        pltpu.VMEM((rows // 2, width), BF),
        pltpu.VMEM((rows // 2, width), BF),
        pltpu.SemaphoreType.DMA((4, subs)),
        pltpu.SemaphoreType.DMA((4, subs)),
    ]


SUBS, LAG = 16, 2
ANY = pl.BlockSpec(memory_space=pl.ANY)
BIG = VMEM_BYTES - (1 << 20)


def norm_parts(values):
    r = lax.rsqrt(jnp.mean(values * values, axis=-1, keepdims=True) + EPSILON)
    return r, values * r


def fold8(x):
    return jnp.sum(x.reshape(x.shape[0] // 8, 8, x.shape[1]), axis=0)


def half_loads(z, n, half, whole, halves, sem):
    at = pl.ds(pl.multiple_of(jnp.where(z == 0, 0, half), half), half)
    pairs = [(ref.at[at], to) for ref, to in whole] + halves
    return [pltpu.make_async_copy(ref, to, sem.at[i]) for i, (ref, to) in enumerate(pairs)]


def run_with_loads(ch, end, loads):
    @pl.when(end)
    def _():
        for c in loads:
            c.start()

    need = ch.lag * (ch.n - 1)
    ch.run(0, need)

    @pl.when(end)
    def _():
        for c in loads:
            c.wait()

    ch.run(need, ch.steps)


def ffn_kernel(
    n, subs, lag, blocks, tile,
    h_any, g_any, wgu_any, wd_any, x_any, attn_any, live_ref, vec_ref,
    out_ref, sum_ref, dmid_any, fpart_any, wg_any,
    rbuf, lbuf, ssem, rsem, hv, gv, wgu, wd, xv, av, part_ref, dgu, hid, dffn, fpart, dmid, wbuf, csem, osem, tsem,
):
    z = lax.axis_index("head")
    rows, width = hv.shape
    ff = wd.shape[0]
    half = rows // 2
    rb = half // blocks
    end = jnp.logical_or(z == 0, z == n - 1)
    loads = [pltpu.make_async_copy(a, b, csem.at[i]) for i, (a, b) in enumerate(((h_any, hv), (wgu_any, wgu), (g_any, gv), (wd_any, wd)))]
    for c in loads:
        c.start()
    mine = pl.ds(pl.multiple_of(jnp.where(z == 0, 0, half), half), half)
    end_loads = [pltpu.make_async_copy(a.at[mine], b, csem.at[4 + i]) for i, (a, b) in enumerate(((x_any, xv), (attn_any, av)))]

    @pl.when(end)
    def _():
        for c in end_loads:
            c.start()

    sum_ref[...] = jnp.zeros_like(sum_ref)
    line_barrier(z, n)
    tanh_attn, gain, tanh_ffn = vec_ref[0:1], vec_ref[1:2], vec_ref[3:4]

    def finalize(at, to, dh):
        attn, live = av[at], live_ref[to, 0:1]
        mid = xv[at].astype(F32) + live * tanh_attn * attn
        r, u = norm_parts(mid)
        w = dh * gain
        grad = gv[to].astype(F32) + r * (w - u * jnp.mean(w * u, axis=-1, keepdims=True))
        dmid[at] = grad
        masked = grad * live
        sum_ref[0:8] += fold8(dh * u)
        sum_ref[8:16] += fold8(masked * attn)
        return masked * tanh_attn

    ch = Chain(n, subs, lag, part_ref, out_ref, rbuf, lbuf, ssem, rsem, finalize)

    def step(k):
        @pl.when(jnp.logical_and(end, k == lag * (n - 1)))
        def _():
            for c in end_loads:
                c.wait()

        ch.step(k)

    per = subs // blocks

    def block(t, c):
        near = pl.ds(pl.multiple_of(t * rb, rb), rb)
        far = pl.ds(pl.multiple_of(half + t * rb, rb), rb)

        def put(ref, v):
            ref[near] = v[:rb]
            ref[far] = v[rb:]

        @pl.when(t == 0)
        def _():
            loads[0].wait()
            loads[1].wait()

        gu = nn(jnp.concatenate([hv[near], hv[far]], axis=0), wgu[...])
        gate, up = gu[:, :ff], gu[:, ff:]
        sig = 1.0 / (1.0 + jnp.exp(-gate))
        act = gate * sig
        hidden = (act * up).astype(BF)
        put(hid, hidden)

        @pl.when(t == 0)
        def _():
            loads[2].wait()
            loads[3].wait()

        grad = jnp.concatenate([gv[near].astype(F32) * live_ref[near, 0:1], gv[far].astype(F32) * live_ref[far, 0:1]], axis=0)
        low = (grad * tanh_ffn).astype(BF)
        put(dffn, low)
        dhid = nt(low, wd[...])
        both_grads = jnp.concatenate(
            [(dhid * up * (sig + act * (1.0 - sig))).astype(BF), (dhid * act).astype(BF)], axis=1
        )
        put(dgu, both_grads)
        put(part_ref, nt(both_grads, wgu[...]).astype(BF))

        def some(i, c):
            step(t * per + i)
            return c

        lax.fori_loop(0, per, some, 0)
        put(fpart, nn(hidden, wd[...]).astype(BF))
        return c

    lax.fori_loop(0, blocks, block, 0)
    fcopy = pltpu.make_async_copy(fpart, fpart_any, osem.at[0])
    fcopy.start()

    tiles = width // tile
    every = max(1, (ch.steps - subs) // tiles)

    def tile_copy(j):
        return pltpu.make_async_copy(wbuf.at[lax.rem(j, 2)], wg_any.at[pl.ds(pl.multiple_of(j * tile, tile), tile)], tsem.at[j])

    def weights(j, c):
        def some(i, c):
            step(subs + j * every + i)
            return c

        lax.fori_loop(0, every, some, 0)

        @pl.when(j >= 2)
        def _():
            tile_copy(j - 2).wait()

        cols = pl.ds(pl.multiple_of(j * tile, tile), tile)
        slot = lax.rem(j, 2)
        wbuf[slot, :, : 2 * ff] = tn(hv[:, cols], dgu[...]).astype(BF)
        wbuf[slot, :, 2 * ff :] = tn(dffn[:, cols], hid[...]).astype(BF)
        tile_copy(j).start()
        return c

    lax.fori_loop(0, tiles, weights, 0)

    def rest(k, c):
        step(k)
        return c

    lax.fori_loop(subs + tiles * every, ch.steps, rest, 0)
    dcopy = pltpu.make_async_copy(dmid, dmid_any, osem.at[1])

    @pl.when(end)
    def _():
        dcopy.start()

    for j in range(max(0, tiles - 2), tiles):
        tile_copy(j).wait()
    fcopy.wait()
    ch.drain()

    @pl.when(end)
    def _():
        dcopy.wait()


def ffn_exchange(h, g, wgu, wd, x, attn, live, vec, cid, subs=16, lag=4, blocks=4, tile=256):
    n = lax.axis_size("head")
    rows, width = h.shape
    ff = wd.shape[0]
    half = rows // 2
    vm = pltpu.VMEM
    return pl.pallas_call(
        functools.partial(ffn_kernel, n, subs, lag, blocks, tile),
        out_shape=(
            S((rows, width), BF),
            S((16, width), F32),
            S((half, width), F32),
            S((rows, width), BF),
            S((width, 3 * ff), BF),
        ),
        in_specs=[ANY] * 6 + [VM] * 2,
        out_specs=(VM, VM, ANY, ANY, ANY),
        scratch_shapes=chain_scratch(rows, width, subs)
        + [
            vm((rows, width), BF),
            vm((rows, width), BF),
            vm((width, 2 * ff), BF),
            vm((ff, width), BF),
            vm((half, width), BF),
            vm((half, width), F32),
            vm((rows, width), BF),
            vm((rows, 2 * ff), BF),
            vm((rows, ff), BF),
            vm((rows, width), BF),
            vm((rows, width), BF),
            vm((half, width), F32),
            vm((2, tile, 3 * ff), BF),
            pltpu.SemaphoreType.DMA((6,)),
            pltpu.SemaphoreType.DMA((2,)),
            pltpu.SemaphoreType.DMA((width // tile,)),
        ],
        compiler_params=pltpu.CompilerParams(collective_id=cid, has_side_effects=True, vmem_limit_bytes=BIG),
        cost_estimate=pl.CostEstimate(flops=100_000_000_000, bytes_accessed=30 * rows * width, transcendentals=0),
        name="ffn_exchange",
    )(h, g, wgu, wd, x, attn, live, vec)


def chain_rows_kernel(
    n, part_ref, x_ref, dmid_ref, gain_ref, sum_ref, out_ref, tot_ref, rbuf, lbuf, ssem, rsem, xv, dv, csem, acc, ends, esem, fsem
):
    z = lax.axis_index("head")
    line_barrier(z, n)
    acc[...] = jnp.zeros_like(acc)
    gain = gain_ref[0:1]

    def finalize(at, to, dh):
        r, u = norm_parts(xv[at].astype(F32))
        w = dh * gain
        acc[...] += fold8(dh * u)
        return dv[at] + r * (w - u * jnp.mean(w * u, axis=-1, keepdims=True))

    ch = Chain(n, SUBS, LAG, part_ref, out_ref, rbuf, lbuf, ssem, rsem, finalize)
    loads = half_loads(z, n, ch.half, [(x_ref, xv)], [(dmid_ref, dv)], csem)
    run_with_loads(ch, jnp.logical_or(z == 0, z == n - 1), loads)

    width = acc.shape[1]
    rows = [sum_ref[0:8], sum_ref[8:16], acc[...]]
    mine = jnp.concatenate([jnp.sum(r, axis=0, keepdims=True) for r in rows] + [jnp.zeros((5, width), F32)], axis=0)
    for e, where in ((0, 0), (1, n - 1)):

        @pl.when(z == where)
        def _(e=e):
            ends[e] = mine

    def copy(e):
        return pltpu.make_async_remote_copy(
            src_ref=ends.at[e],
            dst_ref=ends.at[e],
            send_sem=esem.at[e],
            recv_sem=fsem.at[e],
            device_id=to_head(z + (1 if e == 0 else -1)),
            device_id_type=pl.DeviceIdType.MESH,
        )

    for e, source, sink in ((0, 0, n - 1), (1, n - 1, 0)):

        @pl.when(z == source)
        def _(e=e):
            copy(e).start()

    for e, source, sink in ((0, 0, n - 1), (1, n - 1, 0)):

        @pl.when(z != source)
        def _(e=e, sink=sink):
            copy(e).wait_recv()

            @pl.when(z != sink)
            def _():
                copy(e).start()

    tot_ref[...] = ends[0] + ends[1]
    for e, sink in ((0, n - 1), (1, 0)):

        @pl.when(z != sink)
        def _(e=e):
            copy(e).wait_send()

    ch.drain()


def chain_rows(part, x, dmid, gain, sums, cid):
    n = lax.axis_size("head")
    rows, width = part.shape
    half = rows // 2
    return pl.pallas_call(
        functools.partial(chain_rows_kernel, n),
        out_shape=(S((rows, width), BF), S((8, width), F32)),
        in_specs=[VM, ANY, ANY, VM, VM],
        out_specs=(VM,) * 2,
        scratch_shapes=chain_scratch(rows, width, SUBS)
        + [
            pltpu.VMEM((half, width), BF),
            pltpu.VMEM((half, width), F32),
            pltpu.SemaphoreType.DMA((2,)),
            pltpu.VMEM((8, width), F32),
            pltpu.VMEM((2, 8, width), F32),
            pltpu.SemaphoreType.DMA((2,)),
            pltpu.SemaphoreType.DMA((2,)),
        ],
        compiler_params=pltpu.CompilerParams(collective_id=cid, has_side_effects=True, vmem_limit_bytes=VMEM_BYTES // 2),
        cost_estimate=pl.CostEstimate(flops=80_000_000_000, bytes_accessed=20 * rows * width, transcendentals=0),
        name="chain_rows",
    )(part, x, dmid, gain, sums)


def share_kernel(n, piece_ref, all_ref, ssem, rsem):
    z = lax.axis_index("head")
    head_barrier(z, n)

    def copy(i):
        return pltpu.make_async_remote_copy(
            src_ref=piece_ref,
            dst_ref=all_ref.at[z],
            send_sem=ssem.at[i],
            recv_sem=rsem.at[i],
            device_id=to_head(lax.rem(z + i, n)),
            device_id_type=pl.DeviceIdType.MESH,
        )

    for i in range(1, n):
        copy(i).start()
    all_ref[z] = piece_ref[...]
    for i in range(1, n):
        copy(i).wait()


def share(piece, cid):
    n = lax.axis_size("head")
    return pl.pallas_call(
        functools.partial(share_kernel, n),
        out_shape=S((n,) + piece.shape, piece.dtype),
        in_specs=[VM],
        out_specs=VM,
        scratch_shapes=[pltpu.SemaphoreType.DMA((n,)), pltpu.SemaphoreType.DMA((n,))],
        compiler_params=pltpu.CompilerParams(collective_id=cid, has_side_effects=True, vmem_limit_bytes=VMEM_BYTES // 2),
        name="share",
    )(piece)


def wgrad_kernel(a_ref, b_ref, c_ref, d_ref, o_ref):
    nb = b_ref.shape[1]
    o_ref[:, :nb] = tn(a_ref[...], b_ref[...]).astype(BF)
    o_ref[:, nb:] = tn(c_ref[...], d_ref[...]).astype(BF)


def wgrad_pair(a, b, c, d):
    rows, width = a.shape
    cols = b.shape[1] + d.shape[1]
    wb = min(256, width)
    return pl.pallas_call(
        wgrad_kernel,
        grid=(width // wb,),
        in_specs=[
            pl.BlockSpec((rows, wb), lambda i: (0, i)),
            pl.BlockSpec(b.shape, lambda i: (0, 0)),
            pl.BlockSpec((rows, wb), lambda i: (0, i)),
            pl.BlockSpec(d.shape, lambda i: (0, 0)),
        ],
        out_specs=pl.BlockSpec((wb, cols), lambda i: (i, 0)),
        out_shape=S((width, cols), BF),
        compiler_params=pltpu.CompilerParams(vmem_limit_bytes=VMEM_BYTES // 2),
        cost_estimate=pl.CostEstimate(flops=2 * rows * width * cols, bytes_accessed=2 * width * cols, transcendentals=0),
        name="wgrad_pair",
    )(a, b, c, d)


def qkv_kernel(
    n, x_ref, gain_ref, w_ref, hg_ref, cos_ref, sin_ref, live_ref, slice_ref, h_ref, pre_ref, q_ref, kv_ref, all_ref, ssem, rsem
):
    z = lax.axis_index("head")

    def copy(i):
        return pltpu.make_async_remote_copy(
            src_ref=slice_ref,
            dst_ref=all_ref.at[z],
            send_sem=ssem.at[i],
            recv_sem=rsem.at[i],
            device_id=to_head(lax.rem(z + i, n)),
            device_id_type=pl.DeviceIdType.MESH,
        )

    own = pltpu.make_async_copy(slice_ref, all_ref.at[z], ssem.at[0])

    @pl.when(pl.program_id(0) == 0)
    def _():
        head_barrier(z, n)
        own.start()
        for i in range(1, n):
            copy(i).start()

    x = x_ref[...].astype(F32)
    h = (x * lax.rsqrt(jnp.mean(x * x, axis=-1, keepdims=True) + EPSILON) * gain_ref[...]).astype(BF)
    h_ref[...] = h
    width = w_ref.shape[2]
    cos, sin, live = cos_ref[...], sin_ref[...], live_ref[...]
    for part in range(2):
        pre = nn(h, w_ref[part])
        pre_ref[:, part * width : (part + 1) * width] = pre
        for p in range(width // 128):
            v = pre[:, p * 128 : (p + 1) * 128]
            r = lax.rsqrt(head_mean(v * v) + EPSILON)
            t = v * r * hg_ref[part : part + 1, p * 128 : (p + 1) * 128]
            y = t * cos + swap_halves(t) * sin
            if part == 0:
                q_ref[:, p * 128 : (p + 1) * 128] = y.astype(BF)
            else:
                kv_ref[:, p * 128 : (p + 1) * 128] = (y * live).astype(BF)
    val = nn(h, w_ref[2])
    for p in range(width // 128):
        kv_ref[:, width + p * 128 : width + (p + 1) * 128] = (val[:, p * 128 : (p + 1) * 128] * live).astype(BF)

    @pl.when(pl.program_id(0) == pl.num_programs(0) - 1)
    def _():
        own.wait()
        for i in range(1, n):
            copy(i).wait()


def make_qkv(x, gain, w, head_gains, cos, sin, live, out_slice, cid):
    n = lax.axis_size("head")
    rows, width = x.shape
    inner = w.shape[2]
    rb = min(256, rows)
    return pl.pallas_call(
        functools.partial(qkv_kernel, n),
        grid=(rows // rb,),
        in_specs=[
            pl.BlockSpec((rb, width), lambda i: (i, 0)),
            pl.BlockSpec((1, width), lambda i: (0, 0)),
            pl.BlockSpec(w.shape, lambda i: (0, 0, 0)),
            pl.BlockSpec((8, inner), lambda i: (0, 0)),
            pl.BlockSpec((rb, 128), lambda i: (i, 0)),
            pl.BlockSpec((rb, 128), lambda i: (i, 0)),
            pl.BlockSpec((rb, 128), lambda i: (i, 0)),
            ANY,
        ],
        out_specs=(
            pl.BlockSpec((rb, width), lambda i: (i, 0)),
            pl.BlockSpec((rb, 2 * inner), lambda i: (i, 0)),
            pl.BlockSpec((rb, inner), lambda i: (i, 0)),
            pl.BlockSpec((rb, 2 * inner), lambda i: (i, 0)),
            ANY,
        ),
        out_shape=(
            S((rows, width), BF),
            S((rows, 2 * inner), F32),
            S((rows, inner), BF),
            S((rows, 2 * inner), BF),
            S((n,) + out_slice.shape, BF),
        ),
        scratch_shapes=[pltpu.SemaphoreType.DMA((n,)), pltpu.SemaphoreType.DMA((n,))],
        compiler_params=pltpu.CompilerParams(collective_id=cid, has_side_effects=True, vmem_limit_bytes=VMEM_BYTES // 2),
        cost_estimate=pl.CostEstimate(flops=6 * rows * width * inner, bytes_accessed=12 * rows * width, transcendentals=0),
        name="make_qkv",
    )(x, gain, w, head_gains, cos, sin, live, out_slice)


def qkv_back_kernel(dq_ref, dkv_ref, peer_ref, pre_ref, hg_ref, cos_ref, sin_ref, w_ref, dpre_ref, gg_ref, dh_ref):
    width = dq_ref.shape[1]
    rows = dq_ref.shape[0]

    @pl.when(pl.program_id(0) == 0)
    def _():
        gg_ref[...] = jnp.zeros_like(gg_ref)

    cos, sin = cos_ref[...], sin_ref[...]
    total = None
    for part in range(2):
        for p in range(width // 128):
            ls = slice(p * 128, (p + 1) * 128)
            pls = slice(part * width + p * 128, part * width + (p + 1) * 128)
            if part == 0:
                dy = dq_ref[:, ls]
            else:
                dy = dkv_ref[:, ls] + peer_ref[:, ls].astype(F32)
            dt = dy * cos - swap_halves(dy) * sin
            v = pre_ref[:, pls]
            r = lax.rsqrt(head_mean(v * v) + EPSILON)
            u = v * r
            w = dt * hg_ref[part : part + 1, ls]
            dv = r * (w - u * head_mean(w * u))
            dpre_ref[:, pls] = dv.astype(BF)
            gg_ref[part * 8 : part * 8 + 8, ls] += jnp.sum((dt * u).reshape(rows // 8, 8, 128), axis=0)
        g = nt(dpre_ref[:, part * width : (part + 1) * width], w_ref[part])
        total = g if total is None else total + g
    dpre_ref[:, 2 * width :] = (dkv_ref[:, width:] + peer_ref[:, width:].astype(F32)).astype(BF)
    total = total + nt(dpre_ref[:, 2 * width :], w_ref[2])
    dh_ref[...] = total.astype(BF)


def qkv_back(dq, dkv, peer, pre, head_gains, cos, sin, w):
    rows, inner = dq.shape
    width = w.shape[1]
    rb = min(256, rows)
    blk = lambda c: pl.BlockSpec((rb, c), lambda i: (i, 0))
    return pl.pallas_call(
        qkv_back_kernel,
        grid=(rows // rb,),
        in_specs=[
            blk(inner),
            blk(2 * inner),
            blk(2 * inner),
            blk(2 * inner),
            pl.BlockSpec((8, inner), lambda i: (0, 0)),
            blk(128),
            blk(128),
            pl.BlockSpec(w.shape, lambda i: (0, 0, 0)),
        ],
        out_specs=(blk(3 * inner), pl.BlockSpec((16, inner), lambda i: (0, 0)), blk(width)),
        out_shape=(S((rows, 3 * inner), BF), S((16, inner), F32), S((rows, width), BF)),
        compiler_params=pltpu.CompilerParams(vmem_limit_bytes=VMEM_BYTES // 2),
        cost_estimate=pl.CostEstimate(flops=6 * rows * width * inner, bytes_accessed=12 * rows * width, transcendentals=0),
        name="qkv_back",
    )(dq, dkv, peer, pre, head_gains, cos, sin, w)


def middle_kernel(mixed_ref, w_ref, x_ref, live_ref, vec_ref, attn_ref, h_ref):
    total = None
    for g in range(mixed_ref.shape[0]):
        t = nn(mixed_ref[g], w_ref[g]).astype(BF).astype(F32)
        total = t if total is None else total + t
    attn_ref[...] = total
    mid = x_ref[...].astype(F32) + live_ref[:, 0:1] * vec_ref[0:1] * total
    _, u = norm_parts(mid)
    h_ref[...] = (u * vec_ref[1:2]).astype(BF)


def make_middle(mixed_all, w_all, x, live, vec):
    n, rows, inner = mixed_all.shape
    width = x.shape[1]
    rb = min(256, rows)
    blk = lambda c: pl.BlockSpec((rb, c), lambda i: (i, 0))
    return pl.pallas_call(
        middle_kernel,
        grid=(rows // rb,),
        in_specs=[
            pl.BlockSpec((n, rb, inner), lambda i: (0, i, 0)),
            pl.BlockSpec(w_all.shape, lambda i: (0, 0, 0)),
            blk(width),
            blk(128),
            pl.BlockSpec((8, width), lambda i: (0, 0)),
        ],
        out_specs=(blk(width), blk(width)),
        out_shape=(S((rows, width), F32), S((rows, width), BF)),
        compiler_params=pltpu.CompilerParams(vmem_limit_bytes=VMEM_BYTES // 2),
        cost_estimate=pl.CostEstimate(flops=2 * n * rows * width * inner, bytes_accessed=14 * rows * width, transcendentals=0),
        name="make_middle",
    )(mixed_all, w_all, x, live, vec)


def attend_kernel(
    n, scale, qb, kc, q_ref, kv_ref, peer_ref, live_ref, ck_ref, cv_ref, gate_ref, mixed_ref, self_ref, cross_ref, lse_ref,
    va_ref, cva_ref, ssem, rsem,
):
    z = lax.axis_index("head")
    line_barrier(z, n)
    rows, width = q_ref.shape
    txt = ck_ref.shape[0]
    c = scale * LOG2E
    va_ref[:, 128:] = live_ref[...]
    cva_ref[:, 128:] = jnp.ones((txt, 128), BF)
    first = lax.broadcasted_iota(jnp.int32, (qb, 128), 1) < 64

    def copy(kind, o, p):
        view = mixed_ref.at[o, :, pl.ds(pl.multiple_of(p * 128, 128), 128)]
        return pltpu.make_async_remote_copy(
            src_ref=view,
            dst_ref=view,
            send_sem=ssem.at[kind, o, p],
            recv_sem=rsem.at[kind, o, p],
            device_id=to_head(z + (1 if kind == 0 else -1)),
            device_id_type=pl.DeviceIdType.MESH,
        )

    def send_own(p):
        @pl.when(z < n - 1)
        def _():
            copy(0, z, p).start()

        @pl.when(z > 0)
        def _():
            copy(1, z, p).start()

    def relay(d, p):
        @pl.when(z - d >= 0)
        def _():
            copy(0, z - d, p).wait_recv()

            @pl.when(z < n - 1)
            def _():
                copy(0, z - d, p).start()

        @pl.when(z + d < n)
        def _():
            copy(1, z + d, p).wait_recv()

            @pl.when(z > 0)
            def _():
                copy(1, z + d, p).start()

    def pair(p, _):
        lanes = pl.ds(pl.multiple_of(p * 128, 128), 128)
        vlanes = pl.ds(pl.multiple_of(width + p * 128, 128), 128)
        va_ref[:rows, :128] = kv_ref[:, vlanes]
        va_ref[rows:, :128] = peer_ref[:, vlanes]
        cva_ref[:, :128] = cv_ref[:, lanes]
        gate = gate_ref[:, lanes]

        def block(b, _):
            rs = pl.ds(pl.multiple_of(b * qb, qb), qb)
            qp = q_ref[rs, lanes]
            outs, couts = [], []
            for a in range(2):
                qm = jnp.where(first if a == 0 else jnp.logical_not(first), qp, jnp.zeros_like(qp))
                acc = None
                for side in range(2):
                    keys = kv_ref if side == 0 else peer_ref
                    for j in range(0, rows, kc):
                        s = nt(qm, keys[j : j + kc, lanes])
                        pr = jnp.exp2(s * c).astype(BF)
                        o = nn(pr, va_ref[side * rows + j : side * rows + j + kc, :])
                        acc = o if acc is None else acc + o
                outs.append(acc)
                s = nt(qm, ck_ref[:, lanes])
                couts.append(nn(jnp.exp2(s * c).astype(BF), cva_ref[...]))
            so = jnp.where(first, outs[0][:, :128], outs[1][:, :128])
            sl = jnp.where(first, outs[0][:, 128:], outs[1][:, 128:])
            co = jnp.where(first, couts[0][:, :128], couts[1][:, :128])
            cl = jnp.where(first, couts[0][:, 128:], couts[1][:, 128:])
            so = so / sl
            co = co / cl
            mixed_ref[z, rs, lanes] = (so + gate * co).astype(BF)
            self_ref[rs, lanes] = so
            cross_ref[rs, lanes] = co
            lt = jnp.log2(sl).T
            ct = jnp.log2(cl).T
            lse_ref[p, :, rs] = jnp.concatenate([lt[0:1], lt[64:65], ct[0:1], ct[64:65], lt[0:4]], axis=0)
            return 0

        lax.fori_loop(0, rows // qb, block, 0)

        @pl.when(p >= 1)
        def _():
            relay(1, p - 1)

        send_own(p)
        return 0

    pairs = width // 128
    lax.fori_loop(0, pairs, pair, 0)
    for t in range(pairs + n - 2):
        for d in range(1, n):
            if 0 <= t - (d - 1) < pairs and (d > 1 or t == pairs - 1):
                relay(d, t - (d - 1))
    for p in range(pairs):
        for o in range(n):

            @pl.when(both(z >= o, z < n - 1))
            def _(o=o, p=p):
                copy(0, o, p).wait_send()

            @pl.when(both(z <= o, z > 0))
            def _(o=o, p=p):
                copy(1, o, p).wait_send()


def attend(q, kv, peer, live, ck, cv, gate, scale, cid, qb=256, kc=1024):
    n = lax.axis_size("head")
    rows, width = q.shape
    txt = ck.shape[0]
    qb, kc = min(qb, rows), min(kc, rows)
    return pl.pallas_call(
        functools.partial(attend_kernel, n, scale, qb, kc),
        out_shape=(S((n, rows, width), BF), S((rows, width), F32), S((rows, width), F32), S((width // 128, 8, rows), F32)),
        in_specs=[VM] * 7,
        out_specs=(VM,) * 4,
        scratch_shapes=[
            pltpu.VMEM((2 * rows, 256), BF),
            pltpu.VMEM((txt, 256), BF),
            pltpu.SemaphoreType.DMA((2, n, width // 128)),
            pltpu.SemaphoreType.DMA((2, n, width // 128)),
        ],
        compiler_params=pltpu.CompilerParams(collective_id=cid, has_side_effects=True, vmem_limit_bytes=VMEM_BYTES // 2),
        cost_estimate=pl.CostEstimate(flops=32 * rows * rows * width, bytes_accessed=12 * rows * width, transcendentals=0),
        name="attend",
    )(q, kv, peer, live, ck, cv, gate)


def head_sum(x):
    ind = (lax.broadcasted_iota(jnp.int32, (8, 128), 0) == lax.broadcasted_iota(jnp.int32, (8, 128), 1) // 64).astype(F32)
    return lax.dot_general(ind, x, (((1,), (1,)), ((), ())), preferred_element_type=F32, precision=HIGHEST)


def cross_back_kernel(
    scale, qb, q_ref, ck_ref, cv_ref, gate_ref, cross_ref, lse_ref, dm_ref, dq_ref, dck_ref, dcv_ref, gg_ref, ckt_ref, p_ref, d_ref
):
    rows, width = q_ref.shape
    txt = ck_ref.shape[0]
    c = scale * LOG2E
    first = lax.broadcasted_iota(jnp.int32, (qb, 128), 1) < 64

    def pair(p, _):
        lanes = pl.ds(pl.multiple_of(p * 128, 128), 128)
        ckt_ref[...] = ck_ref[:, lanes].T
        gate = gate_ref[:, lanes]
        dck_ref[:, lanes] = jnp.zeros((txt, 128), F32)
        dcv_ref[:, lanes] = jnp.zeros((txt, 128), F32)
        gg_ref[:, lanes] = jnp.zeros((8, 128), F32)

        def block(b, _):
            rs = pl.ds(pl.multiple_of(b * qb, qb), qb)
            qp = q_ref[rs, lanes]
            dmf = dm_ref[rs, lanes].astype(F32)
            dcf = (gate * dmf).astype(BF)
            cross = cross_ref[rs, lanes]
            gg_ref[:, lanes] += fold8(dmf * cross)
            delta = head_sum(dcf.astype(F32) * cross)
            z = jnp.zeros_like(qp)
            masks = (first, jnp.logical_not(first))
            qs = [jnp.where(m, qp, z) for m in masks]
            dcs = [jnp.where(m, dcf, z) for m in masks]
            lse = lse_ref[p, :, rs]
            dqt = []
            for a in range(2):
                s = nt(ck_ref[:, lanes], qs[a])
                pr = jnp.exp2(s * c - lse[2 + a : 3 + a])
                dp = nt(cv_ref[:, lanes], dcs[a])
                p_ref[:, a * qb : (a + 1) * qb] = pr.astype(BF)
                dd = (pr * (dp - delta[a : a + 1])).astype(BF)
                d_ref[:, a * qb : (a + 1) * qb] = dd
                dqt.append(nn(ckt_ref[a * 64 : (a + 1) * 64, :], dd))
            dcv_ref[:, lanes] += nn(p_ref[...], jnp.concatenate(dcs, axis=0))
            dck_ref[:, lanes] += nn(d_ref[...], jnp.concatenate(qs, axis=0))
            dq_ref[rs, lanes] = (jnp.concatenate(dqt, axis=0) * scale).T
            return 0

        lax.fori_loop(0, rows // qb, block, 0)
        dck_ref[:, lanes] = dck_ref[:, lanes] * scale
        return 0

    lax.fori_loop(0, width // 128, pair, 0)


def cross_back(q, ck, cv, gate, co, lse, dm, scale, qb=512):
    rows, width = q.shape
    txt = ck.shape[0]
    qb = min(qb, rows)
    return pl.pallas_call(
        functools.partial(cross_back_kernel, scale, qb),
        out_shape=(S((rows, width), F32), S((txt, width), F32), S((txt, width), F32), S((8, width), F32)),
        in_specs=[VM] * 7,
        out_specs=(VM,) * 4,
        scratch_shapes=[pltpu.VMEM((128, txt), BF), pltpu.VMEM((txt, 2 * qb), BF), pltpu.VMEM((txt, 2 * qb), BF)],
        compiler_params=pltpu.CompilerParams(vmem_limit_bytes=VMEM_BYTES // 2),
        cost_estimate=pl.CostEstimate(flops=24 * rows * txt * width, bytes_accessed=12 * rows * width, transcendentals=0),
        name="cross_back",
    )(q, ck, cv, gate, co, lse, dm)


def attend_back_kernel(
    n,
    per,
    scale,
    qb,
    kc,
    q_ref,
    kv_ref,
    peer_ref,
    live_ref,
    self_ref,
    lse_ref,
    dm_ref,
    dqc_ref,
    part_ref,
    dq_ref,
    dkv_ref,
    dpeer_ref,
    fsum_ref,
    kt_ref,
    p_ref,
    d_ref,
    ak_ref,
    av_ref,
    rbuf,
    lbuf,
    ssem,
    rsem,
):
    line_barrier(lax.axis_index("head"), n)
    ch = Chain(n, SUBS, LAG, part_ref, fsum_ref, rbuf, lbuf, ssem, rsem)
    rows, width = q_ref.shape
    c = scale * LOG2E
    first = lax.broadcasted_iota(jnp.int32, (qb, 128), 1) < 64

    def pair(p, _):
        lanes = pl.ds(pl.multiple_of(p * 128, 128), 128)
        vlanes = pl.ds(pl.multiple_of(width + p * 128, 128), 128)
        kt_ref[:, :rows] = kv_ref[:, lanes].T
        kt_ref[:, rows:] = peer_ref[:, lanes].T
        ak_ref[...] = jnp.zeros_like(ak_ref)
        av_ref[...] = jnp.zeros_like(av_ref)

        def block(b, _):
            rs = pl.ds(pl.multiple_of(b * qb, qb), qb)
            qp = q_ref[rs, lanes]
            dm = dm_ref[rs, lanes]
            dmf = dm.astype(F32)
            delta = head_sum(dmf * self_ref[rs, lanes])
            z = jnp.zeros_like(qp)
            masks = (first, jnp.logical_not(first))
            qs = [jnp.where(m, qp, z) for m in masks]
            dms = [jnp.where(m, dm, z) for m in masks]
            qstack = jnp.concatenate(qs, axis=0)
            dstack = jnp.concatenate(dms, axis=0)
            lse = lse_ref[p, :, rs]
            dqt = [None, None]
            for side in range(2):
                src = kv_ref if side == 0 else peer_ref
                for j in range(0, rows, kc):
                    at = side * rows + j
                    for a in range(2):
                        s = nt(src[j : j + kc, lanes], qs[a])
                        pr = jnp.exp2(s * c - lse[a : a + 1])
                        dp = nt(src[j : j + kc, vlanes], dms[a])
                        p_ref[:, a * qb : (a + 1) * qb] = pr.astype(BF)
                        dd = (pr * (dp - delta[a : a + 1])).astype(BF)
                        d_ref[:, a * qb : (a + 1) * qb] = dd
                        t = nn(kt_ref[a * 64 : (a + 1) * 64, at : at + kc], dd)
                        dqt[a] = t if dqt[a] is None else dqt[a] + t
                    av_ref[at : at + kc] += nn(p_ref[...], dstack)
                    ak_ref[at : at + kc] += nn(d_ref[...], qstack)
            dq_ref[rs, lanes] = (jnp.concatenate(dqt, axis=0) * scale).T + dqc_ref[rs, lanes]
            for i in range(per):
                k = (p * (rows // qb) + b) * per + i

                @pl.when(k < ch.steps)
                def _(k=k):
                    ch.step(k)

            return 0

        lax.fori_loop(0, rows // qb, block, 0)
        live = live_ref[...].astype(F32)
        dkv_ref[:, lanes] = ak_ref[:rows] * (live[:rows] * scale)
        dkv_ref[:, vlanes] = av_ref[:rows] * live[:rows]
        dpeer_ref[:, lanes] = (ak_ref[rows:] * (live[rows:] * scale)).astype(BF)
        dpeer_ref[:, vlanes] = (av_ref[rows:] * live[rows:]).astype(BF)
        return 0

    lax.fori_loop(0, width // 128, pair, 0)
    ch.run(min(ch.steps, (width // 128) * (rows // qb) * per), ch.steps)
    ch.drain()


def attend_back(q, kv, peer, live, so, lse, dm, dqc, part, scale, cid, qb=256, kc=512, per=2):
    n = lax.axis_size("head")
    rows, width = q.shape
    qb, kc = min(qb, rows), min(kc, rows)
    return pl.pallas_call(
        functools.partial(attend_back_kernel, n, per, scale, qb, kc),
        out_shape=(
            S((rows, width), F32),
            S((rows, 2 * width), F32),
            S((rows, 2 * width), BF),
            S(part.shape, BF),
        ),
        in_specs=[VM] * 9,
        out_specs=(VM,) * 4,
        scratch_shapes=[
            pltpu.VMEM((128, 2 * rows), BF),
            pltpu.VMEM((kc, 2 * qb), BF),
            pltpu.VMEM((kc, 2 * qb), BF),
            pltpu.VMEM((2 * rows, 128), F32),
            pltpu.VMEM((2 * rows, 128), F32),
        ]
        + chain_scratch(*part.shape, SUBS),
        compiler_params=pltpu.CompilerParams(collective_id=cid, has_side_effects=True, vmem_limit_bytes=BIG),
        cost_estimate=pl.CostEstimate(flops=80 * rows * rows * width, bytes_accessed=20 * rows * width, transcendentals=0),
        name="attend_back",
    )(q, kv, peer, live, so, lse, dm, dqc, part)


def pair_swap(value):
    pairs = [(source, source ^ 1) for source in range(lax.axis_size("seq"))]
    return lax.ppermute(value, "seq", pairs)


def rope_tables(grid_rows, grid_cols, first_token, row_count, head_size):
    stride = grid_cols + 1
    tokens = first_token + jnp.arange(row_count, dtype=jnp.int32)
    valid = tokens < grid_rows * stride
    row_pos = (tokens // stride).astype(F32)
    col_pos = (tokens % stride).astype(F32)
    quarter = head_size // 4
    half = head_size // 2
    lane = jnp.arange(128, dtype=jnp.int32) % half
    frequency = ROPE_BASE ** (-(lane % quarter).astype(F32) / quarter)
    angles = jnp.where(lane[None, :] < quarter, row_pos[:, None], col_pos[:, None]) * frequency[None, :]
    sign = jnp.where(jnp.arange(128) % head_size < half, -1.0, 1.0)
    return jnp.cos(angles), jnp.sin(angles) * sign[None, :], valid


def scatter(v):
    return lax.psum_scatter(v, "seq", scatter_dimension=0, tiled=True)


def local(
    image_rows,
    condition,
    text_feats,
    grid_shape,
    text_slot,
    attn_gain,
    ffn_gain,
    mod_weight,
    mod_bias,
    qkv_weight,
    qk_gains,
    text_kv_weight,
    cross_gate,
    out_weight,
    gate_up_weight,
    down_weight,
    cotangent,
):
    row_count, model_width = image_rows.shape
    head_local, head_size = qk_gains.shape[1], qk_gains.shape[2]
    inner = head_local * head_size
    ff_local = down_weight.shape[0]
    text_local, cap_width = text_feats.shape
    head_count = lax.axis_size("head")
    seq_count = lax.axis_size("seq")
    seq_index = lax.axis_index("seq")
    head_index = lax.axis_index("head")
    image_index = seq_index // 2
    pair_half = seq_index % 2
    score_scale = head_size ** (-0.5)
    image_count = condition.shape[0]

    grid_pair = lax.dynamic_index_in_dim(grid_shape, image_index, 0, keepdims=False)
    cos, sin, valid = rope_tables(grid_pair[0], grid_pair[1], pair_half * row_count, row_count, head_size)
    keep = valid.astype(F32)[:, None]
    live_own = jnp.broadcast_to(keep, (row_count, 128))
    peer_tokens = (1 - pair_half) * row_count + jnp.arange(row_count, dtype=jnp.int32)
    keep_peer = (peer_tokens < grid_pair[0] * (grid_pair[1] + 1)).astype(F32)[:, None]
    live_all = jnp.concatenate([live_own, jnp.broadcast_to(keep_peer, (row_count, 128))], axis=0).astype(BF)

    cond_all = jax.nn.silu(condition.astype(F32)).astype(BF)
    cond_low = lax.dynamic_index_in_dim(cond_all, image_index, 0, keepdims=True)
    mod_piece = jnp.dot(cond_low, mod_weight, preferred_element_type=F32) + mod_bias
    modulation = share(jnp.broadcast_to(mod_piece, (8, model_width)), 4)[:, 0]
    one_attn = 1.0 + modulation[0]
    one_ffn = 1.0 + modulation[2]
    tanh_attn = jnp.tanh(modulation[1])
    tanh_ffn = jnp.tanh(modulation[3])

    head_gains = jnp.concatenate([qk_gains.reshape(3, inner), jnp.zeros((5, inner), F32)], axis=0)
    gate_head = jnp.tanh(cross_gate)
    gate_lanes = jnp.repeat(gate_head, head_size)[None, :]
    qkv_mats = jnp.transpose(qkv_weight, (1, 0, 2))
    same_head = (jnp.arange(inner)[:, None] // head_size == jnp.arange(inner)[None, :] // head_size).astype(F32) / head_size

    text_kv_flat = text_kv_weight.reshape(cap_width, 2 * inner)
    text_proj = jnp.dot(text_feats, text_kv_flat, preferred_element_type=F32)
    cap_pre = text_proj[:, :inner]
    cap_r = lax.rsqrt(jnp.dot(cap_pre * cap_pre, same_head, precision=HIGHEST) + EPSILON)
    cap_u = cap_pre * cap_r
    cap_kv = jnp.concatenate([cap_u * head_gains[2:3], text_proj[:, inner:]], axis=1).astype(BF)
    caps = lax.all_gather(cap_kv, "seq", axis=0, tiled=False)
    slot = lax.dynamic_index_in_dim(text_slot, image_index, 0, keepdims=False)
    cap_own = lax.dynamic_index_in_dim(caps, slot, 0, keepdims=False)
    cap_key, cap_value = cap_own[:, :inner], cap_own[:, inner:]

    slice_rows = inner // seq_count
    out_slice = lax.dynamic_slice_in_dim(out_weight, seq_index * slice_rows, slice_rows, 0)

    normed, pre, query, kv, out_slices = make_qkv(
        image_rows, (attn_gain * one_attn)[None, :], qkv_mats, head_gains, cos, sin, live_own, out_slice, 5
    )
    out_all = lax.all_gather(out_slices, "seq", axis=1, tiled=True)
    kv_peer = pair_swap(kv)
    mixed_all, self_out, cross_out, lse = attend(query, kv, kv_peer, live_all, cap_key, cap_value, gate_lanes, score_scale, 0)
    mixed = lax.dynamic_index_in_dim(mixed_all, head_index, 0, keepdims=False)
    vec = jnp.concatenate([jnp.stack([tanh_attn, ffn_gain * one_ffn, attn_gain * one_attn, tanh_ffn]), jnp.zeros((4, model_width), F32)])
    attn_out, ffn_low = make_middle(mixed_all, out_all, image_rows, live_own, vec)

    gate_up_flat = gate_up_weight.reshape(model_width, 2 * ff_local)
    attn_grad_low, ffn_rows, middle_grad_half, ffn_part, ffn_wgrad = ffn_exchange(
        ffn_low, cotangent, gate_up_flat, down_weight, image_rows, attn_out, live_own, vec, 1
    )
    ffn_wsum = scatter(ffn_wgrad)
    grad_out = cotangent.astype(F32)
    mixed_grad = nt(attn_grad_low, out_weight).astype(BF)
    dq_cross, dck, dcv, gate_rows = cross_back(query, cap_key, cap_value, gate_lanes, cross_out, lse, mixed_grad, score_scale)
    cap_grads = lax.all_gather(jnp.concatenate([dck, dcv], axis=1).astype(BF), "seq", axis=0, tiled=False)
    dq, dkv, dpeer, ffn_out = attend_back(query, kv, kv_peer, live_all, self_out, lse, mixed_grad, dq_cross, ffn_part, score_scale, 2)
    from_peer = pair_swap(dpeer)
    dq, cap_grads, ffn_wsum = lax.optimization_barrier((dq, cap_grads, ffn_wsum))

    own_image = jnp.sum(jnp.where(text_slot == seq_index, jnp.arange(image_count), 0))
    used = jnp.any(text_slot == seq_index).astype(F32)
    two = lax.dynamic_slice_in_dim(cap_grads, 2 * own_image, 2, 0).astype(F32)
    cap_grad = (two[0] + two[1]) * used
    cap_dy, cap_dv = cap_grad[:, :inner], cap_grad[:, inner:]
    cap_w = cap_dy * head_gains[2:3]
    cap_pre_grad = cap_r * (cap_w - cap_u * jnp.dot(cap_w * cap_u, same_head, precision=HIGHEST))
    cap_gain = jnp.sum(cap_dy * cap_u, axis=0)
    text_low = jnp.concatenate([cap_pre_grad, cap_dv], axis=1).astype(BF)
    text_weight_grad = tn(text_feats, text_low).astype(BF)
    text_part = nt(text_low, text_kv_flat).astype(BF)
    dq, dkv, text_part, text_weight_grad = lax.optimization_barrier((dq, dkv, text_part, text_weight_grad))
    text_sum = lax.psum_scatter(text_part, "head", scatter_dimension=1, tiled=True)
    text_weight_sum = scatter(text_weight_grad)

    ffn_out = ffn_out.astype(F32)
    output = (image_rows.astype(F32) + keep * tanh_attn * attn_out + keep * tanh_ffn * ffn_out).astype(BF)
    gate_ffn_grad = jnp.sum(grad_out * keep * ffn_out, axis=0) * (1.0 - tanh_ffn * tanh_ffn)
    grad_pre, gain_rows, attn_in_part = qkv_back(dq, dkv, from_peer, pre, head_gains, cos, sin, qkv_mats)
    attn_wgrad = wgrad_pair(normed, grad_pre, attn_grad_low, mixed)
    attn_in_part, attn_wgrad, text_sum = lax.optimization_barrier((attn_in_part, attn_wgrad, text_sum))
    attn_wsum = scatter(attn_wgrad)
    text_grad = text_sum.astype(F32)
    rows_grad, row_sums = chain_rows(attn_in_part, image_rows, middle_grad_half, vec[2:], ffn_rows, 3)
    ffn_sum, attn_sum = row_sums[0], row_sums[2]
    gate_attn_grad = row_sums[1] * (1.0 - tanh_attn * tanh_attn)

    mod_grad = jnp.stack([attn_sum * attn_gain, gate_attn_grad, ffn_sum * ffn_gain, gate_ffn_grad])
    own_mod = lax.dynamic_index_in_dim(mod_grad, head_index, 0, keepdims=False)
    gain_grad = jnp.concatenate([gain_rows[0:8].sum(0), gain_rows[8:16].sum(0), cap_gain])
    gate_grad_head = gate_rows.sum(0)
    small = jnp.concatenate([attn_sum * one_attn, ffn_sum * one_ffn, own_mod, gain_grad, gate_grad_head])
    smalls = lax.all_gather(small, "seq", axis=0, tiled=False)
    total = jnp.sum(smalls, axis=0)
    d = model_width
    dl = d // seq_count
    attn_gain_sum = lax.dynamic_slice_in_dim(total[:d], seq_index * dl, dl)
    ffn_gain_sum = lax.dynamic_slice_in_dim(total[d : 2 * d], seq_index * dl, dl)
    mod_bias_sum = lax.dynamic_slice_in_dim(total[2 * d : 3 * d], seq_index * dl, dl)[None, :]
    qk_all = total[3 * d : 3 * d + 3 * inner].reshape(3, head_local, seq_count, head_size // seq_count)
    qk_gain_sum = lax.dynamic_index_in_dim(qk_all, seq_index, 2, keepdims=False)
    gate_sum = total[3 * d + 3 * inner :].reshape(head_local, head_size).sum(-1) * (1.0 - gate_head * gate_head)
    cond_cols = condition.shape[1] // seq_count
    cond_part = lax.dynamic_slice_in_dim(cond_all, seq_index * cond_cols, cond_cols, 1).astype(F32)
    image_mods = smalls[:, 2 * d : 3 * d].reshape(image_count, 2, d).sum(1)
    mod_weight_sum = lax.dot_general(cond_part, image_mods, (((0,), (0,)), ((), ())), precision=HIGHEST)

    split = 2 * ff_local
    ffn_wsum, attn_wsum = ffn_wsum.astype(F32), attn_wsum.astype(F32)
    gate_up_sum = ffn_wsum[:, :split].reshape(-1, 2, ff_local)
    down_sum = ffn_wsum[:, split:].T
    qkv_sum = attn_wsum[:, : 3 * inner].reshape(-1, 3, inner)
    out_sum = attn_wsum[:, 3 * inner :].T
    text_weight_sum = text_weight_sum.astype(F32).reshape(-1, 2, inner)
    return (
        output,
        rows_grad,
        text_grad,
        attn_gain_sum,
        ffn_gain_sum,
        mod_weight_sum,
        mod_bias_sum,
        qkv_sum,
        qk_gain_sum,
        text_weight_sum,
        gate_sum,
        out_sum,
        gate_up_sum,
        down_sum,
    )


def solution(mesh):
    return jax.shard_map(
        local,
        mesh=mesh,
        in_specs=(
            P("seq", None),
            P(),
            P("seq", None),
            P(),
            P(),
            P(),
            P(),
            P(None, "head"),
            P("head", None),
            P(None, None, "head"),
            P(None, "head", None),
            P(None, None, "head"),
            P("head"),
            P("head", None),
            P(None, None, "head"),
            P("head", None),
            P("seq", None),
        ),
        out_specs=(
            P("seq", None),
            P("seq", None),
            P("seq", "head"),
            P("seq"),
            P("seq"),
            P("seq", "head"),
            P("head", "seq"),
            P("seq", None, "head"),
            P(None, "head", "seq"),
            P("seq", None, "head"),
            P("head"),
            P("head", "seq"),
            P("seq", None, "head"),
            P("head", "seq"),
        ),
        check_vma=False,
    )
```

```python
import functools

import jax
import jax.numpy as jnp
from jax import lax
from jax.experimental import pallas as pl
from jax.experimental.pallas import tpu as pltpu
from jax.sharding import PartitionSpec as P

TXT = 256
EPSILON = 1e-06
ROPE_BASE = 10000.0
LOG2E = 1.4426950408889634
F32 = jnp.float32
BF = jnp.bfloat16
VMEM_BYTES = 67043328
HIGHEST = lax.Precision.HIGHEST
VM = pl.BlockSpec(memory_space=pltpu.VMEM)
S = jax.ShapeDtypeStruct


def nt(a, b):
    return lax.dot_general(a, b, (((1,), (1,)), ((), ())), preferred_element_type=F32)


def nn(a, b):
    return lax.dot_general(a, b, (((1,), (0,)), ((), ())), preferred_element_type=F32)


def tn(a, b):
    return lax.dot_general(a, b, (((0,), (0,)), ((), ())), preferred_element_type=F32)


def head_mean(x):
    rows = lax.broadcasted_iota(jnp.int32, (128, 128), 0) // 64
    cols = lax.broadcasted_iota(jnp.int32, (128, 128), 1) // 64
    same = jnp.where(rows == cols, 1.0 / 64, 0.0).astype(BF)
    high = x.astype(BF)
    rest = (x - high.astype(F32)).astype(BF)
    return nn(high, same) + nn(rest, same)


def swap_halves(x):
    lane = lax.broadcasted_iota(jnp.int32, x.shape, 1) % 64
    return jnp.where(lane < 32, pltpu.roll(x, 96, 1), pltpu.roll(x, 32, 1))


def to_head(z):
    return {"head": z}


def both(a, b):
    return jnp.logical_and(a, b)


def line_barrier(z, n):
    bar = pltpu.get_barrier_semaphore()
    for ok, other in ((z > 0, z - 1), (z < n - 1, z + 1)):

        @pl.when(ok)
        def _(other=other):
            pl.semaphore_signal(bar, inc=1, device_id=to_head(other), device_id_type=pl.DeviceIdType.MESH)

    end = jnp.logical_or(z == 0, z == n - 1)

    @pl.when(end)
    def _():
        pl.semaphore_wait(bar, 1)

    @pl.when(jnp.logical_not(end))
    def _():
        pl.semaphore_wait(bar, 2)


def head_barrier(z, n):
    bar = pltpu.get_barrier_semaphore()
    for i in range(1, n):
        pl.semaphore_signal(bar, inc=1, device_id=to_head(lax.rem(z + i, n)), device_id_type=pl.DeviceIdType.MESH)
    pl.semaphore_wait(bar, n - 1)


class Chain:
    def __init__(self, n, subs, lag, part_ref, out_ref, rbuf, lbuf, ssem, rsem, finalize=None):
        self.z, self.n, self.subs, self.lag = lax.axis_index("head"), n, subs, lag
        self.part, self.out, self.rbuf, self.lbuf, self.ssem, self.rsem = part_ref, out_ref, rbuf, lbuf, ssem, rsem
        self.half = part_ref.shape[0] // 2
        self.unit = self.half // subs
        self.finalize = finalize
        self.steps = subs + 2 * lag * (n - 1)

    def near(self, s):
        return pl.ds(pl.multiple_of(s * self.unit, self.unit), self.unit)

    def far(self, s):
        return pl.ds(pl.multiple_of(self.half + s * self.unit, self.unit), self.unit)

    def copy(self, kind, s, first=False):
        src, at, to = (
            (self.rbuf, self.near(s), self.near(s)),
            (self.lbuf, self.near(s), self.near(s)),
            (self.out, self.near(s), self.near(s)),
            (self.out, self.far(s), self.far(s)),
        )[kind]
        dst = src
        if first:
            src, at = self.part, (self.far(s) if kind == 0 else self.near(s))
        return pltpu.make_async_remote_copy(
            src_ref=src.at[at],
            dst_ref=dst.at[to],
            send_sem=self.ssem.at[kind, s],
            recv_sem=self.rsem.at[kind, s],
            device_id=to_head(self.z + (1 if kind % 2 == 0 else -1)),
            device_id_type=pl.DeviceIdType.MESH,
        )

    def step(self, k):
        z, lag, last = self.z, self.lag, self.n - 1

        def inside(s):
            return both(s >= 0, s < self.subs)

        for kind, buf in ((0, self.rbuf), (1, self.lbuf)):
            hops = z if kind == 0 else last - z
            s = k - lag * hops

            @pl.when(both(inside(s), hops == 0))
            def _(kind=kind, s=s):
                self.copy(kind, s, True).start()

            @pl.when(both(inside(s), both(hops > 0, hops < last)))
            def _(kind=kind, s=s, buf=buf):
                self.copy(kind, s).wait_recv()
                at = self.near(s)
                own = self.part[self.far(s) if kind == 0 else at]
                buf[at] = (buf[at].astype(F32) + own.astype(F32)).astype(BF)
                self.copy(kind, s).start()

            @pl.when(both(inside(s), hops == last))
            def _(kind=kind, s=s, buf=buf):
                self.copy(kind, s).wait_recv()
                to = self.far(s) if kind == 0 else self.near(s)
                total = buf[self.near(s)].astype(F32) + self.part[to].astype(F32)
                if self.finalize is not None:
                    total = self.finalize(self.near(s), to, total)
                self.out[to] = total.astype(BF)
                self.copy(3 - kind, s).start()

        for kind in (2, 3):
            hops = z if kind == 2 else last - z
            s = k - lag * (last + hops)

            @pl.when(both(inside(s), hops > 0))
            def _(kind=kind, s=s, hops=hops):
                self.copy(kind, s).wait_recv()

                @pl.when(hops < last)
                def _():
                    self.copy(kind, s).start()

    def run(self, first, last):
        def one(k, c):
            self.step(k)
            return c

        lax.fori_loop(first, last, one, 0)

    def drain(self):
        def one(s, c):
            for kind in range(4):

                @pl.when(self.z < self.n - 1 if kind % 2 == 0 else self.z > 0)
                def _(kind=kind):
                    self.copy(kind, s).wait_send()

            return c

        lax.fori_loop(0, self.subs, one, 0)


def chain_scratch(rows, width, subs):
    return [
        pltpu.VMEM((rows // 2, width), BF),
        pltpu.VMEM((rows // 2, width), BF),
        pltpu.SemaphoreType.DMA((4, subs)),
        pltpu.SemaphoreType.DMA((4, subs)),
    ]


SUBS, LAG, BACK_LAG = 16, 2, 2
ANY = pl.BlockSpec(memory_space=pl.ANY)
BIG = VMEM_BYTES - (1 << 20)


def norm_parts(values):
    r = lax.rsqrt(jnp.mean(values * values, axis=-1, keepdims=True) + EPSILON)
    return r, values * r


def fold8(x):
    return jnp.sum(x.reshape(x.shape[0] // 8, 8, x.shape[1]), axis=0)


def half_loads(z, n, half, whole, halves, sem):
    at = pl.ds(pl.multiple_of(jnp.where(z == 0, 0, half), half), half)
    pairs = [(ref.at[at], to) for ref, to in whole] + halves
    return [pltpu.make_async_copy(ref, to, sem.at[i]) for i, (ref, to) in enumerate(pairs)]


def run_with_loads(ch, end, loads):
    @pl.when(end)
    def _():
        for c in loads:
            c.start()

    need = ch.lag * (ch.n - 1)
    ch.run(0, need)

    @pl.when(end)
    def _():
        for c in loads:
            c.wait()

    ch.run(need, ch.steps)


def ffn_kernel(
    n, subs, lag, blocks, tile,
    h_any, g_any, wgu_any, wd_any, x_any, attn_any, live_ref, vec_ref,
    out_ref, sum_ref, dmid_any, fpart_any, wg_any,
    rbuf, lbuf, ssem, rsem, hv, gv, wgu, wd, xv, av, part_ref, dgu, hid, dffn, fpart, dmid, wbuf, csem, osem, tsem,
):
    z = lax.axis_index("head")
    rows, width = hv.shape
    ff = wd.shape[0]
    half = rows // 2
    rb = half // blocks
    end = jnp.logical_or(z == 0, z == n - 1)
    loads = [pltpu.make_async_copy(a, b, csem.at[i]) for i, (a, b) in enumerate(((h_any, hv), (wgu_any, wgu), (g_any, gv), (wd_any, wd)))]
    for c in loads:
        c.start()
    mine = pl.ds(pl.multiple_of(jnp.where(z == 0, 0, half), half), half)
    end_loads = [pltpu.make_async_copy(a.at[mine], b, csem.at[4 + i]) for i, (a, b) in enumerate(((x_any, xv), (attn_any, av)))]

    @pl.when(end)
    def _():
        for c in end_loads:
            c.start()

    sum_ref[...] = jnp.zeros_like(sum_ref)
    line_barrier(z, n)
    tanh_attn, gain, tanh_ffn = vec_ref[0:1], vec_ref[1:2], vec_ref[3:4]

    def finalize(at, to, dh):
        attn, live = av[at], live_ref[to, 0:1]
        mid = xv[at].astype(F32) + live * tanh_attn * attn
        r, u = norm_parts(mid)
        w = dh * gain
        grad = gv[to].astype(F32) + r * (w - u * jnp.mean(w * u, axis=-1, keepdims=True))
        dmid[at] = grad
        masked = grad * live
        sum_ref[0:8] += fold8(dh * u)
        sum_ref[8:16] += fold8(masked * attn)
        return masked * tanh_attn

    ch = Chain(n, subs, lag, part_ref, out_ref, rbuf, lbuf, ssem, rsem, finalize)

    def step(k):
        @pl.when(jnp.logical_and(end, k == lag * (n - 1)))
        def _():
            for c in end_loads:
                c.wait()

        ch.step(k)

    per = subs // blocks

    def block(t, c):
        near = pl.ds(pl.multiple_of(t * rb, rb), rb)
        far = pl.ds(pl.multiple_of(half + t * rb, rb), rb)

        def put(ref, v):
            ref[near] = v[:rb]
            ref[far] = v[rb:]

        @pl.when(t == 0)
        def _():
            loads[0].wait()
            loads[1].wait()

        gu = nn(jnp.concatenate([hv[near], hv[far]], axis=0), wgu[...])
        gate, up = gu[:, :ff], gu[:, ff:]
        sig = 1.0 / (1.0 + jnp.exp(-gate))
        act = gate * sig
        hidden = (act * up).astype(BF)
        put(hid, hidden)

        @pl.when(t == 0)
        def _():
            loads[2].wait()
            loads[3].wait()

        grad = jnp.concatenate([gv[near].astype(F32) * live_ref[near, 0:1], gv[far].astype(F32) * live_ref[far, 0:1]], axis=0)
        low = (grad * tanh_ffn).astype(BF)
        put(dffn, low)
        dhid = nt(low, wd[...])
        both_grads = jnp.concatenate(
            [(dhid * up * (sig + act * (1.0 - sig))).astype(BF), (dhid * act).astype(BF)], axis=1
        )
        put(dgu, both_grads)
        put(part_ref, nt(both_grads, wgu[...]).astype(BF))

        def some(i, c):
            step(t * per + i)
            return c

        lax.fori_loop(0, per, some, 0)
        put(fpart, nn(hidden, wd[...]).astype(BF))
        return c

    lax.fori_loop(0, blocks, block, 0)
    fcopy = pltpu.make_async_copy(fpart, fpart_any, osem.at[0])
    fcopy.start()

    tiles = width // tile
    every = max(1, (ch.steps - subs) // tiles)

    def tile_copy(j):
        return pltpu.make_async_copy(wbuf.at[lax.rem(j, 2)], wg_any.at[pl.ds(pl.multiple_of(j * tile, tile), tile)], tsem.at[j])

    def weights(j, c):
        def some(i, c):
            step(subs + j * every + i)
            return c

        lax.fori_loop(0, every, some, 0)

        @pl.when(j >= 2)
        def _():
            tile_copy(j - 2).wait()

        cols = pl.ds(pl.multiple_of(j * tile, tile), tile)
        slot = lax.rem(j, 2)
        wbuf[slot, :, : 2 * ff] = tn(hv[:, cols], dgu[...]).astype(BF)
        wbuf[slot, :, 2 * ff :] = tn(dffn[:, cols], hid[...]).astype(BF)
        tile_copy(j).start()
        return c

    lax.fori_loop(0, tiles, weights, 0)

    def rest(k, c):
        step(k)
        return c

    lax.fori_loop(subs + tiles * every, ch.steps, rest, 0)
    dcopy = pltpu.make_async_copy(dmid, dmid_any, osem.at[1])

    @pl.when(end)
    def _():
        dcopy.start()

    for j in range(max(0, tiles - 2), tiles):
        tile_copy(j).wait()
    fcopy.wait()
    ch.drain()

    @pl.when(end)
    def _():
        dcopy.wait()


def ffn_exchange(h, g, wgu, wd, x, attn, live, vec, cid, subs=16, lag=4, blocks=4, tile=256):
    n = lax.axis_size("head")
    rows, width = h.shape
    ff = wd.shape[0]
    half = rows // 2
    vm = pltpu.VMEM
    return pl.pallas_call(
        functools.partial(ffn_kernel, n, subs, lag, blocks, tile),
        out_shape=(
            S((rows, width), BF),
            S((16, width), F32),
            S((half, width), F32),
            S((rows, width), BF),
            S((width, 3 * ff), BF),
        ),
        in_specs=[ANY] * 6 + [VM] * 2,
        out_specs=(VM, VM, ANY, ANY, ANY),
        scratch_shapes=chain_scratch(rows, width, subs)
        + [
            vm((rows, width), BF),
            vm((rows, width), BF),
            vm((width, 2 * ff), BF),
            vm((ff, width), BF),
            vm((half, width), BF),
            vm((half, width), F32),
            vm((rows, width), BF),
            vm((rows, 2 * ff), BF),
            vm((rows, ff), BF),
            vm((rows, width), BF),
            vm((rows, width), BF),
            vm((half, width), F32),
            vm((2, tile, 3 * ff), BF),
            pltpu.SemaphoreType.DMA((6,)),
            pltpu.SemaphoreType.DMA((2,)),
            pltpu.SemaphoreType.DMA((width // tile,)),
        ],
        compiler_params=pltpu.CompilerParams(collective_id=cid, has_side_effects=True, vmem_limit_bytes=BIG),
        cost_estimate=pl.CostEstimate(flops=100_000_000_000, bytes_accessed=30 * rows * width, transcendentals=0),
        name="ffn_exchange",
    )(h, g, wgu, wd, x, attn, live, vec)


def chain_rows_kernel(
    n, part_ref, x_ref, dmid_ref, gain_ref, sum_ref, out_ref, tot_ref, rbuf, lbuf, ssem, rsem, xv, dv, csem, acc, ends, esem, fsem
):
    z = lax.axis_index("head")
    line_barrier(z, n)
    acc[...] = jnp.zeros_like(acc)
    gain = gain_ref[0:1]

    def finalize(at, to, dh):
        r, u = norm_parts(xv[at].astype(F32))
        w = dh * gain
        acc[...] += fold8(dh * u)
        return dv[at] + r * (w - u * jnp.mean(w * u, axis=-1, keepdims=True))

    ch = Chain(n, SUBS, LAG, part_ref, out_ref, rbuf, lbuf, ssem, rsem, finalize)
    loads = half_loads(z, n, ch.half, [(x_ref, xv)], [(dmid_ref, dv)], csem)
    run_with_loads(ch, jnp.logical_or(z == 0, z == n - 1), loads)

    width = acc.shape[1]
    rows = [sum_ref[0:8], sum_ref[8:16], acc[...]]
    mine = jnp.concatenate([jnp.sum(r, axis=0, keepdims=True) for r in rows] + [jnp.zeros((5, width), F32)], axis=0)
    for e, where in ((0, 0), (1, n - 1)):

        @pl.when(z == where)
        def _(e=e):
            ends[e] = mine

    def copy(e):
        return pltpu.make_async_remote_copy(
            src_ref=ends.at[e],
            dst_ref=ends.at[e],
            send_sem=esem.at[e],
            recv_sem=fsem.at[e],
            device_id=to_head(z + (1 if e == 0 else -1)),
            device_id_type=pl.DeviceIdType.MESH,
        )

    for e, source, sink in ((0, 0, n - 1), (1, n - 1, 0)):

        @pl.when(z == source)
        def _(e=e):
            copy(e).start()

    for e, source, sink in ((0, 0, n - 1), (1, n - 1, 0)):

        @pl.when(z != source)
        def _(e=e, sink=sink):
            copy(e).wait_recv()

            @pl.when(z != sink)
            def _():
                copy(e).start()

    tot_ref[...] = ends[0] + ends[1]
    for e, sink in ((0, n - 1), (1, 0)):

        @pl.when(z != sink)
        def _(e=e):
            copy(e).wait_send()

    ch.drain()


def chain_rows(part, x, dmid, gain, sums, cid):
    n = lax.axis_size("head")
    rows, width = part.shape
    half = rows // 2
    return pl.pallas_call(
        functools.partial(chain_rows_kernel, n),
        out_shape=(S((rows, width), BF), S((8, width), F32)),
        in_specs=[VM, ANY, ANY, VM, VM],
        out_specs=(VM,) * 2,
        scratch_shapes=chain_scratch(rows, width, SUBS)
        + [
            pltpu.VMEM((half, width), BF),
            pltpu.VMEM((half, width), F32),
            pltpu.SemaphoreType.DMA((2,)),
            pltpu.VMEM((8, width), F32),
            pltpu.VMEM((2, 8, width), F32),
            pltpu.SemaphoreType.DMA((2,)),
            pltpu.SemaphoreType.DMA((2,)),
        ],
        compiler_params=pltpu.CompilerParams(collective_id=cid, has_side_effects=True, vmem_limit_bytes=BIG),
        cost_estimate=pl.CostEstimate(flops=80_000_000_000, bytes_accessed=20 * rows * width, transcendentals=0),
        name="chain_rows",
    )(part, x, dmid, gain, sums)


def share_kernel(n, piece_ref, all_ref, ssem, rsem):
    z = lax.axis_index("head")
    head_barrier(z, n)

    def copy(i):
        return pltpu.make_async_remote_copy(
            src_ref=piece_ref,
            dst_ref=all_ref.at[z],
            send_sem=ssem.at[i],
            recv_sem=rsem.at[i],
            device_id=to_head(lax.rem(z + i, n)),
            device_id_type=pl.DeviceIdType.MESH,
        )

    for i in range(1, n):
        copy(i).start()
    all_ref[z] = piece_ref[...]
    for i in range(1, n):
        copy(i).wait()


def share(piece, cid):
    n = lax.axis_size("head")
    return pl.pallas_call(
        functools.partial(share_kernel, n),
        out_shape=S((n,) + piece.shape, piece.dtype),
        in_specs=[VM],
        out_specs=VM,
        scratch_shapes=[pltpu.SemaphoreType.DMA((n,)), pltpu.SemaphoreType.DMA((n,))],
        compiler_params=pltpu.CompilerParams(collective_id=cid, has_side_effects=True, vmem_limit_bytes=BIG),
        name="share",
    )(piece)


def wgrad_kernel(a_ref, b_ref, c_ref, d_ref, o_ref):
    nb = b_ref.shape[1]
    o_ref[:, :nb] = tn(a_ref[...], b_ref[...]).astype(BF)
    o_ref[:, nb:] = tn(c_ref[...], d_ref[...]).astype(BF)


def wgrad_pair(a, b, c, d):
    rows, width = a.shape
    cols = b.shape[1] + d.shape[1]
    wb = min(256, width)
    return pl.pallas_call(
        wgrad_kernel,
        grid=(width // wb,),
        in_specs=[
            pl.BlockSpec((rows, wb), lambda i: (0, i)),
            pl.BlockSpec(b.shape, lambda i: (0, 0)),
            pl.BlockSpec((rows, wb), lambda i: (0, i)),
            pl.BlockSpec(d.shape, lambda i: (0, 0)),
        ],
        out_specs=pl.BlockSpec((wb, cols), lambda i: (i, 0)),
        out_shape=S((width, cols), BF),
        compiler_params=pltpu.CompilerParams(vmem_limit_bytes=BIG),
        cost_estimate=pl.CostEstimate(flops=2 * rows * width * cols, bytes_accessed=2 * width * cols, transcendentals=0),
        name="wgrad_pair",
    )(a, b, c, d)


def qkv_kernel(
    n, x_ref, gain_ref, w_ref, hg_ref, cos_ref, sin_ref, live_ref, slice_ref, h_ref, pre_ref, q_ref, kv_ref, all_ref, ssem, rsem
):
    z = lax.axis_index("head")

    def copy(i):
        return pltpu.make_async_remote_copy(
            src_ref=slice_ref,
            dst_ref=all_ref.at[z],
            send_sem=ssem.at[i],
            recv_sem=rsem.at[i],
            device_id=to_head(lax.rem(z + i, n)),
            device_id_type=pl.DeviceIdType.MESH,
        )

    own = pltpu.make_async_copy(slice_ref, all_ref.at[z], ssem.at[0])

    @pl.when(pl.program_id(0) == 0)
    def _():
        head_barrier(z, n)
        own.start()
        for i in range(1, n):
            copy(i).start()

    x = x_ref[...].astype(F32)
    h = (x * lax.rsqrt(jnp.mean(x * x, axis=-1, keepdims=True) + EPSILON) * gain_ref[...]).astype(BF)
    h_ref[...] = h
    width = w_ref.shape[2]
    cos, sin, live = cos_ref[...], sin_ref[...], live_ref[...]
    for part in range(2):
        pre = nn(h, w_ref[part])
        pre_ref[:, part * width : (part + 1) * width] = pre
        for p in range(width // 128):
            v = pre[:, p * 128 : (p + 1) * 128]
            r = lax.rsqrt(head_mean(v * v) + EPSILON)
            t = v * r * hg_ref[part : part + 1, p * 128 : (p + 1) * 128]
            y = t * cos + swap_halves(t) * sin
            if part == 0:
                q_ref[:, p * 128 : (p + 1) * 128] = y.astype(BF)
            else:
                kv_ref[:, p * 128 : (p + 1) * 128] = (y * live).astype(BF)
    val = nn(h, w_ref[2])
    for p in range(width // 128):
        kv_ref[:, width + p * 128 : width + (p + 1) * 128] = (val[:, p * 128 : (p + 1) * 128] * live).astype(BF)

    @pl.when(pl.program_id(0) == pl.num_programs(0) - 1)
    def _():
        own.wait()
        for i in range(1, n):
            copy(i).wait()


def make_qkv(x, gain, w, head_gains, cos, sin, live, out_slice, cid):
    n = lax.axis_size("head")
    rows, width = x.shape
    inner = w.shape[2]
    rb = min(256, rows)
    return pl.pallas_call(
        functools.partial(qkv_kernel, n),
        grid=(rows // rb,),
        in_specs=[
            pl.BlockSpec((rb, width), lambda i: (i, 0)),
            pl.BlockSpec((1, width), lambda i: (0, 0)),
            pl.BlockSpec(w.shape, lambda i: (0, 0, 0)),
            pl.BlockSpec((8, inner), lambda i: (0, 0)),
            pl.BlockSpec((rb, 128), lambda i: (i, 0)),
            pl.BlockSpec((rb, 128), lambda i: (i, 0)),
            pl.BlockSpec((rb, 128), lambda i: (i, 0)),
            ANY,
        ],
        out_specs=(
            pl.BlockSpec((rb, width), lambda i: (i, 0)),
            pl.BlockSpec((rb, 2 * inner), lambda i: (i, 0)),
            pl.BlockSpec((rb, inner), lambda i: (i, 0)),
            pl.BlockSpec((rb, 2 * inner), lambda i: (i, 0)),
            ANY,
        ),
        out_shape=(
            S((rows, width), BF),
            S((rows, 2 * inner), F32),
            S((rows, inner), BF),
            S((rows, 2 * inner), BF),
            S((n,) + out_slice.shape, BF),
        ),
        scratch_shapes=[pltpu.SemaphoreType.DMA((n,)), pltpu.SemaphoreType.DMA((n,))],
        compiler_params=pltpu.CompilerParams(collective_id=cid, has_side_effects=True, vmem_limit_bytes=BIG),
        cost_estimate=pl.CostEstimate(flops=6 * rows * width * inner, bytes_accessed=12 * rows * width, transcendentals=0),
        name="make_qkv",
    )(x, gain, w, head_gains, cos, sin, live, out_slice)


def qkv_back_kernel(dq_ref, dkv_ref, peer_ref, pre_ref, hg_ref, cos_ref, sin_ref, w_ref, dpre_ref, gg_ref, dh_ref):
    width = dq_ref.shape[1]
    rows = dq_ref.shape[0]

    @pl.when(pl.program_id(0) == 0)
    def _():
        gg_ref[...] = jnp.zeros_like(gg_ref)

    cos, sin = cos_ref[...], sin_ref[...]
    total = None
    for part in range(2):
        for p in range(width // 128):
            ls = slice(p * 128, (p + 1) * 128)
            pls = slice(part * width + p * 128, part * width + (p + 1) * 128)
            if part == 0:
                dy = dq_ref[:, ls]
            else:
                dy = dkv_ref[:, ls] + peer_ref[:, ls].astype(F32)
            dt = dy * cos - swap_halves(dy) * sin
            v = pre_ref[:, pls]
            r = lax.rsqrt(head_mean(v * v) + EPSILON)
            u = v * r
            w = dt * hg_ref[part : part + 1, ls]
            dv = r * (w - u * head_mean(w * u))
            dpre_ref[:, pls] = dv.astype(BF)
            gg_ref[part * 8 : part * 8 + 8, ls] += jnp.sum((dt * u).reshape(rows // 8, 8, 128), axis=0)
        g = nt(dpre_ref[:, part * width : (part + 1) * width], w_ref[part])
        total = g if total is None else total + g
    dpre_ref[:, 2 * width :] = (dkv_ref[:, width:] + peer_ref[:, width:].astype(F32)).astype(BF)
    total = total + nt(dpre_ref[:, 2 * width :], w_ref[2])
    dh_ref[...] = total.astype(BF)


def qkv_back(dq, dkv, peer, pre, head_gains, cos, sin, w):
    rows, inner = dq.shape
    width = w.shape[1]
    rb = min(256, rows)
    blk = lambda c: pl.BlockSpec((rb, c), lambda i: (i, 0))
    return pl.pallas_call(
        qkv_back_kernel,
        grid=(rows // rb,),
        in_specs=[
            blk(inner),
            blk(2 * inner),
            blk(2 * inner),
            blk(2 * inner),
            pl.BlockSpec((8, inner), lambda i: (0, 0)),
            blk(128),
            blk(128),
            pl.BlockSpec(w.shape, lambda i: (0, 0, 0)),
        ],
        out_specs=(blk(3 * inner), pl.BlockSpec((16, inner), lambda i: (0, 0)), blk(width)),
        out_shape=(S((rows, 3 * inner), BF), S((16, inner), F32), S((rows, width), BF)),
        compiler_params=pltpu.CompilerParams(vmem_limit_bytes=BIG),
        cost_estimate=pl.CostEstimate(flops=6 * rows * width * inner, bytes_accessed=12 * rows * width, transcendentals=0),
        name="qkv_back",
    )(dq, dkv, peer, pre, head_gains, cos, sin, w)


def middle_kernel(mixed_ref, w_ref, x_ref, live_ref, vec_ref, attn_ref, h_ref):
    total = None
    for g in range(mixed_ref.shape[0]):
        t = nn(mixed_ref[g], w_ref[g]).astype(BF).astype(F32)
        total = t if total is None else total + t
    attn_ref[...] = total
    mid = x_ref[...].astype(F32) + live_ref[:, 0:1] * vec_ref[0:1] * total
    _, u = norm_parts(mid)
    h_ref[...] = (u * vec_ref[1:2]).astype(BF)


def make_middle(mixed_all, w_all, x, live, vec):
    n, rows, inner = mixed_all.shape
    width = x.shape[1]
    rb = min(256, rows)
    blk = lambda c: pl.BlockSpec((rb, c), lambda i: (i, 0))
    return pl.pallas_call(
        middle_kernel,
        grid=(rows // rb,),
        in_specs=[
            pl.BlockSpec((n, rb, inner), lambda i: (0, i, 0)),
            pl.BlockSpec(w_all.shape, lambda i: (0, 0, 0)),
            blk(width),
            blk(128),
            pl.BlockSpec((8, width), lambda i: (0, 0)),
        ],
        out_specs=(blk(width), blk(width)),
        out_shape=(S((rows, width), F32), S((rows, width), BF)),
        compiler_params=pltpu.CompilerParams(vmem_limit_bytes=BIG),
        cost_estimate=pl.CostEstimate(flops=2 * n * rows * width * inner, bytes_accessed=14 * rows * width, transcendentals=0),
        name="make_middle",
    )(mixed_all, w_all, x, live, vec)


def attend_kernel(
    n, scale, qb, kc, q_ref, kv_ref, peer_ref, live_ref, ck_ref, cv_ref, gate_ref, mixed_ref, self_ref, cross_ref, lse_ref,
    va_ref, cva_ref, ssem, rsem,
):
    z = lax.axis_index("head")
    line_barrier(z, n)
    rows, width = q_ref.shape
    txt = ck_ref.shape[0]
    c = scale * LOG2E
    va_ref[:, 128:] = live_ref[...]
    cva_ref[:, 128:] = jnp.ones((txt, 128), BF)
    first = lax.broadcasted_iota(jnp.int32, (qb, 128), 1) < 64

    def copy(kind, o, p):
        view = mixed_ref.at[o, :, pl.ds(pl.multiple_of(p * 128, 128), 128)]
        return pltpu.make_async_remote_copy(
            src_ref=view,
            dst_ref=view,
            send_sem=ssem.at[kind, o, p],
            recv_sem=rsem.at[kind, o, p],
            device_id=to_head(z + (1 if kind == 0 else -1)),
            device_id_type=pl.DeviceIdType.MESH,
        )

    def send_own(p):
        @pl.when(z < n - 1)
        def _():
            copy(0, z, p).start()

        @pl.when(z > 0)
        def _():
            copy(1, z, p).start()

    def relay(d, p):
        @pl.when(z - d >= 0)
        def _():
            copy(0, z - d, p).wait_recv()

            @pl.when(z < n - 1)
            def _():
                copy(0, z - d, p).start()

        @pl.when(z + d < n)
        def _():
            copy(1, z + d, p).wait_recv()

            @pl.when(z > 0)
            def _():
                copy(1, z + d, p).start()

    def pair(p, _):
        lanes = pl.ds(pl.multiple_of(p * 128, 128), 128)
        vlanes = pl.ds(pl.multiple_of(width + p * 128, 128), 128)
        va_ref[:rows, :128] = kv_ref[:, vlanes]
        va_ref[rows:, :128] = peer_ref[:, vlanes]
        cva_ref[:, :128] = cv_ref[:, lanes]
        gate = gate_ref[:, lanes]

        def block(b, _):
            rs = pl.ds(pl.multiple_of(b * qb, qb), qb)
            qp = q_ref[rs, lanes]
            outs, couts = [], []
            for a in range(2):
                qm = jnp.where(first if a == 0 else jnp.logical_not(first), qp, jnp.zeros_like(qp))
                acc = None
                for side in range(2):
                    keys = kv_ref if side == 0 else peer_ref
                    for j in range(0, rows, kc):
                        s = nt(qm, keys[j : j + kc, lanes])
                        pr = jnp.exp2(s * c).astype(BF)
                        o = nn(pr, va_ref[side * rows + j : side * rows + j + kc, :])
                        acc = o if acc is None else acc + o
                outs.append(acc)
                s = nt(qm, ck_ref[:, lanes])
                couts.append(nn(jnp.exp2(s * c).astype(BF), cva_ref[...]))
            so = jnp.where(first, outs[0][:, :128], outs[1][:, :128])
            sl = jnp.where(first, outs[0][:, 128:], outs[1][:, 128:])
            co = jnp.where(first, couts[0][:, :128], couts[1][:, :128])
            cl = jnp.where(first, couts[0][:, 128:], couts[1][:, 128:])
            so = so / sl
            co = co / cl
            mixed_ref[z, rs, lanes] = (so + gate * co).astype(BF)
            self_ref[rs, lanes] = so
            cross_ref[rs, lanes] = co
            lt = jnp.log2(sl).T
            ct = jnp.log2(cl).T
            lse_ref[p, :, rs] = jnp.concatenate([lt[0:1], lt[64:65], ct[0:1], ct[64:65], lt[0:4]], axis=0)
            return 0

        lax.fori_loop(0, rows // qb, block, 0)

        @pl.when(p >= 1)
        def _():
            relay(1, p - 1)

        send_own(p)
        return 0

    pairs = width // 128
    lax.fori_loop(0, pairs, pair, 0)
    for t in range(pairs + n - 2):
        for d in range(1, n):
            if 0 <= t - (d - 1) < pairs and (d > 1 or t == pairs - 1):
                relay(d, t - (d - 1))
    for p in range(pairs):
        for o in range(n):

            @pl.when(both(z >= o, z < n - 1))
            def _(o=o, p=p):
                copy(0, o, p).wait_send()

            @pl.when(both(z <= o, z > 0))
            def _(o=o, p=p):
                copy(1, o, p).wait_send()


def attend(q, kv, peer, live, ck, cv, gate, scale, cid, qb=256, kc=1024):
    n = lax.axis_size("head")
    rows, width = q.shape
    txt = ck.shape[0]
    qb, kc = min(qb, rows), min(kc, rows)
    return pl.pallas_call(
        functools.partial(attend_kernel, n, scale, qb, kc),
        out_shape=(S((n, rows, width), BF), S((rows, width), F32), S((rows, width), F32), S((width // 128, 8, rows), F32)),
        in_specs=[VM] * 7,
        out_specs=(VM,) * 4,
        scratch_shapes=[
            pltpu.VMEM((2 * rows, 256), BF),
            pltpu.VMEM((txt, 256), BF),
            pltpu.SemaphoreType.DMA((2, n, width // 128)),
            pltpu.SemaphoreType.DMA((2, n, width // 128)),
        ],
        compiler_params=pltpu.CompilerParams(collective_id=cid, has_side_effects=True, vmem_limit_bytes=BIG),
        cost_estimate=pl.CostEstimate(flops=32 * rows * rows * width, bytes_accessed=12 * rows * width, transcendentals=0),
        name="attend",
    )(q, kv, peer, live, ck, cv, gate)


def head_sum(x):
    ind = (lax.broadcasted_iota(jnp.int32, (8, 128), 0) == lax.broadcasted_iota(jnp.int32, (8, 128), 1) // 64).astype(F32)
    return lax.dot_general(ind, x, (((1,), (1,)), ((), ())), preferred_element_type=F32, precision=HIGHEST)


def cross_back_kernel(
    scale, qb, q_ref, ck_ref, cv_ref, gate_ref, cross_ref, lse_ref, dm_ref, dq_ref, dck_ref, dcv_ref, gg_ref, ckt_ref, p_ref, d_ref
):
    rows, width = q_ref.shape
    txt = ck_ref.shape[0]
    c = scale * LOG2E
    first = lax.broadcasted_iota(jnp.int32, (qb, 128), 1) < 64

    def pair(p, _):
        lanes = pl.ds(pl.multiple_of(p * 128, 128), 128)
        ckt_ref[...] = ck_ref[:, lanes].T
        gate = gate_ref[:, lanes]
        dck_ref[:, lanes] = jnp.zeros((txt, 128), F32)
        dcv_ref[:, lanes] = jnp.zeros((txt, 128), F32)
        gg_ref[:, lanes] = jnp.zeros((8, 128), F32)

        def block(b, _):
            rs = pl.ds(pl.multiple_of(b * qb, qb), qb)
            qp = q_ref[rs, lanes]
            dmf = dm_ref[rs, lanes].astype(F32)
            dcf = (gate * dmf).astype(BF)
            cross = cross_ref[rs, lanes]
            gg_ref[:, lanes] += fold8(dmf * cross)
            delta = head_sum(dcf.astype(F32) * cross)
            z = jnp.zeros_like(qp)
            masks = (first, jnp.logical_not(first))
            qs = [jnp.where(m, qp, z) for m in masks]
            dcs = [jnp.where(m, dcf, z) for m in masks]
            lse = lse_ref[p, :, rs]
            dqt = []
            for a in range(2):
                s = nt(ck_ref[:, lanes], qs[a])
                pr = jnp.exp2(s * c - lse[2 + a : 3 + a])
                dp = nt(cv_ref[:, lanes], dcs[a])
                p_ref[:, a * qb : (a + 1) * qb] = pr.astype(BF)
                dd = (pr * (dp - delta[a : a + 1])).astype(BF)
                d_ref[:, a * qb : (a + 1) * qb] = dd
                dqt.append(nn(ckt_ref[a * 64 : (a + 1) * 64, :], dd))
            dcv_ref[:, lanes] += nn(p_ref[...], jnp.concatenate(dcs, axis=0))
            dck_ref[:, lanes] += nn(d_ref[...], jnp.concatenate(qs, axis=0))
            dq_ref[rs, lanes] = (jnp.concatenate(dqt, axis=0) * scale).T
            return 0

        lax.fori_loop(0, rows // qb, block, 0)
        dck_ref[:, lanes] = dck_ref[:, lanes] * scale
        return 0

    lax.fori_loop(0, width // 128, pair, 0)


def cross_back(q, ck, cv, gate, co, lse, dm, scale, qb=512):
    rows, width = q.shape
    txt = ck.shape[0]
    qb = min(qb, rows)
    return pl.pallas_call(
        functools.partial(cross_back_kernel, scale, qb),
        out_shape=(S((rows, width), F32), S((txt, width), F32), S((txt, width), F32), S((8, width), F32)),
        in_specs=[VM] * 7,
        out_specs=(VM,) * 4,
        scratch_shapes=[pltpu.VMEM((128, txt), BF), pltpu.VMEM((txt, 2 * qb), BF), pltpu.VMEM((txt, 2 * qb), BF)],
        compiler_params=pltpu.CompilerParams(vmem_limit_bytes=BIG),
        cost_estimate=pl.CostEstimate(flops=24 * rows * txt * width, bytes_accessed=12 * rows * width, transcendentals=0),
        name="cross_back",
    )(q, ck, cv, gate, co, lse, dm)


def attend_back_kernel(
    n,
    per,
    scale,
    qb,
    kc,
    q_ref,
    kv_ref,
    peer_ref,
    live_ref,
    self_ref,
    lse_ref,
    dm_ref,
    dqc_ref,
    part_ref,
    dq_ref,
    dkv_ref,
    dpeer_ref,
    fsum_ref,
    kt_ref,
    p_ref,
    d_ref,
    ak_ref,
    av_ref,
    rbuf,
    lbuf,
    ssem,
    rsem,
):
    line_barrier(lax.axis_index("head"), n)
    ch = Chain(n, SUBS, BACK_LAG, part_ref, fsum_ref, rbuf, lbuf, ssem, rsem)
    rows, width = q_ref.shape
    c = scale * LOG2E
    first = lax.broadcasted_iota(jnp.int32, (qb, 128), 1) < 64

    def pair(p, _):
        lanes = pl.ds(pl.multiple_of(p * 128, 128), 128)
        vlanes = pl.ds(pl.multiple_of(width + p * 128, 128), 128)
        kt_ref[:, :rows] = kv_ref[:, lanes].T
        kt_ref[:, rows:] = peer_ref[:, lanes].T
        ak_ref[...] = jnp.zeros_like(ak_ref)
        av_ref[...] = jnp.zeros_like(av_ref)

        def block(b, _):
            rs = pl.ds(pl.multiple_of(b * qb, qb), qb)
            qp = q_ref[rs, lanes]
            dm = dm_ref[rs, lanes]
            dmf = dm.astype(F32)
            delta = head_sum(dmf * self_ref[rs, lanes])
            z = jnp.zeros_like(qp)
            masks = (first, jnp.logical_not(first))
            qs = [jnp.where(m, qp, z) for m in masks]
            dms = [jnp.where(m, dm, z) for m in masks]
            qstack = jnp.concatenate(qs, axis=0)
            dstack = jnp.concatenate(dms, axis=0)
            lse = lse_ref[p, :, rs]
            dqt = [None, None]
            for side in range(2):
                src = kv_ref if side == 0 else peer_ref
                for j in range(0, rows, kc):
                    at = side * rows + j
                    for a in range(2):
                        s = nt(src[j : j + kc, lanes], qs[a])
                        pr = jnp.exp2(s * c - lse[a : a + 1])
                        dp = nt(src[j : j + kc, vlanes], dms[a])
                        p_ref[:, a * qb : (a + 1) * qb] = pr.astype(BF)
                        dd = (pr * (dp - delta[a : a + 1])).astype(BF)
                        d_ref[:, a * qb : (a + 1) * qb] = dd
                        t = nn(kt_ref[a * 64 : (a + 1) * 64, at : at + kc], dd)
                        dqt[a] = t if dqt[a] is None else dqt[a] + t
                    av_ref[at : at + kc] += nn(p_ref[...], dstack)
                    ak_ref[at : at + kc] += nn(d_ref[...], qstack)
            dq_ref[rs, lanes] = (jnp.concatenate(dqt, axis=0) * scale).T + dqc_ref[rs, lanes]
            for i in range(per):
                k = (p * (rows // qb) + b) * per + i

                @pl.when(k < ch.steps)
                def _(k=k):
                    ch.step(k)

            return 0

        lax.fori_loop(0, rows // qb, block, 0)
        live = live_ref[...].astype(F32)
        dkv_ref[:, lanes] = ak_ref[:rows] * (live[:rows] * scale)
        dkv_ref[:, vlanes] = av_ref[:rows] * live[:rows]
        dpeer_ref[:, lanes] = (ak_ref[rows:] * (live[rows:] * scale)).astype(BF)
        dpeer_ref[:, vlanes] = (av_ref[rows:] * live[rows:]).astype(BF)
        return 0

    lax.fori_loop(0, width // 128, pair, 0)
    ch.run(min(ch.steps, (width // 128) * (rows // qb) * per), ch.steps)
    ch.drain()


def attend_back(q, kv, peer, live, so, lse, dm, dqc, part, scale, cid, qb=256, kc=512, per=2):
    n = lax.axis_size("head")
    rows, width = q.shape
    qb, kc = min(qb, rows), min(kc, rows)
    return pl.pallas_call(
        functools.partial(attend_back_kernel, n, per, scale, qb, kc),
        out_shape=(
            S((rows, width), F32),
            S((rows, 2 * width), F32),
            S((rows, 2 * width), BF),
            S(part.shape, BF),
        ),
        in_specs=[VM] * 9,
        out_specs=(VM,) * 4,
        scratch_shapes=[
            pltpu.VMEM((128, 2 * rows), BF),
            pltpu.VMEM((kc, 2 * qb), BF),
            pltpu.VMEM((kc, 2 * qb), BF),
            pltpu.VMEM((2 * rows, 128), F32),
            pltpu.VMEM((2 * rows, 128), F32),
        ]
        + chain_scratch(*part.shape, SUBS),
        compiler_params=pltpu.CompilerParams(collective_id=cid, has_side_effects=True, vmem_limit_bytes=BIG),
        cost_estimate=pl.CostEstimate(flops=80 * rows * rows * width, bytes_accessed=20 * rows * width, transcendentals=0),
        name="attend_back",
    )(q, kv, peer, live, so, lse, dm, dqc, part)


def pair_swap(value):
    pairs = [(source, source ^ 1) for source in range(lax.axis_size("seq"))]
    return lax.ppermute(value, "seq", pairs)


def rope_tables(grid_rows, grid_cols, first_token, row_count, head_size):
    stride = grid_cols + 1
    tokens = first_token + jnp.arange(row_count, dtype=jnp.int32)
    valid = tokens < grid_rows * stride
    row_pos = (tokens // stride).astype(F32)
    col_pos = (tokens % stride).astype(F32)
    quarter = head_size // 4
    half = head_size // 2
    lane = jnp.arange(128, dtype=jnp.int32) % half
    frequency = ROPE_BASE ** (-(lane % quarter).astype(F32) / quarter)
    angles = jnp.where(lane[None, :] < quarter, row_pos[:, None], col_pos[:, None]) * frequency[None, :]
    sign = jnp.where(jnp.arange(128) % head_size < half, -1.0, 1.0)
    return jnp.cos(angles), jnp.sin(angles) * sign[None, :], valid


def scatter(v):
    return lax.psum_scatter(v, "seq", scatter_dimension=0, tiled=True)


def local(
    image_rows,
    condition,
    text_feats,
    grid_shape,
    text_slot,
    attn_gain,
    ffn_gain,
    mod_weight,
    mod_bias,
    qkv_weight,
    qk_gains,
    text_kv_weight,
    cross_gate,
    out_weight,
    gate_up_weight,
    down_weight,
    cotangent,
):
    row_count, model_width = image_rows.shape
    head_local, head_size = qk_gains.shape[1], qk_gains.shape[2]
    inner = head_local * head_size
    ff_local = down_weight.shape[0]
    text_local, cap_width = text_feats.shape
    head_count = lax.axis_size("head")
    seq_count = lax.axis_size("seq")
    seq_index = lax.axis_index("seq")
    head_index = lax.axis_index("head")
    image_index = seq_index // 2
    pair_half = seq_index % 2
    score_scale = head_size ** (-0.5)
    image_count = condition.shape[0]

    grid_pair = lax.dynamic_index_in_dim(grid_shape, image_index, 0, keepdims=False)
    cos, sin, valid = rope_tables(grid_pair[0], grid_pair[1], pair_half * row_count, row_count, head_size)
    keep = valid.astype(F32)[:, None]
    live_own = jnp.broadcast_to(keep, (row_count, 128))
    peer_tokens = (1 - pair_half) * row_count + jnp.arange(row_count, dtype=jnp.int32)
    keep_peer = (peer_tokens < grid_pair[0] * (grid_pair[1] + 1)).astype(F32)[:, None]
    live_all = jnp.concatenate([live_own, jnp.broadcast_to(keep_peer, (row_count, 128))], axis=0).astype(BF)

    cond_all = jax.nn.silu(condition.astype(F32)).astype(BF)
    cond_low = lax.dynamic_index_in_dim(cond_all, image_index, 0, keepdims=True)
    mod_piece = jnp.dot(cond_low, mod_weight, preferred_element_type=F32) + mod_bias
    modulation = share(jnp.broadcast_to(mod_piece, (8, model_width)), 4)[:, 0]
    one_attn = 1.0 + modulation[0]
    one_ffn = 1.0 + modulation[2]
    tanh_attn = jnp.tanh(modulation[1])
    tanh_ffn = jnp.tanh(modulation[3])

    head_gains = jnp.concatenate([qk_gains.reshape(3, inner), jnp.zeros((5, inner), F32)], axis=0)
    gate_head = jnp.tanh(cross_gate)
    gate_lanes = jnp.repeat(gate_head, head_size)[None, :]
    qkv_mats = jnp.transpose(qkv_weight, (1, 0, 2))
    same_head = (jnp.arange(inner)[:, None] // head_size == jnp.arange(inner)[None, :] // head_size).astype(F32) / head_size

    text_kv_flat = text_kv_weight.reshape(cap_width, 2 * inner)
    text_proj = jnp.dot(text_feats, text_kv_flat, preferred_element_type=F32)
    cap_pre = text_proj[:, :inner]
    cap_r = lax.rsqrt(jnp.dot(cap_pre * cap_pre, same_head, precision=HIGHEST) + EPSILON)
    cap_u = cap_pre * cap_r
    cap_kv = jnp.concatenate([cap_u * head_gains[2:3], text_proj[:, inner:]], axis=1).astype(BF)
    caps = lax.all_gather(cap_kv, "seq", axis=0, tiled=False)
    slot = lax.dynamic_index_in_dim(text_slot, image_index, 0, keepdims=False)
    cap_own = lax.dynamic_index_in_dim(caps, slot, 0, keepdims=False)
    cap_key, cap_value = cap_own[:, :inner], cap_own[:, inner:]

    slice_rows = inner // seq_count
    out_slice = lax.dynamic_slice_in_dim(out_weight, seq_index * slice_rows, slice_rows, 0)

    normed, pre, query, kv, out_slices = make_qkv(
        image_rows, (attn_gain * one_attn)[None, :], qkv_mats, head_gains, cos, sin, live_own, out_slice, 5
    )
    out_all = lax.all_gather(out_slices, "seq", axis=1, tiled=True)
    kv_peer = pair_swap(kv)
    mixed_all, self_out, cross_out, lse = attend(query, kv, kv_peer, live_all, cap_key, cap_value, gate_lanes, score_scale, 0)
    mixed = lax.dynamic_index_in_dim(mixed_all, head_index, 0, keepdims=False)
    vec = jnp.concatenate([jnp.stack([tanh_attn, ffn_gain * one_ffn, attn_gain * one_attn, tanh_ffn]), jnp.zeros((4, model_width), F32)])
    attn_out, ffn_low = make_middle(mixed_all, out_all, image_rows, live_own, vec)

    gate_up_flat = gate_up_weight.reshape(model_width, 2 * ff_local)
    attn_grad_low, ffn_rows, middle_grad_half, ffn_part, ffn_wgrad = ffn_exchange(
        ffn_low, cotangent, gate_up_flat, down_weight, image_rows, attn_out, live_own, vec, 1
    )
    ffn_wsum = scatter(ffn_wgrad)
    grad_out = cotangent.astype(F32)
    mixed_grad = nt(attn_grad_low, out_weight).astype(BF)
    dq_cross, dck, dcv, gate_rows = cross_back(query, cap_key, cap_value, gate_lanes, cross_out, lse, mixed_grad, score_scale)
    cap_grads = lax.all_gather(jnp.concatenate([dck, dcv], axis=1).astype(BF), "seq", axis=0, tiled=False)
    dq, dkv, dpeer, ffn_out = attend_back(query, kv, kv_peer, live_all, self_out, lse, mixed_grad, dq_cross, ffn_part, score_scale, 2)
    from_peer = pair_swap(dpeer)
    dq, cap_grads = lax.optimization_barrier((dq, cap_grads))

    own_image = jnp.sum(jnp.where(text_slot == seq_index, jnp.arange(image_count), 0))
    used = jnp.any(text_slot == seq_index).astype(F32)
    two = lax.dynamic_slice_in_dim(cap_grads, 2 * own_image, 2, 0).astype(F32)
    cap_grad = (two[0] + two[1]) * used
    cap_dy, cap_dv = cap_grad[:, :inner], cap_grad[:, inner:]
    cap_w = cap_dy * head_gains[2:3]
    cap_pre_grad = cap_r * (cap_w - cap_u * jnp.dot(cap_w * cap_u, same_head, precision=HIGHEST))
    cap_gain = jnp.sum(cap_dy * cap_u, axis=0)
    text_low = jnp.concatenate([cap_pre_grad, cap_dv], axis=1).astype(BF)
    text_weight_grad = tn(text_feats, text_low).astype(BF)
    text_part = nt(text_low, text_kv_flat).astype(BF)
    dq, dkv, text_part, text_weight_grad, ffn_wsum = lax.optimization_barrier(
        (dq, dkv, text_part, text_weight_grad, ffn_wsum)
    )
    text_sum = lax.psum_scatter(text_part, "head", scatter_dimension=1, tiled=True)
    text_weight_sum = scatter(text_weight_grad)

    ffn_out = ffn_out.astype(F32)
    output = (image_rows.astype(F32) + keep * tanh_attn * attn_out + keep * tanh_ffn * ffn_out).astype(BF)
    gate_ffn_grad = jnp.sum(grad_out * keep * ffn_out, axis=0) * (1.0 - tanh_ffn * tanh_ffn)
    grad_pre, gain_rows, attn_in_part = qkv_back(dq, dkv, from_peer, pre, head_gains, cos, sin, qkv_mats)
    attn_wgrad = wgrad_pair(normed, grad_pre, attn_grad_low, mixed)
    attn_in_part, attn_wgrad, text_sum = lax.optimization_barrier((attn_in_part, attn_wgrad, text_sum))
    attn_wsum = scatter(attn_wgrad)
    text_grad = text_sum.astype(F32)
    rows_grad, row_sums = chain_rows(attn_in_part, image_rows, middle_grad_half, vec[2:], ffn_rows, 3)
    ffn_sum, attn_sum = row_sums[0], row_sums[2]
    gate_attn_grad = row_sums[1] * (1.0 - tanh_attn * tanh_attn)

    mod_grad = jnp.stack([attn_sum * attn_gain, gate_attn_grad, ffn_sum * ffn_gain, gate_ffn_grad])
    own_mod = lax.dynamic_index_in_dim(mod_grad, head_index, 0, keepdims=False)
    gain_grad = jnp.concatenate([gain_rows[0:8].sum(0), gain_rows[8:16].sum(0), cap_gain])
    gate_grad_head = gate_rows.sum(0)
    small = jnp.concatenate([attn_sum * one_attn, ffn_sum * one_ffn, own_mod, gain_grad, gate_grad_head])
    smalls = lax.all_gather(small, "seq", axis=0, tiled=False)
    total = jnp.sum(smalls, axis=0)
    d = model_width
    dl = d // seq_count
    attn_gain_sum = lax.dynamic_slice_in_dim(total[:d], seq_index * dl, dl)
    ffn_gain_sum = lax.dynamic_slice_in_dim(total[d : 2 * d], seq_index * dl, dl)
    mod_bias_sum = lax.dynamic_slice_in_dim(total[2 * d : 3 * d], seq_index * dl, dl)[None, :]
    qk_all = total[3 * d : 3 * d + 3 * inner].reshape(3, head_local, seq_count, head_size // seq_count)
    qk_gain_sum = lax.dynamic_index_in_dim(qk_all, seq_index, 2, keepdims=False)
    gate_sum = total[3 * d + 3 * inner :].reshape(head_local, head_size).sum(-1) * (1.0 - gate_head * gate_head)
    cond_cols = condition.shape[1] // seq_count
    cond_part = lax.dynamic_slice_in_dim(cond_all, seq_index * cond_cols, cond_cols, 1).astype(F32)
    image_mods = smalls[:, 2 * d : 3 * d].reshape(image_count, 2, d).sum(1)
    mod_weight_sum = lax.dot_general(cond_part, image_mods, (((0,), (0,)), ((), ())), precision=HIGHEST)

    split = 2 * ff_local
    ffn_wsum, attn_wsum = ffn_wsum.astype(F32), attn_wsum.astype(F32)
    gate_up_sum = ffn_wsum[:, :split].reshape(-1, 2, ff_local)
    down_sum = ffn_wsum[:, split:].T
    qkv_sum = attn_wsum[:, : 3 * inner].reshape(-1, 3, inner)
    out_sum = attn_wsum[:, 3 * inner :].T
    text_weight_sum = text_weight_sum.astype(F32).reshape(-1, 2, inner)
    return (
        output,
        rows_grad,
        text_grad,
        attn_gain_sum,
        ffn_gain_sum,
        mod_weight_sum,
        mod_bias_sum,
        qkv_sum,
        qk_gain_sum,
        text_weight_sum,
        gate_sum,
        out_sum,
        gate_up_sum,
        down_sum,
    )


def solution(mesh):
    return jax.shard_map(
        local,
        mesh=mesh,
        in_specs=(
            P("seq", None),
            P(),
            P("seq", None),
            P(),
            P(),
            P(),
            P(),
            P(None, "head"),
            P("head", None),
            P(None, None, "head"),
            P(None, "head", None),
            P(None, None, "head"),
            P("head"),
            P("head", None),
            P(None, None, "head"),
            P("head", None),
            P("seq", None),
        ),
        out_specs=(
            P("seq", None),
            P("seq", None),
            P("seq", "head"),
            P("seq"),
            P("seq"),
            P("seq", "head"),
            P("head", "seq"),
            P("seq", None, "head"),
            P(None, "head", "seq"),
            P("seq", None, "head"),
            P("head"),
            P("head", "seq"),
            P("seq", None, "head"),
            P("head", "seq"),
        ),
        check_vma=False,
    )
```

```python
import functools

import jax
import jax.numpy as jnp
from jax import lax
from jax.experimental import pallas as pl
from jax.experimental.pallas import tpu as pltpu
from jax.sharding import PartitionSpec as P

TXT = 256
EPSILON = 1e-06
ROPE_BASE = 10000.0
LOG2E = 1.4426950408889634
F32 = jnp.float32
BF = jnp.bfloat16
VMEM_BYTES = 67043328
HIGHEST = lax.Precision.HIGHEST
VM = pl.BlockSpec(memory_space=pltpu.VMEM)
S = jax.ShapeDtypeStruct


def nt(a, b):
    return lax.dot_general(a, b, (((1,), (1,)), ((), ())), preferred_element_type=F32)


def nn(a, b):
    return lax.dot_general(a, b, (((1,), (0,)), ((), ())), preferred_element_type=F32)


def tn(a, b):
    return lax.dot_general(a, b, (((0,), (0,)), ((), ())), preferred_element_type=F32)


def head_mean(x):
    rows = lax.broadcasted_iota(jnp.int32, (128, 128), 0) // 64
    cols = lax.broadcasted_iota(jnp.int32, (128, 128), 1) // 64
    same = jnp.where(rows == cols, 1.0 / 64, 0.0).astype(BF)
    high = x.astype(BF)
    rest = (x - high.astype(F32)).astype(BF)
    return nn(high, same) + nn(rest, same)


def swap_halves(x):
    lane = lax.broadcasted_iota(jnp.int32, x.shape, 1) % 64
    return jnp.where(lane < 32, pltpu.roll(x, 96, 1), pltpu.roll(x, 32, 1))


def to_head(z):
    return {"head": z}


def both(a, b):
    return jnp.logical_and(a, b)


def line_barrier(z, n):
    bar = pltpu.get_barrier_semaphore()
    for ok, other in ((z > 0, z - 1), (z < n - 1, z + 1)):

        @pl.when(ok)
        def _(other=other):
            pl.semaphore_signal(bar, inc=1, device_id=to_head(other), device_id_type=pl.DeviceIdType.MESH)

    end = jnp.logical_or(z == 0, z == n - 1)

    @pl.when(end)
    def _():
        pl.semaphore_wait(bar, 1)

    @pl.when(jnp.logical_not(end))
    def _():
        pl.semaphore_wait(bar, 2)


def head_barrier(z, n):
    bar = pltpu.get_barrier_semaphore()
    for i in range(1, n):
        pl.semaphore_signal(bar, inc=1, device_id=to_head(lax.rem(z + i, n)), device_id_type=pl.DeviceIdType.MESH)
    pl.semaphore_wait(bar, n - 1)


class Chain:
    def __init__(self, n, subs, lag, part_ref, out_ref, rbuf, lbuf, ssem, rsem, finalize=None):
        self.z, self.n, self.subs, self.lag = lax.axis_index("head"), n, subs, lag
        self.part, self.out, self.rbuf, self.lbuf, self.ssem, self.rsem = part_ref, out_ref, rbuf, lbuf, ssem, rsem
        self.half = part_ref.shape[0] // 2
        self.unit = self.half // subs
        self.finalize = finalize
        self.steps = subs + 2 * lag * (n - 1)

    def near(self, s):
        return pl.ds(pl.multiple_of(s * self.unit, self.unit), self.unit)

    def far(self, s):
        return pl.ds(pl.multiple_of(self.half + s * self.unit, self.unit), self.unit)

    def copy(self, kind, s, first=False):
        src, at, to = (
            (self.rbuf, self.near(s), self.near(s)),
            (self.lbuf, self.near(s), self.near(s)),
            (self.out, self.near(s), self.near(s)),
            (self.out, self.far(s), self.far(s)),
        )[kind]
        dst = src
        if first:
            src, at = self.part, (self.far(s) if kind == 0 else self.near(s))
        return pltpu.make_async_remote_copy(
            src_ref=src.at[at],
            dst_ref=dst.at[to],
            send_sem=self.ssem.at[kind, s],
            recv_sem=self.rsem.at[kind, s],
            device_id=to_head(self.z + (1 if kind % 2 == 0 else -1)),
            device_id_type=pl.DeviceIdType.MESH,
        )

    def step(self, k):
        z, lag, last = self.z, self.lag, self.n - 1

        def inside(s):
            return both(s >= 0, s < self.subs)

        for kind, buf in ((0, self.rbuf), (1, self.lbuf)):
            hops = z if kind == 0 else last - z
            s = k - lag * hops

            @pl.when(both(inside(s), hops == 0))
            def _(kind=kind, s=s):
                self.copy(kind, s, True).start()

            @pl.when(both(inside(s), both(hops > 0, hops < last)))
            def _(kind=kind, s=s, buf=buf):
                self.copy(kind, s).wait_recv()
                at = self.near(s)
                own = self.part[self.far(s) if kind == 0 else at]
                buf[at] = (buf[at].astype(F32) + own.astype(F32)).astype(BF)
                self.copy(kind, s).start()

            @pl.when(both(inside(s), hops == last))
            def _(kind=kind, s=s, buf=buf):
                self.copy(kind, s).wait_recv()
                to = self.far(s) if kind == 0 else self.near(s)
                total = buf[self.near(s)].astype(F32) + self.part[to].astype(F32)
                if self.finalize is not None:
                    total = self.finalize(self.near(s), to, total)
                self.out[to] = total.astype(BF)
                self.copy(3 - kind, s).start()

        for kind in (2, 3):
            hops = z if kind == 2 else last - z
            s = k - lag * (last + hops)

            @pl.when(both(inside(s), hops > 0))
            def _(kind=kind, s=s, hops=hops):
                self.copy(kind, s).wait_recv()

                @pl.when(hops < last)
                def _():
                    self.copy(kind, s).start()

    def run(self, first, last):
        def one(k, c):
            self.step(k)
            return c

        lax.fori_loop(first, last, one, 0)

    def drain(self):
        def one(s, c):
            for kind in range(4):

                @pl.when(self.z < self.n - 1 if kind % 2 == 0 else self.z > 0)
                def _(kind=kind):
                    self.copy(kind, s).wait_send()

            return c

        lax.fori_loop(0, self.subs, one, 0)


def chain_scratch(rows, width, subs):
    return [
        pltpu.VMEM((rows // 2, width), BF),
        pltpu.VMEM((rows // 2, width), BF),
        pltpu.SemaphoreType.DMA((4, subs)),
        pltpu.SemaphoreType.DMA((4, subs)),
    ]


SUBS, LAG, BACK_LAG = 16, 2, 2
ANY = pl.BlockSpec(memory_space=pl.ANY)
BIG = VMEM_BYTES - (1 << 20)


def norm_parts(values):
    r = lax.rsqrt(jnp.mean(values * values, axis=-1, keepdims=True) + EPSILON)
    return r, values * r


def fold8(x):
    return jnp.sum(x.reshape(x.shape[0] // 8, 8, x.shape[1]), axis=0)


def half_loads(z, n, half, whole, halves, sem):
    at = pl.ds(pl.multiple_of(jnp.where(z == 0, 0, half), half), half)
    pairs = [(ref.at[at], to) for ref, to in whole] + halves
    return [pltpu.make_async_copy(ref, to, sem.at[i]) for i, (ref, to) in enumerate(pairs)]


def run_with_loads(ch, end, loads, after_sums):
    @pl.when(end)
    def _():
        for c in loads:
            c.start()

    need = ch.lag * (ch.n - 1)
    ch.run(0, need)

    @pl.when(end)
    def _():
        for c in loads:
            c.wait()

    ch.run(need, need + ch.subs)
    after_sums()
    ch.run(need + ch.subs, ch.steps)


def ffn_kernel(
    n, subs, lag, blocks, tile,
    h_any, g_any, wgu_any, wd_any, x_any, attn_any, live_ref, vec_ref,
    out_ref, sum_ref, dmid_any, fpart_any, wg_any,
    rbuf, lbuf, ssem, rsem, hv, gv, wgu, wd, xv, av, part_ref, dgu, hid, dffn, fpart, dmid, wbuf, csem, osem, tsem,
):
    z = lax.axis_index("head")
    rows, width = hv.shape
    ff = wd.shape[0]
    half = rows // 2
    rb = half // blocks
    end = jnp.logical_or(z == 0, z == n - 1)
    loads = [pltpu.make_async_copy(a, b, csem.at[i]) for i, (a, b) in enumerate(((h_any, hv), (wgu_any, wgu), (g_any, gv), (wd_any, wd)))]
    for c in loads:
        c.start()
    mine = pl.ds(pl.multiple_of(jnp.where(z == 0, 0, half), half), half)
    end_loads = [pltpu.make_async_copy(a.at[mine], b, csem.at[4 + i]) for i, (a, b) in enumerate(((x_any, xv), (attn_any, av)))]

    @pl.when(end)
    def _():
        for c in end_loads:
            c.start()

    sum_ref[...] = jnp.zeros_like(sum_ref)
    line_barrier(z, n)
    tanh_attn, gain, tanh_ffn = vec_ref[0:1], vec_ref[1:2], vec_ref[3:4]

    def finalize(at, to, dh):
        attn, live = av[at], live_ref[to, 0:1]
        mid = xv[at].astype(F32) + live * tanh_attn * attn
        r, u = norm_parts(mid)
        w = dh * gain
        grad = gv[to].astype(F32) + r * (w - u * jnp.mean(w * u, axis=-1, keepdims=True))
        dmid[at] = grad
        masked = grad * live
        sum_ref[0:8] += fold8(dh * u)
        sum_ref[8:16] += fold8(masked * attn)
        return masked * tanh_attn

    ch = Chain(n, subs, lag, part_ref, out_ref, rbuf, lbuf, ssem, rsem, finalize)

    def step(k):
        @pl.when(jnp.logical_and(end, k == lag * (n - 1)))
        def _():
            for c in end_loads:
                c.wait()

        ch.step(k)

    per = subs // blocks

    def block(t, c):
        near = pl.ds(pl.multiple_of(t * rb, rb), rb)
        far = pl.ds(pl.multiple_of(half + t * rb, rb), rb)

        def put(ref, v):
            ref[near] = v[:rb]
            ref[far] = v[rb:]

        @pl.when(t == 0)
        def _():
            loads[0].wait()
            loads[1].wait()

        gu = nn(jnp.concatenate([hv[near], hv[far]], axis=0), wgu[...])
        gate, up = gu[:, :ff], gu[:, ff:]
        sig = 1.0 / (1.0 + jnp.exp(-gate))
        act = gate * sig
        hidden = (act * up).astype(BF)
        put(hid, hidden)

        @pl.when(t == 0)
        def _():
            loads[2].wait()
            loads[3].wait()

        grad = jnp.concatenate([gv[near].astype(F32) * live_ref[near, 0:1], gv[far].astype(F32) * live_ref[far, 0:1]], axis=0)
        low = (grad * tanh_ffn).astype(BF)
        put(dffn, low)
        dhid = nt(low, wd[...])
        both_grads = jnp.concatenate(
            [(dhid * up * (sig + act * (1.0 - sig))).astype(BF), (dhid * act).astype(BF)], axis=1
        )
        put(dgu, both_grads)
        put(part_ref, nt(both_grads, wgu[...]).astype(BF))

        def some(i, c):
            step(t * per + i)
            return c

        lax.fori_loop(0, per, some, 0)
        put(fpart, nn(hidden, wd[...]).astype(BF))
        return c

    lax.fori_loop(0, blocks, block, 0)
    fcopy = pltpu.make_async_copy(fpart, fpart_any, osem.at[0])
    fcopy.start()

    tiles = width // tile
    every = max(1, (ch.steps - subs) // tiles)

    def tile_copy(j):
        return pltpu.make_async_copy(wbuf.at[lax.rem(j, 2)], wg_any.at[pl.ds(pl.multiple_of(j * tile, tile), tile)], tsem.at[j])

    def weights(j, c):
        def some(i, c):
            step(subs + j * every + i)
            return c

        lax.fori_loop(0, every, some, 0)

        @pl.when(j >= 2)
        def _():
            tile_copy(j - 2).wait()

        cols = pl.ds(pl.multiple_of(j * tile, tile), tile)
        slot = lax.rem(j, 2)
        wbuf[slot, :, : 2 * ff] = tn(hv[:, cols], dgu[...]).astype(BF)
        wbuf[slot, :, 2 * ff :] = tn(dffn[:, cols], hid[...]).astype(BF)
        tile_copy(j).start()
        return c

    lax.fori_loop(0, tiles, weights, 0)

    def rest(k, c):
        step(k)
        return c

    lax.fori_loop(subs + tiles * every, ch.steps, rest, 0)
    dcopy = pltpu.make_async_copy(dmid, dmid_any, osem.at[1])

    @pl.when(end)
    def _():
        dcopy.start()

    for j in range(max(0, tiles - 2), tiles):
        tile_copy(j).wait()
    fcopy.wait()
    ch.drain()

    @pl.when(end)
    def _():
        dcopy.wait()


def ffn_exchange(h, g, wgu, wd, x, attn, live, vec, cid, subs=16, lag=4, blocks=4, tile=256):
    n = lax.axis_size("head")
    rows, width = h.shape
    ff = wd.shape[0]
    half = rows // 2
    vm = pltpu.VMEM
    return pl.pallas_call(
        functools.partial(ffn_kernel, n, subs, lag, blocks, tile),
        out_shape=(
            S((rows, width), BF),
            S((16, width), F32),
            S((half, width), F32),
            S((rows, width), BF),
            S((width, 3 * ff), BF),
        ),
        in_specs=[ANY] * 6 + [VM] * 2,
        out_specs=(VM, VM, ANY, ANY, ANY),
        scratch_shapes=chain_scratch(rows, width, subs)
        + [
            vm((rows, width), BF),
            vm((rows, width), BF),
            vm((width, 2 * ff), BF),
            vm((ff, width), BF),
            vm((half, width), BF),
            vm((half, width), F32),
            vm((rows, width), BF),
            vm((rows, 2 * ff), BF),
            vm((rows, ff), BF),
            vm((rows, width), BF),
            vm((rows, width), BF),
            vm((half, width), F32),
            vm((2, tile, 3 * ff), BF),
            pltpu.SemaphoreType.DMA((6,)),
            pltpu.SemaphoreType.DMA((2,)),
            pltpu.SemaphoreType.DMA((width // tile,)),
        ],
        compiler_params=pltpu.CompilerParams(collective_id=cid, has_side_effects=True, vmem_limit_bytes=BIG),
        cost_estimate=pl.CostEstimate(flops=100_000_000_000, bytes_accessed=30 * rows * width, transcendentals=0),
        name="ffn_exchange",
    )(h, g, wgu, wd, x, attn, live, vec)


def chain_rows_kernel(
    n, part_ref, x_ref, dmid_ref, gain_ref, sum_ref, out_ref, tot_ref, rbuf, lbuf, ssem, rsem, xv, dv, csem, acc, ends, esem, fsem
):
    z = lax.axis_index("head")
    line_barrier(z, n)
    acc[...] = jnp.zeros_like(acc)
    gain = gain_ref[0:1]

    def finalize(at, to, dh):
        r, u = norm_parts(xv[at].astype(F32))
        w = dh * gain
        acc[...] += fold8(dh * u)
        return dv[at] + r * (w - u * jnp.mean(w * u, axis=-1, keepdims=True))

    ch = Chain(n, SUBS, LAG, part_ref, out_ref, rbuf, lbuf, ssem, rsem, finalize)
    loads = half_loads(z, n, ch.half, [(x_ref, xv)], [(dmid_ref, dv)], csem)
    width = acc.shape[1]

    def copy(e):
        return pltpu.make_async_remote_copy(
            src_ref=ends.at[e],
            dst_ref=ends.at[e],
            send_sem=esem.at[e],
            recv_sem=fsem.at[e],
            device_id=to_head(z + (1 if e == 0 else -1)),
            device_id_type=pl.DeviceIdType.MESH,
        )

    def send_sums():
        rows = [sum_ref[0:8], sum_ref[8:16], acc[...]]
        mine = jnp.concatenate([jnp.sum(r, axis=0, keepdims=True) for r in rows] + [jnp.zeros((5, width), F32)], axis=0)
        for e, source in ((0, 0), (1, n - 1)):

            @pl.when(z == source)
            def _(e=e):
                ends[e] = mine
                copy(e).start()

    run_with_loads(ch, jnp.logical_or(z == 0, z == n - 1), loads, send_sums)

    for e, source, sink in ((0, 0, n - 1), (1, n - 1, 0)):

        @pl.when(z != source)
        def _(e=e, sink=sink):
            copy(e).wait_recv()

            @pl.when(z != sink)
            def _():
                copy(e).start()

    tot_ref[...] = ends[0] + ends[1]
    for e, sink in ((0, n - 1), (1, 0)):

        @pl.when(z != sink)
        def _(e=e):
            copy(e).wait_send()

    ch.drain()


def chain_rows(part, x, dmid, gain, sums, cid):
    n = lax.axis_size("head")
    rows, width = part.shape
    half = rows // 2
    return pl.pallas_call(
        functools.partial(chain_rows_kernel, n),
        out_shape=(S((rows, width), BF), S((8, width), F32)),
        in_specs=[VM, ANY, ANY, VM, VM],
        out_specs=(VM,) * 2,
        scratch_shapes=chain_scratch(rows, width, SUBS)
        + [
            pltpu.VMEM((half, width), BF),
            pltpu.VMEM((half, width), F32),
            pltpu.SemaphoreType.DMA((2,)),
            pltpu.VMEM((8, width), F32),
            pltpu.VMEM((2, 8, width), F32),
            pltpu.SemaphoreType.DMA((2,)),
            pltpu.SemaphoreType.DMA((2,)),
        ],
        compiler_params=pltpu.CompilerParams(collective_id=cid, has_side_effects=True, vmem_limit_bytes=BIG),
        cost_estimate=pl.CostEstimate(flops=80_000_000_000, bytes_accessed=20 * rows * width, transcendentals=0),
        name="chain_rows",
    )(part, x, dmid, gain, sums)


def share_kernel(n, piece_ref, all_ref, ssem, rsem):
    z = lax.axis_index("head")
    head_barrier(z, n)

    def copy(i):
        return pltpu.make_async_remote_copy(
            src_ref=piece_ref,
            dst_ref=all_ref.at[z],
            send_sem=ssem.at[i],
            recv_sem=rsem.at[i],
            device_id=to_head(lax.rem(z + i, n)),
            device_id_type=pl.DeviceIdType.MESH,
        )

    for i in range(1, n):
        copy(i).start()
    all_ref[z] = piece_ref[...]
    for i in range(1, n):
        copy(i).wait()


def share(piece, cid):
    n = lax.axis_size("head")
    return pl.pallas_call(
        functools.partial(share_kernel, n),
        out_shape=S((n,) + piece.shape, piece.dtype),
        in_specs=[VM],
        out_specs=VM,
        scratch_shapes=[pltpu.SemaphoreType.DMA((n,)), pltpu.SemaphoreType.DMA((n,))],
        compiler_params=pltpu.CompilerParams(collective_id=cid, has_side_effects=True, vmem_limit_bytes=BIG),
        name="share",
    )(piece)


def wgrad_kernel(a_ref, b_ref, c_ref, d_ref, o_ref):
    nb = b_ref.shape[1]
    o_ref[:, :nb] = tn(a_ref[...], b_ref[...]).astype(BF)
    o_ref[:, nb:] = tn(c_ref[...], d_ref[...]).astype(BF)


def wgrad_pair(a, b, c, d):
    rows, width = a.shape
    cols = b.shape[1] + d.shape[1]
    wb = min(256, width)
    return pl.pallas_call(
        wgrad_kernel,
        grid=(width // wb,),
        in_specs=[
            pl.BlockSpec((rows, wb), lambda i: (0, i)),
            pl.BlockSpec(b.shape, lambda i: (0, 0)),
            pl.BlockSpec((rows, wb), lambda i: (0, i)),
            pl.BlockSpec(d.shape, lambda i: (0, 0)),
        ],
        out_specs=pl.BlockSpec((wb, cols), lambda i: (i, 0)),
        out_shape=S((width, cols), BF),
        compiler_params=pltpu.CompilerParams(vmem_limit_bytes=BIG),
        cost_estimate=pl.CostEstimate(flops=2 * rows * width * cols, bytes_accessed=2 * width * cols, transcendentals=0),
        name="wgrad_pair",
    )(a, b, c, d)


def qkv_kernel(
    n, x_ref, gain_ref, w_ref, hg_ref, cos_ref, sin_ref, live_ref, slice_ref, h_ref, pre_ref, q_ref, kv_ref, all_ref, ssem, rsem
):
    z = lax.axis_index("head")

    def copy(i):
        return pltpu.make_async_remote_copy(
            src_ref=slice_ref,
            dst_ref=all_ref.at[z],
            send_sem=ssem.at[i],
            recv_sem=rsem.at[i],
            device_id=to_head(lax.rem(z + i, n)),
            device_id_type=pl.DeviceIdType.MESH,
        )

    own = pltpu.make_async_copy(slice_ref, all_ref.at[z], ssem.at[0])

    @pl.when(pl.program_id(0) == 0)
    def _():
        head_barrier(z, n)
        own.start()
        for i in range(1, n):
            copy(i).start()

    x = x_ref[...].astype(F32)
    h = (x * lax.rsqrt(jnp.mean(x * x, axis=-1, keepdims=True) + EPSILON) * gain_ref[...]).astype(BF)
    h_ref[...] = h
    width = w_ref.shape[2]
    cos, sin, live = cos_ref[...], sin_ref[...], live_ref[...]
    for part in range(2):
        pre = nn(h, w_ref[part])
        pre_ref[:, part * width : (part + 1) * width] = pre
        for p in range(width // 128):
            v = pre[:, p * 128 : (p + 1) * 128]
            r = lax.rsqrt(head_mean(v * v) + EPSILON)
            t = v * r * hg_ref[part : part + 1, p * 128 : (p + 1) * 128]
            y = t * cos + swap_halves(t) * sin
            if part == 0:
                q_ref[:, p * 128 : (p + 1) * 128] = y.astype(BF)
            else:
                kv_ref[:, p * 128 : (p + 1) * 128] = (y * live).astype(BF)
    val = nn(h, w_ref[2])
    for p in range(width // 128):
        kv_ref[:, width + p * 128 : width + (p + 1) * 128] = (val[:, p * 128 : (p + 1) * 128] * live).astype(BF)

    @pl.when(pl.program_id(0) == pl.num_programs(0) - 1)
    def _():
        own.wait()
        for i in range(1, n):
            copy(i).wait()


def make_qkv(x, gain, w, head_gains, cos, sin, live, out_slice, cid):
    n = lax.axis_size("head")
    rows, width = x.shape
    inner = w.shape[2]
    rb = min(256, rows)
    return pl.pallas_call(
        functools.partial(qkv_kernel, n),
        grid=(rows // rb,),
        in_specs=[
            pl.BlockSpec((rb, width), lambda i: (i, 0)),
            pl.BlockSpec((1, width), lambda i: (0, 0)),
            pl.BlockSpec(w.shape, lambda i: (0, 0, 0)),
            pl.BlockSpec((8, inner), lambda i: (0, 0)),
            pl.BlockSpec((rb, 128), lambda i: (i, 0)),
            pl.BlockSpec((rb, 128), lambda i: (i, 0)),
            pl.BlockSpec((rb, 128), lambda i: (i, 0)),
            ANY,
        ],
        out_specs=(
            pl.BlockSpec((rb, width), lambda i: (i, 0)),
            pl.BlockSpec((rb, 2 * inner), lambda i: (i, 0)),
            pl.BlockSpec((rb, inner), lambda i: (i, 0)),
            pl.BlockSpec((rb, 2 * inner), lambda i: (i, 0)),
            ANY,
        ),
        out_shape=(
            S((rows, width), BF),
            S((rows, 2 * inner), F32),
            S((rows, inner), BF),
            S((rows, 2 * inner), BF),
            S((n,) + out_slice.shape, BF),
        ),
        scratch_shapes=[pltpu.SemaphoreType.DMA((n,)), pltpu.SemaphoreType.DMA((n,))],
        compiler_params=pltpu.CompilerParams(collective_id=cid, has_side_effects=True, vmem_limit_bytes=BIG),
        cost_estimate=pl.CostEstimate(flops=6 * rows * width * inner, bytes_accessed=12 * rows * width, transcendentals=0),
        name="make_qkv",
    )(x, gain, w, head_gains, cos, sin, live, out_slice)


def qkv_back_kernel(dq_ref, dkv_ref, peer_ref, pre_ref, hg_ref, cos_ref, sin_ref, w_ref, dpre_ref, gg_ref, dh_ref):
    width = dq_ref.shape[1]
    rows = dq_ref.shape[0]

    @pl.when(pl.program_id(0) == 0)
    def _():
        gg_ref[...] = jnp.zeros_like(gg_ref)

    cos, sin = cos_ref[...], sin_ref[...]
    total = None
    for part in range(2):
        for p in range(width // 128):
            ls = slice(p * 128, (p + 1) * 128)
            pls = slice(part * width + p * 128, part * width + (p + 1) * 128)
            if part == 0:
                dy = dq_ref[:, ls]
            else:
                dy = dkv_ref[:, ls] + peer_ref[:, ls].astype(F32)
            dt = dy * cos - swap_halves(dy) * sin
            v = pre_ref[:, pls]
            r = lax.rsqrt(head_mean(v * v) + EPSILON)
            u = v * r
            w = dt * hg_ref[part : part + 1, ls]
            dv = r * (w - u * head_mean(w * u))
            dpre_ref[:, pls] = dv.astype(BF)
            gg_ref[part * 8 : part * 8 + 8, ls] += jnp.sum((dt * u).reshape(rows // 8, 8, 128), axis=0)
        g = nt(dpre_ref[:, part * width : (part + 1) * width], w_ref[part])
        total = g if total is None else total + g
    dpre_ref[:, 2 * width :] = (dkv_ref[:, width:] + peer_ref[:, width:].astype(F32)).astype(BF)
    total = total + nt(dpre_ref[:, 2 * width :], w_ref[2])
    dh_ref[...] = total.astype(BF)


def qkv_back(dq, dkv, peer, pre, head_gains, cos, sin, w):
    rows, inner = dq.shape
    width = w.shape[1]
    rb = min(256, rows)
    blk = lambda c: pl.BlockSpec((rb, c), lambda i: (i, 0))
    return pl.pallas_call(
        qkv_back_kernel,
        grid=(rows // rb,),
        in_specs=[
            blk(inner),
            blk(2 * inner),
            blk(2 * inner),
            blk(2 * inner),
            pl.BlockSpec((8, inner), lambda i: (0, 0)),
            blk(128),
            blk(128),
            pl.BlockSpec(w.shape, lambda i: (0, 0, 0)),
        ],
        out_specs=(blk(3 * inner), pl.BlockSpec((16, inner), lambda i: (0, 0)), blk(width)),
        out_shape=(S((rows, 3 * inner), BF), S((16, inner), F32), S((rows, width), BF)),
        compiler_params=pltpu.CompilerParams(vmem_limit_bytes=BIG),
        cost_estimate=pl.CostEstimate(flops=6 * rows * width * inner, bytes_accessed=12 * rows * width, transcendentals=0),
        name="qkv_back",
    )(dq, dkv, peer, pre, head_gains, cos, sin, w)


def middle_kernel(mixed_ref, w_ref, x_ref, live_ref, vec_ref, attn_ref, h_ref):
    total = None
    for g in range(mixed_ref.shape[0]):
        t = nn(mixed_ref[g], w_ref[g]).astype(BF).astype(F32)
        total = t if total is None else total + t
    attn_ref[...] = total
    mid = x_ref[...].astype(F32) + live_ref[:, 0:1] * vec_ref[0:1] * total
    _, u = norm_parts(mid)
    h_ref[...] = (u * vec_ref[1:2]).astype(BF)


def make_middle(mixed_all, w_all, x, live, vec):
    n, rows, inner = mixed_all.shape
    width = x.shape[1]
    rb = min(256, rows)
    blk = lambda c: pl.BlockSpec((rb, c), lambda i: (i, 0))
    return pl.pallas_call(
        middle_kernel,
        grid=(rows // rb,),
        in_specs=[
            pl.BlockSpec((n, rb, inner), lambda i: (0, i, 0)),
            pl.BlockSpec(w_all.shape, lambda i: (0, 0, 0)),
            blk(width),
            blk(128),
            pl.BlockSpec((8, width), lambda i: (0, 0)),
        ],
        out_specs=(blk(width), blk(width)),
        out_shape=(S((rows, width), F32), S((rows, width), BF)),
        compiler_params=pltpu.CompilerParams(vmem_limit_bytes=BIG),
        cost_estimate=pl.CostEstimate(flops=2 * n * rows * width * inner, bytes_accessed=14 * rows * width, transcendentals=0),
        name="make_middle",
    )(mixed_all, w_all, x, live, vec)


def attend_kernel(
    n, scale, qb, kc, q_ref, kv_ref, peer_ref, live_ref, ck_ref, cv_ref, gate_ref, mixed_ref, self_ref, cross_ref, lse_ref,
    va_ref, cva_ref, ssem, rsem,
):
    z = lax.axis_index("head")
    line_barrier(z, n)
    rows, width = q_ref.shape
    txt = ck_ref.shape[0]
    c = scale * LOG2E
    va_ref[:, 128:] = live_ref[...]
    cva_ref[:, 128:] = jnp.ones((txt, 128), BF)
    first = lax.broadcasted_iota(jnp.int32, (qb, 128), 1) < 64

    blocks = rows // qb
    units = width // 128 * blocks

    def copy(kind, o, u):
        at = pl.ds(pl.multiple_of(lax.rem(u, blocks) * qb, qb), qb)
        view = mixed_ref.at[o, at, pl.ds(pl.multiple_of(lax.div(u, blocks) * 128, 128), 128)]
        return pltpu.make_async_remote_copy(
            src_ref=view,
            dst_ref=view,
            send_sem=ssem.at[kind, o, u],
            recv_sem=rsem.at[kind, o, u],
            device_id=to_head(z + (1 if kind == 0 else -1)),
            device_id_type=pl.DeviceIdType.MESH,
        )

    def send_own(u):
        @pl.when(z < n - 1)
        def _():
            copy(0, z, u).start()

        @pl.when(z > 0)
        def _():
            copy(1, z, u).start()

    def relay(d, u):
        @pl.when(z - d >= 0)
        def _():
            copy(0, z - d, u).wait_recv()

            @pl.when(z < n - 1)
            def _():
                copy(0, z - d, u).start()

        @pl.when(z + d < n)
        def _():
            copy(1, z + d, u).wait_recv()

            @pl.when(z > 0)
            def _():
                copy(1, z + d, u).start()

    def pair(p, _):
        lanes = pl.ds(pl.multiple_of(p * 128, 128), 128)
        vlanes = pl.ds(pl.multiple_of(width + p * 128, 128), 128)
        va_ref[:rows, :128] = kv_ref[:, vlanes]
        va_ref[rows:, :128] = peer_ref[:, vlanes]
        cva_ref[:, :128] = cv_ref[:, lanes]
        gate = gate_ref[:, lanes]

        def block(b, _):
            rs = pl.ds(pl.multiple_of(b * qb, qb), qb)
            qp = q_ref[rs, lanes]
            outs, couts = [], []
            for a in range(2):
                qm = jnp.where(first if a == 0 else jnp.logical_not(first), qp, jnp.zeros_like(qp))
                acc = None
                for side in range(2):
                    keys = kv_ref if side == 0 else peer_ref
                    for j in range(0, rows, kc):
                        s = nt(qm, keys[j : j + kc, lanes])
                        pr = jnp.exp2(s * c).astype(BF)
                        o = nn(pr, va_ref[side * rows + j : side * rows + j + kc, :])
                        acc = o if acc is None else acc + o
                outs.append(acc)
                s = nt(qm, ck_ref[:, lanes])
                couts.append(nn(jnp.exp2(s * c).astype(BF), cva_ref[...]))
            so = jnp.where(first, outs[0][:, :128], outs[1][:, :128])
            sl = jnp.where(first, outs[0][:, 128:], outs[1][:, 128:])
            co = jnp.where(first, couts[0][:, :128], couts[1][:, :128])
            cl = jnp.where(first, couts[0][:, 128:], couts[1][:, 128:])
            so = so / sl
            co = co / cl
            mixed_ref[z, rs, lanes] = (so + gate * co).astype(BF)
            self_ref[rs, lanes] = so
            cross_ref[rs, lanes] = co
            lt = jnp.log2(sl).T
            ct = jnp.log2(cl).T
            lse_ref[p, :, rs] = jnp.concatenate([lt[0:1], lt[64:65], ct[0:1], ct[64:65], lt[0:4]], axis=0)
            u = p * blocks + b
            send_own(u)

            @pl.when(u >= 2)
            def _():
                relay(1, u - 2)

            return 0

        lax.fori_loop(0, blocks, block, 0)
        return 0

    lax.fori_loop(0, width // 128, pair, 0)
    for u in range(max(0, units - 2), units):
        relay(1, u)

    def pass_on(t, _):
        for d in range(2, n):

            @pl.when(both(t >= d - 2, t - (d - 2) < units))
            def _(d=d):
                relay(d, t - (d - 2))

        return 0

    lax.fori_loop(0, units + max(0, n - 3), pass_on, 0)

    def drain(u, _):
        for o in range(n):

            @pl.when(both(z >= o, z < n - 1))
            def _(o=o):
                copy(0, o, u).wait_send()

            @pl.when(both(z <= o, z > 0))
            def _(o=o):
                copy(1, o, u).wait_send()

        return 0

    lax.fori_loop(0, units, drain, 0)


def attend(q, kv, peer, live, ck, cv, gate, scale, cid, qb=256, kc=1024):
    n = lax.axis_size("head")
    rows, width = q.shape
    txt = ck.shape[0]
    qb, kc = min(qb, rows), min(kc, rows)
    return pl.pallas_call(
        functools.partial(attend_kernel, n, scale, qb, kc),
        out_shape=(S((n, rows, width), BF), S((rows, width), F32), S((rows, width), F32), S((width // 128, 8, rows), F32)),
        in_specs=[VM] * 7,
        out_specs=(VM,) * 4,
        scratch_shapes=[
            pltpu.VMEM((2 * rows, 256), BF),
            pltpu.VMEM((txt, 256), BF),
            pltpu.SemaphoreType.DMA((2, n, width // 128 * (rows // qb))),
            pltpu.SemaphoreType.DMA((2, n, width // 128 * (rows // qb))),
        ],
        compiler_params=pltpu.CompilerParams(collective_id=cid, has_side_effects=True, vmem_limit_bytes=BIG),
        cost_estimate=pl.CostEstimate(flops=32 * rows * rows * width, bytes_accessed=12 * rows * width, transcendentals=0),
        name="attend",
    )(q, kv, peer, live, ck, cv, gate)


def head_sum(x):
    ind = (lax.broadcasted_iota(jnp.int32, (8, 128), 0) == lax.broadcasted_iota(jnp.int32, (8, 128), 1) // 64).astype(F32)
    return lax.dot_general(ind, x, (((1,), (1,)), ((), ())), preferred_element_type=F32, precision=HIGHEST)


def cross_back_kernel(
    scale, qb, q_ref, ck_ref, cv_ref, gate_ref, cross_ref, lse_ref, dm_ref, dq_ref, dck_ref, dcv_ref, gg_ref, ckt_ref, p_ref, d_ref
):
    rows, width = q_ref.shape
    txt = ck_ref.shape[0]
    c = scale * LOG2E
    first = lax.broadcasted_iota(jnp.int32, (qb, 128), 1) < 64

    def pair(p, _):
        lanes = pl.ds(pl.multiple_of(p * 128, 128), 128)
        ckt_ref[...] = ck_ref[:, lanes].T
        gate = gate_ref[:, lanes]
        dck_ref[:, lanes] = jnp.zeros((txt, 128), F32)
        dcv_ref[:, lanes] = jnp.zeros((txt, 128), F32)
        gg_ref[:, lanes] = jnp.zeros((8, 128), F32)

        def block(b, _):
            rs = pl.ds(pl.multiple_of(b * qb, qb), qb)
            qp = q_ref[rs, lanes]
            dmf = dm_ref[rs, lanes].astype(F32)
            dcf = (gate * dmf).astype(BF)
            cross = cross_ref[rs, lanes]
            gg_ref[:, lanes] += fold8(dmf * cross)
            delta = head_sum(dcf.astype(F32) * cross)
            z = jnp.zeros_like(qp)
            masks = (first, jnp.logical_not(first))
            qs = [jnp.where(m, qp, z) for m in masks]
            dcs = [jnp.where(m, dcf, z) for m in masks]
            lse = lse_ref[p, :, rs]
            dqt = []
            for a in range(2):
                s = nt(ck_ref[:, lanes], qs[a])
                pr = jnp.exp2(s * c - lse[2 + a : 3 + a])
                dp = nt(cv_ref[:, lanes], dcs[a])
                p_ref[:, a * qb : (a + 1) * qb] = pr.astype(BF)
                dd = (pr * (dp - delta[a : a + 1])).astype(BF)
                d_ref[:, a * qb : (a + 1) * qb] = dd
                dqt.append(nn(ckt_ref[a * 64 : (a + 1) * 64, :], dd))
            dcv_ref[:, lanes] += nn(p_ref[...], jnp.concatenate(dcs, axis=0))
            dck_ref[:, lanes] += nn(d_ref[...], jnp.concatenate(qs, axis=0))
            dq_ref[rs, lanes] = (jnp.concatenate(dqt, axis=0) * scale).T
            return 0

        lax.fori_loop(0, rows // qb, block, 0)
        dck_ref[:, lanes] = dck_ref[:, lanes] * scale
        return 0

    lax.fori_loop(0, width // 128, pair, 0)


def cross_back(q, ck, cv, gate, co, lse, dm, scale, qb=512):
    rows, width = q.shape
    txt = ck.shape[0]
    qb = min(qb, rows)
    return pl.pallas_call(
        functools.partial(cross_back_kernel, scale, qb),
        out_shape=(S((rows, width), F32), S((txt, width), F32), S((txt, width), F32), S((8, width), F32)),
        in_specs=[VM] * 7,
        out_specs=(VM,) * 4,
        scratch_shapes=[pltpu.VMEM((128, txt), BF), pltpu.VMEM((txt, 2 * qb), BF), pltpu.VMEM((txt, 2 * qb), BF)],
        compiler_params=pltpu.CompilerParams(vmem_limit_bytes=BIG),
        cost_estimate=pl.CostEstimate(flops=24 * rows * txt * width, bytes_accessed=12 * rows * width, transcendentals=0),
        name="cross_back",
    )(q, ck, cv, gate, co, lse, dm)


def attend_back_kernel(
    n,
    per,
    scale,
    qb,
    kc,
    q_ref,
    kv_ref,
    peer_ref,
    live_ref,
    self_ref,
    lse_ref,
    dm_ref,
    dqc_ref,
    part_ref,
    dq_ref,
    dkv_ref,
    dpeer_ref,
    fsum_ref,
    kt_ref,
    p_ref,
    d_ref,
    ak_ref,
    av_ref,
    rbuf,
    lbuf,
    ssem,
    rsem,
):
    line_barrier(lax.axis_index("head"), n)
    ch = Chain(n, SUBS, BACK_LAG, part_ref, fsum_ref, rbuf, lbuf, ssem, rsem)
    rows, width = q_ref.shape
    c = scale * LOG2E
    first = lax.broadcasted_iota(jnp.int32, (qb, 128), 1) < 64

    def pair(p, _):
        lanes = pl.ds(pl.multiple_of(p * 128, 128), 128)
        vlanes = pl.ds(pl.multiple_of(width + p * 128, 128), 128)
        kt_ref[:, :rows] = kv_ref[:, lanes].T
        kt_ref[:, rows:] = peer_ref[:, lanes].T
        ak_ref[...] = jnp.zeros_like(ak_ref)
        av_ref[...] = jnp.zeros_like(av_ref)

        def block(b, _):
            rs = pl.ds(pl.multiple_of(b * qb, qb), qb)
            qp = q_ref[rs, lanes]
            dm = dm_ref[rs, lanes]
            dmf = dm.astype(F32)
            delta = head_sum(dmf * self_ref[rs, lanes])
            z = jnp.zeros_like(qp)
            masks = (first, jnp.logical_not(first))
            qs = [jnp.where(m, qp, z) for m in masks]
            dms = [jnp.where(m, dm, z) for m in masks]
            qstack = jnp.concatenate(qs, axis=0)
            dstack = jnp.concatenate(dms, axis=0)
            lse = lse_ref[p, :, rs]
            dqt = [None, None]
            for side in range(2):
                src = kv_ref if side == 0 else peer_ref
                for j in range(0, rows, kc):
                    at = side * rows + j
                    for a in range(2):
                        s = nt(src[j : j + kc, lanes], qs[a])
                        pr = jnp.exp2(s * c - lse[a : a + 1])
                        dp = nt(src[j : j + kc, vlanes], dms[a])
                        p_ref[:, a * qb : (a + 1) * qb] = pr.astype(BF)
                        dd = (pr * (dp - delta[a : a + 1])).astype(BF)
                        d_ref[:, a * qb : (a + 1) * qb] = dd
                        t = nn(kt_ref[a * 64 : (a + 1) * 64, at : at + kc], dd)
                        dqt[a] = t if dqt[a] is None else dqt[a] + t
                    av_ref[at : at + kc] += nn(p_ref[...], dstack)
                    ak_ref[at : at + kc] += nn(d_ref[...], qstack)
            dq_ref[rs, lanes] = (jnp.concatenate(dqt, axis=0) * scale).T + dqc_ref[rs, lanes]
            for i in range(per):
                k = (p * (rows // qb) + b) * per + i

                @pl.when(k < ch.steps)
                def _(k=k):
                    ch.step(k)

            return 0

        lax.fori_loop(0, rows // qb, block, 0)
        live = live_ref[...].astype(F32)
        dkv_ref[:, lanes] = ak_ref[:rows] * (live[:rows] * scale)
        dkv_ref[:, vlanes] = av_ref[:rows] * live[:rows]
        dpeer_ref[:, lanes] = (ak_ref[rows:] * (live[rows:] * scale)).astype(BF)
        dpeer_ref[:, vlanes] = (av_ref[rows:] * live[rows:]).astype(BF)
        return 0

    lax.fori_loop(0, width // 128, pair, 0)
    ch.run(min(ch.steps, (width // 128) * (rows // qb) * per), ch.steps)
    ch.drain()


def attend_back(q, kv, peer, live, so, lse, dm, dqc, part, scale, cid, qb=256, kc=512, per=2):
    n = lax.axis_size("head")
    rows, width = q.shape
    qb, kc = min(qb, rows), min(kc, rows)
    return pl.pallas_call(
        functools.partial(attend_back_kernel, n, per, scale, qb, kc),
        out_shape=(
            S((rows, width), F32),
            S((rows, 2 * width), F32),
            S((rows, 2 * width), BF),
            S(part.shape, BF),
        ),
        in_specs=[VM] * 9,
        out_specs=(VM,) * 4,
        scratch_shapes=[
            pltpu.VMEM((128, 2 * rows), BF),
            pltpu.VMEM((kc, 2 * qb), BF),
            pltpu.VMEM((kc, 2 * qb), BF),
            pltpu.VMEM((2 * rows, 128), F32),
            pltpu.VMEM((2 * rows, 128), F32),
        ]
        + chain_scratch(*part.shape, SUBS),
        compiler_params=pltpu.CompilerParams(collective_id=cid, has_side_effects=True, vmem_limit_bytes=BIG),
        cost_estimate=pl.CostEstimate(flops=800 * rows * rows * width, bytes_accessed=20 * rows * width, transcendentals=0),
        name="attend_back",
    )(q, kv, peer, live, so, lse, dm, dqc, part)


def pair_swap(value):
    pairs = [(source, source ^ 1) for source in range(lax.axis_size("seq"))]
    return lax.ppermute(value, "seq", pairs)


def rope_tables(grid_rows, grid_cols, first_token, row_count, head_size):
    stride = grid_cols + 1
    tokens = first_token + jnp.arange(row_count, dtype=jnp.int32)
    valid = tokens < grid_rows * stride
    row_pos = (tokens // stride).astype(F32)
    col_pos = (tokens % stride).astype(F32)
    quarter = head_size // 4
    half = head_size // 2
    lane = jnp.arange(128, dtype=jnp.int32) % half
    frequency = ROPE_BASE ** (-(lane % quarter).astype(F32) / quarter)
    angles = jnp.where(lane[None, :] < quarter, row_pos[:, None], col_pos[:, None]) * frequency[None, :]
    sign = jnp.where(jnp.arange(128) % head_size < half, -1.0, 1.0)
    return jnp.cos(angles), jnp.sin(angles) * sign[None, :], valid


def scatter(v):
    return lax.psum_scatter(v, "seq", scatter_dimension=0, tiled=True)


def local(
    image_rows,
    condition,
    text_feats,
    grid_shape,
    text_slot,
    attn_gain,
    ffn_gain,
    mod_weight,
    mod_bias,
    qkv_weight,
    qk_gains,
    text_kv_weight,
    cross_gate,
    out_weight,
    gate_up_weight,
    down_weight,
    cotangent,
):
    row_count, model_width = image_rows.shape
    head_local, head_size = qk_gains.shape[1], qk_gains.shape[2]
    inner = head_local * head_size
    ff_local = down_weight.shape[0]
    text_local, cap_width = text_feats.shape
    head_count = lax.axis_size("head")
    seq_count = lax.axis_size("seq")
    seq_index = lax.axis_index("seq")
    head_index = lax.axis_index("head")
    image_index = seq_index // 2
    pair_half = seq_index % 2
    score_scale = head_size ** (-0.5)
    image_count = condition.shape[0]

    grid_pair = lax.dynamic_index_in_dim(grid_shape, image_index, 0, keepdims=False)
    cos, sin, valid = rope_tables(grid_pair[0], grid_pair[1], pair_half * row_count, row_count, head_size)
    keep = valid.astype(F32)[:, None]
    live_own = jnp.broadcast_to(keep, (row_count, 128))
    peer_tokens = (1 - pair_half) * row_count + jnp.arange(row_count, dtype=jnp.int32)
    keep_peer = (peer_tokens < grid_pair[0] * (grid_pair[1] + 1)).astype(F32)[:, None]
    live_all = jnp.concatenate([live_own, jnp.broadcast_to(keep_peer, (row_count, 128))], axis=0).astype(BF)

    cond_all = jax.nn.silu(condition.astype(F32)).astype(BF)
    cond_low = lax.dynamic_index_in_dim(cond_all, image_index, 0, keepdims=True)
    mod_piece = jnp.dot(cond_low, mod_weight, preferred_element_type=F32) + mod_bias
    modulation = share(jnp.broadcast_to(mod_piece, (8, model_width)), 4)[:, 0]
    one_attn = 1.0 + modulation[0]
    one_ffn = 1.0 + modulation[2]
    tanh_attn = jnp.tanh(modulation[1])
    tanh_ffn = jnp.tanh(modulation[3])

    head_gains = jnp.concatenate([qk_gains.reshape(3, inner), jnp.zeros((5, inner), F32)], axis=0)
    gate_head = jnp.tanh(cross_gate)
    gate_lanes = jnp.repeat(gate_head, head_size)[None, :]
    qkv_mats = jnp.transpose(qkv_weight, (1, 0, 2))
    same_head = (jnp.arange(inner)[:, None] // head_size == jnp.arange(inner)[None, :] // head_size).astype(F32) / head_size

    text_kv_flat = text_kv_weight.reshape(cap_width, 2 * inner)
    text_proj = jnp.dot(text_feats, text_kv_flat, preferred_element_type=F32)
    cap_pre = text_proj[:, :inner]
    cap_r = lax.rsqrt(jnp.dot(cap_pre * cap_pre, same_head, precision=HIGHEST) + EPSILON)
    cap_u = cap_pre * cap_r
    cap_kv = jnp.concatenate([cap_u * head_gains[2:3], text_proj[:, inner:]], axis=1).astype(BF)
    caps = lax.all_gather(cap_kv, "seq", axis=0, tiled=False)
    slot = lax.dynamic_index_in_dim(text_slot, image_index, 0, keepdims=False)
    cap_own = lax.dynamic_index_in_dim(caps, slot, 0, keepdims=False)
    cap_key, cap_value = cap_own[:, :inner], cap_own[:, inner:]

    slice_rows = inner // seq_count
    out_slice = lax.dynamic_slice_in_dim(out_weight, seq_index * slice_rows, slice_rows, 0)

    normed, pre, query, kv, out_slices = make_qkv(
        image_rows, (attn_gain * one_attn)[None, :], qkv_mats, head_gains, cos, sin, live_own, out_slice, 5
    )
    out_all = lax.all_gather(out_slices, "seq", axis=1, tiled=True)
    kv_peer = pair_swap(kv)
    mixed_all, self_out, cross_out, lse = attend(query, kv, kv_peer, live_all, cap_key, cap_value, gate_lanes, score_scale, 0)
    mixed = lax.dynamic_index_in_dim(mixed_all, head_index, 0, keepdims=False)
    vec = jnp.concatenate([jnp.stack([tanh_attn, ffn_gain * one_ffn, attn_gain * one_attn, tanh_ffn]), jnp.zeros((4, model_width), F32)])
    attn_out, ffn_low = make_middle(mixed_all, out_all, image_rows, live_own, vec)

    gate_up_flat = gate_up_weight.reshape(model_width, 2 * ff_local)
    attn_grad_low, ffn_rows, middle_grad_half, ffn_part, ffn_wgrad = ffn_exchange(
        ffn_low, cotangent, gate_up_flat, down_weight, image_rows, attn_out, live_own, vec, 1
    )
    ffn_wsum = scatter(ffn_wgrad)
    grad_out = cotangent.astype(F32)
    mixed_grad = nt(attn_grad_low, out_weight).astype(BF)
    dq_cross, dck, dcv, gate_rows = cross_back(query, cap_key, cap_value, gate_lanes, cross_out, lse, mixed_grad, score_scale)
    cap_grads = lax.all_gather(jnp.concatenate([dck, dcv], axis=1).astype(BF), "seq", axis=0, tiled=False)
    dq, dkv, dpeer, ffn_out = attend_back(query, kv, kv_peer, live_all, self_out, lse, mixed_grad, dq_cross, ffn_part, score_scale, 2)
    from_peer = pair_swap(dpeer)
    dq, cap_grads = lax.optimization_barrier((dq, cap_grads))

    own_image = jnp.sum(jnp.where(text_slot == seq_index, jnp.arange(image_count), 0))
    used = jnp.any(text_slot == seq_index).astype(F32)
    two = lax.dynamic_slice_in_dim(cap_grads, 2 * own_image, 2, 0).astype(F32)
    cap_grad = (two[0] + two[1]) * used
    cap_dy, cap_dv = cap_grad[:, :inner], cap_grad[:, inner:]
    cap_w = cap_dy * head_gains[2:3]
    cap_pre_grad = cap_r * (cap_w - cap_u * jnp.dot(cap_w * cap_u, same_head, precision=HIGHEST))
    cap_gain = jnp.sum(cap_dy * cap_u, axis=0)
    text_low = jnp.concatenate([cap_pre_grad, cap_dv], axis=1).astype(BF)
    text_weight_grad = tn(text_feats, text_low).astype(BF)
    text_part = nt(text_low, text_kv_flat).astype(BF)
    dq, dkv, text_part, text_weight_grad, ffn_wsum = lax.optimization_barrier(
        (dq, dkv, text_part, text_weight_grad, ffn_wsum)
    )
    text_sum = lax.psum_scatter(text_part, "head", scatter_dimension=1, tiled=True)
    text_weight_sum = scatter(text_weight_grad)

    ffn_out = ffn_out.astype(F32)
    output = (image_rows.astype(F32) + keep * tanh_attn * attn_out + keep * tanh_ffn * ffn_out).astype(BF)
    gate_ffn_grad = jnp.sum(grad_out * keep * ffn_out, axis=0) * (1.0 - tanh_ffn * tanh_ffn)
    grad_pre, gain_rows, attn_in_part = qkv_back(dq, dkv, from_peer, pre, head_gains, cos, sin, qkv_mats)
    attn_wgrad = wgrad_pair(normed, grad_pre, attn_grad_low, mixed)
    attn_in_part, attn_wgrad, text_sum = lax.optimization_barrier((attn_in_part, attn_wgrad, text_sum))
    attn_wsum = scatter(attn_wgrad)
    text_grad = text_sum.astype(F32)
    rows_grad, row_sums = chain_rows(attn_in_part, image_rows, middle_grad_half, vec[2:], ffn_rows, 3)
    row_sums, ffn_wsum = lax.optimization_barrier((row_sums, ffn_wsum))
    ffn_sum, attn_sum = row_sums[0], row_sums[2]
    gate_attn_grad = row_sums[1] * (1.0 - tanh_attn * tanh_attn)

    mod_grad = jnp.stack([attn_sum * attn_gain, gate_attn_grad, ffn_sum * ffn_gain, gate_ffn_grad])
    own_mod = lax.dynamic_index_in_dim(mod_grad, head_index, 0, keepdims=False)
    gain_grad = jnp.concatenate([gain_rows[0:8].sum(0), gain_rows[8:16].sum(0), cap_gain])
    gate_grad_head = gate_rows.sum(0)
    small = jnp.concatenate([attn_sum * one_attn, ffn_sum * one_ffn, own_mod, gain_grad, gate_grad_head])
    smalls = lax.all_gather(small, "seq", axis=0, tiled=False)
    total = jnp.sum(smalls, axis=0)
    d = model_width
    dl = d // seq_count
    attn_gain_sum = lax.dynamic_slice_in_dim(total[:d], seq_index * dl, dl)
    ffn_gain_sum = lax.dynamic_slice_in_dim(total[d : 2 * d], seq_index * dl, dl)
    mod_bias_sum = lax.dynamic_slice_in_dim(total[2 * d : 3 * d], seq_index * dl, dl)[None, :]
    qk_all = total[3 * d : 3 * d + 3 * inner].reshape(3, head_local, seq_count, head_size // seq_count)
    qk_gain_sum = lax.dynamic_index_in_dim(qk_all, seq_index, 2, keepdims=False)
    gate_sum = total[3 * d + 3 * inner :].reshape(head_local, head_size).sum(-1) * (1.0 - gate_head * gate_head)
    cond_cols = condition.shape[1] // seq_count
    cond_part = lax.dynamic_slice_in_dim(cond_all, seq_index * cond_cols, cond_cols, 1).astype(F32)
    image_mods = smalls[:, 2 * d : 3 * d].reshape(image_count, 2, d).sum(1)
    mod_weight_sum = lax.dot_general(cond_part, image_mods, (((0,), (0,)), ((), ())), precision=HIGHEST)

    split = 2 * ff_local
    ffn_wsum, attn_wsum = ffn_wsum.astype(F32), attn_wsum.astype(F32)
    gate_up_sum = ffn_wsum[:, :split].reshape(-1, 2, ff_local)
    down_sum = ffn_wsum[:, split:].T
    qkv_sum = attn_wsum[:, : 3 * inner].reshape(-1, 3, inner)
    out_sum = attn_wsum[:, 3 * inner :].T
    text_weight_sum = text_weight_sum.astype(F32).reshape(-1, 2, inner)
    return (
        output,
        rows_grad,
        text_grad,
        attn_gain_sum,
        ffn_gain_sum,
        mod_weight_sum,
        mod_bias_sum,
        qkv_sum,
        qk_gain_sum,
        text_weight_sum,
        gate_sum,
        out_sum,
        gate_up_sum,
        down_sum,
    )


def solution(mesh):
    return jax.shard_map(
        local,
        mesh=mesh,
        in_specs=(
            P("seq", None),
            P(),
            P("seq", None),
            P(),
            P(),
            P(),
            P(),
            P(None, "head"),
            P("head", None),
            P(None, None, "head"),
            P(None, "head", None),
            P(None, None, "head"),
            P("head"),
            P("head", None),
            P(None, None, "head"),
            P("head", None),
            P("seq", None),
        ),
        out_specs=(
            P("seq", None),
            P("seq", None),
            P("seq", "head"),
            P("seq"),
            P("seq"),
            P("seq", "head"),
            P("head", "seq"),
            P("seq", None, "head"),
            P(None, "head", "seq"),
            P("seq", None, "head"),
            P("head"),
            P("head", "seq"),
            P("seq", None, "head"),
            P("head", "seq"),
        ),
        check_vma=False,
    )
```

```python
import functools

import jax
import jax.numpy as jnp
from jax import lax
from jax.experimental import pallas as pl
from jax.experimental.pallas import tpu as pltpu
from jax.sharding import PartitionSpec as P

TXT = 256
EPSILON = 1e-06
ROPE_BASE = 10000.0
LOG2E = 1.4426950408889634
F32 = jnp.float32
BF = jnp.bfloat16
VMEM_BYTES = 67043328
HIGHEST = lax.Precision.HIGHEST
VM = pl.BlockSpec(memory_space=pltpu.VMEM)
S = jax.ShapeDtypeStruct


def nt(a, b):
    return lax.dot_general(a, b, (((1,), (1,)), ((), ())), preferred_element_type=F32)


def nn(a, b):
    return lax.dot_general(a, b, (((1,), (0,)), ((), ())), preferred_element_type=F32)


def tn(a, b):
    return lax.dot_general(a, b, (((0,), (0,)), ((), ())), preferred_element_type=F32)


def head_mean(x):
    rows = lax.broadcasted_iota(jnp.int32, (128, 128), 0) // 64
    cols = lax.broadcasted_iota(jnp.int32, (128, 128), 1) // 64
    same = jnp.where(rows == cols, 1.0 / 64, 0.0).astype(BF)
    high = x.astype(BF)
    rest = (x - high.astype(F32)).astype(BF)
    return nn(high, same) + nn(rest, same)


def swap_halves(x):
    lane = lax.broadcasted_iota(jnp.int32, x.shape, 1) % 64
    return jnp.where(lane < 32, pltpu.roll(x, 96, 1), pltpu.roll(x, 32, 1))


def to_head(z):
    return {"head": z}


def both(a, b):
    return jnp.logical_and(a, b)


def line_barrier(z, n):
    bar = pltpu.get_barrier_semaphore()
    for ok, other in ((z > 0, z - 1), (z < n - 1, z + 1)):

        @pl.when(ok)
        def _(other=other):
            pl.semaphore_signal(bar, inc=1, device_id=to_head(other), device_id_type=pl.DeviceIdType.MESH)

    end = jnp.logical_or(z == 0, z == n - 1)

    @pl.when(end)
    def _():
        pl.semaphore_wait(bar, 1)

    @pl.when(jnp.logical_not(end))
    def _():
        pl.semaphore_wait(bar, 2)


def head_barrier(z, n):
    bar = pltpu.get_barrier_semaphore()
    for i in range(1, n):
        pl.semaphore_signal(bar, inc=1, device_id=to_head(lax.rem(z + i, n)), device_id_type=pl.DeviceIdType.MESH)
    pl.semaphore_wait(bar, n - 1)


class Chain:
    def __init__(self, n, subs, lag, part_ref, out_ref, rbuf, lbuf, ssem, rsem, finalize=None):
        self.z, self.n, self.subs, self.lag = lax.axis_index("head"), n, subs, lag
        self.part, self.out, self.rbuf, self.lbuf, self.ssem, self.rsem = part_ref, out_ref, rbuf, lbuf, ssem, rsem
        self.half = part_ref.shape[0] // 2
        self.unit = self.half // subs
        self.finalize = finalize
        self.steps = subs + 2 * lag * (n - 1)

    def near(self, s):
        return pl.ds(pl.multiple_of(s * self.unit, self.unit), self.unit)

    def far(self, s):
        return pl.ds(pl.multiple_of(self.half + s * self.unit, self.unit), self.unit)

    def copy(self, kind, s, first=False):
        src, at, to = (
            (self.rbuf, self.near(s), self.near(s)),
            (self.lbuf, self.near(s), self.near(s)),
            (self.out, self.near(s), self.near(s)),
            (self.out, self.far(s), self.far(s)),
        )[kind]
        dst = src
        if first:
            src, at = self.part, (self.far(s) if kind == 0 else self.near(s))
        return pltpu.make_async_remote_copy(
            src_ref=src.at[at],
            dst_ref=dst.at[to],
            send_sem=self.ssem.at[kind, s],
            recv_sem=self.rsem.at[kind, s],
            device_id=to_head(self.z + (1 if kind % 2 == 0 else -1)),
            device_id_type=pl.DeviceIdType.MESH,
        )

    def step(self, k):
        z, lag, last = self.z, self.lag, self.n - 1

        def inside(s):
            return both(s >= 0, s < self.subs)

        for kind, buf in ((0, self.rbuf), (1, self.lbuf)):
            hops = z if kind == 0 else last - z
            s = k - lag * hops

            @pl.when(both(inside(s), hops == 0))
            def _(kind=kind, s=s):
                self.copy(kind, s, True).start()

            @pl.when(both(inside(s), both(hops > 0, hops < last)))
            def _(kind=kind, s=s, buf=buf):
                self.copy(kind, s).wait_recv()
                at = self.near(s)
                own = self.part[self.far(s) if kind == 0 else at]
                buf[at] = (buf[at].astype(F32) + own.astype(F32)).astype(BF)
                self.copy(kind, s).start()

            @pl.when(both(inside(s), hops == last))
            def _(kind=kind, s=s, buf=buf):
                self.copy(kind, s).wait_recv()
                to = self.far(s) if kind == 0 else self.near(s)
                total = buf[self.near(s)].astype(F32) + self.part[to].astype(F32)
                if self.finalize is not None:
                    total = self.finalize(self.near(s), to, total)
                self.out[to] = total.astype(BF)
                self.copy(3 - kind, s).start()

        for kind in (2, 3):
            hops = z if kind == 2 else last - z
            s = k - lag * (last + hops)

            @pl.when(both(inside(s), hops > 0))
            def _(kind=kind, s=s, hops=hops):
                self.copy(kind, s).wait_recv()

                @pl.when(hops < last)
                def _():
                    self.copy(kind, s).start()

    def run(self, first, last):
        def one(k, c):
            self.step(k)
            return c

        lax.fori_loop(first, last, one, 0)

    def drain(self):
        def one(s, c):
            for kind in range(4):

                @pl.when(self.z < self.n - 1 if kind % 2 == 0 else self.z > 0)
                def _(kind=kind):
                    self.copy(kind, s).wait_send()

            return c

        lax.fori_loop(0, self.subs, one, 0)


def chain_scratch(rows, width, subs):
    return [
        pltpu.VMEM((rows // 2, width), BF),
        pltpu.VMEM((rows // 2, width), BF),
        pltpu.SemaphoreType.DMA((4, subs)),
        pltpu.SemaphoreType.DMA((4, subs)),
    ]


SUBS, LAG, BACK_LAG = 16, 2, 2
ANY = pl.BlockSpec(memory_space=pl.ANY)
BIG = VMEM_BYTES - (1 << 20)


def norm_parts(values):
    r = lax.rsqrt(jnp.mean(values * values, axis=-1, keepdims=True) + EPSILON)
    return r, values * r


def fold8(x):
    return jnp.sum(x.reshape(x.shape[0] // 8, 8, x.shape[1]), axis=0)


def half_loads(z, n, half, whole, halves, sem):
    at = pl.ds(pl.multiple_of(jnp.where(z == 0, 0, half), half), half)
    pairs = [(ref.at[at], to) for ref, to in whole] + halves
    return [pltpu.make_async_copy(ref, to, sem.at[i]) for i, (ref, to) in enumerate(pairs)]


def run_with_loads(ch, end, loads, after_sums):
    @pl.when(end)
    def _():
        for c in loads:
            c.start()

    need = ch.lag * (ch.n - 1)
    ch.run(0, need)

    @pl.when(end)
    def _():
        for c in loads:
            c.wait()

    ch.run(need, need + ch.subs)
    after_sums()
    ch.run(need + ch.subs, ch.steps)


def ffn_kernel(
    n, subs, lag, blocks, tile,
    h_any, g_any, wgu_any, wd_any, x_any, attn_any, live_ref, vec_ref,
    out_ref, sum_ref, dmid_any, fpart_any, wg_any,
    rbuf, lbuf, ssem, rsem, hv, gv, wgu, wd, xv, av, part_ref, dgu, hid, dffn, fpart, dmid, wbuf, csem, osem, tsem,
):
    z = lax.axis_index("head")
    rows, width = hv.shape
    ff = wd.shape[0]
    half = rows // 2
    rb = half // blocks
    end = jnp.logical_or(z == 0, z == n - 1)
    loads = [pltpu.make_async_copy(a, b, csem.at[i]) for i, (a, b) in enumerate(((h_any, hv), (wgu_any, wgu), (g_any, gv), (wd_any, wd)))]
    for c in loads:
        c.start()
    mine = pl.ds(pl.multiple_of(jnp.where(z == 0, 0, half), half), half)
    end_loads = [pltpu.make_async_copy(a.at[mine], b, csem.at[4 + i]) for i, (a, b) in enumerate(((x_any, xv), (attn_any, av)))]

    @pl.when(end)
    def _():
        for c in end_loads:
            c.start()

    sum_ref[...] = jnp.zeros_like(sum_ref)
    line_barrier(z, n)
    tanh_attn, gain, tanh_ffn = vec_ref[0:1], vec_ref[1:2], vec_ref[3:4]

    def finalize(at, to, dh):
        attn, live = av[at], live_ref[to, 0:1]
        mid = xv[at].astype(F32) + live * tanh_attn * attn
        r, u = norm_parts(mid)
        w = dh * gain
        grad = gv[to].astype(F32) + r * (w - u * jnp.mean(w * u, axis=-1, keepdims=True))
        dmid[at] = grad
        masked = grad * live
        sum_ref[0:8] += fold8(dh * u)
        sum_ref[8:16] += fold8(masked * attn)
        return masked * tanh_attn

    ch = Chain(n, subs, lag, part_ref, out_ref, rbuf, lbuf, ssem, rsem, finalize)

    def step(k):
        @pl.when(jnp.logical_and(end, k == lag * (n - 1)))
        def _():
            for c in end_loads:
                c.wait()

        ch.step(k)

    per = subs // blocks

    def block(t, c):
        near = pl.ds(pl.multiple_of(t * rb, rb), rb)
        far = pl.ds(pl.multiple_of(half + t * rb, rb), rb)

        def put(ref, v):
            ref[near] = v[:rb]
            ref[far] = v[rb:]

        @pl.when(t == 0)
        def _():
            loads[0].wait()
            loads[1].wait()

        gu = nn(jnp.concatenate([hv[near], hv[far]], axis=0), wgu[...])
        gate, up = gu[:, :ff], gu[:, ff:]
        sig = 1.0 / (1.0 + jnp.exp(-gate))
        act = gate * sig
        hidden = (act * up).astype(BF)
        put(hid, hidden)

        @pl.when(t == 0)
        def _():
            loads[2].wait()
            loads[3].wait()

        grad = jnp.concatenate([gv[near].astype(F32) * live_ref[near, 0:1], gv[far].astype(F32) * live_ref[far, 0:1]], axis=0)
        low = (grad * tanh_ffn).astype(BF)
        put(dffn, low)
        dhid = nt(low, wd[...])
        both_grads = jnp.concatenate(
            [(dhid * up * (sig + act * (1.0 - sig))).astype(BF), (dhid * act).astype(BF)], axis=1
        )
        put(dgu, both_grads)
        put(part_ref, nt(both_grads, wgu[...]).astype(BF))

        def some(i, c):
            step(t * per + i)
            return c

        lax.fori_loop(0, per, some, 0)
        put(fpart, nn(hidden, wd[...]).astype(BF))
        return c

    lax.fori_loop(0, blocks, block, 0)
    fcopy = pltpu.make_async_copy(fpart, fpart_any, osem.at[0])
    fcopy.start()

    tiles = width // tile
    every = max(1, (ch.steps - subs) // tiles)

    def tile_copy(j):
        return pltpu.make_async_copy(wbuf.at[lax.rem(j, 2)], wg_any.at[pl.ds(pl.multiple_of(j * tile, tile), tile)], tsem.at[j])

    def weights(j, c):
        def some(i, c):
            step(subs + j * every + i)
            return c

        lax.fori_loop(0, every, some, 0)

        @pl.when(j >= 2)
        def _():
            tile_copy(j - 2).wait()

        cols = pl.ds(pl.multiple_of(j * tile, tile), tile)
        slot = lax.rem(j, 2)
        wbuf[slot, :, : 2 * ff] = tn(hv[:, cols], dgu[...]).astype(BF)
        wbuf[slot, :, 2 * ff :] = tn(dffn[:, cols], hid[...]).astype(BF)
        tile_copy(j).start()
        return c

    lax.fori_loop(0, tiles, weights, 0)

    def rest(k, c):
        step(k)
        return c

    lax.fori_loop(subs + tiles * every, ch.steps, rest, 0)
    dcopy = pltpu.make_async_copy(dmid, dmid_any, osem.at[1])

    @pl.when(end)
    def _():
        dcopy.start()

    for j in range(max(0, tiles - 2), tiles):
        tile_copy(j).wait()
    fcopy.wait()
    ch.drain()

    @pl.when(end)
    def _():
        dcopy.wait()


def ffn_exchange(h, g, wgu, wd, x, attn, live, vec, cid, subs=16, lag=4, blocks=4, tile=256):
    n = lax.axis_size("head")
    rows, width = h.shape
    ff = wd.shape[0]
    half = rows // 2
    vm = pltpu.VMEM
    return pl.pallas_call(
        functools.partial(ffn_kernel, n, subs, lag, blocks, tile),
        out_shape=(
            S((rows, width), BF),
            S((16, width), F32),
            S((half, width), F32),
            S((rows, width), BF),
            S((width, 3 * ff), BF),
        ),
        in_specs=[ANY] * 6 + [VM] * 2,
        out_specs=(VM, VM, ANY, ANY, ANY),
        scratch_shapes=chain_scratch(rows, width, subs)
        + [
            vm((rows, width), BF),
            vm((rows, width), BF),
            vm((width, 2 * ff), BF),
            vm((ff, width), BF),
            vm((half, width), BF),
            vm((half, width), F32),
            vm((rows, width), BF),
            vm((rows, 2 * ff), BF),
            vm((rows, ff), BF),
            vm((rows, width), BF),
            vm((rows, width), BF),
            vm((half, width), F32),
            vm((2, tile, 3 * ff), BF),
            pltpu.SemaphoreType.DMA((6,)),
            pltpu.SemaphoreType.DMA((2,)),
            pltpu.SemaphoreType.DMA((width // tile,)),
        ],
        compiler_params=pltpu.CompilerParams(collective_id=cid, has_side_effects=True, vmem_limit_bytes=BIG),
        cost_estimate=pl.CostEstimate(flops=100_000_000_000, bytes_accessed=30 * rows * width, transcendentals=0),
        name="ffn_exchange",
    )(h, g, wgu, wd, x, attn, live, vec)


def chain_rows_kernel(
    n, part_ref, x_ref, dmid_ref, gain_ref, sum_ref, out_ref, tot_ref, rbuf, lbuf, ssem, rsem, xv, dv, csem, acc, ends, esem, fsem
):
    z = lax.axis_index("head")
    line_barrier(z, n)
    acc[...] = jnp.zeros_like(acc)
    gain = gain_ref[0:1]

    def finalize(at, to, dh):
        r, u = norm_parts(xv[at].astype(F32))
        w = dh * gain
        acc[...] += fold8(dh * u)
        return dv[at] + r * (w - u * jnp.mean(w * u, axis=-1, keepdims=True))

    ch = Chain(n, SUBS, LAG, part_ref, out_ref, rbuf, lbuf, ssem, rsem, finalize)
    loads = half_loads(z, n, ch.half, [(x_ref, xv)], [(dmid_ref, dv)], csem)
    width = acc.shape[1]

    def copy(e):
        return pltpu.make_async_remote_copy(
            src_ref=ends.at[e],
            dst_ref=ends.at[e],
            send_sem=esem.at[e],
            recv_sem=fsem.at[e],
            device_id=to_head(z + (1 if e == 0 else -1)),
            device_id_type=pl.DeviceIdType.MESH,
        )

    def send_sums():
        rows = [sum_ref[0:8], sum_ref[8:16], acc[...]]
        mine = jnp.concatenate([jnp.sum(r, axis=0, keepdims=True) for r in rows] + [jnp.zeros((5, width), F32)], axis=0)
        for e, source in ((0, 0), (1, n - 1)):

            @pl.when(z == source)
            def _(e=e):
                ends[e] = mine
                copy(e).start()

    run_with_loads(ch, jnp.logical_or(z == 0, z == n - 1), loads, send_sums)

    for e, source, sink in ((0, 0, n - 1), (1, n - 1, 0)):

        @pl.when(z != source)
        def _(e=e, sink=sink):
            copy(e).wait_recv()

            @pl.when(z != sink)
            def _():
                copy(e).start()

    tot_ref[...] = ends[0] + ends[1]
    for e, sink in ((0, n - 1), (1, 0)):

        @pl.when(z != sink)
        def _(e=e):
            copy(e).wait_send()

    ch.drain()


def chain_rows(part, x, dmid, gain, sums, cid):
    n = lax.axis_size("head")
    rows, width = part.shape
    half = rows // 2
    return pl.pallas_call(
        functools.partial(chain_rows_kernel, n),
        out_shape=(S((rows, width), BF), S((8, width), F32)),
        in_specs=[VM, ANY, ANY, VM, VM],
        out_specs=(VM,) * 2,
        scratch_shapes=chain_scratch(rows, width, SUBS)
        + [
            pltpu.VMEM((half, width), BF),
            pltpu.VMEM((half, width), F32),
            pltpu.SemaphoreType.DMA((2,)),
            pltpu.VMEM((8, width), F32),
            pltpu.VMEM((2, 8, width), F32),
            pltpu.SemaphoreType.DMA((2,)),
            pltpu.SemaphoreType.DMA((2,)),
        ],
        compiler_params=pltpu.CompilerParams(collective_id=cid, has_side_effects=True, vmem_limit_bytes=BIG),
        cost_estimate=pl.CostEstimate(flops=80_000_000_000, bytes_accessed=20 * rows * width, transcendentals=0),
        name="chain_rows",
    )(part, x, dmid, gain, sums)


def share_kernel(n, piece_ref, all_ref, ssem, rsem):
    z = lax.axis_index("head")
    head_barrier(z, n)

    def copy(i):
        return pltpu.make_async_remote_copy(
            src_ref=piece_ref,
            dst_ref=all_ref.at[z],
            send_sem=ssem.at[i],
            recv_sem=rsem.at[i],
            device_id=to_head(lax.rem(z + i, n)),
            device_id_type=pl.DeviceIdType.MESH,
        )

    for i in range(1, n):
        copy(i).start()
    all_ref[z] = piece_ref[...]
    for i in range(1, n):
        copy(i).wait()


def share(piece, cid):
    n = lax.axis_size("head")
    return pl.pallas_call(
        functools.partial(share_kernel, n),
        out_shape=S((n,) + piece.shape, piece.dtype),
        in_specs=[VM],
        out_specs=VM,
        scratch_shapes=[pltpu.SemaphoreType.DMA((n,)), pltpu.SemaphoreType.DMA((n,))],
        compiler_params=pltpu.CompilerParams(collective_id=cid, has_side_effects=True, vmem_limit_bytes=BIG),
        name="share",
    )(piece)


def wgrad_kernel(a_ref, b_ref, c_ref, d_ref, o_ref):
    nb = b_ref.shape[1]
    o_ref[:, :nb] = tn(a_ref[...], b_ref[...]).astype(BF)
    o_ref[:, nb:] = tn(c_ref[...], d_ref[...]).astype(BF)


def wgrad_pair(a, b, c, d):
    rows, width = a.shape
    cols = b.shape[1] + d.shape[1]
    wb = min(256, width)
    return pl.pallas_call(
        wgrad_kernel,
        grid=(width // wb,),
        in_specs=[
            pl.BlockSpec((rows, wb), lambda i: (0, i)),
            pl.BlockSpec(b.shape, lambda i: (0, 0)),
            pl.BlockSpec((rows, wb), lambda i: (0, i)),
            pl.BlockSpec(d.shape, lambda i: (0, 0)),
        ],
        out_specs=pl.BlockSpec((wb, cols), lambda i: (i, 0)),
        out_shape=S((width, cols), BF),
        compiler_params=pltpu.CompilerParams(vmem_limit_bytes=BIG),
        cost_estimate=pl.CostEstimate(flops=2 * rows * width * cols, bytes_accessed=2 * width * cols, transcendentals=0),
        name="wgrad_pair",
    )(a, b, c, d)


def qkv_kernel(
    n, x_ref, gain_ref, w_ref, hg_ref, cos_ref, sin_ref, live_ref, slice_ref, h_ref, pre_ref, q_ref, kv_ref, all_ref, ssem, rsem
):
    z = lax.axis_index("head")

    def copy(i):
        return pltpu.make_async_remote_copy(
            src_ref=slice_ref,
            dst_ref=all_ref.at[z],
            send_sem=ssem.at[i],
            recv_sem=rsem.at[i],
            device_id=to_head(lax.rem(z + i, n)),
            device_id_type=pl.DeviceIdType.MESH,
        )

    own = pltpu.make_async_copy(slice_ref, all_ref.at[z], ssem.at[0])

    @pl.when(pl.program_id(0) == 0)
    def _():
        head_barrier(z, n)
        own.start()
        for i in range(1, n):
            copy(i).start()

    x = x_ref[...].astype(F32)
    h = (x * lax.rsqrt(jnp.mean(x * x, axis=-1, keepdims=True) + EPSILON) * gain_ref[...]).astype(BF)
    h_ref[...] = h
    width = w_ref.shape[2]
    cos, sin, live = cos_ref[...], sin_ref[...], live_ref[...]
    for part in range(2):
        pre = nn(h, w_ref[part])
        pre_ref[:, part * width : (part + 1) * width] = pre
        for p in range(width // 128):
            v = pre[:, p * 128 : (p + 1) * 128]
            r = lax.rsqrt(head_mean(v * v) + EPSILON)
            t = v * r * hg_ref[part : part + 1, p * 128 : (p + 1) * 128]
            y = t * cos + swap_halves(t) * sin
            if part == 0:
                q_ref[:, p * 128 : (p + 1) * 128] = y.astype(BF)
            else:
                kv_ref[:, p * 128 : (p + 1) * 128] = (y * live).astype(BF)
    val = nn(h, w_ref[2])
    for p in range(width // 128):
        kv_ref[:, width + p * 128 : width + (p + 1) * 128] = (val[:, p * 128 : (p + 1) * 128] * live).astype(BF)

    @pl.when(pl.program_id(0) == pl.num_programs(0) - 1)
    def _():
        own.wait()
        for i in range(1, n):
            copy(i).wait()


def make_qkv(x, gain, w, head_gains, cos, sin, live, out_slice, cid):
    n = lax.axis_size("head")
    rows, width = x.shape
    inner = w.shape[2]
    rb = min(256, rows)
    return pl.pallas_call(
        functools.partial(qkv_kernel, n),
        grid=(rows // rb,),
        in_specs=[
            pl.BlockSpec((rb, width), lambda i: (i, 0)),
            pl.BlockSpec((1, width), lambda i: (0, 0)),
            pl.BlockSpec(w.shape, lambda i: (0, 0, 0)),
            pl.BlockSpec((8, inner), lambda i: (0, 0)),
            pl.BlockSpec((rb, 128), lambda i: (i, 0)),
            pl.BlockSpec((rb, 128), lambda i: (i, 0)),
            pl.BlockSpec((rb, 128), lambda i: (i, 0)),
            ANY,
        ],
        out_specs=(
            pl.BlockSpec((rb, width), lambda i: (i, 0)),
            pl.BlockSpec((rb, 2 * inner), lambda i: (i, 0)),
            pl.BlockSpec((rb, inner), lambda i: (i, 0)),
            pl.BlockSpec((rb, 2 * inner), lambda i: (i, 0)),
            ANY,
        ),
        out_shape=(
            S((rows, width), BF),
            S((rows, 2 * inner), F32),
            S((rows, inner), BF),
            S((rows, 2 * inner), BF),
            S((n,) + out_slice.shape, BF),
        ),
        scratch_shapes=[pltpu.SemaphoreType.DMA((n,)), pltpu.SemaphoreType.DMA((n,))],
        compiler_params=pltpu.CompilerParams(collective_id=cid, has_side_effects=True, vmem_limit_bytes=BIG),
        cost_estimate=pl.CostEstimate(flops=6 * rows * width * inner, bytes_accessed=12 * rows * width, transcendentals=0),
        name="make_qkv",
    )(x, gain, w, head_gains, cos, sin, live, out_slice)


def qkv_back_kernel(dq_ref, dkv_ref, peer_ref, pre_ref, hg_ref, cos_ref, sin_ref, w_ref, dpre_ref, gg_ref, dh_ref):
    width = dq_ref.shape[1]
    rows = dq_ref.shape[0]

    @pl.when(pl.program_id(0) == 0)
    def _():
        gg_ref[...] = jnp.zeros_like(gg_ref)

    cos, sin = cos_ref[...], sin_ref[...]
    total = None
    for part in range(2):
        for p in range(width // 128):
            ls = slice(p * 128, (p + 1) * 128)
            pls = slice(part * width + p * 128, part * width + (p + 1) * 128)
            if part == 0:
                dy = dq_ref[:, ls]
            else:
                dy = dkv_ref[:, ls] + peer_ref[:, ls].astype(F32)
            dt = dy * cos - swap_halves(dy) * sin
            v = pre_ref[:, pls]
            r = lax.rsqrt(head_mean(v * v) + EPSILON)
            u = v * r
            w = dt * hg_ref[part : part + 1, ls]
            dv = r * (w - u * head_mean(w * u))
            dpre_ref[:, pls] = dv.astype(BF)
            gg_ref[part * 8 : part * 8 + 8, ls] += jnp.sum((dt * u).reshape(rows // 8, 8, 128), axis=0)
        g = nt(dpre_ref[:, part * width : (part + 1) * width], w_ref[part])
        total = g if total is None else total + g
    dpre_ref[:, 2 * width :] = (dkv_ref[:, width:] + peer_ref[:, width:].astype(F32)).astype(BF)
    total = total + nt(dpre_ref[:, 2 * width :], w_ref[2])
    dh_ref[...] = total.astype(BF)


def qkv_back(dq, dkv, peer, pre, head_gains, cos, sin, w):
    rows, inner = dq.shape
    width = w.shape[1]
    rb = min(256, rows)
    blk = lambda c: pl.BlockSpec((rb, c), lambda i: (i, 0))
    return pl.pallas_call(
        qkv_back_kernel,
        grid=(rows // rb,),
        in_specs=[
            blk(inner),
            blk(2 * inner),
            blk(2 * inner),
            blk(2 * inner),
            pl.BlockSpec((8, inner), lambda i: (0, 0)),
            blk(128),
            blk(128),
            pl.BlockSpec(w.shape, lambda i: (0, 0, 0)),
        ],
        out_specs=(blk(3 * inner), pl.BlockSpec((16, inner), lambda i: (0, 0)), blk(width)),
        out_shape=(S((rows, 3 * inner), BF), S((16, inner), F32), S((rows, width), BF)),
        compiler_params=pltpu.CompilerParams(vmem_limit_bytes=BIG),
        cost_estimate=pl.CostEstimate(flops=6 * rows * width * inner, bytes_accessed=12 * rows * width, transcendentals=0),
        name="qkv_back",
    )(dq, dkv, peer, pre, head_gains, cos, sin, w)


def middle_kernel(mixed_ref, w_ref, x_ref, live_ref, vec_ref, attn_ref, h_ref):
    total = None
    for g in range(mixed_ref.shape[0]):
        t = nn(mixed_ref[g], w_ref[g]).astype(BF).astype(F32)
        total = t if total is None else total + t
    attn_ref[...] = total
    mid = x_ref[...].astype(F32) + live_ref[:, 0:1] * vec_ref[0:1] * total
    _, u = norm_parts(mid)
    h_ref[...] = (u * vec_ref[1:2]).astype(BF)


def make_middle(mixed_all, w_all, x, live, vec):
    n, rows, inner = mixed_all.shape
    width = x.shape[1]
    rb = min(256, rows)
    blk = lambda c: pl.BlockSpec((rb, c), lambda i: (i, 0))
    return pl.pallas_call(
        middle_kernel,
        grid=(rows // rb,),
        in_specs=[
            pl.BlockSpec((n, rb, inner), lambda i: (0, i, 0)),
            pl.BlockSpec(w_all.shape, lambda i: (0, 0, 0)),
            blk(width),
            blk(128),
            pl.BlockSpec((8, width), lambda i: (0, 0)),
        ],
        out_specs=(blk(width), blk(width)),
        out_shape=(S((rows, width), F32), S((rows, width), BF)),
        compiler_params=pltpu.CompilerParams(vmem_limit_bytes=BIG),
        cost_estimate=pl.CostEstimate(flops=2 * n * rows * width * inner, bytes_accessed=14 * rows * width, transcendentals=0),
        name="make_middle",
    )(mixed_all, w_all, x, live, vec)


def attend_kernel(
    n, scale, qb, kc, q_ref, kv_ref, peer_ref, live_ref, ck_ref, cv_ref, gate_ref, mixed_ref, self_ref, cross_ref, lse_ref,
    va_ref, cva_ref, ssem, rsem,
):
    z = lax.axis_index("head")
    line_barrier(z, n)
    rows, width = q_ref.shape
    txt = ck_ref.shape[0]
    c = scale * LOG2E
    va_ref[:, 128:] = live_ref[...]
    cva_ref[:, 128:] = jnp.ones((txt, 128), BF)
    first = lax.broadcasted_iota(jnp.int32, (qb, 128), 1) < 64

    def copy(kind, o, p):
        view = mixed_ref.at[o, :, pl.ds(pl.multiple_of(p * 128, 128), 128)]
        return pltpu.make_async_remote_copy(
            src_ref=view,
            dst_ref=view,
            send_sem=ssem.at[kind, o, p],
            recv_sem=rsem.at[kind, o, p],
            device_id=to_head(z + (1 if kind == 0 else -1)),
            device_id_type=pl.DeviceIdType.MESH,
        )

    def send_own(p):
        @pl.when(z < n - 1)
        def _():
            copy(0, z, p).start()

        @pl.when(z > 0)
        def _():
            copy(1, z, p).start()

    def relay(d, p):
        @pl.when(z - d >= 0)
        def _():
            copy(0, z - d, p).wait_recv()

            @pl.when(z < n - 1)
            def _():
                copy(0, z - d, p).start()

        @pl.when(z + d < n)
        def _():
            copy(1, z + d, p).wait_recv()

            @pl.when(z > 0)
            def _():
                copy(1, z + d, p).start()

    def pair(p, _):
        lanes = pl.ds(pl.multiple_of(p * 128, 128), 128)
        vlanes = pl.ds(pl.multiple_of(width + p * 128, 128), 128)
        va_ref[:rows, :128] = kv_ref[:, vlanes]
        va_ref[rows:, :128] = peer_ref[:, vlanes]
        cva_ref[:, :128] = cv_ref[:, lanes]
        gate = gate_ref[:, lanes]

        def block(b, _):
            rs = pl.ds(pl.multiple_of(b * qb, qb), qb)
            qp = q_ref[rs, lanes]
            outs, couts = [], []
            for a in range(2):
                qm = jnp.where(first if a == 0 else jnp.logical_not(first), qp, jnp.zeros_like(qp))
                acc = None
                for side in range(2):
                    keys = kv_ref if side == 0 else peer_ref
                    for j in range(0, rows, kc):
                        s = nt(qm, keys[j : j + kc, lanes])
                        pr = jnp.exp2(s * c).astype(BF)
                        o = nn(pr, va_ref[side * rows + j : side * rows + j + kc, :])
                        acc = o if acc is None else acc + o
                outs.append(acc)
                s = nt(qm, ck_ref[:, lanes])
                couts.append(nn(jnp.exp2(s * c).astype(BF), cva_ref[...]))
            so = jnp.where(first, outs[0][:, :128], outs[1][:, :128])
            sl = jnp.where(first, outs[0][:, 128:], outs[1][:, 128:])
            co = jnp.where(first, couts[0][:, :128], couts[1][:, :128])
            cl = jnp.where(first, couts[0][:, 128:], couts[1][:, 128:])
            so = so / sl
            co = co / cl
            mixed_ref[z, rs, lanes] = (so + gate * co).astype(BF)
            self_ref[rs, lanes] = so
            cross_ref[rs, lanes] = co
            lt = jnp.log2(sl).T
            ct = jnp.log2(cl).T
            lse_ref[p, :, rs] = jnp.concatenate([lt[0:1], lt[64:65], ct[0:1], ct[64:65], lt[0:4]], axis=0)
            return 0

        lax.fori_loop(0, rows // qb, block, 0)

        @pl.when(p >= 1)
        def _():
            relay(1, p - 1)

        send_own(p)
        return 0

    pairs = width // 128
    lax.fori_loop(0, pairs, pair, 0)
    for t in range(pairs + n - 2):
        for d in range(1, n):
            if 0 <= t - (d - 1) < pairs and (d > 1 or t == pairs - 1):
                relay(d, t - (d - 1))
    for p in range(pairs):
        for o in range(n):

            @pl.when(both(z >= o, z < n - 1))
            def _(o=o, p=p):
                copy(0, o, p).wait_send()

            @pl.when(both(z <= o, z > 0))
            def _(o=o, p=p):
                copy(1, o, p).wait_send()


def attend(q, kv, peer, live, ck, cv, gate, scale, cid, qb=256, kc=1024):
    n = lax.axis_size("head")
    rows, width = q.shape
    txt = ck.shape[0]
    qb, kc = min(qb, rows), min(kc, rows)
    return pl.pallas_call(
        functools.partial(attend_kernel, n, scale, qb, kc),
        out_shape=(S((n, rows, width), BF), S((rows, width), F32), S((rows, width), F32), S((width // 128, 8, rows), F32)),
        in_specs=[VM] * 7,
        out_specs=(VM,) * 4,
        scratch_shapes=[
            pltpu.VMEM((2 * rows, 256), BF),
            pltpu.VMEM((txt, 256), BF),
            pltpu.SemaphoreType.DMA((2, n, width // 128)),
            pltpu.SemaphoreType.DMA((2, n, width // 128)),
        ],
        compiler_params=pltpu.CompilerParams(collective_id=cid, has_side_effects=True, vmem_limit_bytes=BIG),
        cost_estimate=pl.CostEstimate(flops=32 * rows * rows * width, bytes_accessed=12 * rows * width, transcendentals=0),
        name="attend",
    )(q, kv, peer, live, ck, cv, gate)


def head_sum(x):
    ind = (lax.broadcasted_iota(jnp.int32, (8, 128), 0) == lax.broadcasted_iota(jnp.int32, (8, 128), 1) // 64).astype(F32)
    return lax.dot_general(ind, x, (((1,), (1,)), ((), ())), preferred_element_type=F32, precision=HIGHEST)


def cross_back_kernel(
    scale, qb, q_ref, ck_ref, cv_ref, gate_ref, cross_ref, lse_ref, da_ref, wo_ref,
    dq_ref, dck_ref, dcv_ref, gg_ref, dm_ref, ckt_ref, p_ref, d_ref,
):
    rows, width = q_ref.shape

    def project(b, _):
        rs = pl.ds(pl.multiple_of(b * qb, qb), qb)
        dm_ref[rs] = nt(da_ref[rs], wo_ref[...]).astype(BF)
        return 0

    lax.fori_loop(0, rows // qb, project, 0)
    txt = ck_ref.shape[0]
    c = scale * LOG2E
    first = lax.broadcasted_iota(jnp.int32, (qb, 128), 1) < 64

    def pair(p, _):
        lanes = pl.ds(pl.multiple_of(p * 128, 128), 128)
        ckt_ref[...] = ck_ref[:, lanes].T
        gate = gate_ref[:, lanes]
        dck_ref[:, lanes] = jnp.zeros((txt, 128), F32)
        dcv_ref[:, lanes] = jnp.zeros((txt, 128), F32)
        gg_ref[:, lanes] = jnp.zeros((8, 128), F32)

        def block(b, _):
            rs = pl.ds(pl.multiple_of(b * qb, qb), qb)
            qp = q_ref[rs, lanes]
            dmf = dm_ref[rs, lanes].astype(F32)
            dcf = (gate * dmf).astype(BF)
            cross = cross_ref[rs, lanes]
            gg_ref[:, lanes] += fold8(dmf * cross)
            delta = head_sum(dcf.astype(F32) * cross)
            z = jnp.zeros_like(qp)
            masks = (first, jnp.logical_not(first))
            qs = [jnp.where(m, qp, z) for m in masks]
            dcs = [jnp.where(m, dcf, z) for m in masks]
            lse = lse_ref[p, :, rs]
            dqt = []
            for a in range(2):
                s = nt(ck_ref[:, lanes], qs[a])
                pr = jnp.exp2(s * c - lse[2 + a : 3 + a])
                dp = nt(cv_ref[:, lanes], dcs[a])
                p_ref[:, a * qb : (a + 1) * qb] = pr.astype(BF)
                dd = (pr * (dp - delta[a : a + 1])).astype(BF)
                d_ref[:, a * qb : (a + 1) * qb] = dd
                dqt.append(nn(ckt_ref[a * 64 : (a + 1) * 64, :], dd))
            dcv_ref[:, lanes] += nn(p_ref[...], jnp.concatenate(dcs, axis=0))
            dck_ref[:, lanes] += nn(d_ref[...], jnp.concatenate(qs, axis=0))
            dq_ref[rs, lanes] = (jnp.concatenate(dqt, axis=0) * scale).T
            return 0

        lax.fori_loop(0, rows // qb, block, 0)
        dck_ref[:, lanes] = dck_ref[:, lanes] * scale
        return 0

    lax.fori_loop(0, width // 128, pair, 0)


def cross_back(q, ck, cv, gate, co, lse, da, wo, scale, qb=512):
    rows, width = q.shape
    txt = ck.shape[0]
    qb = min(qb, rows)
    return pl.pallas_call(
        functools.partial(cross_back_kernel, scale, qb),
        out_shape=(S((rows, width), F32), S((txt, width), F32), S((txt, width), F32), S((8, width), F32), S((rows, width), BF)),
        in_specs=[VM] * 8,
        out_specs=(VM,) * 5,
        scratch_shapes=[pltpu.VMEM((128, txt), BF), pltpu.VMEM((txt, 2 * qb), BF), pltpu.VMEM((txt, 2 * qb), BF)],
        compiler_params=pltpu.CompilerParams(vmem_limit_bytes=BIG),
        cost_estimate=pl.CostEstimate(flops=24 * rows * txt * width, bytes_accessed=12 * rows * width, transcendentals=0),
        name="cross_back",
    )(q, ck, cv, gate, co, lse, da, wo)


def attend_back_kernel(
    n,
    per,
    scale,
    qb,
    kc,
    q_ref,
    kv_ref,
    peer_ref,
    live_ref,
    self_ref,
    lse_ref,
    dm_ref,
    dqc_ref,
    part_ref,
    dq_ref,
    dkv_ref,
    dpeer_ref,
    fsum_ref,
    kt_ref,
    p_ref,
    d_ref,
    ak_ref,
    av_ref,
    rbuf,
    lbuf,
    ssem,
    rsem,
):
    line_barrier(lax.axis_index("head"), n)
    ch = Chain(n, SUBS, BACK_LAG, part_ref, fsum_ref, rbuf, lbuf, ssem, rsem)
    rows, width = q_ref.shape
    c = scale * LOG2E
    first = lax.broadcasted_iota(jnp.int32, (qb, 128), 1) < 64

    def pair(p, _):
        lanes = pl.ds(pl.multiple_of(p * 128, 128), 128)
        vlanes = pl.ds(pl.multiple_of(width + p * 128, 128), 128)
        kt_ref[:, :rows] = kv_ref[:, lanes].T
        kt_ref[:, rows:] = peer_ref[:, lanes].T
        ak_ref[...] = jnp.zeros_like(ak_ref)
        av_ref[...] = jnp.zeros_like(av_ref)

        def block(b, _):
            rs = pl.ds(pl.multiple_of(b * qb, qb), qb)
            qp = q_ref[rs, lanes]
            dm = dm_ref[rs, lanes]
            dmf = dm.astype(F32)
            delta = head_sum(dmf * self_ref[rs, lanes])
            z = jnp.zeros_like(qp)
            masks = (first, jnp.logical_not(first))
            qs = [jnp.where(m, qp, z) for m in masks]
            dms = [jnp.where(m, dm, z) for m in masks]
            qstack = jnp.concatenate(qs, axis=0)
            dstack = jnp.concatenate(dms, axis=0)
            lse = lse_ref[p, :, rs]
            dqt = [None, None]
            for side in range(2):
                src = kv_ref if side == 0 else peer_ref
                for j in range(0, rows, kc):
                    at = side * rows + j
                    for a in range(2):
                        s = nt(src[j : j + kc, lanes], qs[a])
                        pr = jnp.exp2(s * c - lse[a : a + 1])
                        dp = nt(src[j : j + kc, vlanes], dms[a])
                        p_ref[:, a * qb : (a + 1) * qb] = pr.astype(BF)
                        dd = (pr * (dp - delta[a : a + 1])).astype(BF)
                        d_ref[:, a * qb : (a + 1) * qb] = dd
                        t = nn(kt_ref[a * 64 : (a + 1) * 64, at : at + kc], dd)
                        dqt[a] = t if dqt[a] is None else dqt[a] + t
                    av_ref[at : at + kc] += nn(p_ref[...], dstack)
                    ak_ref[at : at + kc] += nn(d_ref[...], qstack)
            dq_ref[rs, lanes] = (jnp.concatenate(dqt, axis=0) * scale).T + dqc_ref[rs, lanes]
            for i in range(per):
                k = (p * (rows // qb) + b) * per + i

                @pl.when(k < ch.steps)
                def _(k=k):
                    ch.step(k)

            return 0

        lax.fori_loop(0, rows // qb, block, 0)
        live = live_ref[...].astype(F32)
        dkv_ref[:, lanes] = ak_ref[:rows] * (live[:rows] * scale)
        dkv_ref[:, vlanes] = av_ref[:rows] * live[:rows]
        dpeer_ref[:, lanes] = (ak_ref[rows:] * (live[rows:] * scale)).astype(BF)
        dpeer_ref[:, vlanes] = (av_ref[rows:] * live[rows:]).astype(BF)
        return 0

    lax.fori_loop(0, width // 128, pair, 0)
    ch.run(min(ch.steps, (width // 128) * (rows // qb) * per), ch.steps)
    ch.drain()


def attend_back(q, kv, peer, live, so, lse, dm, dqc, part, scale, cid, qb=256, kc=512, per=2):
    n = lax.axis_size("head")
    rows, width = q.shape
    qb, kc = min(qb, rows), min(kc, rows)
    return pl.pallas_call(
        functools.partial(attend_back_kernel, n, per, scale, qb, kc),
        out_shape=(
            S((rows, width), F32),
            S((rows, 2 * width), F32),
            S((rows, 2 * width), BF),
            S(part.shape, BF),
        ),
        in_specs=[VM] * 9,
        out_specs=(VM,) * 4,
        scratch_shapes=[
            pltpu.VMEM((128, 2 * rows), BF),
            pltpu.VMEM((kc, 2 * qb), BF),
            pltpu.VMEM((kc, 2 * qb), BF),
            pltpu.VMEM((2 * rows, 128), F32),
            pltpu.VMEM((2 * rows, 128), F32),
        ]
        + chain_scratch(*part.shape, SUBS),
        compiler_params=pltpu.CompilerParams(collective_id=cid, has_side_effects=True, vmem_limit_bytes=BIG),
        cost_estimate=pl.CostEstimate(flops=80 * rows * rows * width, bytes_accessed=20 * rows * width, transcendentals=0),
        name="attend_back",
    )(q, kv, peer, live, so, lse, dm, dqc, part)


def pair_swap(value):
    pairs = [(source, source ^ 1) for source in range(lax.axis_size("seq"))]
    return lax.ppermute(value, "seq", pairs)


def rope_tables(grid_rows, grid_cols, first_token, row_count, head_size):
    stride = grid_cols + 1
    tokens = first_token + jnp.arange(row_count, dtype=jnp.int32)
    valid = tokens < grid_rows * stride
    row_pos = (tokens // stride).astype(F32)
    col_pos = (tokens % stride).astype(F32)
    quarter = head_size // 4
    half = head_size // 2
    lane = jnp.arange(128, dtype=jnp.int32) % half
    frequency = ROPE_BASE ** (-(lane % quarter).astype(F32) / quarter)
    angles = jnp.where(lane[None, :] < quarter, row_pos[:, None], col_pos[:, None]) * frequency[None, :]
    sign = jnp.where(jnp.arange(128) % head_size < half, -1.0, 1.0)
    return jnp.cos(angles), jnp.sin(angles) * sign[None, :], valid


def scatter(v):
    return lax.psum_scatter(v, "seq", scatter_dimension=0, tiled=True)


def local(
    image_rows,
    condition,
    text_feats,
    grid_shape,
    text_slot,
    attn_gain,
    ffn_gain,
    mod_weight,
    mod_bias,
    qkv_weight,
    qk_gains,
    text_kv_weight,
    cross_gate,
    out_weight,
    gate_up_weight,
    down_weight,
    cotangent,
):
    row_count, model_width = image_rows.shape
    head_local, head_size = qk_gains.shape[1], qk_gains.shape[2]
    inner = head_local * head_size
    ff_local = down_weight.shape[0]
    text_local, cap_width = text_feats.shape
    head_count = lax.axis_size("head")
    seq_count = lax.axis_size("seq")
    seq_index = lax.axis_index("seq")
    head_index = lax.axis_index("head")
    image_index = seq_index // 2
    pair_half = seq_index % 2
    score_scale = head_size ** (-0.5)
    image_count = condition.shape[0]

    grid_pair = lax.dynamic_index_in_dim(grid_shape, image_index, 0, keepdims=False)
    cos, sin, valid = rope_tables(grid_pair[0], grid_pair[1], pair_half * row_count, row_count, head_size)
    keep = valid.astype(F32)[:, None]
    live_own = jnp.broadcast_to(keep, (row_count, 128))
    peer_tokens = (1 - pair_half) * row_count + jnp.arange(row_count, dtype=jnp.int32)
    keep_peer = (peer_tokens < grid_pair[0] * (grid_pair[1] + 1)).astype(F32)[:, None]
    live_all = jnp.concatenate([live_own, jnp.broadcast_to(keep_peer, (row_count, 128))], axis=0).astype(BF)

    cond_all = jax.nn.silu(condition.astype(F32)).astype(BF)
    cond_low = lax.dynamic_index_in_dim(cond_all, image_index, 0, keepdims=True)
    mod_piece = jnp.dot(cond_low, mod_weight, preferred_element_type=F32) + mod_bias
    modulation = share(jnp.broadcast_to(mod_piece, (8, model_width)), 4)[:, 0]
    one_attn = 1.0 + modulation[0]
    one_ffn = 1.0 + modulation[2]
    tanh_attn = jnp.tanh(modulation[1])
    tanh_ffn = jnp.tanh(modulation[3])

    head_gains = jnp.concatenate([qk_gains.reshape(3, inner), jnp.zeros((5, inner), F32)], axis=0)
    gate_head = jnp.tanh(cross_gate)
    gate_lanes = jnp.repeat(gate_head, head_size)[None, :]
    qkv_mats = jnp.transpose(qkv_weight, (1, 0, 2))
    same_head = (jnp.arange(inner)[:, None] // head_size == jnp.arange(inner)[None, :] // head_size).astype(F32) / head_size

    text_kv_flat = text_kv_weight.reshape(cap_width, 2 * inner)
    text_proj = jnp.dot(text_feats, text_kv_flat, preferred_element_type=F32)
    cap_pre = text_proj[:, :inner]
    cap_r = lax.rsqrt(jnp.dot(cap_pre * cap_pre, same_head, precision=HIGHEST) + EPSILON)
    cap_u = cap_pre * cap_r
    cap_kv = jnp.concatenate([cap_u * head_gains[2:3], text_proj[:, inner:]], axis=1).astype(BF)
    caps = lax.all_gather(cap_kv, "seq", axis=0, tiled=False)
    slot = lax.dynamic_index_in_dim(text_slot, image_index, 0, keepdims=False)
    cap_own = lax.dynamic_index_in_dim(caps, slot, 0, keepdims=False)
    cap_key, cap_value = cap_own[:, :inner], cap_own[:, inner:]

    slice_rows = inner // seq_count
    out_slice = lax.dynamic_slice_in_dim(out_weight, seq_index * slice_rows, slice_rows, 0)

    normed, pre, query, kv, out_slices = make_qkv(
        image_rows, (attn_gain * one_attn)[None, :], qkv_mats, head_gains, cos, sin, live_own, out_slice, 5
    )
    out_all = lax.all_gather(out_slices, "seq", axis=1, tiled=True)
    kv_peer = pair_swap(kv)
    mixed_all, self_out, cross_out, lse = attend(query, kv, kv_peer, live_all, cap_key, cap_value, gate_lanes, score_scale, 0)
    mixed = lax.dynamic_index_in_dim(mixed_all, head_index, 0, keepdims=False)
    vec = jnp.concatenate([jnp.stack([tanh_attn, ffn_gain * one_ffn, attn_gain * one_attn, tanh_ffn]), jnp.zeros((4, model_width), F32)])
    attn_out, ffn_low = make_middle(mixed_all, out_all, image_rows, live_own, vec)

    gate_up_flat = gate_up_weight.reshape(model_width, 2 * ff_local)
    attn_grad_low, ffn_rows, middle_grad_half, ffn_part, ffn_wgrad = ffn_exchange(
        ffn_low, cotangent, gate_up_flat, down_weight, image_rows, attn_out, live_own, vec, 1
    )
    ffn_wsum = scatter(ffn_wgrad)
    grad_out = cotangent.astype(F32)
    dq_cross, dck, dcv, gate_rows, mixed_grad = cross_back(
        query, cap_key, cap_value, gate_lanes, cross_out, lse, attn_grad_low, out_weight, score_scale
    )
    cap_grads = lax.all_gather(jnp.concatenate([dck, dcv], axis=1).astype(BF), "seq", axis=0, tiled=False)
    dq, dkv, dpeer, ffn_out = attend_back(query, kv, kv_peer, live_all, self_out, lse, mixed_grad, dq_cross, ffn_part, score_scale, 2)
    from_peer = pair_swap(dpeer)
    dq, cap_grads = lax.optimization_barrier((dq, cap_grads))

    own_image = jnp.sum(jnp.where(text_slot == seq_index, jnp.arange(image_count), 0))
    used = jnp.any(text_slot == seq_index).astype(F32)
    two = lax.dynamic_slice_in_dim(cap_grads, 2 * own_image, 2, 0).astype(F32)
    cap_grad = (two[0] + two[1]) * used
    cap_dy, cap_dv = cap_grad[:, :inner], cap_grad[:, inner:]
    cap_w = cap_dy * head_gains[2:3]
    cap_pre_grad = cap_r * (cap_w - cap_u * jnp.dot(cap_w * cap_u, same_head, precision=HIGHEST))
    cap_gain = jnp.sum(cap_dy * cap_u, axis=0)
    text_low = jnp.concatenate([cap_pre_grad, cap_dv], axis=1).astype(BF)
    text_weight_grad = tn(text_feats, text_low).astype(BF)
    text_part = nt(text_low, text_kv_flat).astype(BF)
    dq, dkv, text_part, text_weight_grad, ffn_wsum = lax.optimization_barrier(
        (dq, dkv, text_part, text_weight_grad, ffn_wsum)
    )
    text_sum = lax.psum_scatter(text_part, "head", scatter_dimension=1, tiled=True)
    text_weight_sum = scatter(text_weight_grad)

    ffn_out = ffn_out.astype(F32)
    output = (image_rows.astype(F32) + keep * tanh_attn * attn_out + keep * tanh_ffn * ffn_out).astype(BF)
    gate_ffn_grad = jnp.sum(grad_out * keep * ffn_out, axis=0) * (1.0 - tanh_ffn * tanh_ffn)
    grad_pre, gain_rows, attn_in_part = qkv_back(dq, dkv, from_peer, pre, head_gains, cos, sin, qkv_mats)
    attn_wgrad = wgrad_pair(normed, grad_pre, attn_grad_low, mixed)
    attn_in_part, attn_wgrad, text_sum = lax.optimization_barrier((attn_in_part, attn_wgrad, text_sum))
    attn_wsum = scatter(attn_wgrad)
    text_grad = text_sum.astype(F32)
    rows_grad, row_sums = chain_rows(attn_in_part, image_rows, middle_grad_half, vec[2:], ffn_rows, 3)
    ffn_sum, attn_sum = row_sums[0], row_sums[2]
    gate_attn_grad = row_sums[1] * (1.0 - tanh_attn * tanh_attn)

    mod_grad = jnp.stack([attn_sum * attn_gain, gate_attn_grad, ffn_sum * ffn_gain, gate_ffn_grad])
    own_mod = lax.dynamic_index_in_dim(mod_grad, head_index, 0, keepdims=False)
    gain_grad = jnp.concatenate([gain_rows[0:8].sum(0), gain_rows[8:16].sum(0), cap_gain])
    gate_grad_head = gate_rows.sum(0)
    small = jnp.concatenate([attn_sum * one_attn, ffn_sum * one_ffn, own_mod, gain_grad, gate_grad_head])
    smalls = lax.all_gather(small, "seq", axis=0, tiled=False)
    total = jnp.sum(smalls, axis=0)
    d = model_width
    dl = d // seq_count
    attn_gain_sum = lax.dynamic_slice_in_dim(total[:d], seq_index * dl, dl)
    ffn_gain_sum = lax.dynamic_slice_in_dim(total[d : 2 * d], seq_index * dl, dl)
    mod_bias_sum = lax.dynamic_slice_in_dim(total[2 * d : 3 * d], seq_index * dl, dl)[None, :]
    qk_all = total[3 * d : 3 * d + 3 * inner].reshape(3, head_local, seq_count, head_size // seq_count)
    qk_gain_sum = lax.dynamic_index_in_dim(qk_all, seq_index, 2, keepdims=False)
    gate_sum = total[3 * d + 3 * inner :].reshape(head_local, head_size).sum(-1) * (1.0 - gate_head * gate_head)
    cond_cols = condition.shape[1] // seq_count
    cond_part = lax.dynamic_slice_in_dim(cond_all, seq_index * cond_cols, cond_cols, 1).astype(F32)
    image_mods = smalls[:, 2 * d : 3 * d].reshape(image_count, 2, d).sum(1)
    mod_weight_sum = lax.dot_general(cond_part, image_mods, (((0,), (0,)), ((), ())), precision=HIGHEST)

    split = 2 * ff_local
    ffn_wsum, attn_wsum = ffn_wsum.astype(F32), attn_wsum.astype(F32)
    gate_up_sum = ffn_wsum[:, :split].reshape(-1, 2, ff_local)
    down_sum = ffn_wsum[:, split:].T
    qkv_sum = attn_wsum[:, : 3 * inner].reshape(-1, 3, inner)
    out_sum = attn_wsum[:, 3 * inner :].T
    text_weight_sum = text_weight_sum.astype(F32).reshape(-1, 2, inner)
    return (
        output,
        rows_grad,
        text_grad,
        attn_gain_sum,
        ffn_gain_sum,
        mod_weight_sum,
        mod_bias_sum,
        qkv_sum,
        qk_gain_sum,
        text_weight_sum,
        gate_sum,
        out_sum,
        gate_up_sum,
        down_sum,
    )


def solution(mesh):
    return jax.shard_map(
        local,
        mesh=mesh,
        in_specs=(
            P("seq", None),
            P(),
            P("seq", None),
            P(),
            P(),
            P(),
            P(),
            P(None, "head"),
            P("head", None),
            P(None, None, "head"),
            P(None, "head", None),
            P(None, None, "head"),
            P("head"),
            P("head", None),
            P(None, None, "head"),
            P("head", None),
            P("seq", None),
        ),
        out_specs=(
            P("seq", None),
            P("seq", None),
            P("seq", "head"),
            P("seq"),
            P("seq"),
            P("seq", "head"),
            P("head", "seq"),
            P("seq", None, "head"),
            P(None, "head", "seq"),
            P("seq", None, "head"),
            P("head"),
            P("head", "seq"),
            P("seq", None, "head"),
            P("head", "seq"),
        ),
        check_vma=False,
    )
```

```python
import functools

import jax
import jax.numpy as jnp
from jax import lax
from jax.experimental import pallas as pl
from jax.experimental.pallas import tpu as pltpu
from jax.sharding import PartitionSpec as P

TXT = 256
EPSILON = 1e-06
ROPE_BASE = 10000.0
LOG2E = 1.4426950408889634
F32 = jnp.float32
BF = jnp.bfloat16
VMEM_BYTES = 67043328
HIGHEST = lax.Precision.HIGHEST
VM = pl.BlockSpec(memory_space=pltpu.VMEM)
S = jax.ShapeDtypeStruct


def nt(a, b):
    return lax.dot_general(a, b, (((1,), (1,)), ((), ())), preferred_element_type=F32)


def nn(a, b):
    return lax.dot_general(a, b, (((1,), (0,)), ((), ())), preferred_element_type=F32)


def tn(a, b):
    return lax.dot_general(a, b, (((0,), (0,)), ((), ())), preferred_element_type=F32)


def head_mean(x):
    rows = lax.broadcasted_iota(jnp.int32, (128, 128), 0) // 64
    cols = lax.broadcasted_iota(jnp.int32, (128, 128), 1) // 64
    same = jnp.where(rows == cols, 1.0 / 64, 0.0).astype(BF)
    high = x.astype(BF)
    rest = (x - high.astype(F32)).astype(BF)
    return nn(high, same) + nn(rest, same)


def swap_halves(x):
    lane = lax.broadcasted_iota(jnp.int32, x.shape, 1) % 64
    return jnp.where(lane < 32, pltpu.roll(x, 96, 1), pltpu.roll(x, 32, 1))


def to_head(z):
    return {"head": z}


def both(a, b):
    return jnp.logical_and(a, b)


def line_barrier(z, n):
    bar = pltpu.get_barrier_semaphore()
    for ok, other in ((z > 0, z - 1), (z < n - 1, z + 1)):

        @pl.when(ok)
        def _(other=other):
            pl.semaphore_signal(bar, inc=1, device_id=to_head(other), device_id_type=pl.DeviceIdType.MESH)

    end = jnp.logical_or(z == 0, z == n - 1)

    @pl.when(end)
    def _():
        pl.semaphore_wait(bar, 1)

    @pl.when(jnp.logical_not(end))
    def _():
        pl.semaphore_wait(bar, 2)


def head_barrier(z, n):
    bar = pltpu.get_barrier_semaphore()
    for i in range(1, n):
        pl.semaphore_signal(bar, inc=1, device_id=to_head(lax.rem(z + i, n)), device_id_type=pl.DeviceIdType.MESH)
    pl.semaphore_wait(bar, n - 1)


class Chain:
    def __init__(self, n, subs, lag, part_ref, out_ref, rbuf, lbuf, ssem, rsem, finalize=None):
        self.z, self.n, self.subs, self.lag = lax.axis_index("head"), n, subs, lag
        self.part, self.out, self.rbuf, self.lbuf, self.ssem, self.rsem = part_ref, out_ref, rbuf, lbuf, ssem, rsem
        self.half = part_ref.shape[0] // 2
        self.unit = self.half // subs
        self.finalize = finalize
        self.steps = subs + 2 * lag * (n - 1)

    def near(self, s):
        return pl.ds(pl.multiple_of(s * self.unit, self.unit), self.unit)

    def far(self, s):
        return pl.ds(pl.multiple_of(self.half + s * self.unit, self.unit), self.unit)

    def copy(self, kind, s, first=False):
        src, at, to = (
            (self.rbuf, self.near(s), self.near(s)),
            (self.lbuf, self.near(s), self.near(s)),
            (self.out, self.near(s), self.near(s)),
            (self.out, self.far(s), self.far(s)),
        )[kind]
        dst = src
        if first:
            src, at = self.part, (self.far(s) if kind == 0 else self.near(s))
        return pltpu.make_async_remote_copy(
            src_ref=src.at[at],
            dst_ref=dst.at[to],
            send_sem=self.ssem.at[kind, s],
            recv_sem=self.rsem.at[kind, s],
            device_id=to_head(self.z + (1 if kind % 2 == 0 else -1)),
            device_id_type=pl.DeviceIdType.MESH,
        )

    def step(self, k):
        z, lag, last = self.z, self.lag, self.n - 1

        def inside(s):
            return both(s >= 0, s < self.subs)

        for kind, buf in ((0, self.rbuf), (1, self.lbuf)):
            hops = z if kind == 0 else last - z
            s = k - lag * hops

            @pl.when(both(inside(s), hops == 0))
            def _(kind=kind, s=s):
                self.copy(kind, s, True).start()

            @pl.when(both(inside(s), both(hops > 0, hops < last)))
            def _(kind=kind, s=s, buf=buf):
                self.copy(kind, s).wait_recv()
                at = self.near(s)
                own = self.part[self.far(s) if kind == 0 else at]
                buf[at] = (buf[at].astype(F32) + own.astype(F32)).astype(BF)
                self.copy(kind, s).start()

            @pl.when(both(inside(s), hops == last))
            def _(kind=kind, s=s, buf=buf):
                self.copy(kind, s).wait_recv()
                to = self.far(s) if kind == 0 else self.near(s)
                total = buf[self.near(s)].astype(F32) + self.part[to].astype(F32)
                if self.finalize is not None:
                    total = self.finalize(self.near(s), to, total)
                self.out[to] = total.astype(BF)
                self.copy(3 - kind, s).start()

        for kind in (2, 3):
            hops = z if kind == 2 else last - z
            s = k - lag * (last + hops)

            @pl.when(both(inside(s), hops > 0))
            def _(kind=kind, s=s, hops=hops):
                self.copy(kind, s).wait_recv()

                @pl.when(hops < last)
                def _():
                    self.copy(kind, s).start()

    def run(self, first, last):
        def one(k, c):
            self.step(k)
            return c

        lax.fori_loop(first, last, one, 0)

    def drain(self):
        def one(s, c):
            for kind in range(4):

                @pl.when(self.z < self.n - 1 if kind % 2 == 0 else self.z > 0)
                def _(kind=kind):
                    self.copy(kind, s).wait_send()

            return c

        lax.fori_loop(0, self.subs, one, 0)


def chain_scratch(rows, width, subs):
    return [
        pltpu.VMEM((rows // 2, width), BF),
        pltpu.VMEM((rows // 2, width), BF),
        pltpu.SemaphoreType.DMA((4, subs)),
        pltpu.SemaphoreType.DMA((4, subs)),
    ]


SUBS, LAG, BACK_LAG = 16, 2, 2
ANY = pl.BlockSpec(memory_space=pl.ANY)
BIG = VMEM_BYTES - (1 << 20)


def norm_parts(values):
    r = lax.rsqrt(jnp.mean(values * values, axis=-1, keepdims=True) + EPSILON)
    return r, values * r


def fold8(x):
    return jnp.sum(x.reshape(x.shape[0] // 8, 8, x.shape[1]), axis=0)


def half_loads(z, n, half, whole, halves, sem):
    at = pl.ds(pl.multiple_of(jnp.where(z == 0, 0, half), half), half)
    pairs = [(ref.at[at], to) for ref, to in whole] + halves
    return [pltpu.make_async_copy(ref, to, sem.at[i]) for i, (ref, to) in enumerate(pairs)]


def run_with_loads(ch, end, loads, after_sums):
    @pl.when(end)
    def _():
        for c in loads:
            c.start()

    need = ch.lag * (ch.n - 1)
    ch.run(0, need)

    @pl.when(end)
    def _():
        for c in loads:
            c.wait()

    ch.run(need, need + ch.subs)
    after_sums()
    ch.run(need + ch.subs, ch.steps)


def ffn_kernel(
    n, subs, lag, blocks, tile,
    h_any, g_any, wgu_any, wd_any, x_any, attn_any, live_ref, vec_ref,
    out_ref, sum_ref, dmid_any, fpart_any, wg_any,
    rbuf, lbuf, ssem, rsem, hv, gv, wgu, wd, xv, av, part_ref, dgu, hid, dffn, fpart, dmid, wbuf, csem, osem, tsem,
):
    z = lax.axis_index("head")
    rows, width = hv.shape
    ff = wd.shape[0]
    half = rows // 2
    rb = half // blocks
    end = jnp.logical_or(z == 0, z == n - 1)
    loads = [pltpu.make_async_copy(a, b, csem.at[i]) for i, (a, b) in enumerate(((h_any, hv), (wgu_any, wgu), (g_any, gv), (wd_any, wd)))]
    for c in loads:
        c.start()
    mine = pl.ds(pl.multiple_of(jnp.where(z == 0, 0, half), half), half)
    end_loads = [pltpu.make_async_copy(a.at[mine], b, csem.at[4 + i]) for i, (a, b) in enumerate(((x_any, xv), (attn_any, av)))]

    @pl.when(end)
    def _():
        for c in end_loads:
            c.start()

    sum_ref[...] = jnp.zeros_like(sum_ref)
    line_barrier(z, n)
    tanh_attn, gain, tanh_ffn = vec_ref[0:1], vec_ref[1:2], vec_ref[3:4]

    def finalize(at, to, dh):
        attn, live = av[at], live_ref[to, 0:1]
        mid = xv[at].astype(F32) + live * tanh_attn * attn
        r, u = norm_parts(mid)
        w = dh * gain
        grad = gv[to].astype(F32) + r * (w - u * jnp.mean(w * u, axis=-1, keepdims=True))
        dmid[at] = grad
        masked = grad * live
        sum_ref[0:8] += fold8(dh * u)
        sum_ref[8:16] += fold8(masked * attn)
        return masked * tanh_attn

    ch = Chain(n, subs, lag, part_ref, out_ref, rbuf, lbuf, ssem, rsem, finalize)

    def step(k):
        @pl.when(jnp.logical_and(end, k == lag * (n - 1)))
        def _():
            for c in end_loads:
                c.wait()

        ch.step(k)

    per = subs // blocks

    def block(t, c):
        near = pl.ds(pl.multiple_of(t * rb, rb), rb)
        far = pl.ds(pl.multiple_of(half + t * rb, rb), rb)

        def put(ref, v):
            ref[near] = v[:rb]
            ref[far] = v[rb:]

        @pl.when(t == 0)
        def _():
            loads[0].wait()
            loads[1].wait()

        gu = nn(jnp.concatenate([hv[near], hv[far]], axis=0), wgu[...])
        gate, up = gu[:, :ff], gu[:, ff:]
        sig = 1.0 / (1.0 + jnp.exp(-gate))
        act = gate * sig
        hidden = (act * up).astype(BF)
        put(hid, hidden)

        @pl.when(t == 0)
        def _():
            loads[2].wait()
            loads[3].wait()

        grad = jnp.concatenate([gv[near].astype(F32) * live_ref[near, 0:1], gv[far].astype(F32) * live_ref[far, 0:1]], axis=0)
        low = (grad * tanh_ffn).astype(BF)
        put(dffn, low)
        dhid = nt(low, wd[...])
        both_grads = jnp.concatenate(
            [(dhid * up * (sig + act * (1.0 - sig))).astype(BF), (dhid * act).astype(BF)], axis=1
        )
        put(dgu, both_grads)
        put(part_ref, nt(both_grads, wgu[...]).astype(BF))

        def some(i, c):
            step(t * per + i)
            return c

        lax.fori_loop(0, per, some, 0)
        put(fpart, nn(hidden, wd[...]).astype(BF))
        return c

    lax.fori_loop(0, blocks, block, 0)
    fcopy = pltpu.make_async_copy(fpart, fpart_any, osem.at[0])
    fcopy.start()

    tiles = width // tile
    every = max(1, (ch.steps - subs) // tiles)

    def tile_copy(j):
        return pltpu.make_async_copy(wbuf.at[lax.rem(j, 2)], wg_any.at[pl.ds(pl.multiple_of(j * tile, tile), tile)], tsem.at[j])

    def weights(j, c):
        def some(i, c):
            step(subs + j * every + i)
            return c

        lax.fori_loop(0, every, some, 0)

        @pl.when(j >= 2)
        def _():
            tile_copy(j - 2).wait()

        cols = pl.ds(pl.multiple_of(j * tile, tile), tile)
        slot = lax.rem(j, 2)
        wbuf[slot, :, : 2 * ff] = tn(hv[:, cols], dgu[...]).astype(BF)
        wbuf[slot, :, 2 * ff :] = tn(dffn[:, cols], hid[...]).astype(BF)
        tile_copy(j).start()
        return c

    lax.fori_loop(0, tiles, weights, 0)

    def rest(k, c):
        step(k)
        return c

    lax.fori_loop(subs + tiles * every, ch.steps, rest, 0)
    dcopy = pltpu.make_async_copy(dmid, dmid_any, osem.at[1])

    @pl.when(end)
    def _():
        dcopy.start()

    for j in range(max(0, tiles - 2), tiles):
        tile_copy(j).wait()
    fcopy.wait()
    ch.drain()

    @pl.when(end)
    def _():
        dcopy.wait()


def ffn_exchange(h, g, wgu, wd, x, attn, live, vec, cid, subs=16, lag=4, blocks=4, tile=256):
    n = lax.axis_size("head")
    rows, width = h.shape
    ff = wd.shape[0]
    half = rows // 2
    vm = pltpu.VMEM
    return pl.pallas_call(
        functools.partial(ffn_kernel, n, subs, lag, blocks, tile),
        out_shape=(
            S((rows, width), BF),
            S((16, width), F32),
            S((half, width), F32),
            S((rows, width), BF),
            S((width, 3 * ff), BF),
        ),
        in_specs=[ANY] * 6 + [VM] * 2,
        out_specs=(VM, VM, ANY, ANY, ANY),
        scratch_shapes=chain_scratch(rows, width, subs)
        + [
            vm((rows, width), BF),
            vm((rows, width), BF),
            vm((width, 2 * ff), BF),
            vm((ff, width), BF),
            vm((half, width), BF),
            vm((half, width), F32),
            vm((rows, width), BF),
            vm((rows, 2 * ff), BF),
            vm((rows, ff), BF),
            vm((rows, width), BF),
            vm((rows, width), BF),
            vm((half, width), F32),
            vm((2, tile, 3 * ff), BF),
            pltpu.SemaphoreType.DMA((6,)),
            pltpu.SemaphoreType.DMA((2,)),
            pltpu.SemaphoreType.DMA((width // tile,)),
        ],
        compiler_params=pltpu.CompilerParams(collective_id=cid, has_side_effects=True, vmem_limit_bytes=BIG),
        cost_estimate=pl.CostEstimate(flops=100_000_000_000, bytes_accessed=30 * rows * width, transcendentals=0),
        name="ffn_exchange",
    )(h, g, wgu, wd, x, attn, live, vec)


def chain_rows_kernel(
    n, part_ref, x_ref, dmid_ref, gain_ref, sum_ref, out_ref, tot_ref, rbuf, lbuf, ssem, rsem, xv, dv, csem, acc, ends, esem, fsem
):
    z = lax.axis_index("head")
    line_barrier(z, n)
    acc[...] = jnp.zeros_like(acc)
    gain = gain_ref[0:1]

    def finalize(at, to, dh):
        r, u = norm_parts(xv[at].astype(F32))
        w = dh * gain
        acc[...] += fold8(dh * u)
        return dv[at] + r * (w - u * jnp.mean(w * u, axis=-1, keepdims=True))

    ch = Chain(n, SUBS, LAG, part_ref, out_ref, rbuf, lbuf, ssem, rsem, finalize)
    loads = half_loads(z, n, ch.half, [(x_ref, xv)], [(dmid_ref, dv)], csem)
    width = acc.shape[1]

    def copy(e):
        return pltpu.make_async_remote_copy(
            src_ref=ends.at[e],
            dst_ref=ends.at[e],
            send_sem=esem.at[e],
            recv_sem=fsem.at[e],
            device_id=to_head(z + (1 if e == 0 else -1)),
            device_id_type=pl.DeviceIdType.MESH,
        )

    def send_sums():
        rows = [sum_ref[0:8], sum_ref[8:16], acc[...]]
        mine = jnp.concatenate([jnp.sum(r, axis=0, keepdims=True) for r in rows] + [jnp.zeros((5, width), F32)], axis=0)
        for e, source in ((0, 0), (1, n - 1)):

            @pl.when(z == source)
            def _(e=e):
                ends[e] = mine
                copy(e).start()

    run_with_loads(ch, jnp.logical_or(z == 0, z == n - 1), loads, send_sums)

    for e, source, sink in ((0, 0, n - 1), (1, n - 1, 0)):

        @pl.when(z != source)
        def _(e=e, sink=sink):
            copy(e).wait_recv()

            @pl.when(z != sink)
            def _():
                copy(e).start()

    tot_ref[...] = ends[0] + ends[1]
    for e, sink in ((0, n - 1), (1, 0)):

        @pl.when(z != sink)
        def _(e=e):
            copy(e).wait_send()

    ch.drain()


def chain_rows(part, x, dmid, gain, sums, cid):
    n = lax.axis_size("head")
    rows, width = part.shape
    half = rows // 2
    return pl.pallas_call(
        functools.partial(chain_rows_kernel, n),
        out_shape=(S((rows, width), BF), S((8, width), F32)),
        in_specs=[VM, ANY, ANY, VM, VM],
        out_specs=(VM,) * 2,
        scratch_shapes=chain_scratch(rows, width, SUBS)
        + [
            pltpu.VMEM((half, width), BF),
            pltpu.VMEM((half, width), F32),
            pltpu.SemaphoreType.DMA((2,)),
            pltpu.VMEM((8, width), F32),
            pltpu.VMEM((2, 8, width), F32),
            pltpu.SemaphoreType.DMA((2,)),
            pltpu.SemaphoreType.DMA((2,)),
        ],
        compiler_params=pltpu.CompilerParams(collective_id=cid, has_side_effects=True, vmem_limit_bytes=BIG),
        cost_estimate=pl.CostEstimate(flops=80_000_000_000, bytes_accessed=20 * rows * width, transcendentals=0),
        name="chain_rows",
    )(part, x, dmid, gain, sums)


def share_kernel(n, piece_ref, all_ref, ssem, rsem):
    z = lax.axis_index("head")
    head_barrier(z, n)

    def copy(i):
        return pltpu.make_async_remote_copy(
            src_ref=piece_ref,
            dst_ref=all_ref.at[z],
            send_sem=ssem.at[i],
            recv_sem=rsem.at[i],
            device_id=to_head(lax.rem(z + i, n)),
            device_id_type=pl.DeviceIdType.MESH,
        )

    for i in range(1, n):
        copy(i).start()
    all_ref[z] = piece_ref[...]
    for i in range(1, n):
        copy(i).wait()


def share(piece, cid):
    n = lax.axis_size("head")
    return pl.pallas_call(
        functools.partial(share_kernel, n),
        out_shape=S((n,) + piece.shape, piece.dtype),
        in_specs=[VM],
        out_specs=VM,
        scratch_shapes=[pltpu.SemaphoreType.DMA((n,)), pltpu.SemaphoreType.DMA((n,))],
        compiler_params=pltpu.CompilerParams(collective_id=cid, has_side_effects=True, vmem_limit_bytes=BIG),
        name="share",
    )(piece)


def wgrad_kernel(a_ref, b_ref, c_ref, d_ref, o_ref):
    nb = b_ref.shape[1]
    o_ref[:, :nb] = tn(a_ref[...], b_ref[...]).astype(BF)
    o_ref[:, nb:] = tn(c_ref[...], d_ref[...]).astype(BF)


def wgrad_pair(a, b, c, d):
    rows, width = a.shape
    cols = b.shape[1] + d.shape[1]
    wb = min(256, width)
    return pl.pallas_call(
        wgrad_kernel,
        grid=(width // wb,),
        in_specs=[
            pl.BlockSpec((rows, wb), lambda i: (0, i)),
            pl.BlockSpec(b.shape, lambda i: (0, 0)),
            pl.BlockSpec((rows, wb), lambda i: (0, i)),
            pl.BlockSpec(d.shape, lambda i: (0, 0)),
        ],
        out_specs=pl.BlockSpec((wb, cols), lambda i: (i, 0)),
        out_shape=S((width, cols), BF),
        compiler_params=pltpu.CompilerParams(vmem_limit_bytes=BIG),
        cost_estimate=pl.CostEstimate(flops=2 * rows * width * cols, bytes_accessed=2 * width * cols, transcendentals=0),
        name="wgrad_pair",
    )(a, b, c, d)


def qkv_kernel(
    n, x_ref, gain_ref, w_ref, hg_ref, cos_ref, sin_ref, live_ref, slice_ref, h_ref, pre_ref, q_ref, kv_ref, all_ref, ssem, rsem
):
    z = lax.axis_index("head")

    def copy(i):
        return pltpu.make_async_remote_copy(
            src_ref=slice_ref,
            dst_ref=all_ref.at[z],
            send_sem=ssem.at[i],
            recv_sem=rsem.at[i],
            device_id=to_head(lax.rem(z + i, n)),
            device_id_type=pl.DeviceIdType.MESH,
        )

    own = pltpu.make_async_copy(slice_ref, all_ref.at[z], ssem.at[0])

    @pl.when(pl.program_id(0) == 0)
    def _():
        head_barrier(z, n)
        own.start()
        for i in range(1, n):
            copy(i).start()

    x = x_ref[...].astype(F32)
    h = (x * lax.rsqrt(jnp.mean(x * x, axis=-1, keepdims=True) + EPSILON) * gain_ref[...]).astype(BF)
    h_ref[...] = h
    width = w_ref.shape[2]
    cos, sin, live = cos_ref[...], sin_ref[...], live_ref[...]
    for part in range(2):
        pre = nn(h, w_ref[part])
        pre_ref[:, part * width : (part + 1) * width] = pre
        for p in range(width // 128):
            v = pre[:, p * 128 : (p + 1) * 128]
            r = lax.rsqrt(head_mean(v * v) + EPSILON)
            t = v * r * hg_ref[part : part + 1, p * 128 : (p + 1) * 128]
            y = t * cos + swap_halves(t) * sin
            if part == 0:
                q_ref[:, p * 128 : (p + 1) * 128] = y.astype(BF)
            else:
                kv_ref[:, p * 128 : (p + 1) * 128] = (y * live).astype(BF)
    val = nn(h, w_ref[2])
    for p in range(width // 128):
        kv_ref[:, width + p * 128 : width + (p + 1) * 128] = (val[:, p * 128 : (p + 1) * 128] * live).astype(BF)

    @pl.when(pl.program_id(0) == pl.num_programs(0) - 1)
    def _():
        own.wait()
        for i in range(1, n):
            copy(i).wait()


def make_qkv(x, gain, w, head_gains, cos, sin, live, out_slice, cid):
    n = lax.axis_size("head")
    rows, width = x.shape
    inner = w.shape[2]
    rb = min(256, rows)
    return pl.pallas_call(
        functools.partial(qkv_kernel, n),
        grid=(rows // rb,),
        in_specs=[
            pl.BlockSpec((rb, width), lambda i: (i, 0)),
            pl.BlockSpec((1, width), lambda i: (0, 0)),
            pl.BlockSpec(w.shape, lambda i: (0, 0, 0)),
            pl.BlockSpec((8, inner), lambda i: (0, 0)),
            pl.BlockSpec((rb, 128), lambda i: (i, 0)),
            pl.BlockSpec((rb, 128), lambda i: (i, 0)),
            pl.BlockSpec((rb, 128), lambda i: (i, 0)),
            ANY,
        ],
        out_specs=(
            pl.BlockSpec((rb, width), lambda i: (i, 0)),
            pl.BlockSpec((rb, 2 * inner), lambda i: (i, 0)),
            pl.BlockSpec((rb, inner), lambda i: (i, 0)),
            pl.BlockSpec((rb, 2 * inner), lambda i: (i, 0)),
            ANY,
        ),
        out_shape=(
            S((rows, width), BF),
            S((rows, 2 * inner), F32),
            S((rows, inner), BF),
            S((rows, 2 * inner), BF),
            S((n,) + out_slice.shape, BF),
        ),
        scratch_shapes=[pltpu.SemaphoreType.DMA((n,)), pltpu.SemaphoreType.DMA((n,))],
        compiler_params=pltpu.CompilerParams(collective_id=cid, has_side_effects=True, vmem_limit_bytes=BIG),
        cost_estimate=pl.CostEstimate(flops=6 * rows * width * inner, bytes_accessed=12 * rows * width, transcendentals=0),
        name="make_qkv",
    )(x, gain, w, head_gains, cos, sin, live, out_slice)


def qkv_back_kernel(dq_ref, dkv_ref, peer_ref, pre_ref, hg_ref, cos_ref, sin_ref, w_ref, dpre_ref, gg_ref, dh_ref):
    width = dq_ref.shape[1]
    rows = dq_ref.shape[0]

    @pl.when(pl.program_id(0) == 0)
    def _():
        gg_ref[...] = jnp.zeros_like(gg_ref)

    cos, sin = cos_ref[...], sin_ref[...]
    total = None
    for part in range(2):
        for p in range(width // 128):
            ls = slice(p * 128, (p + 1) * 128)
            pls = slice(part * width + p * 128, part * width + (p + 1) * 128)
            if part == 0:
                dy = dq_ref[:, ls]
            else:
                dy = dkv_ref[:, ls] + peer_ref[:, ls].astype(F32)
            dt = dy * cos - swap_halves(dy) * sin
            v = pre_ref[:, pls]
            r = lax.rsqrt(head_mean(v * v) + EPSILON)
            u = v * r
            w = dt * hg_ref[part : part + 1, ls]
            dv = r * (w - u * head_mean(w * u))
            dpre_ref[:, pls] = dv.astype(BF)
            gg_ref[part * 8 : part * 8 + 8, ls] += jnp.sum((dt * u).reshape(rows // 8, 8, 128), axis=0)
        g = nt(dpre_ref[:, part * width : (part + 1) * width], w_ref[part])
        total = g if total is None else total + g
    dpre_ref[:, 2 * width :] = (dkv_ref[:, width:] + peer_ref[:, width:].astype(F32)).astype(BF)
    total = total + nt(dpre_ref[:, 2 * width :], w_ref[2])
    dh_ref[...] = total.astype(BF)


def qkv_back(dq, dkv, peer, pre, head_gains, cos, sin, w):
    rows, inner = dq.shape
    width = w.shape[1]
    rb = min(256, rows)
    blk = lambda c: pl.BlockSpec((rb, c), lambda i: (i, 0))
    return pl.pallas_call(
        qkv_back_kernel,
        grid=(rows // rb,),
        in_specs=[
            blk(inner),
            blk(2 * inner),
            blk(2 * inner),
            blk(2 * inner),
            pl.BlockSpec((8, inner), lambda i: (0, 0)),
            blk(128),
            blk(128),
            pl.BlockSpec(w.shape, lambda i: (0, 0, 0)),
        ],
        out_specs=(blk(3 * inner), pl.BlockSpec((16, inner), lambda i: (0, 0)), blk(width)),
        out_shape=(S((rows, 3 * inner), BF), S((16, inner), F32), S((rows, width), BF)),
        compiler_params=pltpu.CompilerParams(vmem_limit_bytes=BIG),
        cost_estimate=pl.CostEstimate(flops=6 * rows * width * inner, bytes_accessed=12 * rows * width, transcendentals=0),
        name="qkv_back",
    )(dq, dkv, peer, pre, head_gains, cos, sin, w)


def middle_kernel(mixed_ref, w_ref, x_ref, live_ref, vec_ref, attn_ref, h_ref):
    total = None
    for g in range(mixed_ref.shape[0]):
        t = nn(mixed_ref[g], w_ref[g]).astype(BF).astype(F32)
        total = t if total is None else total + t
    attn_ref[...] = total
    mid = x_ref[...].astype(F32) + live_ref[:, 0:1] * vec_ref[0:1] * total
    _, u = norm_parts(mid)
    h_ref[...] = (u * vec_ref[1:2]).astype(BF)


def make_middle(mixed_all, w_all, x, live, vec):
    n, rows, inner = mixed_all.shape
    width = x.shape[1]
    rb = min(256, rows)
    blk = lambda c: pl.BlockSpec((rb, c), lambda i: (i, 0))
    return pl.pallas_call(
        middle_kernel,
        grid=(rows // rb,),
        in_specs=[
            pl.BlockSpec((n, rb, inner), lambda i: (0, i, 0)),
            pl.BlockSpec(w_all.shape, lambda i: (0, 0, 0)),
            blk(width),
            blk(128),
            pl.BlockSpec((8, width), lambda i: (0, 0)),
        ],
        out_specs=(blk(width), blk(width)),
        out_shape=(S((rows, width), F32), S((rows, width), BF)),
        compiler_params=pltpu.CompilerParams(vmem_limit_bytes=BIG),
        cost_estimate=pl.CostEstimate(flops=2 * n * rows * width * inner, bytes_accessed=14 * rows * width, transcendentals=0),
        name="make_middle",
    )(mixed_all, w_all, x, live, vec)


def attend_kernel(
    n, scale, qb, kc, q_ref, kv_ref, peer_ref, live_ref, ck_ref, cv_ref, gate_ref, mixed_ref, self_ref, cross_ref, lse_ref,
    va_ref, cva_ref, ssem, rsem,
):
    z = lax.axis_index("head")
    line_barrier(z, n)
    rows, width = q_ref.shape
    txt = ck_ref.shape[0]
    c = scale * LOG2E
    va_ref[:, 128:] = live_ref[...]
    cva_ref[:, 128:] = jnp.ones((txt, 128), BF)
    first = lax.broadcasted_iota(jnp.int32, (qb, 128), 1) < 64

    def copy(kind, o, p):
        view = mixed_ref.at[o, :, pl.ds(pl.multiple_of(p * 128, 128), 128)]
        return pltpu.make_async_remote_copy(
            src_ref=view,
            dst_ref=view,
            send_sem=ssem.at[kind, o, p],
            recv_sem=rsem.at[kind, o, p],
            device_id=to_head(z + (1 if kind == 0 else -1)),
            device_id_type=pl.DeviceIdType.MESH,
        )

    def send_own(p):
        @pl.when(z < n - 1)
        def _():
            copy(0, z, p).start()

        @pl.when(z > 0)
        def _():
            copy(1, z, p).start()

    def relay(d, p):
        @pl.when(z - d >= 0)
        def _():
            copy(0, z - d, p).wait_recv()

            @pl.when(z < n - 1)
            def _():
                copy(0, z - d, p).start()

        @pl.when(z + d < n)
        def _():
            copy(1, z + d, p).wait_recv()

            @pl.when(z > 0)
            def _():
                copy(1, z + d, p).start()

    def pair(p, _):
        lanes = pl.ds(pl.multiple_of(p * 128, 128), 128)
        vlanes = pl.ds(pl.multiple_of(width + p * 128, 128), 128)
        va_ref[:rows, :128] = kv_ref[:, vlanes]
        va_ref[rows:, :128] = peer_ref[:, vlanes]
        cva_ref[:, :128] = cv_ref[:, lanes]
        gate = gate_ref[:, lanes]

        def block(b, _):
            rs = pl.ds(pl.multiple_of(b * qb, qb), qb)
            qp = q_ref[rs, lanes]
            outs, couts = [], []
            for a in range(2):
                qm = jnp.where(first if a == 0 else jnp.logical_not(first), qp, jnp.zeros_like(qp))
                acc = None
                for side in range(2):
                    keys = kv_ref if side == 0 else peer_ref
                    for j in range(0, rows, kc):
                        s = nt(qm, keys[j : j + kc, lanes])
                        pr = jnp.exp2(s * c).astype(BF)
                        o = nn(pr, va_ref[side * rows + j : side * rows + j + kc, :])
                        acc = o if acc is None else acc + o
                outs.append(acc)
                s = nt(qm, ck_ref[:, lanes])
                couts.append(nn(jnp.exp2(s * c).astype(BF), cva_ref[...]))
            so = jnp.where(first, outs[0][:, :128], outs[1][:, :128])
            sl = jnp.where(first, outs[0][:, 128:], outs[1][:, 128:])
            co = jnp.where(first, couts[0][:, :128], couts[1][:, :128])
            cl = jnp.where(first, couts[0][:, 128:], couts[1][:, 128:])
            so = so / sl
            co = co / cl
            mixed_ref[z, rs, lanes] = (so + gate * co).astype(BF)
            self_ref[rs, lanes] = so
            cross_ref[rs, lanes] = co
            lt = jnp.log2(sl).T
            ct = jnp.log2(cl).T
            lse_ref[p, :, rs] = jnp.concatenate([lt[0:1], lt[64:65], ct[0:1], ct[64:65], lt[0:4]], axis=0)
            return 0

        lax.fori_loop(0, rows // qb, block, 0)

        @pl.when(p >= 1)
        def _():
            relay(1, p - 1)

        send_own(p)
        return 0

    pairs = width // 128
    lax.fori_loop(0, pairs, pair, 0)
    for t in range(pairs + n - 2):
        for d in range(1, n):
            if 0 <= t - (d - 1) < pairs and (d > 1 or t == pairs - 1):
                relay(d, t - (d - 1))
    for p in range(pairs):
        for o in range(n):

            @pl.when(both(z >= o, z < n - 1))
            def _(o=o, p=p):
                copy(0, o, p).wait_send()

            @pl.when(both(z <= o, z > 0))
            def _(o=o, p=p):
                copy(1, o, p).wait_send()


def attend(q, kv, peer, live, ck, cv, gate, scale, cid, qb=256, kc=1024):
    n = lax.axis_size("head")
    rows, width = q.shape
    txt = ck.shape[0]
    qb, kc = min(qb, rows), min(kc, rows)
    return pl.pallas_call(
        functools.partial(attend_kernel, n, scale, qb, kc),
        out_shape=(S((n, rows, width), BF), S((rows, width), F32), S((rows, width), F32), S((width // 128, 8, rows), F32)),
        in_specs=[VM] * 7,
        out_specs=(VM,) * 4,
        scratch_shapes=[
            pltpu.VMEM((2 * rows, 256), BF),
            pltpu.VMEM((txt, 256), BF),
            pltpu.SemaphoreType.DMA((2, n, width // 128)),
            pltpu.SemaphoreType.DMA((2, n, width // 128)),
        ],
        compiler_params=pltpu.CompilerParams(collective_id=cid, has_side_effects=True, vmem_limit_bytes=BIG),
        cost_estimate=pl.CostEstimate(flops=32 * rows * rows * width, bytes_accessed=12 * rows * width, transcendentals=0),
        name="attend",
    )(q, kv, peer, live, ck, cv, gate)


def head_sum(x):
    ind = (lax.broadcasted_iota(jnp.int32, (8, 128), 0) == lax.broadcasted_iota(jnp.int32, (8, 128), 1) // 64).astype(F32)
    return lax.dot_general(ind, x, (((1,), (1,)), ((), ())), preferred_element_type=F32, precision=HIGHEST)


def cross_back_kernel(
    scale, qb, q_ref, ck_ref, cv_ref, gate_ref, cross_ref, lse_ref, da_ref, wo_ref,
    dq_ref, dckv_ref, gg_ref, dm_ref, ckt_ref, p_ref, d_ref, dk_ref, dv_ref,
):
    rows, width = q_ref.shape

    def project(b, _):
        rs = pl.ds(pl.multiple_of(b * qb, qb), qb)
        dm_ref[rs] = nt(da_ref[rs], wo_ref[...]).astype(BF)
        return 0

    lax.fori_loop(0, rows // qb, project, 0)
    txt = ck_ref.shape[0]
    c = scale * LOG2E
    first = lax.broadcasted_iota(jnp.int32, (qb, 128), 1) < 64

    def pair(p, _):
        lanes = pl.ds(pl.multiple_of(p * 128, 128), 128)
        ckt_ref[...] = ck_ref[:, lanes].T
        gate = gate_ref[:, lanes]
        dk_ref[...] = jnp.zeros_like(dk_ref)
        dv_ref[...] = jnp.zeros_like(dv_ref)
        gg_ref[:, lanes] = jnp.zeros((8, 128), F32)

        def block(b, _):
            rs = pl.ds(pl.multiple_of(b * qb, qb), qb)
            qp = q_ref[rs, lanes]
            dmf = dm_ref[rs, lanes].astype(F32)
            dcf = (gate * dmf).astype(BF)
            cross = cross_ref[rs, lanes]
            gg_ref[:, lanes] += fold8(dmf * cross)
            delta = head_sum(dcf.astype(F32) * cross)
            z = jnp.zeros_like(qp)
            masks = (first, jnp.logical_not(first))
            qs = [jnp.where(m, qp, z) for m in masks]
            dcs = [jnp.where(m, dcf, z) for m in masks]
            lse = lse_ref[p, :, rs]
            dqt = []
            for a in range(2):
                s = nt(ck_ref[:, lanes], qs[a])
                pr = jnp.exp2(s * c - lse[2 + a : 3 + a])
                dp = nt(cv_ref[:, lanes], dcs[a])
                p_ref[:, a * qb : (a + 1) * qb] = pr.astype(BF)
                dd = (pr * (dp - delta[a : a + 1])).astype(BF)
                d_ref[:, a * qb : (a + 1) * qb] = dd
                dqt.append(nn(ckt_ref[a * 64 : (a + 1) * 64, :], dd))
            dv_ref[...] += nn(p_ref[...], jnp.concatenate(dcs, axis=0))
            dk_ref[...] += nn(d_ref[...], jnp.concatenate(qs, axis=0))
            dq_ref[rs, lanes] = (jnp.concatenate(dqt, axis=0) * scale).T
            return 0

        lax.fori_loop(0, rows // qb, block, 0)
        dckv_ref[:, lanes] = (dk_ref[...] * scale).astype(BF)
        dckv_ref[:, pl.ds(pl.multiple_of(width + p * 128, 128), 128)] = dv_ref[...].astype(BF)
        return 0

    lax.fori_loop(0, width // 128, pair, 0)


def cross_back(q, ck, cv, gate, co, lse, da, wo, scale, qb=512):
    rows, width = q.shape
    txt = ck.shape[0]
    qb = min(qb, rows)
    return pl.pallas_call(
        functools.partial(cross_back_kernel, scale, qb),
        out_shape=(S((rows, width), F32), S((txt, 2 * width), BF), S((8, width), F32), S((rows, width), BF)),
        in_specs=[VM] * 8,
        out_specs=(VM,) * 4,
        scratch_shapes=[pltpu.VMEM((128, txt), BF), pltpu.VMEM((txt, 2 * qb), BF), pltpu.VMEM((txt, 2 * qb), BF), pltpu.VMEM((txt, 128), F32), pltpu.VMEM((txt, 128), F32)],
        compiler_params=pltpu.CompilerParams(vmem_limit_bytes=BIG),
        cost_estimate=pl.CostEstimate(flops=24 * rows * txt * width, bytes_accessed=12 * rows * width, transcendentals=0),
        name="cross_back",
    )(q, ck, cv, gate, co, lse, da, wo)


def attend_back_kernel(
    n,
    per,
    scale,
    qb,
    kc,
    q_ref,
    kv_ref,
    peer_ref,
    live_ref,
    self_ref,
    lse_ref,
    dm_ref,
    dqc_ref,
    part_ref,
    dq_ref,
    dkv_ref,
    dpeer_ref,
    fsum_ref,
    kt_ref,
    p_ref,
    d_ref,
    ak_ref,
    av_ref,
    rbuf,
    lbuf,
    ssem,
    rsem,
):
    line_barrier(lax.axis_index("head"), n)
    ch = Chain(n, SUBS, BACK_LAG, part_ref, fsum_ref, rbuf, lbuf, ssem, rsem)
    rows, width = q_ref.shape
    c = scale * LOG2E
    first = lax.broadcasted_iota(jnp.int32, (qb, 128), 1) < 64

    def pair(p, _):
        lanes = pl.ds(pl.multiple_of(p * 128, 128), 128)
        vlanes = pl.ds(pl.multiple_of(width + p * 128, 128), 128)
        kt_ref[:, :rows] = kv_ref[:, lanes].T
        kt_ref[:, rows:] = peer_ref[:, lanes].T
        ak_ref[...] = jnp.zeros_like(ak_ref)
        av_ref[...] = jnp.zeros_like(av_ref)

        def block(b, _):
            rs = pl.ds(pl.multiple_of(b * qb, qb), qb)
            qp = q_ref[rs, lanes]
            dm = dm_ref[rs, lanes]
            dmf = dm.astype(F32)
            delta = head_sum(dmf * self_ref[rs, lanes])
            z = jnp.zeros_like(qp)
            masks = (first, jnp.logical_not(first))
            qs = [jnp.where(m, qp, z) for m in masks]
            dms = [jnp.where(m, dm, z) for m in masks]
            qstack = jnp.concatenate(qs, axis=0)
            dstack = jnp.concatenate(dms, axis=0)
            lse = lse_ref[p, :, rs]
            dqt = [None, None]
            for side in range(2):
                src = kv_ref if side == 0 else peer_ref
                for j in range(0, rows, kc):
                    at = side * rows + j
                    for a in range(2):
                        s = nt(src[j : j + kc, lanes], qs[a])
                        pr = jnp.exp2(s * c - lse[a : a + 1])
                        dp = nt(src[j : j + kc, vlanes], dms[a])
                        p_ref[:, a * qb : (a + 1) * qb] = pr.astype(BF)
                        dd = (pr * (dp - delta[a : a + 1])).astype(BF)
                        d_ref[:, a * qb : (a + 1) * qb] = dd
                        t = nn(kt_ref[a * 64 : (a + 1) * 64, at : at + kc], dd)
                        dqt[a] = t if dqt[a] is None else dqt[a] + t
                    av_ref[at : at + kc] += nn(p_ref[...], dstack)
                    ak_ref[at : at + kc] += nn(d_ref[...], qstack)
            dq_ref[rs, lanes] = (jnp.concatenate(dqt, axis=0) * scale).T + dqc_ref[rs, lanes]
            for i in range(per):
                k = (p * (rows // qb) + b) * per + i

                @pl.when(k < ch.steps)
                def _(k=k):
                    ch.step(k)

            return 0

        lax.fori_loop(0, rows // qb, block, 0)
        live = live_ref[...].astype(F32)
        dkv_ref[:, lanes] = ak_ref[:rows] * (live[:rows] * scale)
        dkv_ref[:, vlanes] = av_ref[:rows] * live[:rows]
        dpeer_ref[:, lanes] = (ak_ref[rows:] * (live[rows:] * scale)).astype(BF)
        dpeer_ref[:, vlanes] = (av_ref[rows:] * live[rows:]).astype(BF)
        return 0

    lax.fori_loop(0, width // 128, pair, 0)
    ch.run(min(ch.steps, (width // 128) * (rows // qb) * per), ch.steps)
    ch.drain()


def attend_back(q, kv, peer, live, so, lse, dm, dqc, part, scale, cid, qb=256, kc=512, per=2):
    n = lax.axis_size("head")
    rows, width = q.shape
    qb, kc = min(qb, rows), min(kc, rows)
    return pl.pallas_call(
        functools.partial(attend_back_kernel, n, per, scale, qb, kc),
        out_shape=(
            S((rows, width), F32),
            S((rows, 2 * width), F32),
            S((rows, 2 * width), BF),
            S(part.shape, BF),
        ),
        in_specs=[VM] * 9,
        out_specs=(VM,) * 4,
        scratch_shapes=[
            pltpu.VMEM((128, 2 * rows), BF),
            pltpu.VMEM((kc, 2 * qb), BF),
            pltpu.VMEM((kc, 2 * qb), BF),
            pltpu.VMEM((2 * rows, 128), F32),
            pltpu.VMEM((2 * rows, 128), F32),
        ]
        + chain_scratch(*part.shape, SUBS),
        compiler_params=pltpu.CompilerParams(collective_id=cid, has_side_effects=True, vmem_limit_bytes=BIG),
        cost_estimate=pl.CostEstimate(flops=80 * rows * rows * width, bytes_accessed=20 * rows * width, transcendentals=0),
        name="attend_back",
    )(q, kv, peer, live, so, lse, dm, dqc, part)


def pair_swap(value):
    pairs = [(source, source ^ 1) for source in range(lax.axis_size("seq"))]
    return lax.ppermute(value, "seq", pairs)


def rope_tables(grid_rows, grid_cols, first_token, row_count, head_size):
    stride = grid_cols + 1
    tokens = first_token + jnp.arange(row_count, dtype=jnp.int32)
    valid = tokens < grid_rows * stride
    row_pos = (tokens // stride).astype(F32)
    col_pos = (tokens % stride).astype(F32)
    quarter = head_size // 4
    half = head_size // 2
    lane = jnp.arange(128, dtype=jnp.int32) % half
    frequency = ROPE_BASE ** (-(lane % quarter).astype(F32) / quarter)
    angles = jnp.where(lane[None, :] < quarter, row_pos[:, None], col_pos[:, None]) * frequency[None, :]
    sign = jnp.where(jnp.arange(128) % head_size < half, -1.0, 1.0)
    return jnp.cos(angles), jnp.sin(angles) * sign[None, :], valid


def scatter(v):
    return lax.psum_scatter(v, "seq", scatter_dimension=0, tiled=True)


def local(
    image_rows,
    condition,
    text_feats,
    grid_shape,
    text_slot,
    attn_gain,
    ffn_gain,
    mod_weight,
    mod_bias,
    qkv_weight,
    qk_gains,
    text_kv_weight,
    cross_gate,
    out_weight,
    gate_up_weight,
    down_weight,
    cotangent,
):
    row_count, model_width = image_rows.shape
    head_local, head_size = qk_gains.shape[1], qk_gains.shape[2]
    inner = head_local * head_size
    ff_local = down_weight.shape[0]
    text_local, cap_width = text_feats.shape
    head_count = lax.axis_size("head")
    seq_count = lax.axis_size("seq")
    seq_index = lax.axis_index("seq")
    head_index = lax.axis_index("head")
    image_index = seq_index // 2
    pair_half = seq_index % 2
    score_scale = head_size ** (-0.5)
    image_count = condition.shape[0]

    grid_pair = lax.dynamic_index_in_dim(grid_shape, image_index, 0, keepdims=False)
    cos, sin, valid = rope_tables(grid_pair[0], grid_pair[1], pair_half * row_count, row_count, head_size)
    keep = valid.astype(F32)[:, None]
    live_own = jnp.broadcast_to(keep, (row_count, 128))
    peer_tokens = (1 - pair_half) * row_count + jnp.arange(row_count, dtype=jnp.int32)
    keep_peer = (peer_tokens < grid_pair[0] * (grid_pair[1] + 1)).astype(F32)[:, None]
    live_all = jnp.concatenate([live_own, jnp.broadcast_to(keep_peer, (row_count, 128))], axis=0).astype(BF)

    cond_all = jax.nn.silu(condition.astype(F32)).astype(BF)
    cond_low = lax.dynamic_index_in_dim(cond_all, image_index, 0, keepdims=True)
    mod_piece = jnp.dot(cond_low, mod_weight, preferred_element_type=F32) + mod_bias
    modulation = share(jnp.broadcast_to(mod_piece, (8, model_width)), 4)[:, 0]
    one_attn = 1.0 + modulation[0]
    one_ffn = 1.0 + modulation[2]
    tanh_attn = jnp.tanh(modulation[1])
    tanh_ffn = jnp.tanh(modulation[3])

    head_gains = jnp.concatenate([qk_gains.reshape(3, inner), jnp.zeros((5, inner), F32)], axis=0)
    gate_head = jnp.tanh(cross_gate)
    gate_lanes = jnp.repeat(gate_head, head_size)[None, :]
    qkv_mats = jnp.transpose(qkv_weight, (1, 0, 2))
    same_head = (jnp.arange(inner)[:, None] // head_size == jnp.arange(inner)[None, :] // head_size).astype(F32) / head_size

    text_kv_flat = text_kv_weight.reshape(cap_width, 2 * inner)
    text_proj = jnp.dot(text_feats, text_kv_flat, preferred_element_type=F32)
    cap_pre = text_proj[:, :inner]
    cap_r = lax.rsqrt(jnp.dot(cap_pre * cap_pre, same_head, precision=HIGHEST) + EPSILON)
    cap_u = cap_pre * cap_r
    cap_kv = jnp.concatenate([cap_u * head_gains[2:3], text_proj[:, inner:]], axis=1).astype(BF)
    caps = lax.all_gather(cap_kv, "seq", axis=0, tiled=False)
    slot = lax.dynamic_index_in_dim(text_slot, image_index, 0, keepdims=False)
    cap_own = lax.dynamic_index_in_dim(caps, slot, 0, keepdims=False)
    cap_key, cap_value = cap_own[:, :inner], cap_own[:, inner:]

    slice_rows = inner // seq_count
    out_slice = lax.dynamic_slice_in_dim(out_weight, seq_index * slice_rows, slice_rows, 0)

    normed, pre, query, kv, out_slices = make_qkv(
        image_rows, (attn_gain * one_attn)[None, :], qkv_mats, head_gains, cos, sin, live_own, out_slice, 5
    )
    out_all = lax.all_gather(out_slices, "seq", axis=1, tiled=True)
    kv_peer = pair_swap(kv)
    mixed_all, self_out, cross_out, lse = attend(query, kv, kv_peer, live_all, cap_key, cap_value, gate_lanes, score_scale, 0)
    mixed = lax.dynamic_index_in_dim(mixed_all, head_index, 0, keepdims=False)
    vec = jnp.concatenate([jnp.stack([tanh_attn, ffn_gain * one_ffn, attn_gain * one_attn, tanh_ffn]), jnp.zeros((4, model_width), F32)])
    attn_out, ffn_low = make_middle(mixed_all, out_all, image_rows, live_own, vec)

    gate_up_flat = gate_up_weight.reshape(model_width, 2 * ff_local)
    attn_grad_low, ffn_rows, middle_grad_half, ffn_part, ffn_wgrad = ffn_exchange(
        ffn_low, cotangent, gate_up_flat, down_weight, image_rows, attn_out, live_own, vec, 1
    )
    ffn_wsum = scatter(ffn_wgrad)
    grad_out = cotangent.astype(F32)
    dq_cross, cap_half, gate_rows, mixed_grad = cross_back(
        query, cap_key, cap_value, gate_lanes, cross_out, lse, attn_grad_low, out_weight, score_scale
    )
    cap_grads = lax.all_gather(cap_half, "seq", axis=0, tiled=False)
    dq, dkv, dpeer, ffn_out = attend_back(query, kv, kv_peer, live_all, self_out, lse, mixed_grad, dq_cross, ffn_part, score_scale, 2)
    from_peer = pair_swap(dpeer)
    dq, cap_grads = lax.optimization_barrier((dq, cap_grads))

    own_image = jnp.sum(jnp.where(text_slot == seq_index, jnp.arange(image_count), 0))
    used = jnp.any(text_slot == seq_index).astype(F32)
    two = lax.dynamic_slice_in_dim(cap_grads, 2 * own_image, 2, 0).astype(F32)
    cap_grad = (two[0] + two[1]) * used
    cap_dy, cap_dv = cap_grad[:, :inner], cap_grad[:, inner:]
    cap_w = cap_dy * head_gains[2:3]
    cap_pre_grad = cap_r * (cap_w - cap_u * jnp.dot(cap_w * cap_u, same_head, precision=HIGHEST))
    cap_gain = jnp.sum(cap_dy * cap_u, axis=0)
    text_low = jnp.concatenate([cap_pre_grad, cap_dv], axis=1).astype(BF)
    text_weight_grad = tn(text_feats, text_low).astype(BF)
    text_part = nt(text_low, text_kv_flat).astype(BF)
    dq, dkv, text_part, text_weight_grad, ffn_wsum = lax.optimization_barrier(
        (dq, dkv, text_part, text_weight_grad, ffn_wsum)
    )
    text_sum = lax.psum_scatter(text_part, "head", scatter_dimension=1, tiled=True)
    text_weight_sum = scatter(text_weight_grad)

    ffn_out = ffn_out.astype(F32)
    output = (image_rows.astype(F32) + keep * tanh_attn * attn_out + keep * tanh_ffn * ffn_out).astype(BF)
    gate_ffn_grad = jnp.sum(grad_out * keep * ffn_out, axis=0) * (1.0 - tanh_ffn * tanh_ffn)
    grad_pre, gain_rows, attn_in_part = qkv_back(dq, dkv, from_peer, pre, head_gains, cos, sin, qkv_mats)
    attn_wgrad = wgrad_pair(normed, grad_pre, attn_grad_low, mixed)
    attn_in_part, attn_wgrad, text_sum = lax.optimization_barrier((attn_in_part, attn_wgrad, text_sum))
    attn_wsum = scatter(attn_wgrad)
    text_grad = text_sum.astype(F32)
    rows_grad, row_sums = chain_rows(attn_in_part, image_rows, middle_grad_half, vec[2:], ffn_rows, 3)
    ffn_sum, attn_sum = row_sums[0], row_sums[2]
    gate_attn_grad = row_sums[1] * (1.0 - tanh_attn * tanh_attn)

    mod_grad = jnp.stack([attn_sum * attn_gain, gate_attn_grad, ffn_sum * ffn_gain, gate_ffn_grad])
    own_mod = lax.dynamic_index_in_dim(mod_grad, head_index, 0, keepdims=False)
    gain_grad = jnp.concatenate([gain_rows[0:8].sum(0), gain_rows[8:16].sum(0), cap_gain])
    gate_grad_head = gate_rows.sum(0)
    small = jnp.concatenate([attn_sum * one_attn, ffn_sum * one_ffn, own_mod, gain_grad, gate_grad_head])
    smalls = lax.all_gather(small, "seq", axis=0, tiled=False)
    total = jnp.sum(smalls, axis=0)
    d = model_width
    dl = d // seq_count
    attn_gain_sum = lax.dynamic_slice_in_dim(total[:d], seq_index * dl, dl)
    ffn_gain_sum = lax.dynamic_slice_in_dim(total[d : 2 * d], seq_index * dl, dl)
    mod_bias_sum = lax.dynamic_slice_in_dim(total[2 * d : 3 * d], seq_index * dl, dl)[None, :]
    qk_all = total[3 * d : 3 * d + 3 * inner].reshape(3, head_local, seq_count, head_size // seq_count)
    qk_gain_sum = lax.dynamic_index_in_dim(qk_all, seq_index, 2, keepdims=False)
    gate_sum = total[3 * d + 3 * inner :].reshape(head_local, head_size).sum(-1) * (1.0 - gate_head * gate_head)
    cond_cols = condition.shape[1] // seq_count
    cond_part = lax.dynamic_slice_in_dim(cond_all, seq_index * cond_cols, cond_cols, 1).astype(F32)
    image_mods = smalls[:, 2 * d : 3 * d].reshape(image_count, 2, d).sum(1)
    mod_weight_sum = lax.dot_general(cond_part, image_mods, (((0,), (0,)), ((), ())), precision=HIGHEST)

    split = 2 * ff_local
    ffn_wsum, attn_wsum = ffn_wsum.astype(F32), attn_wsum.astype(F32)
    gate_up_sum = ffn_wsum[:, :split].reshape(-1, 2, ff_local)
    down_sum = ffn_wsum[:, split:].T
    qkv_sum = attn_wsum[:, : 3 * inner].reshape(-1, 3, inner)
    out_sum = attn_wsum[:, 3 * inner :].T
    text_weight_sum = text_weight_sum.astype(F32).reshape(-1, 2, inner)
    return (
        output,
        rows_grad,
        text_grad,
        attn_gain_sum,
        ffn_gain_sum,
        mod_weight_sum,
        mod_bias_sum,
        qkv_sum,
        qk_gain_sum,
        text_weight_sum,
        gate_sum,
        out_sum,
        gate_up_sum,
        down_sum,
    )


def solution(mesh):
    return jax.shard_map(
        local,
        mesh=mesh,
        in_specs=(
            P("seq", None),
            P(),
            P("seq", None),
            P(),
            P(),
            P(),
            P(),
            P(None, "head"),
            P("head", None),
            P(None, None, "head"),
            P(None, "head", None),
            P(None, None, "head"),
            P("head"),
            P("head", None),
            P(None, None, "head"),
            P("head", None),
            P("seq", None),
        ),
        out_specs=(
            P("seq", None),
            P("seq", None),
            P("seq", "head"),
            P("seq"),
            P("seq"),
            P("seq", "head"),
            P("head", "seq"),
            P("seq", None, "head"),
            P(None, "head", "seq"),
            P("seq", None, "head"),
            P("head"),
            P("head", "seq"),
            P("seq", None, "head"),
            P("head", "seq"),
        ),
        check_vma=False,
    )
```
